32 devices in a mesh: dp: 2 (over x), row: 4 (over y, core), col: 4 (over z).
Axes of the slice: x: 2, y: 2, z: 4, core: 2. Of those that a mesh axis runs over, the one named last changes fastest.
Arguments:
- hidden_in: bfloat16 [2, 1536, 1536], P(None, ('dp', 'row'), 'col'), may hold values from -6 to 6
- norm_gain: float32 [1536], replicated, may hold values from 0.5 to 1.5
- w_query: bfloat16 [1536, 1536], P('col', 'row'), may hold values from -0.625 to 0.625
- w_key: bfloat16 [1536, 512], P('col', 'row'), may hold values from -0.625 to 0.625
- w_value: bfloat16 [1536, 512], P('col', 'row'), may hold values from -0.15625 to 0.15625
- w_out: bfloat16 [1536, 1536], P('row', 'col'), may hold values from -1.5 to 1.5
- mix_gain: float32 [1536], replicated, may hold values from 0.5 to 1.5
- w_router: bfloat16 [1536, 32], replicated, may hold values from -0.1875 to 0.1875
- w_gate: bfloat16 [32, 1536, 512], P('dp', ('row', 'col')), may hold values from -0.15625 to 0.15625
- w_up: bfloat16 [32, 1536, 512], P('dp', ('row', 'col')), may hold values from -0.15625 to 0.15625
- w_down: bfloat16 [32, 512, 1536], P('dp', ('row', 'col')), may hold values from -3 to 3
- lengths: int32 [2, 2, 3], P(None, 'dp'), may hold values from 1 to 512, 768 in all within a row
- routes: int32 [2, 1536, 8], P(None, ('dp', 'row', 'col')), may hold values from 0 to 31, all different within a row; in each aligned block of 48 rows (0 to 47, 48 to 95, ..., all dimensions but the last counted through in order) at most 18 rows name the same one
- mask: int32 [2, 1536], P(None, ('dp', 'row', 'col')), may hold values from 0 to 1, as said below
- cotangent: bfloat16 [2, 1536, 1536], P(None, ('dp', 'row', 'col')), may hold values from -6 to 6
Outputs:
- layer_out: bfloat16 [2, 1536, 1536], P(None, ('dp', 'row', 'col'))
- grad_input: float32 [2, 1536, 1536], P(None, ('dp', 'row'), 'col')
- grad_norm_gain: float32 [1536], replicated
- grad_query: float32 [1536, 1536], P('col', 'row')
- grad_key: float32 [1536, 512], P('col', 'row')
- grad_value: float32 [1536, 512], P('col', 'row')
- grad_out_proj: float32 [1536, 1536], P('row', 'col')
- grad_mix_gain: float32 [1536], replicated
- grad_router: float32 [1536, 32], replicated
- grad_gate: float32 [32, 1536, 512], P('dp', ('row', 'col'))
- grad_up: float32 [32, 1536, 512], P('dp', ('row', 'col'))
- grad_down: float32 [32, 512, 1536], P('dp', ('row', 'col'))
The draws below stay inside these ranges and needn't reach their ends.
Inputs may be any that keep to these rules, and one draw needn't show every extreme that they name: The 3 lengths of one micro-batch and dp index sum to 768, and the longest of them is exactly 512. `routes`: each token names 8 different experts. In every aligned block of 48 tokens (the tokens of one device) no expert is named more than 18 times, and the bound 18 is reached. `mask`: in each micro-batch the ones of the 768 tokens of one dp index form a prefix of half of them or more.
All inputs are finite; a program needn't handle non-finite values.
Results may differ from the reference program's by a relative error of at most 0.018.
Values may be sent and summed in bfloat16 or wider, within the bound.
A program may use at most 320 MiB of HBM per device.

```python
import math
import jax
import jax.numpy as jnp
import numpy as np
from jax import lax

D = 1536
HEADS = 24
KV_HEADS = 8
HEAD_DIM = 64
FF = 512
TOP = 8
EXPERTS = 32
MICRO = 2
SEQS = 3
T_GROUP = 768
TOKENS = 1536
TQ = 48
CAP = 18
LONGEST = 512
N_DP = 2
N_ROW = 4
N_COL = 4


def draw_mask(key, part):
    padding = jax.random.randint(key, (MICRO, N_DP), 0, T_GROUP // 2 + 1, dtype=jnp.int32)
    positions = jnp.arange(T_GROUP, dtype=jnp.int32)
    keeping = positions[None, None, :] < (T_GROUP - padding)[:, :, None]
    return keeping.astype(jnp.int32).reshape(MICRO, TOKENS)


def block_scale(own_key, shape, cuts, least, top_value):
    level, own = 1.0, jax.random.fold_in(own_key, 6)
    for axis_at, shards_of in cuts:
        draws = jnp.exp(jax.random.uniform(jax.random.fold_in(own, axis_at), (shards_of,), jnp.float32, least / len(cuts), top_value / len(cuts)))
        level = level * jnp.repeat(draws, shape[axis_at] // shards_of).reshape([-1 if axis == axis_at else 1 for axis in range(len(shape))])
    return level


def profile(number_of, total, reach, slope):
    portions = [(1 << 20) // math.isqrt(standing ** slope) + 1 for standing in range(2, number_of + 1)]
    surplus, holding = total - reach - (number_of - 1), [1] * (number_of - 1)
    while surplus > 0:
        movable = [i for i in range(number_of - 1) if holding[i] < reach]
        mass, left = sum([portions[i] for i in movable]), surplus
        for i in movable:
            extra = min(reach - holding[i], max(1, left * portions[i] // mass), surplus)
            holding[i] = holding[i] + extra
            surplus = surplus - extra
    return np.array([reach] + holding)


def uneven(stream_key, amount, total, most, lean):
    if amount == 2:
        one = jax.random.randint(stream_key, (), max(1, total - most), min(most, total - 1) + 1)
        return jnp.stack([one, total - one])
    tallies = jnp.asarray(profile(amount, total, most, lean), jnp.int32)
    twos = (amount - 1) // 2
    source_of, sink = tallies[1:1 + 2 * twos:2], tallies[2:2 + 2 * twos:2]
    slack = jnp.minimum(source_of - 1, most - sink)
    shifted = jax.random.randint(jax.random.fold_in(stream_key, 1), (twos,), 0, 1 << 20) % (slack + 1)
    tallies = tallies.at[1:1 + 2 * twos:2].set(source_of - shifted).at[2:2 + 2 * twos:2].set(sink + shifted)
    return tallies[jax.random.permutation(jax.random.fold_in(stream_key, 2), amount)]


def assign_block(own_key, own, number, rows, count, top, reach, skew):
    sequence = jax.random.permutation(own_key, count)
    crowded, usual = load_shares(count, rows * top, reach, skew, True), load_shares(count, rows * top, reach, skew, False)
    places = jnp.arange(count)

    def named(sizes, offset_by):
        used = int((sizes > 0).sum())
        fixed = max(1, used // 4)
        passed = fixed + (places - fixed + offset_by * (used - fixed)) % max(1, count - fixed)
        return jnp.zeros((count,), jnp.int32).at[sequence[jnp.where(places < fixed, places, passed)]].set(jnp.asarray(sizes, jnp.int32))

    sizes = jnp.where(number % 4 == 0, named(crowded, number // 4), named(usual, number - number // 4 - 1))
    mixed = jax.random.permutation(jax.random.fold_in(own, 3), count)
    giver, receiver = mixed[0:count // 2 * 2:2], mixed[1:count // 2 * 2:2]
    slack = jnp.minimum(sizes[giver] - 1, reach - sizes[receiver]) // 2
    slack = jnp.where((giver == sequence[0]) | (receiver == sequence[0]) | (sizes[receiver] == 0), 0, jnp.maximum(slack, 0))
    passed = jax.random.randint(jax.random.fold_in(own, 4), (count // 2,), 0, 1 << 20) % (slack + 1)
    sizes = sizes.at[giver].add(-passed).at[receiver].add(passed)
    members = jnp.searchsorted(jnp.cumsum(sizes), jnp.arange(rows * top), side="right").astype(jnp.int32)
    listing = members.reshape(top, rows).T
    listing = listing[jax.random.permutation(jax.random.fold_in(own, 1), rows)]
    offset_by = jax.random.randint(jax.random.fold_in(own, 2), (rows, 1), 0, top)
    return jnp.take_along_axis(listing, (jnp.arange(top)[None, :] + offset_by) % top, axis=1)


def load_shares(amount, total, most, lean, full):
    portions = [(1 << 20) // math.isqrt(rank ** lean) + 1 for rank in range(1, amount + 1)]
    largest = most if full else min(most, max(-(-total // amount), total * portions[0] // sum(portions)))
    least = 1 if total - largest >= amount - 1 else 0
    holding, surplus = [largest] + [least] * (amount - 1), total - largest - least * (amount - 1)
    while surplus > 0:
        free = [i for i in range(1, amount) if holding[i] < largest] or [i for i in range(1, amount) if holding[i] < most]
        mass, remaining = sum([portions[i] for i in free]), surplus
        for i in free:
            extra = min(most - holding[i], max(1, remaining * portions[i] // mass), surplus)
            holding[i] = holding[i] + extra
            surplus = surplus - extra
    return np.array(holding)


def centred(rng, shape, width, reach, split=(), kind=jnp.bfloat16):
    drawn = jax.random.normal(rng, shape, jnp.float32) * width
    if len(split) > 0:
        drawn = block_scale(rng, shape, split, -0.22, 0.18) * drawn
    return jnp.clip(drawn, min=-reach, max=reach).astype(kind)


def setup_inputs(seed: int = 0) -> dict:
    arg_keys = jax.random.split(jax.random.key(seed), 16)
    hidden_in = centred(arg_keys[0], (MICRO, TOKENS, D), 1.0, 6.0, ((1, 8), (2, 4)))
    norm_gain = jnp.clip(1.0 + 0.1 * jax.random.normal(arg_keys[1], (D,), jnp.float32), 0.5, 1.5)
    w_query = centred(arg_keys[2], (D, HEADS * HEAD_DIM), (D // 16) ** -0.5, 0.625, ((0, 4), (1, 4)))
    w_key = centred(arg_keys[3], (D, KV_HEADS * HEAD_DIM), (D // 16) ** -0.5, 0.625, ((0, 4), (1, 4)))
    w_value = centred(arg_keys[4], (D, KV_HEADS * HEAD_DIM), D ** -0.5, 0.15625, ((0, 4), (1, 4)))
    w_out = centred(arg_keys[5], (HEADS * HEAD_DIM, D), 16 ** -0.5, 1.5, ((0, 4), (1, 4)))
    mix_gain = jnp.clip(1.0 + 0.1 * jax.random.normal(arg_keys[6], (D,), jnp.float32), 0.5, 1.5)
    w_router = centred(arg_keys[7], (D, EXPERTS), (0.5 * D ** -0.5), 0.1875)
    w_gate = centred(arg_keys[8], (EXPERTS, D, FF), D ** -0.5, 0.15625, ((0, 2), (1, 16)))
    w_up = centred(arg_keys[9], (EXPERTS, D, FF), D ** -0.5, 0.15625, ((0, 2), (1, 16)))
    w_down = centred(arg_keys[10], (EXPERTS, FF, D), (max(1, FF // 128)) ** -0.5, 3.0, ((0, 2), (1, 16)))
    lengths = jax.vmap(lambda own: uneven(own, SEQS, T_GROUP, LONGEST, 1))(jax.random.split(arg_keys[11], MICRO * N_DP)).reshape((MICRO, N_DP, SEQS)).astype(jnp.int32)
    routes_keys = jax.random.split(jax.random.fold_in(arg_keys[12], 1), MICRO * TOKENS // TQ)
    routes_turns = jax.random.permutation(jax.random.fold_in(arg_keys[12], 3), MICRO * TOKENS // TQ)
    routes = jax.vmap(lambda own, number: assign_block(jax.random.fold_in(arg_keys[12], 2), own, number, TQ, EXPERTS, TOP, CAP, 1))(routes_keys, routes_turns).reshape((MICRO, TOKENS, TOP))
    mask = draw_mask(jax.random.fold_in(arg_keys[15], 71), 0)
    cotangent = centred(arg_keys[14], (MICRO, TOKENS, D), 1.0, 6.0, ((1, 32),))
    return {"hidden_in": hidden_in, "norm_gain": norm_gain, "w_query": w_query, "w_key": w_key, "w_value": w_value, "w_out": w_out, "mix_gain": mix_gain, "w_router": w_router, "w_gate": w_gate, "w_up": w_up, "w_down": w_down, "lengths": lengths, "routes": routes, "mask": mask, "cotangent": cotangent}


eps_norm = 1e-06
resid_scale = 0.22
attn_scale = 0.015625
rope_base = 10000.0
highest = lax.Precision.HIGHEST

@jax.custom_vjp
def low(v):
    return lax.optimization_barrier(v.astype(jnp.bfloat16)).astype(jnp.float32)

@jax.custom_vjp
def low_back(v):
    return v

def low_keep(v):
    return (low(v), None)

def low_pass(kept, grad):
    return (grad,)

def back_keep(v):
    return (v, None)

def back_low(kept, grad):
    return (low(grad),)
low.defvjp(low_keep, low_pass)
low_back.defvjp(back_keep, back_low)

def matmul(first_op, second_op):
    return jnp.dot(first_op, second_op, precision=highest)

def documents(doc_lengths, length_all):
    doc_ends = jnp.cumsum(doc_lengths, dtype=jnp.int32)
    doc_starts = doc_ends - doc_lengths
    positions = jnp.arange(length_all, dtype=jnp.int32)
    doc_id = lax.optimization_barrier(jnp.sum((positions[:, None] >= doc_ends[None, :]).astype(jnp.int32), axis=1, dtype=jnp.int32))
    member = doc_id[:, None] == jnp.arange(doc_lengths.shape[0], dtype=jnp.int32)[None, :]
    doc_start = lax.optimization_barrier(jnp.sum(jnp.where(member, doc_starts[None, :], 0), axis=1, dtype=jnp.int32))
    return (doc_id, positions - doc_start)

def angles(position, head_width):
    half_width = head_width // 2
    frequency = rope_base ** (-2.0 * jnp.arange(half_width, dtype=jnp.float32) / head_width)
    turned = position[:, None] * frequency[None, :]
    return (jnp.sin(turned)[:, None, :], jnp.cos(turned)[:, None, :])

def rotate(values, sin_table, cos_table):
    half_width = values.shape[-1] // 2
    front_half = values[..., :half_width]
    back_half = values[..., half_width:]
    return jnp.concatenate([front_half * cos_table - back_half * sin_table, back_half * cos_table + front_half * sin_table], axis=-1)

def layer(x_full, gain_one, w_query, w_key, w_value, w_out, gain_two, w_router, w_gate, w_up, w_down, allowed, sin_table, cos_table, picks):
    row_count = x_full.shape[0]
    group_size = HEADS // KV_HEADS
    scale_one = lax.rsqrt(lax.optimization_barrier(jnp.mean(x_full * x_full, axis=1, keepdims=True)) + eps_norm)
    normed = low(x_full * scale_one * gain_one)
    query = low(rotate(low_back(matmul(normed, w_query)).reshape(row_count, HEADS, HEAD_DIM), sin_table, cos_table))
    keys = low(rotate(low_back(matmul(normed, w_key)).reshape(row_count, KV_HEADS, HEAD_DIM), sin_table, cos_table))
    values = low(low_back(matmul(normed, w_value))).reshape(row_count, KV_HEADS, HEAD_DIM)
    query_heads = query.reshape(row_count, KV_HEADS, group_size, HEAD_DIM).transpose(1, 0, 2, 3)
    key_heads = keys.transpose(1, 0, 2)
    value_heads = values.transpose(1, 0, 2)

    def one_head(head_block):
        query_block, key_block, value_block = head_block
        raw_scores = low_back(jnp.einsum('qgd,kd->gqk', query_block, key_block, precision=highest))
        scores = jnp.where(allowed[None], raw_scores * attn_scale, -1e+30)
        attn_probs = jax.nn.softmax(scores, axis=-1)
        return jnp.einsum('gqk,kd->qgd', low(attn_probs), value_block, precision=highest)
    attended = lax.map(jax.checkpoint(one_head), (query_heads, key_heads, value_heads))
    attended = low_back(low(attended.transpose(1, 0, 2, 3).reshape(row_count, HEADS * HEAD_DIM)))
    mixed = x_full + resid_scale * low_back(matmul(attended, w_out))
    scale_two = lax.rsqrt(lax.optimization_barrier(jnp.mean(mixed * mixed, axis=1, keepdims=True)) + eps_norm)
    normed_two = low(mixed * scale_two * gain_two)
    logits = matmul(normed_two, w_router)
    expert_ids = jnp.arange(EXPERTS, dtype=jnp.int32)
    choose = (picks[:, :, None] == expert_ids[None, None, :]).astype(jnp.float32)
    chosen = lax.optimization_barrier(jnp.sum(choose * logits[:, None, :], axis=-1))
    gate_weights = jax.nn.softmax(chosen, axis=-1)
    flat_picks = picks.reshape(-1)
    hit_table = (flat_picks[:, None] == expert_ids[None, :]).astype(jnp.int32)
    slot_rank = lax.optimization_barrier(jnp.sum(hit_table * (jnp.cumsum(hit_table, axis=0, dtype=jnp.int32) - 1), axis=1, dtype=jnp.int32))
    slot_depth = N_ROW * N_COL * CAP
    slot_index = flat_picks * slot_depth + slot_rank
    token_of = jnp.full((EXPERTS * slot_depth,), row_count, jnp.int32).at[slot_index].set(jnp.arange(row_count * TOP, dtype=jnp.int32) // TOP)
    padded = jnp.concatenate([normed_two, jnp.zeros((1, D), jnp.float32)], axis=0)
    expert_in = low_back(padded[token_of]).reshape(EXPERTS, slot_depth, D)
    gate_proj = low_back(jnp.einsum('ecd,edf->ecf', expert_in, w_gate, precision=highest))
    up_proj = low_back(jnp.einsum('ecd,edf->ecf', expert_in, w_up, precision=highest))
    activated = low(jax.nn.silu(gate_proj) * up_proj)
    expert_out = low_back(low(jnp.einsum('ecf,efd->ecd', activated, w_down, precision=highest)))
    combined = expert_out.reshape(EXPERTS * slot_depth, D)[slot_index].reshape(row_count, TOP, D)
    expert_mix = lax.optimization_barrier(jnp.sum(gate_weights[:, :, None] * combined, axis=1))
    return mixed + resid_scale * expert_mix

def reference(hidden_in, norm_gain, w_query, w_key, w_value, w_out, mix_gain, w_router, w_gate, w_up, w_down, lengths, routes, mask, cotangent):
    group_count = MICRO * N_DP
    params = (norm_gain.astype(jnp.float32), w_query.astype(jnp.float32), w_key.astype(jnp.float32), w_value.astype(jnp.float32), w_out.astype(jnp.float32), mix_gain.astype(jnp.float32), w_router.astype(jnp.float32), w_gate.astype(jnp.float32), w_up.astype(jnp.float32), w_down.astype(jnp.float32))
    x_groups = hidden_in.reshape(group_count, T_GROUP, D)
    len_groups = lengths.reshape(group_count, SEQS)
    pick_groups = routes.reshape(group_count, T_GROUP, TOP)
    mask_groups = mask.reshape(group_count, T_GROUP)
    cot_groups = cotangent.reshape(group_count, T_GROUP, D)

    def one_group(running, group_item):
        x_group, len_group, pick_group, mask_group, cot_group = group_item
        doc_id, position = documents(len_group, T_GROUP)
        positions = jnp.arange(T_GROUP, dtype=jnp.int32)
        allowed = (doc_id[:, None] == doc_id[None, :]) & (positions[None, :] <= positions[:, None])
        sin_table, cos_table = angles(position.astype(jnp.float32), HEAD_DIM)

        def forward(x_full, *weights):
            return layer(x_full, *weights, allowed, sin_table, cos_table, pick_group)
        layer_value, pull_back = jax.vjp(forward, x_group.astype(jnp.float32), *params)
        gradients = pull_back(cot_group.astype(jnp.float32) * mask_group[:, None].astype(jnp.float32))
        updated = tuple((old_sum + new_term for old_sum, new_term in zip(running, gradients[1:])))
        return (updated, (layer_value.astype(jnp.bfloat16), gradients[0]))
    zero_sums = tuple((jnp.zeros_like(weight) for weight in params))
    grad_sums, (out_groups, dx_groups) = lax.scan(one_group, zero_sums, (x_groups, len_groups, pick_groups, mask_groups, cot_groups))
    layer_out = out_groups.reshape(MICRO, TOKENS, D)
    grad_input = dx_groups.reshape(MICRO, TOKENS, D)
    return (layer_out, grad_input, grad_sums[0], grad_sums[1], grad_sums[2], grad_sums[3], grad_sums[4], grad_sums[5], grad_sums[6], grad_sums[7], grad_sums[8], grad_sums[9])
```

```python
import jax
import jax.numpy as jnp
from jax import lax
from jax.sharding import PartitionSpec as P

D = 1536
HEAD_DIM = 64
TOP = 8


eps_norm = 1e-06
resid_scale = 0.22
attn_scale = 0.015625
rope_base = 10000.0
highest = lax.Precision.HIGHEST


def shortened(shard):
    return jax.tree.map(lambda a: a.astype(jnp.bfloat16) if a.dtype == jnp.float32 else a, shard)


def documents(doc_lengths, length_all):
    doc_ends = jnp.cumsum(doc_lengths, dtype=jnp.int32)
    doc_starts = doc_ends - doc_lengths
    positions = jnp.arange(length_all, dtype=jnp.int32)
    doc_id = jnp.sum(
        (positions[:, None] >= doc_ends[None, :]).astype(jnp.int32), axis=1, dtype=jnp.int32
    )
    member = doc_id[:, None] == jnp.arange(doc_lengths.shape[0], dtype=jnp.int32)[None, :]
    doc_start = jnp.sum(jnp.where(member, doc_starts[None, :], 0), axis=1, dtype=jnp.int32)
    return (doc_id, positions - doc_start)


def angles(position, head_width):
    half_width = head_width // 2
    frequency = rope_base ** (-2.0 * jnp.arange(half_width, dtype=jnp.float32) / head_width)
    turned = position[:, None] * frequency[None, :]
    return (jnp.sin(turned)[:, None, :], jnp.cos(turned)[:, None, :])


def rotate(values, sin_table, cos_table):
    half_width = values.shape[-1] // 2
    front_half = values[..., :half_width]
    back_half = values[..., half_width:]
    return jnp.concatenate(
        [
            front_half * cos_table - back_half * sin_table,
            back_half * cos_table + front_half * sin_table,
        ],
        axis=-1,
    )


def gather_rows(value):
    return lax.all_gather(value, "row", axis=0, tiled=True)


def gather_cols(value):
    return jax.tree.map(
        lambda part, own: part.astype(own.dtype),
        lax.all_gather(shortened(value), "col", axis=0, tiled=True),
        value,
    )


def sum_cols(pieces):
    return lax.psum_scatter(pieces, "col", scatter_dimension=0, tiled=True)


def sum_rows(pieces):
    return lax.psum_scatter(pieces, "row", scatter_dimension=0, tiled=True)


def width_total(value):
    return lax.psum(value, "col")


def expert_trade(value):
    return lax.all_to_all(value, "dp", split_axis=1, concat_axis=1, tiled=True)


def attn_total(value):
    return jax.tree.map(lambda part: part.astype(jnp.float32), lax.psum(shortened(value), "dp"))


def expert_total(value):
    return jax.tree.map(
        lambda part: part.astype(jnp.float32),
        lax.psum_scatter(shortened(value), ("row", "col"), scatter_dimension=1, tiled=True),
    )


def add_all(first_set, second_set):
    return tuple((left_one + right_one for left_one, right_one in zip(first_set, second_set)))


def project(left_side, right_side):
    return jnp.dot(left_side, right_side, preferred_element_type=jnp.float32)


def shards(
    hidden_in,
    norm_gain,
    w_query,
    w_key,
    w_value,
    w_out,
    mix_gain,
    w_router,
    w_gate,
    w_up,
    w_down,
    lengths,
    routes,
    mask,
    cotangent,
):
    micro_count = hidden_in.shape[0]
    tok_dev = hidden_in.shape[1]
    width_part = hidden_in.shape[2]
    col_count = lax.axis_size("col")
    row_count = lax.axis_size("row")
    dp_count = lax.axis_size("dp")
    col_at = lax.axis_index("col")
    model_width = D
    heads_here = w_query.shape[1] // HEAD_DIM
    kv_here = w_key.shape[1] // HEAD_DIM
    group_size = heads_here // kv_here
    group_tokens = tok_dev * row_count
    quarter = tok_dev // col_count
    experts_here = w_gate.shape[0]
    experts_all = experts_here * dp_count
    capacity = quarter * 3 // 8
    slot_count = experts_all * capacity
    gain_part = lax.dynamic_slice_in_dim(norm_gain, col_at * width_part, width_part)
    router_wide = w_router.astype(jnp.float32)
    full_gate, full_up, full_down = (
        lax.all_gather(w_gate, ("row", "col"), axis=1, tiled=True),
        lax.all_gather(w_up, ("row", "col"), axis=1, tiled=True),
        lax.all_gather(w_down, ("row", "col"), axis=1, tiled=True),
    )
    expert_ids = jnp.arange(experts_all, dtype=jnp.int32)
    group_index = jnp.arange(group_tokens, dtype=jnp.int32)
    query_start = col_at * tok_dev
    query_index = query_start + jnp.arange(tok_dev, dtype=jnp.int32)
    attn_local = (
        jnp.zeros(w_query.shape, jnp.float32),
        jnp.zeros(w_key.shape, jnp.float32),
        jnp.zeros(w_value.shape, jnp.float32),
        jnp.zeros(w_out.shape, jnp.float32),
    )
    expert_local = (
        jnp.zeros(full_gate.shape, jnp.float32),
        jnp.zeros(full_up.shape, jnp.float32),
        jnp.zeros(full_down.shape, jnp.float32),
    )
    router_acc = jnp.zeros(w_router.shape, jnp.float32)
    norm_acc = jnp.zeros((width_part,), jnp.float32)
    mix_acc = jnp.zeros((model_width,), jnp.float32)
    layer_rows = []
    input_grads = []
    for step in range(micro_count):
        x_full = hidden_in[step].astype(jnp.float32)
        squares = width_total(jnp.sum(x_full * x_full, axis=1))
        scale_one = lax.rsqrt(squares / model_width + eps_norm)[:, None]
        unit_one = x_full * scale_one
        normed = (unit_one * gain_part).astype(jnp.bfloat16)
        normed_all = gather_rows(normed)
        query_p, key_p, value_p = sum_cols(
            (project(normed_all, w_query), project(normed_all, w_key), project(normed_all, w_value))
        )
        doc_all, pos_all = documents(lengths[step, 0], group_tokens)
        doc_query = lax.dynamic_slice_in_dim(doc_all, query_start, tok_dev)
        pos_query = lax.dynamic_slice_in_dim(pos_all, query_start, tok_dev).astype(jnp.float32)
        sin_table, cos_table = angles(pos_query, HEAD_DIM)
        query_rot = rotate(
            query_p.reshape(tok_dev, heads_here, HEAD_DIM), sin_table, cos_table
        ).astype(jnp.bfloat16)
        key_rot = rotate(key_p.reshape(tok_dev, kv_here, HEAD_DIM), sin_table, cos_table).astype(
            jnp.bfloat16
        )
        value_low = value_p.astype(jnp.bfloat16).reshape(tok_dev, kv_here, HEAD_DIM)
        keys_all, values_all = (
            lax.all_gather(key_rot, "col", axis=0, tiled=True),
            lax.all_gather(value_low, "col", axis=0, tiled=True),
        )
        allowed = (doc_query[:, None] == doc_all[None, :]) & (
            group_index[None, :] <= query_index[:, None]
        )
        query_grp = query_rot.reshape(tok_dev, kv_here, group_size, HEAD_DIM)
        raw_scores = jnp.einsum(
            "qhgd,khd->hgqk", query_grp, keys_all, preferred_element_type=jnp.float32
        )
        scores = jnp.where(allowed[None, None], raw_scores * attn_scale, -1e30)
        top_score = jnp.max(scores, axis=-1, keepdims=True)
        expd = jnp.exp(scores - top_score)
        row_total = jnp.sum(expd, axis=-1, keepdims=True)
        attn_probs = expd / row_total
        log_total = top_score + jnp.log(row_total)
        probs_low = attn_probs.astype(jnp.bfloat16)
        attended = jnp.einsum(
            "hgqk,khd->qhgd", probs_low, values_all, preferred_element_type=jnp.float32
        )
        attended_low = attended.reshape(tok_dev, heads_here * HEAD_DIM).astype(jnp.bfloat16)
        attended_all = gather_cols(attended_low)
        attn_branch = sum_rows(project(attended_all, w_out))
        mixed = x_full + resid_scale * attn_branch
        mixed_rows = lax.all_to_all(
            mixed.reshape(col_count, quarter, width_part),
            "col",
            split_axis=0,
            concat_axis=2,
            tiled=True,
        ).reshape(quarter, model_width)
        scale_two = lax.rsqrt(jnp.mean(mixed_rows * mixed_rows, axis=1, keepdims=True) + eps_norm)
        unit_two = mixed_rows * scale_two
        normed_two = (unit_two * mix_gain).astype(jnp.bfloat16)
        logits = project(normed_two, w_router)
        picks = routes[step]
        choose = (picks[:, :, None] == expert_ids[None, None, :]).astype(jnp.float32)
        chosen = jnp.sum(choose * logits[:, None, :], axis=-1)
        gate_weights = jax.nn.softmax(chosen, axis=-1)
        flat_picks = picks.reshape(-1)
        hit_table = (flat_picks[:, None] == expert_ids[None, :]).astype(jnp.int32)
        slot_rank = jnp.sum(
            hit_table * (jnp.cumsum(hit_table, axis=0, dtype=jnp.int32) - 1),
            axis=1,
            dtype=jnp.int32,
        )
        owner_dp = flat_picks // experts_here
        local_expert = flat_picks % experts_here
        slot_index = local_expert * (dp_count * capacity) + owner_dp * capacity + slot_rank
        token_of = (
            jnp.full((slot_count,), quarter, jnp.int32)
            .at[slot_index]
            .set(jnp.arange(quarter * TOP, dtype=jnp.int32) // TOP)
        )
        padded = jnp.concatenate([normed_two, jnp.zeros((1, model_width), jnp.bfloat16)], axis=0)
        send_rows = padded[token_of].reshape(experts_here, dp_count * capacity, model_width)
        expert_in = expert_trade(send_rows)
        gate_proj = jnp.einsum(
            "ecd,edf->ecf", expert_in, full_gate, preferred_element_type=jnp.float32
        )
        up_proj = jnp.einsum("ecd,edf->ecf", expert_in, full_up, preferred_element_type=jnp.float32)
        activated = (jax.nn.silu(gate_proj) * up_proj).astype(jnp.bfloat16)
        expert_out = jnp.einsum(
            "ecf,efd->ecd", activated, full_down, preferred_element_type=jnp.float32
        ).astype(jnp.bfloat16)
        returned = expert_trade(expert_out).reshape(slot_count, model_width)
        combined = returned[slot_index].reshape(quarter, TOP, model_width).astype(jnp.float32)
        expert_mix = jnp.sum(gate_weights[:, :, None] * combined, axis=1)
        layer_rows.append((mixed_rows + resid_scale * expert_mix).astype(jnp.bfloat16))
        grad_rows = cotangent[step].astype(jnp.float32) * mask[step][:, None].astype(jnp.float32)
        grad_mix = resid_scale * grad_rows
        grad_gates = jnp.sum(grad_mix[:, None, :] * combined, axis=-1)
        grad_chosen = gate_weights * (
            grad_gates - jnp.sum(gate_weights * grad_gates, axis=-1, keepdims=True)
        )
        grad_logits = jnp.sum(choose * grad_chosen[:, :, None], axis=1)
        gate_slots = (
            jnp.zeros((slot_count,), jnp.float32).at[slot_index].set(gate_weights.reshape(-1))
        )
        grad_pad = jnp.concatenate([grad_mix, jnp.zeros((1, model_width), jnp.float32)], axis=0)
        grad_send = (gate_slots[:, None] * grad_pad[token_of]).astype(jnp.bfloat16)
        grad_expert = expert_trade(
            grad_send.reshape(experts_here, dp_count * capacity, model_width)
        )
        grad_act = jnp.einsum(
            "ecd,efd->ecf", grad_expert, full_down, preferred_element_type=jnp.float32
        )
        micro_down = jnp.einsum(
            "ecf,ecd->efd", activated, grad_expert, preferred_element_type=jnp.float32
        )
        sigmoid_gate = jax.nn.sigmoid(gate_proj)
        silu_gate = gate_proj * sigmoid_gate
        grad_gate_p = (
            grad_act * up_proj * (sigmoid_gate + gate_proj * sigmoid_gate * (1.0 - sigmoid_gate))
        ).astype(jnp.bfloat16)
        grad_up_p = (grad_act * silu_gate).astype(jnp.bfloat16)
        grad_in = jnp.einsum(
            "ecf,edf->ecd", grad_gate_p, full_gate, preferred_element_type=jnp.float32
        ) + jnp.einsum("ecf,edf->ecd", grad_up_p, full_up, preferred_element_type=jnp.float32)
        micro_gate = jnp.einsum(
            "ecd,ecf->edf", expert_in, grad_gate_p, preferred_element_type=jnp.float32
        )
        micro_up = jnp.einsum(
            "ecd,ecf->edf", expert_in, grad_up_p, preferred_element_type=jnp.float32
        )
        expert_local = add_all(expert_local, (micro_gate, micro_up, micro_down))
        grad_back = expert_trade(grad_in.astype(jnp.bfloat16)).reshape(slot_count, model_width)
        grad_normed = jnp.sum(
            grad_back[slot_index].reshape(quarter, TOP, model_width).astype(jnp.float32), axis=1
        ) + jnp.dot(grad_logits, router_wide.T, precision=highest)
        router_acc = router_acc + jnp.dot(
            normed_two.astype(jnp.float32).T, grad_logits, precision=highest
        )
        mix_acc = mix_acc + jnp.sum(grad_normed * unit_two, axis=0)
        grad_scaled = grad_normed * mix_gain
        grad_mixed_rows = grad_rows + scale_two * (
            grad_scaled - unit_two * jnp.mean(grad_scaled * unit_two, axis=1, keepdims=True)
        )
        grad_mixed = lax.all_to_all(
            grad_mixed_rows.reshape(1, quarter, model_width),
            "col",
            split_axis=2,
            concat_axis=0,
            tiled=True,
        ).reshape(tok_dev, width_part)
        grad_branch = (resid_scale * grad_mixed).astype(jnp.bfloat16)
        grad_branch_all = gather_rows(grad_branch)
        micro_out = jnp.dot(attended_all.T, grad_branch_all, preferred_element_type=jnp.float32)
        grad_attended = sum_cols(
            jnp.dot(grad_branch_all, w_out.T, preferred_element_type=jnp.float32)
        )
        grad_att_low = grad_attended.astype(jnp.bfloat16).reshape(
            tok_dev, kv_here, group_size, HEAD_DIM
        )
        probs_again = jnp.exp(scores - log_total)
        grad_probs = jnp.einsum(
            "qhgd,khd->hgqk", grad_att_low, values_all, preferred_element_type=jnp.float32
        )
        grad_scores = probs_again * (
            grad_probs - jnp.sum(probs_again * grad_probs, axis=-1, keepdims=True)
        )
        grad_raw = (grad_scores * attn_scale).astype(jnp.bfloat16)
        probs_again_low = probs_again.astype(jnp.bfloat16)
        grad_query = jnp.einsum(
            "hgqk,khd->qhgd", grad_raw, keys_all, preferred_element_type=jnp.float32
        )
        grad_key_part = jnp.einsum(
            "hgqk,qhgd->khd", grad_raw, query_grp, preferred_element_type=jnp.float32
        )
        grad_value_part = jnp.einsum(
            "hgqk,qhgd->khd", probs_again_low, grad_att_low, preferred_element_type=jnp.float32
        )
        grad_key, grad_value = sum_cols(
            (
                grad_key_part.reshape(group_tokens, kv_here * HEAD_DIM),
                grad_value_part.reshape(group_tokens, kv_here * HEAD_DIM),
            )
        )
        grad_query_p = (
            rotate(grad_query.reshape(tok_dev, heads_here, HEAD_DIM), -sin_table, cos_table)
            .astype(jnp.bfloat16)
            .reshape(tok_dev, heads_here * HEAD_DIM)
        )
        grad_key_p = (
            rotate(grad_key.reshape(tok_dev, kv_here, HEAD_DIM), -sin_table, cos_table)
            .astype(jnp.bfloat16)
            .reshape(tok_dev, kv_here * HEAD_DIM)
        )
        grad_value_p = grad_value.astype(jnp.bfloat16)
        query_all, key_all, value_all = gather_cols((grad_query_p, grad_key_p, grad_value_p))
        micro_query = jnp.dot(normed_all.T, query_all, preferred_element_type=jnp.float32)
        micro_key = jnp.dot(normed_all.T, key_all, preferred_element_type=jnp.float32)
        micro_value = jnp.dot(normed_all.T, value_all, preferred_element_type=jnp.float32)
        grad_normed_one = sum_rows(
            jnp.dot(query_all, w_query.T, preferred_element_type=jnp.float32)
            + jnp.dot(key_all, w_key.T, preferred_element_type=jnp.float32)
            + jnp.dot(value_all, w_value.T, preferred_element_type=jnp.float32)
        )
        grad_scaled_one = grad_normed_one * gain_part
        inner_sum = width_total(jnp.sum(grad_scaled_one * unit_one, axis=1))
        norm_acc = norm_acc + jnp.sum(grad_normed_one * unit_one, axis=0)
        input_grads.append(
            grad_mixed
            + scale_one * (grad_scaled_one - unit_one * (inner_sum / model_width)[:, None])
        )
        attn_local = add_all(attn_local, (micro_query, micro_key, micro_value, micro_out))
    attn_summed = attn_total(attn_local)
    expert_summed = expert_total(expert_local)
    gain_full = lax.dynamic_update_slice_in_dim(
        jnp.zeros((model_width,), jnp.float32), norm_acc, col_at * width_part, 0
    )
    router_grad, gain_grad, mix_grad = lax.psum(
        (router_acc, gain_full, mix_acc), ("dp", "row", "col")
    )
    return (
        jnp.stack(layer_rows),
        jnp.stack(input_grads),
        gain_grad,
        attn_summed[0],
        attn_summed[1],
        attn_summed[2],
        attn_summed[3],
        mix_grad,
        router_grad,
        expert_summed[0],
        expert_summed[1],
        expert_summed[2],
    )


def spread_plane(blocks):
    return lax.all_to_all(blocks, ("row", "col"), split_axis=0, concat_axis=0, tiled=True)


def spread_cols(blocks):
    return lax.all_to_all(blocks, "col", split_axis=0, concat_axis=0, tiled=True)


def owned(
    hidden_in,
    norm_gain,
    w_query,
    w_key,
    w_value,
    w_out,
    mix_gain,
    w_router,
    w_gate,
    w_up,
    w_down,
    lengths,
    routes,
    mask,
    cotangent,
):
    everyone = ("dp", "row", "col")
    plane = ("row", "col")
    micro_count, tok_row, width_part = hidden_in.shape
    row_count = lax.axis_size("row")
    col_count = lax.axis_size("col")
    dp_count = lax.axis_size("dp")
    row_at = lax.axis_index("row")
    col_at = lax.axis_index("col")
    dp_at = lax.axis_index("dp")
    plane_count = row_count * col_count
    device_count = plane_count * dp_count
    plane_at = row_at * col_count + col_at
    model_width = width_part * col_count
    kv_here = w_key.shape[1] // HEAD_DIM
    group_size = w_query.shape[1] // w_key.shape[1]
    q_width = group_size * HEAD_DIM
    group_tokens = tok_row * row_count
    quarter = tok_row // col_count
    own_rows = micro_count * quarter
    experts_here, slice_width, ff_width = w_gate.shape
    down_slice = w_down.shape[1]
    experts_all = experts_here * dp_count
    expert_at = dp_at * plane_count + plane_at
    micro_at = col_at // kv_here
    half_at = col_at % kv_here

    gate_own = spread_plane(w_gate).reshape(model_width, ff_width)
    up_own = spread_plane(w_up).reshape(model_width, ff_width)
    down_own = spread_plane(w_down).reshape(ff_width, model_width)

    masked_cot = cotangent * mask[:, :, None].astype(cotangent.dtype)
    cot_all = lax.all_gather(
        masked_cot.reshape(own_rows, model_width), everyone, axis=0, tiled=True
    )
    routes_all = lax.all_gather(routes.reshape(own_rows, TOP), everyone, axis=0, tiled=True)

    to_micro = jnp.arange(col_count) // kv_here
    x_send = jnp.broadcast_to(
        hidden_in[to_micro][None], (row_count, col_count, tok_row, width_part)
    ).reshape(plane_count, tok_row, width_part)
    x_micro = (
        spread_plane(x_send)
        .reshape(row_count, col_count, tok_row, width_part)
        .transpose(0, 2, 1, 3)
        .reshape(group_tokens, model_width)
        .astype(jnp.float32)
    )
    x_own = (
        spread_cols(
            hidden_in.reshape(micro_count, col_count, quarter, width_part).transpose(1, 0, 2, 3)
        )
        .transpose(1, 2, 0, 3)
        .reshape(own_rows, model_width)
        .astype(jnp.float32)
    )
    w_qkv = jnp.concatenate(
        [
            w_query.reshape(width_part, kv_here, q_width),
            w_key.reshape(width_part, kv_here, HEAD_DIM),
            w_value.reshape(width_part, kv_here, HEAD_DIM),
        ],
        axis=2,
    ).transpose(1, 0, 2)
    qkv_width = q_width + 2 * HEAD_DIM
    to_half = jnp.arange(col_count) % kv_here
    w_mine = spread_cols(w_qkv[to_half]).reshape(model_width, qkv_width)
    w_qkv_all = (
        lax.all_gather(w_qkv, plane, axis=0, tiled=False)
        .reshape(row_count, col_count, kv_here, width_part, qkv_width)
        .transpose(1, 3, 0, 2, 4)
        .reshape(model_width, row_count * kv_here * qkv_width)
    )
    w_out_all = (
        lax.all_gather(w_out, plane, axis=0, tiled=False)
        .reshape(row_count, col_count, w_out.shape[0], w_out.shape[1])
        .transpose(0, 2, 1, 3)
        .reshape(row_count * w_out.shape[0], model_width)
    )

    scale_m = lax.rsqrt(jnp.mean(x_micro * x_micro, axis=1, keepdims=True) + eps_norm)
    normed_m = (x_micro * scale_m * norm_gain).astype(jnp.bfloat16)
    qkv = project(normed_m, w_mine)
    doc_id, position = documents(lengths[:, 0][micro_at], group_tokens)
    sin_table, cos_table = angles(position.astype(jnp.float32), HEAD_DIM)
    query = rotate(
        qkv[:, :q_width].reshape(group_tokens, group_size, HEAD_DIM), sin_table, cos_table
    ).astype(jnp.bfloat16)
    key = rotate(
        qkv[:, q_width : q_width + HEAD_DIM].reshape(group_tokens, 1, HEAD_DIM),
        sin_table,
        cos_table,
    )[:, 0].astype(jnp.bfloat16)
    value = qkv[:, q_width + HEAD_DIM :].astype(jnp.bfloat16)
    order = jnp.arange(group_tokens, dtype=jnp.int32)
    allowed = (doc_id[:, None] == doc_id[None, :]) & (order[None, :] <= order[:, None])
    raw_scores = jnp.einsum("qgd,kd->gqk", query, key, preferred_element_type=jnp.float32)
    scores = jnp.where(allowed[None], raw_scores * attn_scale, -1e30)
    probs = jax.nn.softmax(scores, axis=-1)
    probs_low = probs.astype(jnp.bfloat16)
    attended = (
        jnp.einsum("gqk,kd->qgd", probs_low, value, preferred_element_type=jnp.float32)
        .reshape(group_tokens, q_width)
        .astype(jnp.bfloat16)
    )

    attended_own = (
        spread_plane(attended.reshape(plane_count, quarter, q_width))
        .reshape(row_count, micro_count, kv_here, quarter, q_width)
        .transpose(1, 3, 0, 2, 4)
        .reshape(own_rows, row_count * kv_here * q_width)
    )
    mixed = x_own + resid_scale * project(attended_own, w_out_all)
    scale_two = lax.rsqrt(jnp.mean(mixed * mixed, axis=1, keepdims=True) + eps_norm)
    unit_two = mixed * scale_two
    normed_two = (unit_two * mix_gain).astype(jnp.bfloat16)
    expert_ids = jnp.arange(experts_all, dtype=jnp.int32)

    def gating(normed_rows, picks):
        chosen = jnp.any(picks[:, :, None] == expert_ids[None, None, :], axis=1)
        logits = jnp.where(chosen, project(normed_rows, w_router), -jnp.inf)
        return jax.nn.softmax(logits, axis=-1)

    normed_all = lax.all_gather(normed_two, everyone, axis=0, tiled=True)
    gates_all = gating(normed_all, routes_all)
    gates_own = gating(normed_two, routes.reshape(own_rows, TOP))
    gate_mine = jnp.sum(
        gates_all * (expert_ids == expert_at).astype(jnp.float32)[None, :], axis=1, keepdims=True
    )

    gate_proj = project(normed_all, gate_own)
    up_proj = project(normed_all, up_own)
    sigmoid_gate = jax.nn.sigmoid(gate_proj)
    silu_gate = gate_proj * sigmoid_gate
    activated = (silu_gate * up_proj).astype(jnp.bfloat16)
    expert_out = project(activated, down_own).astype(jnp.bfloat16).astype(jnp.float32)
    grad_mix = resid_scale * cot_all.astype(jnp.float32)
    grad_gate_mine = jnp.sum(grad_mix * expert_out, axis=1)
    mix_part = (gate_mine * expert_out).astype(jnp.bfloat16)
    grad_out_rows = (gate_mine * grad_mix).astype(jnp.bfloat16)
    grad_act = jnp.dot(grad_out_rows, down_own.T, preferred_element_type=jnp.float32)
    grad_gate_p = (
        grad_act * up_proj * (sigmoid_gate + gate_proj * sigmoid_gate * (1.0 - sigmoid_gate))
    ).astype(jnp.bfloat16)
    grad_up_p = (grad_act * silu_gate).astype(jnp.bfloat16)
    grad_rows_part = (
        jnp.dot(grad_gate_p, gate_own.T, preferred_element_type=jnp.float32)
        + jnp.dot(grad_up_p, up_own.T, preferred_element_type=jnp.float32)
    ).astype(jnp.bfloat16)
    grad_down_own = jnp.dot(activated.T, grad_out_rows, preferred_element_type=jnp.float32)
    grad_gate_own = jnp.dot(normed_all.T, grad_gate_p, preferred_element_type=jnp.float32)
    grad_up_own = jnp.dot(normed_all.T, grad_up_p, preferred_element_type=jnp.float32)

    def back_to_slices(grad, parts, depth):
        return spread_plane(
            grad.astype(jnp.bfloat16).reshape(parts, depth, grad.shape[1])
        ).astype(jnp.float32)

    out_gate = back_to_slices(grad_gate_own, experts_here, slice_width)
    out_up = back_to_slices(grad_up_own, experts_here, slice_width)
    out_down = back_to_slices(grad_down_own, experts_here, down_slice)

    grad_gates = lax.all_to_all(
        grad_gate_mine.reshape(device_count, own_rows), everyone, 0, 0, tiled=True
    ).T
    chosen_own = jnp.any(
        routes.reshape(own_rows, TOP)[:, :, None] == expert_ids[None, None, :], axis=1
    )
    grad_gates = jnp.where(chosen_own, grad_gates, 0.0)
    grad_logits = gates_own * (
        grad_gates - jnp.sum(gates_own * grad_gates, axis=1, keepdims=True)
    )
    grad_logits_all = lax.all_gather(grad_logits, everyone, axis=0, tiled=True)
    router_grad = jnp.dot(
        normed_all.astype(jnp.float32).T, grad_logits_all, precision=highest
    )
    expert_mix = lax.psum_scatter(mix_part, everyone, scatter_dimension=0, tiled=True)
    layer_out = (mixed + resid_scale * expert_mix.astype(jnp.float32)).astype(jnp.bfloat16)
    grad_normed = lax.psum_scatter(
        grad_rows_part, everyone, scatter_dimension=0, tiled=True
    ).astype(jnp.float32) + jnp.dot(
        grad_logits, w_router.astype(jnp.float32).T, precision=highest
    )
    mix_part_grad = jnp.sum(grad_normed * unit_two, axis=0)
    grad_scaled = grad_normed * mix_gain
    grad_mixed = masked_cot.reshape(own_rows, model_width).astype(jnp.float32) + scale_two * (
        grad_scaled - unit_two * jnp.mean(grad_scaled * unit_two, axis=1, keepdims=True)
    )
    grad_branch = (resid_scale * grad_mixed).astype(jnp.bfloat16)

    branch_send = jnp.broadcast_to(
        grad_branch.reshape(micro_count, quarter, model_width)[to_micro][None],
        (row_count, col_count, quarter, model_width),
    ).reshape(plane_count, quarter, model_width)
    branch_m = spread_plane(branch_send).reshape(group_tokens, model_width)
    w_out_mine = lax.dynamic_slice_in_dim(
        w_out_all, (row_at * kv_here + half_at) * q_width, q_width
    )
    grad_att = (
        jnp.dot(branch_m, w_out_mine.T, preferred_element_type=jnp.float32)
        .astype(jnp.bfloat16)
        .reshape(group_tokens, group_size, HEAD_DIM)
    )
    out_part = jnp.dot(attended.T, branch_m, preferred_element_type=jnp.float32)
    grad_probs = jnp.einsum("qgd,kd->gqk", grad_att, value, preferred_element_type=jnp.float32)
    grad_scores = probs * (grad_probs - jnp.sum(probs * grad_probs, axis=-1, keepdims=True))
    grad_raw = (grad_scores * attn_scale).astype(jnp.bfloat16)
    grad_query = jnp.einsum("gqk,kd->qgd", grad_raw, key, preferred_element_type=jnp.float32)
    grad_key = jnp.einsum("gqk,qgd->kd", grad_raw, query, preferred_element_type=jnp.float32)
    grad_value = jnp.einsum("gqk,qgd->kd", probs_low, grad_att, preferred_element_type=jnp.float32)
    grad_qkv = jnp.concatenate(
        [
            rotate(grad_query, -sin_table, cos_table).reshape(group_tokens, q_width),
            rotate(grad_key[:, None], -sin_table, cos_table)[:, 0],
            grad_value,
        ],
        axis=1,
    ).astype(jnp.bfloat16)
    qkv_part = jnp.dot(normed_m.T, grad_qkv, preferred_element_type=jnp.float32)
    grad_qkv_own = (
        spread_plane(grad_qkv.reshape(plane_count, quarter, qkv_width))
        .reshape(row_count, micro_count, kv_here, quarter, qkv_width)
        .transpose(1, 3, 0, 2, 4)
        .reshape(own_rows, row_count * kv_here * qkv_width)
    )
    grad_normed_one = jnp.dot(grad_qkv_own, w_qkv_all.T, preferred_element_type=jnp.float32)
    scale_one = lax.rsqrt(jnp.mean(x_own * x_own, axis=1, keepdims=True) + eps_norm)
    unit_one = x_own * scale_one
    norm_part = jnp.sum(grad_normed_one * unit_one, axis=0)
    grad_scaled_one = grad_normed_one * norm_gain
    grad_x = grad_mixed + scale_one * (
        grad_scaled_one
        - unit_one * jnp.mean(grad_scaled_one * unit_one, axis=1, keepdims=True)
    )
    grad_input = (
        spread_cols(
            grad_x.reshape(micro_count, quarter, col_count, width_part).transpose(2, 0, 1, 3)
        )
        .transpose(1, 0, 2, 3)
        .reshape(micro_count, tok_row, width_part)
    )

    def halves(part):
        low_part = spread_cols(part.astype(jnp.bfloat16)).astype(jnp.float32)
        return jnp.sum(
            low_part.reshape((micro_count, kv_here) + part.shape[1:]), axis=0
        ).astype(jnp.bfloat16)

    qkv_sum = halves(qkv_part.reshape(col_count, width_part, qkv_width))
    out_sum = halves(
        out_part.reshape(q_width, col_count, width_part).transpose(1, 0, 2)
    )
    qkv_sum, out_sum = attn_total(
        (qkv_sum.astype(jnp.float32), out_sum.astype(jnp.float32))
    )
    grad_wq = qkv_sum[:, :, :q_width].transpose(1, 0, 2).reshape(w_query.shape)
    grad_wk = qkv_sum[:, :, q_width : q_width + HEAD_DIM].transpose(1, 0, 2).reshape(w_key.shape)
    grad_wv = qkv_sum[:, :, q_width + HEAD_DIM :].transpose(1, 0, 2).reshape(w_value.shape)
    grad_wo = out_sum.reshape(w_out.shape)
    gain_grads = lax.psum(jnp.stack([norm_part, mix_part_grad]), everyone)
    return (
        layer_out.reshape(micro_count, quarter, model_width),
        grad_input,
        gain_grads[0],
        grad_wq,
        grad_wk,
        grad_wv,
        grad_wo,
        gain_grads[1],
        router_grad,
        out_gate,
        out_up,
        out_down,
    )


def solution(mesh):
    dp_count, row_count, col_count = (mesh.shape[name] for name in ("dp", "row", "col"))

    def body(*args):
        hidden_in, w_key, w_gate = args[0], args[3], args[8]
        kv_here = w_key.shape[1] // HEAD_DIM
        one_each = w_gate.shape[0] == row_count * col_count
        pairs = hidden_in.shape[0] * kv_here == col_count
        return (owned if one_each and pairs else shards)(*args)

    placed = (
        P(None, ("dp", "row"), "col"),
        P(),
        P("col", "row"),
        P("col", "row"),
        P("col", "row"),
        P("row", "col"),
        P(),
        P(),
        P("dp", ("row", "col"), None),
        P("dp", ("row", "col"), None),
        P("dp", ("row", "col"), None),
        P(None, "dp", None),
        P(None, ("dp", "row", "col"), None),
        P(None, ("dp", "row", "col")),
        P(None, ("dp", "row", "col"), None),
    )
    return jax.shard_map(
        body,
        mesh=mesh,
        in_specs=placed,
        out_specs=(
            P(None, ("dp", "row", "col"), None),
            P(None, ("dp", "row"), "col"),
            P(),
            P("col", "row"),
            P("col", "row"),
            P("col", "row"),
            P("row", "col"),
            P(),
            P(),
            P("dp", ("row", "col"), None),
            P("dp", ("row", "col"), None),
            P("dp", ("row", "col"), None),
        ),
        check_vma=False,
    )
```

```python
import functools

import jax
import jax.numpy as jnp
from jax import lax
from jax.experimental import pallas as pl
from jax.experimental.pallas import tpu as pltpu
from jax.sharding import PartitionSpec as P

D = 1536
HEAD_DIM = 64
TOP = 8


eps_norm = 1e-06
resid_scale = 0.22
attn_scale = 0.015625
rope_base = 10000.0
highest = lax.Precision.HIGHEST


def shortened(shard):
    return jax.tree.map(lambda a: a.astype(jnp.bfloat16) if a.dtype == jnp.float32 else a, shard)


def documents(doc_lengths, length_all):
    doc_ends = jnp.cumsum(doc_lengths, dtype=jnp.int32)
    doc_starts = doc_ends - doc_lengths
    positions = jnp.arange(length_all, dtype=jnp.int32)
    doc_id = jnp.sum(
        (positions[:, None] >= doc_ends[None, :]).astype(jnp.int32), axis=1, dtype=jnp.int32
    )
    member = doc_id[:, None] == jnp.arange(doc_lengths.shape[0], dtype=jnp.int32)[None, :]
    doc_start = jnp.sum(jnp.where(member, doc_starts[None, :], 0), axis=1, dtype=jnp.int32)
    return (doc_id, positions - doc_start)


def angles(position, head_width):
    half_width = head_width // 2
    frequency = rope_base ** (-2.0 * jnp.arange(half_width, dtype=jnp.float32) / head_width)
    turned = position[:, None] * frequency[None, :]
    return (jnp.sin(turned)[:, None, :], jnp.cos(turned)[:, None, :])


def rotate(values, sin_table, cos_table):
    half_width = values.shape[-1] // 2
    front_half = values[..., :half_width]
    back_half = values[..., half_width:]
    return jnp.concatenate(
        [
            front_half * cos_table - back_half * sin_table,
            back_half * cos_table + front_half * sin_table,
        ],
        axis=-1,
    )


def gather_rows(value):
    return lax.all_gather(value, "row", axis=0, tiled=True)


def gather_cols(value):
    return jax.tree.map(
        lambda part, own: part.astype(own.dtype),
        lax.all_gather(shortened(value), "col", axis=0, tiled=True),
        value,
    )


def sum_cols(pieces):
    return lax.psum_scatter(pieces, "col", scatter_dimension=0, tiled=True)


def sum_rows(pieces):
    return lax.psum_scatter(pieces, "row", scatter_dimension=0, tiled=True)


def width_total(value):
    return lax.psum(value, "col")


def expert_trade(value):
    return lax.all_to_all(value, "dp", split_axis=1, concat_axis=1, tiled=True)


def attn_total(value):
    return jax.tree.map(lambda part: part.astype(jnp.float32), lax.psum(shortened(value), "dp"))


def expert_total(value):
    return jax.tree.map(
        lambda part: part.astype(jnp.float32),
        lax.psum_scatter(shortened(value), ("row", "col"), scatter_dimension=1, tiled=True),
    )


def add_all(first_set, second_set):
    return tuple((left_one + right_one for left_one, right_one in zip(first_set, second_set)))


def project(left_side, right_side):
    return jnp.dot(left_side, right_side, preferred_element_type=jnp.float32)


def shards(
    hidden_in,
    norm_gain,
    w_query,
    w_key,
    w_value,
    w_out,
    mix_gain,
    w_router,
    w_gate,
    w_up,
    w_down,
    lengths,
    routes,
    mask,
    cotangent,
):
    micro_count = hidden_in.shape[0]
    tok_dev = hidden_in.shape[1]
    width_part = hidden_in.shape[2]
    col_count = lax.axis_size("col")
    row_count = lax.axis_size("row")
    dp_count = lax.axis_size("dp")
    col_at = lax.axis_index("col")
    model_width = D
    heads_here = w_query.shape[1] // HEAD_DIM
    kv_here = w_key.shape[1] // HEAD_DIM
    group_size = heads_here // kv_here
    group_tokens = tok_dev * row_count
    quarter = tok_dev // col_count
    experts_here = w_gate.shape[0]
    experts_all = experts_here * dp_count
    capacity = quarter * 3 // 8
    slot_count = experts_all * capacity
    gain_part = lax.dynamic_slice_in_dim(norm_gain, col_at * width_part, width_part)
    router_wide = w_router.astype(jnp.float32)
    full_gate, full_up, full_down = (
        lax.all_gather(w_gate, ("row", "col"), axis=1, tiled=True),
        lax.all_gather(w_up, ("row", "col"), axis=1, tiled=True),
        lax.all_gather(w_down, ("row", "col"), axis=1, tiled=True),
    )
    expert_ids = jnp.arange(experts_all, dtype=jnp.int32)
    group_index = jnp.arange(group_tokens, dtype=jnp.int32)
    query_start = col_at * tok_dev
    query_index = query_start + jnp.arange(tok_dev, dtype=jnp.int32)
    attn_local = (
        jnp.zeros(w_query.shape, jnp.float32),
        jnp.zeros(w_key.shape, jnp.float32),
        jnp.zeros(w_value.shape, jnp.float32),
        jnp.zeros(w_out.shape, jnp.float32),
    )
    expert_local = (
        jnp.zeros(full_gate.shape, jnp.float32),
        jnp.zeros(full_up.shape, jnp.float32),
        jnp.zeros(full_down.shape, jnp.float32),
    )
    router_acc = jnp.zeros(w_router.shape, jnp.float32)
    norm_acc = jnp.zeros((width_part,), jnp.float32)
    mix_acc = jnp.zeros((model_width,), jnp.float32)
    layer_rows = []
    input_grads = []
    for step in range(micro_count):
        x_full = hidden_in[step].astype(jnp.float32)
        squares = width_total(jnp.sum(x_full * x_full, axis=1))
        scale_one = lax.rsqrt(squares / model_width + eps_norm)[:, None]
        unit_one = x_full * scale_one
        normed = (unit_one * gain_part).astype(jnp.bfloat16)
        normed_all = gather_rows(normed)
        query_p, key_p, value_p = sum_cols(
            (project(normed_all, w_query), project(normed_all, w_key), project(normed_all, w_value))
        )
        doc_all, pos_all = documents(lengths[step, 0], group_tokens)
        doc_query = lax.dynamic_slice_in_dim(doc_all, query_start, tok_dev)
        pos_query = lax.dynamic_slice_in_dim(pos_all, query_start, tok_dev).astype(jnp.float32)
        sin_table, cos_table = angles(pos_query, HEAD_DIM)
        query_rot = rotate(
            query_p.reshape(tok_dev, heads_here, HEAD_DIM), sin_table, cos_table
        ).astype(jnp.bfloat16)
        key_rot = rotate(key_p.reshape(tok_dev, kv_here, HEAD_DIM), sin_table, cos_table).astype(
            jnp.bfloat16
        )
        value_low = value_p.astype(jnp.bfloat16).reshape(tok_dev, kv_here, HEAD_DIM)
        keys_all, values_all = (
            lax.all_gather(key_rot, "col", axis=0, tiled=True),
            lax.all_gather(value_low, "col", axis=0, tiled=True),
        )
        allowed = (doc_query[:, None] == doc_all[None, :]) & (
            group_index[None, :] <= query_index[:, None]
        )
        query_grp = query_rot.reshape(tok_dev, kv_here, group_size, HEAD_DIM)
        raw_scores = jnp.einsum(
            "qhgd,khd->hgqk", query_grp, keys_all, preferred_element_type=jnp.float32
        )
        scores = jnp.where(allowed[None, None], raw_scores * attn_scale, -1e30)
        top_score = jnp.max(scores, axis=-1, keepdims=True)
        expd = jnp.exp(scores - top_score)
        row_total = jnp.sum(expd, axis=-1, keepdims=True)
        attn_probs = expd / row_total
        log_total = top_score + jnp.log(row_total)
        probs_low = attn_probs.astype(jnp.bfloat16)
        attended = jnp.einsum(
            "hgqk,khd->qhgd", probs_low, values_all, preferred_element_type=jnp.float32
        )
        attended_low = attended.reshape(tok_dev, heads_here * HEAD_DIM).astype(jnp.bfloat16)
        attended_all = gather_cols(attended_low)
        attn_branch = sum_rows(project(attended_all, w_out))
        mixed = x_full + resid_scale * attn_branch
        mixed_rows = lax.all_to_all(
            mixed.reshape(col_count, quarter, width_part),
            "col",
            split_axis=0,
            concat_axis=2,
            tiled=True,
        ).reshape(quarter, model_width)
        scale_two = lax.rsqrt(jnp.mean(mixed_rows * mixed_rows, axis=1, keepdims=True) + eps_norm)
        unit_two = mixed_rows * scale_two
        normed_two = (unit_two * mix_gain).astype(jnp.bfloat16)
        logits = project(normed_two, w_router)
        picks = routes[step]
        choose = (picks[:, :, None] == expert_ids[None, None, :]).astype(jnp.float32)
        chosen = jnp.sum(choose * logits[:, None, :], axis=-1)
        gate_weights = jax.nn.softmax(chosen, axis=-1)
        flat_picks = picks.reshape(-1)
        hit_table = (flat_picks[:, None] == expert_ids[None, :]).astype(jnp.int32)
        slot_rank = jnp.sum(
            hit_table * (jnp.cumsum(hit_table, axis=0, dtype=jnp.int32) - 1),
            axis=1,
            dtype=jnp.int32,
        )
        owner_dp = flat_picks // experts_here
        local_expert = flat_picks % experts_here
        slot_index = local_expert * (dp_count * capacity) + owner_dp * capacity + slot_rank
        token_of = (
            jnp.full((slot_count,), quarter, jnp.int32)
            .at[slot_index]
            .set(jnp.arange(quarter * TOP, dtype=jnp.int32) // TOP)
        )
        padded = jnp.concatenate([normed_two, jnp.zeros((1, model_width), jnp.bfloat16)], axis=0)
        send_rows = padded[token_of].reshape(experts_here, dp_count * capacity, model_width)
        expert_in = expert_trade(send_rows)
        gate_proj = jnp.einsum(
            "ecd,edf->ecf", expert_in, full_gate, preferred_element_type=jnp.float32
        )
        up_proj = jnp.einsum("ecd,edf->ecf", expert_in, full_up, preferred_element_type=jnp.float32)
        activated = (jax.nn.silu(gate_proj) * up_proj).astype(jnp.bfloat16)
        expert_out = jnp.einsum(
            "ecf,efd->ecd", activated, full_down, preferred_element_type=jnp.float32
        ).astype(jnp.bfloat16)
        returned = expert_trade(expert_out).reshape(slot_count, model_width)
        combined = returned[slot_index].reshape(quarter, TOP, model_width).astype(jnp.float32)
        expert_mix = jnp.sum(gate_weights[:, :, None] * combined, axis=1)
        layer_rows.append((mixed_rows + resid_scale * expert_mix).astype(jnp.bfloat16))
        grad_rows = cotangent[step].astype(jnp.float32) * mask[step][:, None].astype(jnp.float32)
        grad_mix = resid_scale * grad_rows
        grad_gates = jnp.sum(grad_mix[:, None, :] * combined, axis=-1)
        grad_chosen = gate_weights * (
            grad_gates - jnp.sum(gate_weights * grad_gates, axis=-1, keepdims=True)
        )
        grad_logits = jnp.sum(choose * grad_chosen[:, :, None], axis=1)
        gate_slots = (
            jnp.zeros((slot_count,), jnp.float32).at[slot_index].set(gate_weights.reshape(-1))
        )
        grad_pad = jnp.concatenate([grad_mix, jnp.zeros((1, model_width), jnp.float32)], axis=0)
        grad_send = (gate_slots[:, None] * grad_pad[token_of]).astype(jnp.bfloat16)
        grad_expert = expert_trade(
            grad_send.reshape(experts_here, dp_count * capacity, model_width)
        )
        grad_act = jnp.einsum(
            "ecd,efd->ecf", grad_expert, full_down, preferred_element_type=jnp.float32
        )
        micro_down = jnp.einsum(
            "ecf,ecd->efd", activated, grad_expert, preferred_element_type=jnp.float32
        )
        sigmoid_gate = jax.nn.sigmoid(gate_proj)
        silu_gate = gate_proj * sigmoid_gate
        grad_gate_p = (
            grad_act * up_proj * (sigmoid_gate + gate_proj * sigmoid_gate * (1.0 - sigmoid_gate))
        ).astype(jnp.bfloat16)
        grad_up_p = (grad_act * silu_gate).astype(jnp.bfloat16)
        grad_in = jnp.einsum(
            "ecf,edf->ecd", grad_gate_p, full_gate, preferred_element_type=jnp.float32
        ) + jnp.einsum("ecf,edf->ecd", grad_up_p, full_up, preferred_element_type=jnp.float32)
        micro_gate = jnp.einsum(
            "ecd,ecf->edf", expert_in, grad_gate_p, preferred_element_type=jnp.float32
        )
        micro_up = jnp.einsum(
            "ecd,ecf->edf", expert_in, grad_up_p, preferred_element_type=jnp.float32
        )
        expert_local = add_all(expert_local, (micro_gate, micro_up, micro_down))
        grad_back = expert_trade(grad_in.astype(jnp.bfloat16)).reshape(slot_count, model_width)
        grad_normed = jnp.sum(
            grad_back[slot_index].reshape(quarter, TOP, model_width).astype(jnp.float32), axis=1
        ) + jnp.dot(grad_logits, router_wide.T, precision=highest)
        router_acc = router_acc + jnp.dot(
            normed_two.astype(jnp.float32).T, grad_logits, precision=highest
        )
        mix_acc = mix_acc + jnp.sum(grad_normed * unit_two, axis=0)
        grad_scaled = grad_normed * mix_gain
        grad_mixed_rows = grad_rows + scale_two * (
            grad_scaled - unit_two * jnp.mean(grad_scaled * unit_two, axis=1, keepdims=True)
        )
        grad_mixed = lax.all_to_all(
            grad_mixed_rows.reshape(1, quarter, model_width),
            "col",
            split_axis=2,
            concat_axis=0,
            tiled=True,
        ).reshape(tok_dev, width_part)
        grad_branch = (resid_scale * grad_mixed).astype(jnp.bfloat16)
        grad_branch_all = gather_rows(grad_branch)
        micro_out = jnp.dot(attended_all.T, grad_branch_all, preferred_element_type=jnp.float32)
        grad_attended = sum_cols(
            jnp.dot(grad_branch_all, w_out.T, preferred_element_type=jnp.float32)
        )
        grad_att_low = grad_attended.astype(jnp.bfloat16).reshape(
            tok_dev, kv_here, group_size, HEAD_DIM
        )
        probs_again = jnp.exp(scores - log_total)
        grad_probs = jnp.einsum(
            "qhgd,khd->hgqk", grad_att_low, values_all, preferred_element_type=jnp.float32
        )
        grad_scores = probs_again * (
            grad_probs - jnp.sum(probs_again * grad_probs, axis=-1, keepdims=True)
        )
        grad_raw = (grad_scores * attn_scale).astype(jnp.bfloat16)
        probs_again_low = probs_again.astype(jnp.bfloat16)
        grad_query = jnp.einsum(
            "hgqk,khd->qhgd", grad_raw, keys_all, preferred_element_type=jnp.float32
        )
        grad_key_part = jnp.einsum(
            "hgqk,qhgd->khd", grad_raw, query_grp, preferred_element_type=jnp.float32
        )
        grad_value_part = jnp.einsum(
            "hgqk,qhgd->khd", probs_again_low, grad_att_low, preferred_element_type=jnp.float32
        )
        grad_key, grad_value = sum_cols(
            (
                grad_key_part.reshape(group_tokens, kv_here * HEAD_DIM),
                grad_value_part.reshape(group_tokens, kv_here * HEAD_DIM),
            )
        )
        grad_query_p = (
            rotate(grad_query.reshape(tok_dev, heads_here, HEAD_DIM), -sin_table, cos_table)
            .astype(jnp.bfloat16)
            .reshape(tok_dev, heads_here * HEAD_DIM)
        )
        grad_key_p = (
            rotate(grad_key.reshape(tok_dev, kv_here, HEAD_DIM), -sin_table, cos_table)
            .astype(jnp.bfloat16)
            .reshape(tok_dev, kv_here * HEAD_DIM)
        )
        grad_value_p = grad_value.astype(jnp.bfloat16)
        query_all, key_all, value_all = gather_cols((grad_query_p, grad_key_p, grad_value_p))
        micro_query = jnp.dot(normed_all.T, query_all, preferred_element_type=jnp.float32)
        micro_key = jnp.dot(normed_all.T, key_all, preferred_element_type=jnp.float32)
        micro_value = jnp.dot(normed_all.T, value_all, preferred_element_type=jnp.float32)
        grad_normed_one = sum_rows(
            jnp.dot(query_all, w_query.T, preferred_element_type=jnp.float32)
            + jnp.dot(key_all, w_key.T, preferred_element_type=jnp.float32)
            + jnp.dot(value_all, w_value.T, preferred_element_type=jnp.float32)
        )
        grad_scaled_one = grad_normed_one * gain_part
        inner_sum = width_total(jnp.sum(grad_scaled_one * unit_one, axis=1))
        norm_acc = norm_acc + jnp.sum(grad_normed_one * unit_one, axis=0)
        input_grads.append(
            grad_mixed
            + scale_one * (grad_scaled_one - unit_one * (inner_sum / model_width)[:, None])
        )
        attn_local = add_all(attn_local, (micro_query, micro_key, micro_value, micro_out))
    attn_summed = attn_total(attn_local)
    expert_summed = expert_total(expert_local)
    gain_full = lax.dynamic_update_slice_in_dim(
        jnp.zeros((model_width,), jnp.float32), norm_acc, col_at * width_part, 0
    )
    router_grad, gain_grad, mix_grad = lax.psum(
        (router_acc, gain_full, mix_acc), ("dp", "row", "col")
    )
    return (
        jnp.stack(layer_rows),
        jnp.stack(input_grads),
        gain_grad,
        attn_summed[0],
        attn_summed[1],
        attn_summed[2],
        attn_summed[3],
        mix_grad,
        router_grad,
        expert_summed[0],
        expert_summed[1],
        expert_summed[2],
    )


def spread_plane(blocks):
    return lax.all_to_all(blocks, ("row", "col"), split_axis=0, concat_axis=0, tiled=True)


MESH = pl.DeviceIdType.MESH
ANYWHERE = pl.BlockSpec(memory_space=pl.ANY)


def group_size_of(axes):
    total = 1
    for axis in axes:
        total = total * lax.axis_size(axis)
    return total


def place_in(axes):
    at = 0
    for axis in axes:
        at = at * lax.axis_size(axis) + lax.axis_index(axis)
    return at


def device_at(axes, index):
    place = {}
    for axis in reversed(axes):
        place[axis] = index % lax.axis_size(axis)
        index = index // lax.axis_size(axis)
    return place


def meet(peers):
    barrier = pltpu.get_barrier_semaphore()
    for peer in peers:
        pl.semaphore_signal(barrier, inc=1, device_id=peer, device_id_type=MESH)
    pl.semaphore_wait(barrier, len(peers))


def send(src, dst, send_sem, recv_sem, peer):
    copy = pltpu.make_async_remote_copy(
        src_ref=src,
        dst_ref=dst,
        send_sem=send_sem,
        recv_sem=recv_sem,
        device_id=peer,
        device_id_type=MESH,
    )
    copy.start()
    return copy


def trade_kernel(plans, *refs):
    count = len(plans)
    groups = [axes for axes, _ in plans]
    sources, targets, sems = refs[:count], refs[count : 2 * count], refs[2 * count :]
    widest = max(groups, key=len)
    peers = []
    for axes in (widest, *(g for g in groups if not set(g) <= set(widest))):
        size = group_size_of(axes)
        peers += [device_at(axes, (place_in(axes) + step) % size) for step in range(1, size)]
    meet(peers)
    copies, locals_ = [], []
    for at, (axes, same) in enumerate(plans):
        size, me = group_size_of(axes), place_in(axes)
        own = pltpu.make_async_copy(
            sources[at].at[0 if same else me], targets[at].at[me], sems[3 * at]
        )
        own.start()
        locals_.append(own)
        for step in range(1, size):
            to = (me + step) % size
            copies.append(
                send(
                    sources[at].at[0 if same else to],
                    targets[at].at[me],
                    sems[3 * at + 1].at[step],
                    sems[3 * at + 2].at[step],
                    device_at(axes, to),
                )
            )
    for own in locals_:
        own.wait()
    for copy in copies:
        copy.wait()


def trade(number, *pairs):
    arrays = [array for array, _ in pairs]
    plans = [(axes, array.shape[0] == 1) for array, axes in pairs]
    scratch, shapes = [], []
    for array, axes in pairs:
        shapes.append(jax.ShapeDtypeStruct((group_size_of(axes),) + array.shape[1:], array.dtype))
        size = group_size_of(axes)
        scratch += [
            pltpu.SemaphoreType.DMA,
            pltpu.SemaphoreType.DMA((size,)),
            pltpu.SemaphoreType.DMA((size,)),
        ]
    return pl.pallas_call(
        functools.partial(trade_kernel, plans),
        out_shape=shapes,
        in_specs=[ANYWHERE] * len(arrays),
        out_specs=[ANYWHERE] * len(arrays),
        scratch_shapes=scratch,
        compiler_params=pltpu.CompilerParams(collective_id=number, has_side_effects=True),
        name="trade" + str(number),
    )(*arrays)


def row_peers():
    row = lax.axis_index("row")
    rows = lax.axis_size("row")
    across = (row + rows // 2) % rows
    beside = row + 1 - 2 * (row % 2)
    return row, across, beside


def gather_plane_kernel(kinds, *refs):
    count = len(kinds)
    sources, targets, sems = refs[:count], refs[count : 2 * count], refs[2 * count :]
    row, across, beside = row_peers()
    col, cols = lax.axis_index("col"), lax.axis_size("col")
    meet(
        [{"col": (col + step) % cols} for step in range(1, cols)]
        + [{"row": across}, {"row": beside}]
    )

    def pick(kind, at):
        return {"micro": at // 2, "half": at % 2, "all": 0}[kind]

    copies, locals_ = [], []
    for at, (kind, rows_too) in enumerate(kinds):
        source, target = sources[at], targets[at]
        local_sem, send_sem, col_sem, across_sem, beside_sem = sems[5 * at : 5 * at + 5]
        me = row * cols + col if rows_too else col
        own = pltpu.make_async_copy(source.at[pick(kind, col)], target.at[me], local_sem)
        own.start()
        locals_.append(own)
        for step in range(1, cols):
            to = (col + step) % cols
            copies.append(
                send(
                    source.at[pick(kind, to)],
                    target.at[me],
                    send_sem.at[step],
                    col_sem.at[step],
                    {"col": to},
                )
            )
        if rows_too:
            mine = source.at[pick(kind, col)]
            copies.append(
                send(mine, target.at[me], send_sem.at[4], across_sem.at[0], {"row": across})
            )
            copies.append(
                send(mine, target.at[me], send_sem.at[5], beside_sem.at[0], {"row": beside})
            )

    def arrival(at, block, sem):
        pltpu.make_async_copy(targets[at].at[block], targets[at].at[block], sem).wait()

    for step in range(1, cols):
        for at, (kind, rows_too) in enumerate(kinds):
            _, send_sem, col_sem, across_sem, beside_sem = sems[5 * at : 5 * at + 5]
            origin = (col + cols - step) % cols
            block = row * cols + origin if rows_too else origin
            arrival(at, block, col_sem.at[step])
            if rows_too:
                part = targets[at].at[block]
                copies.append(
                    send(part, part, send_sem.at[5 + step], across_sem.at[step], {"row": across})
                )
                copies.append(
                    send(part, part, send_sem.at[8 + step], beside_sem.at[step], {"row": beside})
                )
    for step in range(cols):
        for at, (kind, rows_too) in enumerate(kinds):
            if not rows_too:
                continue
            _, send_sem, _, across_sem, beside_sem = sems[5 * at : 5 * at + 5]
            block = across * cols + (col + cols - step) % cols
            arrival(at, block, across_sem.at[step])
            part = targets[at].at[block]
            copies.append(
                send(part, part, send_sem.at[12 + step], beside_sem.at[4 + step], {"row": beside})
            )
    for at, (kind, rows_too) in enumerate(kinds):
        if rows_too:
            for step in range(2 * cols):
                side = beside if step < cols else (beside + 2) % lax.axis_size("row")
                arrival(at, side * cols + (col + cols - step) % cols, sems[5 * at + 4].at[step])
    for own in locals_:
        own.wait()
    for copy in copies:
        copy.wait_send()


def gather_plane(number, *items):
    arrays = [array for array, _, _ in items]
    kinds = [(kind, rows_too) for _, kind, rows_too in items]
    cols, plane = lax.axis_size("col"), group_size_of(("row", "col"))
    scratch, shapes = [], []
    for array, kind, rows_too in items:
        scratch += [
            pltpu.SemaphoreType.DMA,
            pltpu.SemaphoreType.DMA((16,)),
            pltpu.SemaphoreType.DMA((cols,)),
            pltpu.SemaphoreType.DMA((cols,)),
            pltpu.SemaphoreType.DMA((2 * cols,)),
        ]
        shapes.append(
            jax.ShapeDtypeStruct(
                (plane if rows_too else cols,) + array.shape[1:], array.dtype
            )
        )
    return pl.pallas_call(
        functools.partial(gather_plane_kernel, kinds),
        out_shape=shapes,
        in_specs=[ANYWHERE] * len(arrays),
        out_specs=[ANYWHERE] * len(arrays),
        scratch_shapes=scratch,
        compiler_params=pltpu.CompilerParams(collective_id=number, has_side_effects=True),
        name="gather_plane" + str(number),
    )(*arrays)


def gather_all_kernel(source, target, local_sem, send_sem, col_sem, dp_sem, across_sem, beside_sem):
    row, across, beside = row_peers()
    rows, cols = lax.axis_size("row"), lax.axis_size("col")
    col, dp = lax.axis_index("col"), lax.axis_index("dp")
    other = 1 - dp
    meet(
        [{"col": (col + step) % cols} for step in range(1, cols)]
        + [{"row": across}, {"row": beside}, {"dp": other}]
    )
    copies = []

    def block_of(dp_from, row_from, step):
        return (dp_from * rows + row_from) * cols + (col + cols - step) % cols

    def arrival(block, sem):
        pltpu.make_async_copy(target.at[block], target.at[block], sem).wait()

    def pass_on(part, block, sem, peer):
        copies.append(send(part, target.at[block], send_sem.at[len(copies)], sem, peer))

    me = block_of(dp, row, 0)
    own = pltpu.make_async_copy(source.at[0], target.at[me], local_sem)
    own.start()
    for step in range(1, cols):
        pass_on(source.at[0], me, col_sem.at[step], {"col": (col + step) % cols})
    for step in range(cols):
        block = block_of(dp, row, step)
        part = source.at[0] if step == 0 else target.at[block]
        if step > 0:
            arrival(block, col_sem.at[step])
        pass_on(part, block, dp_sem.at[step], {"dp": other})
        pass_on(part, block, across_sem.at[step], {"row": across})
        pass_on(part, block, beside_sem.at[step], {"row": beside})
    for step in range(cols):
        block = block_of(other, row, step)
        arrival(block, dp_sem.at[step])
        if step < 2:
            pass_on(target.at[block], block, across_sem.at[cols + step], {"row": across})
        pass_on(target.at[block], block, beside_sem.at[cols + step], {"row": beside})
        block = block_of(dp, across, step)
        arrival(block, across_sem.at[step])
        if step >= 2:
            pass_on(target.at[block], block, dp_sem.at[cols + step], {"dp": other})
        pass_on(target.at[block], block, beside_sem.at[2 * cols + step], {"row": beside})
    for step in range(cols):
        block = block_of(other, across, step)
        arrival(block, (across_sem if step < 2 else dp_sem).at[cols + step])
        pass_on(target.at[block], block, beside_sem.at[3 * cols + step], {"row": beside})
    far = (beside + rows // 2) % rows
    for turn, (dp_from, row_from) in enumerate(
        ((dp, beside), (other, beside), (dp, far), (other, far))
    ):
        for step in range(cols):
            arrival(block_of(dp_from, row_from, step), beside_sem.at[turn * cols + step])
    own.wait()
    for copy in copies:
        copy.wait_send()


def gather_all(number, array):
    cols = lax.axis_size("col")
    total = group_size_of(("dp", "row", "col"))
    return pl.pallas_call(
        gather_all_kernel,
        out_shape=jax.ShapeDtypeStruct((total,) + array.shape, array.dtype),
        in_specs=[ANYWHERE],
        out_specs=ANYWHERE,
        scratch_shapes=[
            pltpu.SemaphoreType.DMA,
            pltpu.SemaphoreType.DMA((40,)),
            pltpu.SemaphoreType.DMA((cols,)),
            pltpu.SemaphoreType.DMA((2 * cols,)),
            pltpu.SemaphoreType.DMA((2 * cols,)),
            pltpu.SemaphoreType.DMA((4 * cols,)),
        ],
        compiler_params=pltpu.CompilerParams(collective_id=number, has_side_effects=True),
        name="gather_all" + str(number),
    )(array[None])


def sum_all_kernel(
    partial,
    scores,
    total_out,
    scores_out,
    near,
    passed,
    stage,
    last,
    small_local,
    small_send,
    small_recv,
    send_sem,
    beside_sem,
    first_sem,
    second_sem,
    col_sem,
):
    row, across, beside = row_peers()
    rows, cols = lax.axis_size("row"), lax.axis_size("col")
    col, dp = lax.axis_index("col"), lax.axis_index("dp")
    other = 1 - dp
    everyone = ("dp", "row", "col")
    size, me = group_size_of(everyone), place_in(everyone)
    meet([device_at(everyone, (me + step) % size) for step in range(1, size)])
    copies = []

    def pass_on(src, dst, sem, peer):
        copies.append(send(src, dst, send_sem.at[len(copies)], sem, peer))

    def arrival(ref, sem):
        pltpu.make_async_copy(ref, ref, sem).wait()

    def block_of(dp_to, row_to, col_to):
        return (dp_to * rows + row_to) * cols + col_to

    small_own = pltpu.make_async_copy(scores.at[me], scores_out.at[me], small_local)
    small_own.start()
    small = []
    for step in range(1, size):
        to = (me + step) % size
        small.append(
            send(
                scores.at[to],
                scores_out.at[me],
                small_send.at[step],
                small_recv.at[step],
                device_at(everyone, to),
            )
        )
    far = (beside + rows // 2) % rows
    theirs = ((other, far), (other, beside), (dp, far), (dp, beside))
    mine = ((other, across), (other, row), (dp, across), (dp, row))
    for turn, (dp_to, row_to) in enumerate(theirs):
        for z in range(cols):
            at = turn * cols + z
            pass_on(
                partial.at[block_of(dp_to, row_to, z)], near.at[at], beside_sem.at[at], {"row": beside}
            )

    def chip_sum(turn, z):
        dp_to, row_to = mine[turn]
        at = turn * cols + z
        arrival(near.at[at], beside_sem.at[at])
        return partial[block_of(dp_to, row_to, z)].astype(jnp.float32) + near[at].astype(
            jnp.float32
        )

    low = jnp.bfloat16
    for z in range(cols):
        passed[z] = chip_sum(0, z).astype(low)
        peer = {"dp": other} if z < 2 else {"row": across}
        pass_on(passed.at[z], stage.at[z], first_sem.at[z], peer)
    for z in range(cols):
        value = chip_sum(1, z)
        if z >= 2:
            arrival(stage.at[z], first_sem.at[z])
            value = value + stage[z].astype(jnp.float32)
        passed[cols + z] = value.astype(low)
        pass_on(passed.at[cols + z], stage.at[cols + z], second_sem.at[z], {"dp": other})
        value = chip_sum(2, z)
        if z < 2:
            arrival(stage.at[z], first_sem.at[z])
            value = value + stage[z].astype(jnp.float32)
        passed[2 * cols + z] = value.astype(low)
        pass_on(
            passed.at[2 * cols + z], stage.at[2 * cols + z], second_sem.at[cols + z], {"row": across}
        )
    for z in range(cols):
        value = chip_sum(3, z)
        arrival(stage.at[cols + z], second_sem.at[z])
        arrival(stage.at[2 * cols + z], second_sem.at[cols + z])
        passed[3 * cols + z] = (
            value + stage[cols + z].astype(jnp.float32) + stage[2 * cols + z].astype(jnp.float32)
        ).astype(low)
    for step in range(1, cols):
        to = (col + step) % cols
        pass_on(passed.at[3 * cols + to], last.at[step], col_sem.at[step], {"col": to})
    value = passed[3 * cols + col].astype(jnp.float32)
    for step in range(1, cols):
        arrival(last.at[step], col_sem.at[step])
        value = value + last[step].astype(jnp.float32)
    total_out[...] = value
    small_own.wait()
    for copy in small:
        copy.wait()
    for copy in copies:
        copy.wait_send()


def sum_all(number, partial, scores):
    cols = lax.axis_size("col")
    total = group_size_of(("dp", "row", "col"))
    block = partial.shape[1:]
    vmem = pl.BlockSpec(memory_space=pltpu.VMEM)
    low = jnp.bfloat16
    return pl.pallas_call(
        sum_all_kernel,
        out_shape=[
            jax.ShapeDtypeStruct(block, jnp.float32),
            jax.ShapeDtypeStruct(scores.shape, scores.dtype),
        ],
        in_specs=[vmem, vmem],
        out_specs=[vmem, vmem],
        scratch_shapes=[
            pltpu.VMEM((4 * cols,) + block, low),
            pltpu.VMEM((4 * cols,) + block, low),
            pltpu.VMEM((3 * cols,) + block, low),
            pltpu.VMEM((cols,) + block, low),
            pltpu.SemaphoreType.DMA,
            pltpu.SemaphoreType.DMA((total,)),
            pltpu.SemaphoreType.DMA((total,)),
            pltpu.SemaphoreType.DMA((48,)),
            pltpu.SemaphoreType.DMA((4 * cols,)),
            pltpu.SemaphoreType.DMA((cols,)),
            pltpu.SemaphoreType.DMA((2 * cols,)),
            pltpu.SemaphoreType.DMA((cols,)),
        ],
        compiler_params=pltpu.CompilerParams(
            collective_id=number, has_side_effects=True, vmem_limit_bytes=48 * 2**20
        ),
        name="sum_all" + str(number),
    )(partial, scores)


def nt(left, right):
    return lax.dot_general(
        left, right, (((1,), (1,)), ((), ())), preferred_element_type=jnp.float32
    )


def tn(left, right):
    return lax.dot_general(
        left, right, (((0,), (0,)), ((), ())), preferred_element_type=jnp.float32
    )


def expert_kernel(
    normed,
    cot,
    table,
    rank,
    mark,
    router,
    weights,
    mix_out,
    rows_out,
    score_out,
    grads_out,
    kept_in,
    kept_dye,
    kept_act,
    kept_gate,
    kept_up,
):
    low = jnp.bfloat16
    step = pl.program_id(0)
    slots = kept_in.shape[1]
    parts, _, ff_width = weights.shape
    depth = normed.shape[1] // parts
    down_depth = ff_width // parts

    gate_w = weights[:, 0:depth, :].reshape(parts * depth, ff_width)
    up_w = weights[:, depth : 2 * depth, :].reshape(parts * depth, ff_width)

    def down_w(chunk):
        at = 2 * depth + chunk * down_depth
        return weights[:, at : at + down_depth, :].reshape(ff_width, ff_width)

    chunks = normed.shape[1] // ff_width
    tokens = normed[...]
    cots = cot[...]
    logits = jnp.where(
        table[...] > 0, project(tokens, router[...]), -jnp.inf
    )
    top = jnp.max(logits, axis=1, keepdims=True)
    raised = jnp.exp(logits - top)
    gates = raised / jnp.sum(raised, axis=1, keepdims=True)
    slot = lax.broadcasted_iota(jnp.int32, (slots, normed.shape[0]), 0)
    picked = slot == rank[0, 0:1, :]
    chosen = picked.astype(jnp.float32)
    select = chosen.astype(low)
    gate = jnp.sum(
        jnp.dot(chosen, gates, precision=highest, preferred_element_type=jnp.float32) * mark[...],
        axis=1,
        keepdims=True,
    )
    expert_in = project(select, tokens).astype(low)
    grad_mix = resid_scale * project(select, cots)
    grad_out = (gate * grad_mix).astype(low)
    gate_proj = project(expert_in, gate_w)
    up_proj = project(expert_in, up_w)
    sigmoid = 1.0 / (1.0 + jnp.exp(-gate_proj))
    silu = gate_proj * sigmoid
    act = (silu * up_proj).astype(low)
    score = jnp.zeros((slots, 1), jnp.float32)
    grad_act = jnp.zeros((slots, ff_width), jnp.float32)
    for chunk in range(chunks):
        lanes = slice(chunk * ff_width, (chunk + 1) * ff_width)
        part = down_w(chunk)
        out = project(act, part).astype(low).astype(jnp.float32)
        score = score + jnp.sum(grad_mix[:, lanes] * out, axis=1, keepdims=True)
        mix_out[:, lanes] = tn(select, (gate * out).astype(low)).astype(low)
        grad_act = grad_act + nt(grad_out[:, lanes], part)
    grad_gate = (grad_act * up_proj * (sigmoid + gate_proj * sigmoid * (1.0 - sigmoid))).astype(low)
    grad_up = (grad_act * silu).astype(low)
    grad_in = (nt(grad_gate, gate_w) + nt(grad_up, up_w)).astype(low)
    rows_out[...] = tn(select, grad_in).astype(low)
    score_row = jnp.sum(chosen * score, axis=0, keepdims=True)
    score_out[0] = jnp.broadcast_to(score_row, score_out.shape[1:])
    kept_in[step] = expert_in
    kept_dye[step] = grad_out
    kept_act[step] = act
    kept_gate[step] = grad_gate
    kept_up[step] = grad_up

    @pl.when(step == pl.num_programs(0) - 1)
    def _():
        def all_of(kept):
            return kept[...].reshape(kept.shape[0] * slots, kept.shape[2])

        rows = all_of(kept_in)
        for at, kept in ((0, kept_gate), (depth, kept_up)):
            grad = tn(rows, all_of(kept)).astype(low)
            grads_out[:, at : at + depth, :] = grad.reshape(parts, depth, ff_width)
        act_all = all_of(kept_act)
        for chunk in range(chunks):
            lanes = slice(chunk * ff_width, (chunk + 1) * ff_width)
            grad = tn(act_all, all_of(kept_dye.at[:, :, lanes])).astype(low)
            at = 2 * depth + chunk * down_depth
            grads_out[:, at : at + down_depth, :] = grad.reshape(parts, down_depth, ff_width)


def expert_pass(normed, cot, table, rank, mark, router, weights, slots):
    tiles, tile = rank.shape[0], rank.shape[2]
    tokens, width = normed.shape
    low = jnp.bfloat16
    ff_width = weights.shape[2]
    rows = pl.BlockSpec((tile, width), lambda i: (i, 0))
    whole = lambda a: pl.BlockSpec(
        a.shape, lambda i: (0,) * len(a.shape), pipeline_mode=pl.Buffered(1)
    )
    return pl.pallas_call(
        expert_kernel,
        grid=(tiles,),
        out_shape=[
            jax.ShapeDtypeStruct((tokens, width), low),
            jax.ShapeDtypeStruct((tokens, width), low),
            jax.ShapeDtypeStruct((tiles, 8, tile), jnp.float32),
            jax.ShapeDtypeStruct(weights.shape, low),
        ],
        in_specs=[
            rows,
            rows,
            pl.BlockSpec((tile, table.shape[1]), lambda i: (i, 0)),
            pl.BlockSpec((1,) + rank.shape[1:], lambda i: (i, 0, 0)),
            whole(mark),
            whole(router),
            whole(weights),
        ],
        out_specs=[
            rows,
            rows,
            pl.BlockSpec((1, 8, tile), lambda i: (i, 0, 0)),
            whole(weights),
        ],
        scratch_shapes=[
            pltpu.VMEM((tiles, slots, width), low),
            pltpu.VMEM((tiles, slots, width), low),
            pltpu.VMEM((tiles, slots, ff_width), low),
            pltpu.VMEM((tiles, slots, ff_width), low),
            pltpu.VMEM((tiles, slots, ff_width), low),
        ],
        compiler_params=pltpu.CompilerParams(vmem_limit_bytes=56 * 2**20),
        cost_estimate=pl.CostEstimate(
            flops=22 * 10**9, bytes_accessed=50 * 10**6, transcendentals=10**6
        ),
        name="expert_pass",
    )(normed, cot, table, rank, mark, router, weights)


def owned(
    hidden_in,
    norm_gain,
    w_query,
    w_key,
    w_value,
    w_out,
    mix_gain,
    w_router,
    w_gate,
    w_up,
    w_down,
    lengths,
    routes,
    mask,
    cotangent,
):
    everyone = ("dp", "row", "col")
    plane = ("row", "col")
    micro_count, tok_row, width_part = hidden_in.shape
    row_count = lax.axis_size("row")
    col_count = lax.axis_size("col")
    dp_count = lax.axis_size("dp")
    row_at = lax.axis_index("row")
    col_at = lax.axis_index("col")
    dp_at = lax.axis_index("dp")
    plane_count = row_count * col_count
    device_count = plane_count * dp_count
    plane_at = row_at * col_count + col_at
    model_width = width_part * col_count
    kv_here = w_key.shape[1] // HEAD_DIM
    group_size = w_query.shape[1] // w_key.shape[1]
    q_width = group_size * HEAD_DIM
    group_tokens = tok_row * row_count
    quarter = tok_row // col_count
    own_rows = micro_count * quarter
    experts_here, slice_width, ff_width = w_gate.shape
    down_slice = w_down.shape[1]
    experts_all = experts_here * dp_count
    expert_at = dp_at * plane_count + plane_at
    micro_at = col_at // kv_here
    half_at = col_at % kv_here

    masked_cot = cotangent * mask[:, :, None].astype(cotangent.dtype)

    w_qkv = jnp.concatenate(
        [
            w_query.reshape(width_part, kv_here, q_width),
            w_key.reshape(width_part, kv_here, HEAD_DIM),
            w_value.reshape(width_part, kv_here, HEAD_DIM),
        ],
        axis=2,
    ).transpose(1, 0, 2)
    qkv_width = q_width + 2 * HEAD_DIM
    x_blocks, w_mine, w_out_all = gather_plane(
        0, (hidden_in, "micro", True), (w_qkv, "half", False), (w_out[None], "all", True)
    )
    weights = jnp.concatenate(
        [w_gate, w_up]
        + [w_down[:, :, at : at + ff_width] for at in range(0, model_width, ff_width)],
        axis=1,
    )
    x_blocks, weights, masked_cot = lax.optimization_barrier((x_blocks, weights, masked_cot))
    cot_all = lax.all_gather(
        masked_cot.reshape(own_rows, model_width), everyone, axis=0, tiled=True
    )
    x_micro = (
        x_blocks.reshape(row_count, col_count, tok_row, width_part)
        .transpose(0, 2, 1, 3)
        .reshape(group_tokens, model_width)
        .astype(jnp.float32)
    )
    w_mine = w_mine.reshape(model_width, qkv_width)
    w_out_all = (
        w_out_all.reshape(row_count, col_count, w_out.shape[0], w_out.shape[1])
        .transpose(0, 2, 1, 3)
        .reshape(row_count * w_out.shape[0], model_width)
    )
    scale_m = lax.rsqrt(jnp.mean(x_micro * x_micro, axis=1, keepdims=True) + eps_norm)
    normed_m = (x_micro * scale_m * norm_gain).astype(jnp.bfloat16)
    qkv = project(normed_m, w_mine)
    doc_id, position = documents(lengths[:, 0][micro_at], group_tokens)
    sin_table, cos_table = angles(position.astype(jnp.float32), HEAD_DIM)
    query = rotate(
        qkv[:, :q_width].reshape(group_tokens, group_size, HEAD_DIM), sin_table, cos_table
    ).astype(jnp.bfloat16)
    key = rotate(
        qkv[:, q_width : q_width + HEAD_DIM].reshape(group_tokens, 1, HEAD_DIM),
        sin_table,
        cos_table,
    )[:, 0].astype(jnp.bfloat16)
    value = qkv[:, q_width + HEAD_DIM :].astype(jnp.bfloat16)
    order = jnp.arange(group_tokens, dtype=jnp.int32)
    allowed = (doc_id[:, None] == doc_id[None, :]) & (order[None, :] <= order[:, None])
    raw_scores = jnp.einsum("qgd,kd->gqk", query, key, preferred_element_type=jnp.float32)
    scores = jnp.where(allowed[None], raw_scores * attn_scale, -1e30)
    probs = jax.nn.softmax(scores, axis=-1)
    probs_low = probs.astype(jnp.bfloat16)
    attended = (
        jnp.einsum("gqk,kd->qgd", probs_low, value, preferred_element_type=jnp.float32)
        .reshape(group_tokens, q_width)
        .astype(jnp.bfloat16)
    )

    picks = jnp.pad(routes.reshape(own_rows, TOP).T, ((0, 0), (0, 128 - own_rows)))
    attended_own, x_own, routes_all = trade(
        1,
        (attended.reshape(plane_count, quarter, q_width), plane),
        (
            hidden_in.reshape(micro_count, col_count, quarter, width_part).transpose(1, 0, 2, 3),
            ("col",),
        ),
        (picks[None], everyone),
    )
    attended_own, weights = lax.optimization_barrier((attended_own, weights))
    weights = spread_plane(weights)
    x_own = (
        x_own.transpose(1, 2, 0, 3).reshape(own_rows, model_width).astype(jnp.float32)
    )
    routes_all = (
        routes_all[:, :, :own_rows].transpose(0, 2, 1).reshape(device_count * own_rows, TOP)
    )
    attended_own = (
        attended_own
        .reshape(row_count, micro_count, kv_here, quarter, q_width)
        .transpose(1, 3, 0, 2, 4)
        .reshape(own_rows, row_count * kv_here * q_width)
    )
    mixed = x_own + resid_scale * project(attended_own, w_out_all)
    scale_two = lax.rsqrt(jnp.mean(mixed * mixed, axis=1, keepdims=True) + eps_norm)
    unit_two = mixed * scale_two
    normed_two = (unit_two * mix_gain).astype(jnp.bfloat16)
    expert_ids = jnp.arange(experts_all, dtype=jnp.int32)

    def gating(normed_rows, picks):
        chosen = jnp.any(picks[:, :, None] == expert_ids[None, None, :], axis=1)
        logits = jnp.where(chosen, project(normed_rows, w_router), -jnp.inf)
        return jax.nn.softmax(logits, axis=-1)

    normed_all = gather_all(2, normed_two).reshape(device_count * own_rows, model_width)
    normed_all, w_mine = lax.optimization_barrier((normed_all, w_mine))
    neighbours = [(at, at + 1 - 2 * (at % 2)) for at in range(col_count)]
    w_pair = jnp.stack([w_mine, lax.ppermute(w_mine, "col", neighbours)])
    w_pair = jnp.where(half_at == 0, w_pair, w_pair[::-1])
    w_qkv_all = (
        lax.all_gather(w_pair, "row", axis=0, tiled=False)
        .transpose(2, 0, 1, 3)
        .reshape(model_width, row_count * kv_here * qkv_width)
    )
    gates_own = gating(normed_two, routes.reshape(own_rows, TOP))

    tile = col_count * own_rows
    slots = col_count * micro_count * (quarter * 3 // 8)
    table = jnp.any(routes_all[:, :, None] == expert_ids[None, None, :], axis=1)
    here = jnp.any(routes_all == expert_at, axis=1).astype(jnp.int32).reshape(-1, tile)
    rank = jnp.where(here > 0, jnp.cumsum(here, axis=1, dtype=jnp.int32) - 1, -1)
    pad_experts = 128 - experts_all
    mix_part, grad_rows_part, grad_gate_mine, grads = expert_pass(
        normed_all,
        cot_all,
        jnp.pad(table.astype(jnp.float32), ((0, 0), (0, pad_experts))),
        jnp.broadcast_to(rank[:, None, :], (rank.shape[0], 8, tile)),
        (jnp.arange(128, dtype=jnp.int32) == expert_at).astype(jnp.float32)[None],
        jnp.pad(w_router, ((0, 0), (0, pad_experts))),
        weights,
        slots,
    )
    grad_gate_mine = grad_gate_mine[:, 0, :].reshape(-1)
    scores_send = jnp.broadcast_to(
        jnp.pad(
            grad_gate_mine.reshape(device_count, 1, own_rows),
            ((0, 0), (0, 0), (0, 128 - own_rows)),
        ),
        (device_count, 8, 128),
    )
    grad_normed, grad_gates = sum_all(
        3, grad_rows_part.reshape(device_count, own_rows, model_width), scores_send
    )
    grad_gates = grad_gates[:, 0, :own_rows].T
    chosen_own = jnp.any(
        routes.reshape(own_rows, TOP)[:, :, None] == expert_ids[None, None, :], axis=1
    )
    grad_gates = jnp.where(chosen_own, grad_gates, 0.0)
    grad_logits = gates_own * (
        grad_gates - jnp.sum(gates_own * grad_gates, axis=1, keepdims=True)
    )
    expert_mix = lax.psum_scatter(mix_part, everyone, scatter_dimension=0, tiled=True)
    layer_out = (mixed + resid_scale * expert_mix.astype(jnp.float32)).astype(jnp.bfloat16)
    grad_normed = grad_normed + jnp.dot(
        grad_logits, w_router.astype(jnp.float32).T, precision=highest
    )
    mix_part_grad = jnp.sum(grad_normed * unit_two, axis=0)
    grad_scaled = grad_normed * mix_gain
    grad_mixed = masked_cot.reshape(own_rows, model_width).astype(jnp.float32) + scale_two * (
        grad_scaled - unit_two * jnp.mean(grad_scaled * unit_two, axis=1, keepdims=True)
    )
    grad_branch = (resid_scale * grad_mixed).astype(jnp.bfloat16)

    lines = lambda row: jnp.pad(row.reshape(-1, 128), ((0, 4), (0, 0)))[None]
    branch_m, logits_plane, mix_parts = gather_plane(
        4,
        (grad_branch.reshape(micro_count, quarter, model_width), "micro", True),
        (jnp.pad(grad_logits.T, ((0, 0), (0, 128 - own_rows)))[None], "all", True),
        (lines(mix_part_grad), "all", True),
    )
    branch_m, grads = lax.optimization_barrier((branch_m, grads))
    grads = spread_plane(grads)
    out_gate = grads[:, :slice_width].astype(jnp.float32)
    out_up = grads[:, slice_width : 2 * slice_width].astype(jnp.float32)
    out_down = jnp.concatenate(
        [
            grads[:, at : at + down_slice]
            for at in range(2 * slice_width, grads.shape[1], down_slice)
        ],
        axis=2,
    ).astype(jnp.float32)
    low = jnp.bfloat16
    left = logits_plane[:, :, :own_rows].transpose(1, 0, 2).reshape(experts_all, -1)
    parts = []
    for _ in range(3):
        parts.append(left.astype(low))
        left = left - parts[-1].astype(jnp.float32)
    normed_plane = lax.dynamic_slice_in_dim(
        normed_all, dp_at * plane_count * own_rows, plane_count * own_rows
    )
    router_part = jnp.sum(
        jnp.dot(
            jnp.concatenate(parts, axis=0), normed_plane, preferred_element_type=jnp.float32
        ).reshape(3, experts_all, model_width),
        axis=0,
    )
    mix_part_grad = jnp.sum(mix_parts, axis=0)
    branch_m = branch_m.reshape(group_tokens, model_width)
    w_out_mine = lax.dynamic_slice_in_dim(
        w_out_all, (row_at * kv_here + half_at) * q_width, q_width
    )
    grad_att = (
        jnp.dot(branch_m, w_out_mine.T, preferred_element_type=jnp.float32)
        .astype(jnp.bfloat16)
        .reshape(group_tokens, group_size, HEAD_DIM)
    )
    out_part = jnp.dot(attended.T, branch_m, preferred_element_type=jnp.float32)
    grad_probs = jnp.einsum("qgd,kd->gqk", grad_att, value, preferred_element_type=jnp.float32)
    grad_scores = probs * (grad_probs - jnp.sum(probs * grad_probs, axis=-1, keepdims=True))
    grad_raw = (grad_scores * attn_scale).astype(jnp.bfloat16)
    grad_query = jnp.einsum("gqk,kd->qgd", grad_raw, key, preferred_element_type=jnp.float32)
    grad_key = jnp.einsum("gqk,qgd->kd", grad_raw, query, preferred_element_type=jnp.float32)
    grad_value = jnp.einsum("gqk,qgd->kd", probs_low, grad_att, preferred_element_type=jnp.float32)
    grad_qkv = jnp.concatenate(
        [
            rotate(grad_query, -sin_table, cos_table).reshape(group_tokens, q_width),
            rotate(grad_key[:, None], -sin_table, cos_table)[:, 0],
            grad_value,
        ],
        axis=1,
    ).astype(jnp.bfloat16)
    qkv_part = jnp.dot(grad_qkv.T, normed_m, preferred_element_type=jnp.float32)
    grad_qkv_own, qkv_part, out_part = trade(
        5,
        (grad_qkv.reshape(plane_count, quarter, qkv_width), plane),
        (
            qkv_part.astype(low).reshape(qkv_width, col_count, width_part).transpose(1, 0, 2),
            ("col",),
        ),
        (
            out_part.astype(low).reshape(q_width, col_count, width_part).transpose(1, 0, 2),
            ("col",),
        ),
    )
    grad_qkv_own = (
        grad_qkv_own.reshape(row_count, micro_count, kv_here, quarter, qkv_width)
        .transpose(1, 3, 0, 2, 4)
        .reshape(own_rows, row_count * kv_here * qkv_width)
    )
    grad_normed_one = jnp.dot(grad_qkv_own, w_qkv_all.T, preferred_element_type=jnp.float32)
    scale_one = lax.rsqrt(jnp.mean(x_own * x_own, axis=1, keepdims=True) + eps_norm)
    unit_one = x_own * scale_one
    norm_part = jnp.sum(grad_normed_one * unit_one, axis=0)
    grad_scaled_one = grad_normed_one * norm_gain
    grad_x = grad_mixed + scale_one * (
        grad_scaled_one
        - unit_one * jnp.mean(grad_scaled_one * unit_one, axis=1, keepdims=True)
    )

    def halves(part):
        part = part.astype(jnp.float32)
        return jnp.sum(part.reshape((micro_count, kv_here) + part.shape[1:]), axis=0).astype(low)

    grad_input, qkv_sum, out_sum, router_grad, mix_grad, norm_grad = trade(
        6,
        (
            grad_x.astype(low)
            .reshape(micro_count, quarter, col_count, width_part)
            .transpose(2, 0, 1, 3),
            ("col",),
        ),
        (halves(qkv_part)[None], ("dp",)),
        (halves(out_part)[None], ("dp",)),
        (router_part[None], ("dp",)),
        (mix_part_grad[None], ("dp",)),
        (lines(norm_part), everyone),
    )
    grad_input = (
        grad_input.transpose(1, 0, 2, 3)
        .reshape(micro_count, tok_row, width_part)
        .astype(jnp.float32)
    )
    qkv_sum = jnp.sum(qkv_sum.astype(jnp.float32), axis=0)
    out_sum = jnp.sum(out_sum.astype(jnp.float32), axis=0)
    router_grad = jnp.sum(router_grad, axis=0).T
    mix_grad = jnp.sum(mix_grad, axis=0).reshape(-1)[:model_width]
    norm_grad = jnp.sum(norm_grad, axis=0).reshape(-1)[:model_width]
    grad_wq = qkv_sum[:, :q_width].reshape(-1, width_part).T
    grad_wk = qkv_sum[:, q_width : q_width + HEAD_DIM].reshape(-1, width_part).T
    grad_wv = qkv_sum[:, q_width + HEAD_DIM :].reshape(-1, width_part).T
    grad_wo = out_sum.reshape(w_out.shape)
    return (
        layer_out.reshape(micro_count, quarter, model_width),
        grad_input,
        norm_grad,
        grad_wq,
        grad_wk,
        grad_wv,
        grad_wo,
        mix_grad,
        router_grad,
        out_gate,
        out_up,
        out_down,
    )


def solution(mesh):
    dp_count, row_count, col_count = (mesh.shape[name] for name in ("dp", "row", "col"))

    def body(*args):
        hidden_in, w_key, w_gate = args[0], args[3], args[8]
        kv_here = w_key.shape[1] // HEAD_DIM
        one_each = w_gate.shape[0] == row_count * col_count
        pairs = hidden_in.shape[0] * kv_here == col_count
        sizes = (dp_count, row_count, col_count, kv_here) == (2, 4, 4, 2)
        return (owned if sizes and one_each and pairs else shards)(*args)

    placed = (
        P(None, ("dp", "row"), "col"),
        P(),
        P("col", "row"),
        P("col", "row"),
        P("col", "row"),
        P("row", "col"),
        P(),
        P(),
        P("dp", ("row", "col"), None),
        P("dp", ("row", "col"), None),
        P("dp", ("row", "col"), None),
        P(None, "dp", None),
        P(None, ("dp", "row", "col"), None),
        P(None, ("dp", "row", "col")),
        P(None, ("dp", "row", "col"), None),
    )
    return jax.shard_map(
        body,
        mesh=mesh,
        in_specs=placed,
        out_specs=(
            P(None, ("dp", "row", "col"), None),
            P(None, ("dp", "row"), "col"),
            P(),
            P("col", "row"),
            P("col", "row"),
            P("col", "row"),
            P("row", "col"),
            P(),
            P(),
            P("dp", ("row", "col"), None),
            P("dp", ("row", "col"), None),
            P("dp", ("row", "col"), None),
        ),
        check_vma=False,
    )
```

```python
import functools

import jax
import jax.numpy as jnp
from jax import lax
from jax.experimental import pallas as pl
from jax.experimental.pallas import tpu as pltpu
from jax.sharding import PartitionSpec as P

D = 1536
HEAD_DIM = 64
TOP = 8


eps_norm = 1e-06
resid_scale = 0.22
attn_scale = 0.015625
rope_base = 10000.0
highest = lax.Precision.HIGHEST


def shortened(shard):
    return jax.tree.map(lambda a: a.astype(jnp.bfloat16) if a.dtype == jnp.float32 else a, shard)


def documents(doc_lengths, length_all):
    doc_ends = jnp.cumsum(doc_lengths, dtype=jnp.int32)
    doc_starts = doc_ends - doc_lengths
    positions = jnp.arange(length_all, dtype=jnp.int32)
    doc_id = jnp.sum(
        (positions[:, None] >= doc_ends[None, :]).astype(jnp.int32), axis=1, dtype=jnp.int32
    )
    member = doc_id[:, None] == jnp.arange(doc_lengths.shape[0], dtype=jnp.int32)[None, :]
    doc_start = jnp.sum(jnp.where(member, doc_starts[None, :], 0), axis=1, dtype=jnp.int32)
    return (doc_id, positions - doc_start)


def angles(position, head_width):
    half_width = head_width // 2
    frequency = rope_base ** (-2.0 * jnp.arange(half_width, dtype=jnp.float32) / head_width)
    turned = position[:, None] * frequency[None, :]
    return (jnp.sin(turned)[:, None, :], jnp.cos(turned)[:, None, :])


def rotate(values, sin_table, cos_table):
    half_width = values.shape[-1] // 2
    front_half = values[..., :half_width]
    back_half = values[..., half_width:]
    return jnp.concatenate(
        [
            front_half * cos_table - back_half * sin_table,
            back_half * cos_table + front_half * sin_table,
        ],
        axis=-1,
    )


def gather_rows(value):
    return lax.all_gather(value, "row", axis=0, tiled=True)


def gather_cols(value):
    return jax.tree.map(
        lambda part, own: part.astype(own.dtype),
        lax.all_gather(shortened(value), "col", axis=0, tiled=True),
        value,
    )


def sum_cols(pieces):
    return lax.psum_scatter(pieces, "col", scatter_dimension=0, tiled=True)


def sum_rows(pieces):
    return lax.psum_scatter(pieces, "row", scatter_dimension=0, tiled=True)


def width_total(value):
    return lax.psum(value, "col")


def expert_trade(value):
    return lax.all_to_all(value, "dp", split_axis=1, concat_axis=1, tiled=True)


def attn_total(value):
    return jax.tree.map(lambda part: part.astype(jnp.float32), lax.psum(shortened(value), "dp"))


def expert_total(value):
    return jax.tree.map(
        lambda part: part.astype(jnp.float32),
        lax.psum_scatter(shortened(value), ("row", "col"), scatter_dimension=1, tiled=True),
    )


def add_all(first_set, second_set):
    return tuple((left_one + right_one for left_one, right_one in zip(first_set, second_set)))


def project(left_side, right_side):
    return jnp.dot(left_side, right_side, preferred_element_type=jnp.float32)


def shards(
    hidden_in,
    norm_gain,
    w_query,
    w_key,
    w_value,
    w_out,
    mix_gain,
    w_router,
    w_gate,
    w_up,
    w_down,
    lengths,
    routes,
    mask,
    cotangent,
):
    micro_count = hidden_in.shape[0]
    tok_dev = hidden_in.shape[1]
    width_part = hidden_in.shape[2]
    col_count = lax.axis_size("col")
    row_count = lax.axis_size("row")
    dp_count = lax.axis_size("dp")
    col_at = lax.axis_index("col")
    model_width = D
    heads_here = w_query.shape[1] // HEAD_DIM
    kv_here = w_key.shape[1] // HEAD_DIM
    group_size = heads_here // kv_here
    group_tokens = tok_dev * row_count
    quarter = tok_dev // col_count
    experts_here = w_gate.shape[0]
    experts_all = experts_here * dp_count
    capacity = quarter * 3 // 8
    slot_count = experts_all * capacity
    gain_part = lax.dynamic_slice_in_dim(norm_gain, col_at * width_part, width_part)
    router_wide = w_router.astype(jnp.float32)
    full_gate, full_up, full_down = (
        lax.all_gather(w_gate, ("row", "col"), axis=1, tiled=True),
        lax.all_gather(w_up, ("row", "col"), axis=1, tiled=True),
        lax.all_gather(w_down, ("row", "col"), axis=1, tiled=True),
    )
    expert_ids = jnp.arange(experts_all, dtype=jnp.int32)
    group_index = jnp.arange(group_tokens, dtype=jnp.int32)
    query_start = col_at * tok_dev
    query_index = query_start + jnp.arange(tok_dev, dtype=jnp.int32)
    attn_local = (
        jnp.zeros(w_query.shape, jnp.float32),
        jnp.zeros(w_key.shape, jnp.float32),
        jnp.zeros(w_value.shape, jnp.float32),
        jnp.zeros(w_out.shape, jnp.float32),
    )
    expert_local = (
        jnp.zeros(full_gate.shape, jnp.float32),
        jnp.zeros(full_up.shape, jnp.float32),
        jnp.zeros(full_down.shape, jnp.float32),
    )
    router_acc = jnp.zeros(w_router.shape, jnp.float32)
    norm_acc = jnp.zeros((width_part,), jnp.float32)
    mix_acc = jnp.zeros((model_width,), jnp.float32)
    layer_rows = []
    input_grads = []
    for step in range(micro_count):
        x_full = hidden_in[step].astype(jnp.float32)
        squares = width_total(jnp.sum(x_full * x_full, axis=1))
        scale_one = lax.rsqrt(squares / model_width + eps_norm)[:, None]
        unit_one = x_full * scale_one
        normed = (unit_one * gain_part).astype(jnp.bfloat16)
        normed_all = gather_rows(normed)
        query_p, key_p, value_p = sum_cols(
            (project(normed_all, w_query), project(normed_all, w_key), project(normed_all, w_value))
        )
        doc_all, pos_all = documents(lengths[step, 0], group_tokens)
        doc_query = lax.dynamic_slice_in_dim(doc_all, query_start, tok_dev)
        pos_query = lax.dynamic_slice_in_dim(pos_all, query_start, tok_dev).astype(jnp.float32)
        sin_table, cos_table = angles(pos_query, HEAD_DIM)
        query_rot = rotate(
            query_p.reshape(tok_dev, heads_here, HEAD_DIM), sin_table, cos_table
        ).astype(jnp.bfloat16)
        key_rot = rotate(key_p.reshape(tok_dev, kv_here, HEAD_DIM), sin_table, cos_table).astype(
            jnp.bfloat16
        )
        value_low = value_p.astype(jnp.bfloat16).reshape(tok_dev, kv_here, HEAD_DIM)
        keys_all, values_all = (
            lax.all_gather(key_rot, "col", axis=0, tiled=True),
            lax.all_gather(value_low, "col", axis=0, tiled=True),
        )
        allowed = (doc_query[:, None] == doc_all[None, :]) & (
            group_index[None, :] <= query_index[:, None]
        )
        query_grp = query_rot.reshape(tok_dev, kv_here, group_size, HEAD_DIM)
        raw_scores = jnp.einsum(
            "qhgd,khd->hgqk", query_grp, keys_all, preferred_element_type=jnp.float32
        )
        scores = jnp.where(allowed[None, None], raw_scores * attn_scale, -1e30)
        top_score = jnp.max(scores, axis=-1, keepdims=True)
        expd = jnp.exp(scores - top_score)
        row_total = jnp.sum(expd, axis=-1, keepdims=True)
        attn_probs = expd / row_total
        log_total = top_score + jnp.log(row_total)
        probs_low = attn_probs.astype(jnp.bfloat16)
        attended = jnp.einsum(
            "hgqk,khd->qhgd", probs_low, values_all, preferred_element_type=jnp.float32
        )
        attended_low = attended.reshape(tok_dev, heads_here * HEAD_DIM).astype(jnp.bfloat16)
        attended_all = gather_cols(attended_low)
        attn_branch = sum_rows(project(attended_all, w_out))
        mixed = x_full + resid_scale * attn_branch
        mixed_rows = lax.all_to_all(
            mixed.reshape(col_count, quarter, width_part),
            "col",
            split_axis=0,
            concat_axis=2,
            tiled=True,
        ).reshape(quarter, model_width)
        scale_two = lax.rsqrt(jnp.mean(mixed_rows * mixed_rows, axis=1, keepdims=True) + eps_norm)
        unit_two = mixed_rows * scale_two
        normed_two = (unit_two * mix_gain).astype(jnp.bfloat16)
        logits = project(normed_two, w_router)
        picks = routes[step]
        choose = (picks[:, :, None] == expert_ids[None, None, :]).astype(jnp.float32)
        chosen = jnp.sum(choose * logits[:, None, :], axis=-1)
        gate_weights = jax.nn.softmax(chosen, axis=-1)
        flat_picks = picks.reshape(-1)
        hit_table = (flat_picks[:, None] == expert_ids[None, :]).astype(jnp.int32)
        slot_rank = jnp.sum(
            hit_table * (jnp.cumsum(hit_table, axis=0, dtype=jnp.int32) - 1),
            axis=1,
            dtype=jnp.int32,
        )
        owner_dp = flat_picks // experts_here
        local_expert = flat_picks % experts_here
        slot_index = local_expert * (dp_count * capacity) + owner_dp * capacity + slot_rank
        token_of = (
            jnp.full((slot_count,), quarter, jnp.int32)
            .at[slot_index]
            .set(jnp.arange(quarter * TOP, dtype=jnp.int32) // TOP)
        )
        padded = jnp.concatenate([normed_two, jnp.zeros((1, model_width), jnp.bfloat16)], axis=0)
        send_rows = padded[token_of].reshape(experts_here, dp_count * capacity, model_width)
        expert_in = expert_trade(send_rows)
        gate_proj = jnp.einsum(
            "ecd,edf->ecf", expert_in, full_gate, preferred_element_type=jnp.float32
        )
        up_proj = jnp.einsum("ecd,edf->ecf", expert_in, full_up, preferred_element_type=jnp.float32)
        activated = (jax.nn.silu(gate_proj) * up_proj).astype(jnp.bfloat16)
        expert_out = jnp.einsum(
            "ecf,efd->ecd", activated, full_down, preferred_element_type=jnp.float32
        ).astype(jnp.bfloat16)
        returned = expert_trade(expert_out).reshape(slot_count, model_width)
        combined = returned[slot_index].reshape(quarter, TOP, model_width).astype(jnp.float32)
        expert_mix = jnp.sum(gate_weights[:, :, None] * combined, axis=1)
        layer_rows.append((mixed_rows + resid_scale * expert_mix).astype(jnp.bfloat16))
        grad_rows = cotangent[step].astype(jnp.float32) * mask[step][:, None].astype(jnp.float32)
        grad_mix = resid_scale * grad_rows
        grad_gates = jnp.sum(grad_mix[:, None, :] * combined, axis=-1)
        grad_chosen = gate_weights * (
            grad_gates - jnp.sum(gate_weights * grad_gates, axis=-1, keepdims=True)
        )
        grad_logits = jnp.sum(choose * grad_chosen[:, :, None], axis=1)
        gate_slots = (
            jnp.zeros((slot_count,), jnp.float32).at[slot_index].set(gate_weights.reshape(-1))
        )
        grad_pad = jnp.concatenate([grad_mix, jnp.zeros((1, model_width), jnp.float32)], axis=0)
        grad_send = (gate_slots[:, None] * grad_pad[token_of]).astype(jnp.bfloat16)
        grad_expert = expert_trade(
            grad_send.reshape(experts_here, dp_count * capacity, model_width)
        )
        grad_act = jnp.einsum(
            "ecd,efd->ecf", grad_expert, full_down, preferred_element_type=jnp.float32
        )
        micro_down = jnp.einsum(
            "ecf,ecd->efd", activated, grad_expert, preferred_element_type=jnp.float32
        )
        sigmoid_gate = jax.nn.sigmoid(gate_proj)
        silu_gate = gate_proj * sigmoid_gate
        grad_gate_p = (
            grad_act * up_proj * (sigmoid_gate + gate_proj * sigmoid_gate * (1.0 - sigmoid_gate))
        ).astype(jnp.bfloat16)
        grad_up_p = (grad_act * silu_gate).astype(jnp.bfloat16)
        grad_in = jnp.einsum(
            "ecf,edf->ecd", grad_gate_p, full_gate, preferred_element_type=jnp.float32
        ) + jnp.einsum("ecf,edf->ecd", grad_up_p, full_up, preferred_element_type=jnp.float32)
        micro_gate = jnp.einsum(
            "ecd,ecf->edf", expert_in, grad_gate_p, preferred_element_type=jnp.float32
        )
        micro_up = jnp.einsum(
            "ecd,ecf->edf", expert_in, grad_up_p, preferred_element_type=jnp.float32
        )
        expert_local = add_all(expert_local, (micro_gate, micro_up, micro_down))
        grad_back = expert_trade(grad_in.astype(jnp.bfloat16)).reshape(slot_count, model_width)
        grad_normed = jnp.sum(
            grad_back[slot_index].reshape(quarter, TOP, model_width).astype(jnp.float32), axis=1
        ) + jnp.dot(grad_logits, router_wide.T, precision=highest)
        router_acc = router_acc + jnp.dot(
            normed_two.astype(jnp.float32).T, grad_logits, precision=highest
        )
        mix_acc = mix_acc + jnp.sum(grad_normed * unit_two, axis=0)
        grad_scaled = grad_normed * mix_gain
        grad_mixed_rows = grad_rows + scale_two * (
            grad_scaled - unit_two * jnp.mean(grad_scaled * unit_two, axis=1, keepdims=True)
        )
        grad_mixed = lax.all_to_all(
            grad_mixed_rows.reshape(1, quarter, model_width),
            "col",
            split_axis=2,
            concat_axis=0,
            tiled=True,
        ).reshape(tok_dev, width_part)
        grad_branch = (resid_scale * grad_mixed).astype(jnp.bfloat16)
        grad_branch_all = gather_rows(grad_branch)
        micro_out = jnp.dot(attended_all.T, grad_branch_all, preferred_element_type=jnp.float32)
        grad_attended = sum_cols(
            jnp.dot(grad_branch_all, w_out.T, preferred_element_type=jnp.float32)
        )
        grad_att_low = grad_attended.astype(jnp.bfloat16).reshape(
            tok_dev, kv_here, group_size, HEAD_DIM
        )
        probs_again = jnp.exp(scores - log_total)
        grad_probs = jnp.einsum(
            "qhgd,khd->hgqk", grad_att_low, values_all, preferred_element_type=jnp.float32
        )
        grad_scores = probs_again * (
            grad_probs - jnp.sum(probs_again * grad_probs, axis=-1, keepdims=True)
        )
        grad_raw = (grad_scores * attn_scale).astype(jnp.bfloat16)
        probs_again_low = probs_again.astype(jnp.bfloat16)
        grad_query = jnp.einsum(
            "hgqk,khd->qhgd", grad_raw, keys_all, preferred_element_type=jnp.float32
        )
        grad_key_part = jnp.einsum(
            "hgqk,qhgd->khd", grad_raw, query_grp, preferred_element_type=jnp.float32
        )
        grad_value_part = jnp.einsum(
            "hgqk,qhgd->khd", probs_again_low, grad_att_low, preferred_element_type=jnp.float32
        )
        grad_key, grad_value = sum_cols(
            (
                grad_key_part.reshape(group_tokens, kv_here * HEAD_DIM),
                grad_value_part.reshape(group_tokens, kv_here * HEAD_DIM),
            )
        )
        grad_query_p = (
            rotate(grad_query.reshape(tok_dev, heads_here, HEAD_DIM), -sin_table, cos_table)
            .astype(jnp.bfloat16)
            .reshape(tok_dev, heads_here * HEAD_DIM)
        )
        grad_key_p = (
            rotate(grad_key.reshape(tok_dev, kv_here, HEAD_DIM), -sin_table, cos_table)
            .astype(jnp.bfloat16)
            .reshape(tok_dev, kv_here * HEAD_DIM)
        )
        grad_value_p = grad_value.astype(jnp.bfloat16)
        query_all, key_all, value_all = gather_cols((grad_query_p, grad_key_p, grad_value_p))
        micro_query = jnp.dot(normed_all.T, query_all, preferred_element_type=jnp.float32)
        micro_key = jnp.dot(normed_all.T, key_all, preferred_element_type=jnp.float32)
        micro_value = jnp.dot(normed_all.T, value_all, preferred_element_type=jnp.float32)
        grad_normed_one = sum_rows(
            jnp.dot(query_all, w_query.T, preferred_element_type=jnp.float32)
            + jnp.dot(key_all, w_key.T, preferred_element_type=jnp.float32)
            + jnp.dot(value_all, w_value.T, preferred_element_type=jnp.float32)
        )
        grad_scaled_one = grad_normed_one * gain_part
        inner_sum = width_total(jnp.sum(grad_scaled_one * unit_one, axis=1))
        norm_acc = norm_acc + jnp.sum(grad_normed_one * unit_one, axis=0)
        input_grads.append(
            grad_mixed
            + scale_one * (grad_scaled_one - unit_one * (inner_sum / model_width)[:, None])
        )
        attn_local = add_all(attn_local, (micro_query, micro_key, micro_value, micro_out))
    attn_summed = attn_total(attn_local)
    expert_summed = expert_total(expert_local)
    gain_full = lax.dynamic_update_slice_in_dim(
        jnp.zeros((model_width,), jnp.float32), norm_acc, col_at * width_part, 0
    )
    router_grad, gain_grad, mix_grad = lax.psum(
        (router_acc, gain_full, mix_acc), ("dp", "row", "col")
    )
    return (
        jnp.stack(layer_rows),
        jnp.stack(input_grads),
        gain_grad,
        attn_summed[0],
        attn_summed[1],
        attn_summed[2],
        attn_summed[3],
        mix_grad,
        router_grad,
        expert_summed[0],
        expert_summed[1],
        expert_summed[2],
    )


def spread_plane(blocks):
    return lax.all_to_all(blocks, ("row", "col"), split_axis=0, concat_axis=0, tiled=True)


MESH = pl.DeviceIdType.MESH
ANYWHERE = pl.BlockSpec(memory_space=pl.ANY)


def group_size_of(axes):
    total = 1
    for axis in axes:
        total = total * lax.axis_size(axis)
    return total


def place_in(axes):
    at = 0
    for axis in axes:
        at = at * lax.axis_size(axis) + lax.axis_index(axis)
    return at


def device_at(axes, index):
    place = {}
    for axis in reversed(axes):
        place[axis] = index % lax.axis_size(axis)
        index = index // lax.axis_size(axis)
    return place


def meet(peers):
    barrier = pltpu.get_barrier_semaphore()
    for peer in peers:
        pl.semaphore_signal(barrier, inc=1, device_id=peer, device_id_type=MESH)
    pl.semaphore_wait(barrier, len(peers))


def send(src, dst, send_sem, recv_sem, peer):
    copy = pltpu.make_async_remote_copy(
        src_ref=src,
        dst_ref=dst,
        send_sem=send_sem,
        recv_sem=recv_sem,
        device_id=peer,
        device_id_type=MESH,
    )
    copy.start()
    return copy


def trade_start(plans, sources, targets, sems):
    copies, locals_, later = [], [], []

    def ship(at, axes, same, step):
        size, me = group_size_of(axes), place_in(axes)
        to = (me + step) % size
        copies.append(
            send(
                sources[at].at[0 if same else to],
                targets[at].at[me],
                sems[3 * at + 1].at[step],
                sems[3 * at + 2].at[step],
                device_at(axes, to),
            )
        )

    for at, (axes, same, bulk) in enumerate(plans):
        size, me = group_size_of(axes), place_in(axes)
        own = pltpu.make_async_copy(
            sources[at].at[0 if same else me], targets[at].at[me], sems[3 * at]
        )
        own.start()
        locals_.append(own)
        for step in range(1, size):
            if bulk:
                later.append((at, axes, same, step))
            else:
                ship(at, axes, same, step)

    def more(count):
        for item in later[:count]:
            ship(*item)
        del later[:count]

    return locals_, copies, more


def trade_kernel(plans, *refs):
    count = len(plans)
    groups = [axes for axes, _, _ in plans]
    sources, targets, sems = refs[:count], refs[count : 2 * count], refs[2 * count :]
    widest = max(groups, key=len)
    peers = []
    for axes in (widest, *(g for g in groups if not set(g) <= set(widest))):
        size = group_size_of(axes)
        peers += [device_at(axes, (place_in(axes) + step) % size) for step in range(1, size)]
    meet(peers)
    locals_, copies, _ = trade_start(plans, sources, targets, sems)
    for own in locals_:
        own.wait()
    for copy in copies:
        copy.wait()


def trade_shapes(pairs):
    scratch, shapes = [], []
    for array, axes in pairs:
        size = group_size_of(axes)
        shapes.append(jax.ShapeDtypeStruct((size,) + array.shape[1:], array.dtype))
        scratch += [
            pltpu.SemaphoreType.DMA,
            pltpu.SemaphoreType.DMA((size,)),
            pltpu.SemaphoreType.DMA((size,)),
        ]
    return scratch, shapes


def trade(number, *pairs):
    arrays = [array for array, _ in pairs]
    plans = [(axes, array.shape[0] == 1, False) for array, axes in pairs]
    scratch, shapes = trade_shapes(pairs)
    return pl.pallas_call(
        functools.partial(trade_kernel, plans),
        out_shape=shapes,
        in_specs=[ANYWHERE] * len(arrays),
        out_specs=[ANYWHERE] * len(arrays),
        scratch_shapes=scratch,
        compiler_params=pltpu.CompilerParams(collective_id=number, has_side_effects=True),
        name="trade" + str(number),
    )(*arrays)


def row_peers():
    row = lax.axis_index("row")
    rows = lax.axis_size("row")
    across = (row + rows // 2) % rows
    beside = row + 1 - 2 * (row % 2)
    return row, across, beside


def gather_plane_kernel(kinds, *refs):
    count = len(kinds)
    sources, targets, sems = refs[:count], refs[count : 2 * count], refs[2 * count :]
    row, across, beside = row_peers()
    col, cols = lax.axis_index("col"), lax.axis_size("col")
    meet(
        [{"col": (col + step) % cols} for step in range(1, cols)]
        + [{"row": across}, {"row": beside}]
    )

    def pick(kind, at):
        return {"micro": at // 2, "half": at % 2, "all": 0}[kind]

    copies, locals_ = [], []
    for at, (kind, rows_too) in enumerate(kinds):
        source, target = sources[at], targets[at]
        local_sem, send_sem, col_sem, across_sem, beside_sem = sems[5 * at : 5 * at + 5]
        me = row * cols + col if rows_too else col
        own = pltpu.make_async_copy(source.at[pick(kind, col)], target.at[me], local_sem)
        own.start()
        locals_.append(own)
        for step in range(1, cols):
            to = (col + step) % cols
            copies.append(
                send(
                    source.at[pick(kind, to)],
                    target.at[me],
                    send_sem.at[step],
                    col_sem.at[step],
                    {"col": to},
                )
            )
        if rows_too:
            mine = source.at[pick(kind, col)]
            copies.append(
                send(mine, target.at[me], send_sem.at[4], across_sem.at[0], {"row": across})
            )
            copies.append(
                send(mine, target.at[me], send_sem.at[5], beside_sem.at[0], {"row": beside})
            )

    def arrival(at, block, sem):
        pltpu.make_async_copy(targets[at].at[block], targets[at].at[block], sem).wait()

    for step in range(1, cols):
        for at, (kind, rows_too) in enumerate(kinds):
            _, send_sem, col_sem, across_sem, beside_sem = sems[5 * at : 5 * at + 5]
            origin = (col + cols - step) % cols
            block = row * cols + origin if rows_too else origin
            arrival(at, block, col_sem.at[step])
            if rows_too:
                part = targets[at].at[block]
                copies.append(
                    send(part, part, send_sem.at[5 + step], across_sem.at[step], {"row": across})
                )
                copies.append(
                    send(part, part, send_sem.at[8 + step], beside_sem.at[step], {"row": beside})
                )
    for step in range(cols):
        for at, (kind, rows_too) in enumerate(kinds):
            if not rows_too:
                continue
            _, send_sem, _, across_sem, beside_sem = sems[5 * at : 5 * at + 5]
            block = across * cols + (col + cols - step) % cols
            arrival(at, block, across_sem.at[step])
            part = targets[at].at[block]
            copies.append(
                send(part, part, send_sem.at[12 + step], beside_sem.at[4 + step], {"row": beside})
            )
    for at, (kind, rows_too) in enumerate(kinds):
        if rows_too:
            for step in range(2 * cols):
                side = beside if step < cols else (beside + 2) % lax.axis_size("row")
                arrival(at, side * cols + (col + cols - step) % cols, sems[5 * at + 4].at[step])
    for own in locals_:
        own.wait()
    for copy in copies:
        copy.wait_send()


def gather_plane(number, *items):
    arrays = [array for array, _, _ in items]
    kinds = [(kind, rows_too) for _, kind, rows_too in items]
    cols, plane = lax.axis_size("col"), group_size_of(("row", "col"))
    scratch, shapes = [], []
    for array, kind, rows_too in items:
        scratch += [
            pltpu.SemaphoreType.DMA,
            pltpu.SemaphoreType.DMA((16,)),
            pltpu.SemaphoreType.DMA((cols,)),
            pltpu.SemaphoreType.DMA((cols,)),
            pltpu.SemaphoreType.DMA((2 * cols,)),
        ]
        shapes.append(
            jax.ShapeDtypeStruct(
                (plane if rows_too else cols,) + array.shape[1:], array.dtype
            )
        )
    return pl.pallas_call(
        functools.partial(gather_plane_kernel, kinds),
        out_shape=shapes,
        in_specs=[ANYWHERE] * len(arrays),
        out_specs=[ANYWHERE] * len(arrays),
        scratch_shapes=scratch,
        compiler_params=pltpu.CompilerParams(collective_id=number, has_side_effects=True),
        name="gather_plane" + str(number),
    )(*arrays)


def gather_line(source, target, sems, copies):
    local_sem, send_sem, col_sem, dp_sem, across_sem, beside_sem = sems
    row, across, beside = row_peers()
    rows, cols = lax.axis_size("row"), lax.axis_size("col")
    col, dp = lax.axis_index("col"), lax.axis_index("dp")
    other = 1 - dp
    far = (beside + rows // 2) % rows
    sent = []

    def block_of(dp_from, row_from, step):
        return (dp_from * rows + row_from) * cols + (col + cols - step) % cols

    def arrival(block, sem):
        pltpu.make_async_copy(target.at[block], target.at[block], sem).wait()

    def pass_on(part, block, sem, peer):
        copy = send(part, target.at[block], send_sem.at[len(sent)], sem, peer)
        sent.append(copy)
        copies.append(copy)

    me = block_of(dp, row, 0)
    own = pltpu.make_async_copy(source.at[0], target.at[me], local_sem)

    def begin():
        own.start()
        for step in range(1, cols):
            pass_on(source.at[0], me, col_sem.at[step], {"col": (col + step) % cols})

    def line(step):
        block = block_of(dp, row, step)
        part = source.at[0] if step == 0 else target.at[block]
        if step > 0:
            arrival(block, col_sem.at[step])
        pass_on(part, block, dp_sem.at[step], {"dp": other})
        pass_on(part, block, across_sem.at[step], {"row": across})
        pass_on(part, block, beside_sem.at[step], {"row": beside})

    def side(step):
        block = block_of(other, row, step)
        arrival(block, dp_sem.at[step])
        if step < 2:
            pass_on(target.at[block], block, across_sem.at[cols + step], {"row": across})
        pass_on(target.at[block], block, beside_sem.at[cols + step], {"row": beside})
        block = block_of(dp, across, step)
        arrival(block, across_sem.at[step])
        if step >= 2:
            pass_on(target.at[block], block, dp_sem.at[cols + step], {"dp": other})
        pass_on(target.at[block], block, beside_sem.at[2 * cols + step], {"row": beside})

    def corner(step):
        block = block_of(other, across, step)
        arrival(block, (across_sem if step < 2 else dp_sem).at[cols + step])
        pass_on(target.at[block], block, beside_sem.at[3 * cols + step], {"row": beside})

    def finish():
        for turn, (dp_from, row_from) in enumerate(
            ((dp, beside), (other, beside), (dp, far), (other, far))
        ):
            for step in range(cols):
                arrival(block_of(dp_from, row_from, step), beside_sem.at[turn * cols + step])
        own.wait()

    return begin, line, side, corner, finish


def gather_sems():
    cols = lax.axis_size("col")
    return [
        pltpu.SemaphoreType.DMA,
        pltpu.SemaphoreType.DMA((40,)),
        pltpu.SemaphoreType.DMA((cols,)),
        pltpu.SemaphoreType.DMA((2 * cols,)),
        pltpu.SemaphoreType.DMA((2 * cols,)),
        pltpu.SemaphoreType.DMA((4 * cols,)),
    ]


def nt(left, right):
    return lax.dot_general(
        left, right, (((1,), (1,)), ((), ())), preferred_element_type=jnp.float32
    )


def tn(left, right):
    return lax.dot_general(
        left, right, (((0,), (0,)), ((), ())), preferred_element_type=jnp.float32
    )


def norm_rows(x, gain):
    scale = lax.rsqrt(jnp.mean(x * x, axis=1, keepdims=True) + eps_norm)
    return scale, (x * scale * gain).astype(jnp.bfloat16)


def turn(values, cos_table, sin_table):
    lane = lax.broadcasted_iota(jnp.int32, values.shape, 1)
    ahead = pltpu.roll(values, values.shape[1] - HEAD_DIM // 2, 1)
    behind = pltpu.roll(values, HEAD_DIM // 2, 1)
    return values * cos_table + jnp.where(lane % HEAD_DIM < HEAD_DIM // 2, ahead, behind) * sin_table


def key_extent(block, rows, total):
    return min(total, -(-(block + 1) * rows // 128) * 128)


def visible(doc_col, doc_row, block, rows, extent):
    query = block * rows + lax.broadcasted_iota(jnp.int32, (rows, extent), 0)
    keys = lax.broadcasted_iota(jnp.int32, (rows, extent), 1)
    same = doc_col[block * rows : (block + 1) * rows, 0:1] == doc_row[0:1, 0:extent]
    return same & (keys <= query)


def attend(query, key, allowed):
    scores = jnp.where(allowed, nt(query, key) * attn_scale, -1e30)
    raised = jnp.exp(scores - jnp.max(scores, axis=1, keepdims=True))
    return raised / jnp.sum(raised, axis=1, keepdims=True)


def front_kernel(
    x,
    w_qkv,
    w_out,
    picks,
    cot,
    weights,
    gain_one,
    gain_two,
    cos_table,
    sin_table,
    doc_col,
    doc_row,
    x_all,
    w_mine,
    w_out_all,
    picks_all,
    cot_all,
    normed_all,
    weights_own,
    qkv,
    attended,
    mixed,
    x_own,
    att_own,
    normed_two,
    local_sem,
    send_sem,
    x_sem,
    q_sem,
    o_sem,
    own_sem,
    att_send,
    att_recv,
    ship_local,
    ship_send,
    ship_recv,
    *line_sems,
):
    row, across, beside = row_peers()
    rows, cols = lax.axis_size("row"), lax.axis_size("col")
    col, dp = lax.axis_index("col"), lax.axis_index("dp")
    other = 1 - dp
    far = (beside + rows // 2) % rows
    plane = ("row", "col")
    size, me = group_size_of(plane), place_in(plane)
    low = jnp.bfloat16
    meet(
        [device_at(plane, (me + step) % size) for step in range(1, size)] + [{"dp": other}]
    )
    copies, locals_, sent, moved = [], [], [], []
    picks_line = gather_line(picks, picks_all, line_sems[0:6], copies)
    cot_line = gather_line(cot, cot_all, line_sems[6:12], copies)
    norm_line = gather_line(normed_two, normed_all, line_sems[12:18], copies)

    def pass_on(src, dst, sem, peer):
        sent.append(send(src, dst, send_sem.at[len(sent)], sem, peer))

    def arrival(ref, sem):
        pltpu.make_async_copy(ref, ref, sem).wait()

    def local(src, dst):
        copy = pltpu.make_async_copy(src, dst, local_sem.at[len(locals_)])
        copy.start()
        locals_.append(copy)

    def ship(first, last):
        for step in range(first, last):
            to = (me + step) % size
            moved.append(
                send(
                    weights.at[to],
                    weights_own.at[me],
                    ship_send.at[step],
                    ship_recv.at[step],
                    device_at(plane, to),
                )
            )

    def origin(step):
        return (col + cols - step) % cols

    micro, depth, width = x.shape
    quarter = depth // cols
    half_depth = w_out.shape[1]

    def lanes(step):
        return pl.ds(pl.multiple_of(origin(step) * width, width), width)

    def x_at(row_from, step):
        return x_all.at[pl.ds(pl.multiple_of(row_from * depth, depth), depth), lanes(step)]

    def out_at(row_from, step, half):
        first = pl.multiple_of((row_from * 2 + half) * half_depth, half_depth)
        return w_out_all.at[pl.ds(first, half_depth), lanes(step)]

    def own_at(m, step):
        return x_own.at[pl.ds(m * quarter, quarter), lanes(step)]

    my_x = x_at(row, 0)
    for step in range(1, cols):
        to = (col + step) % cols
        pass_on(x.at[to // 2], my_x, x_sem.at[step], {"col": to})
        pass_on(w_qkv.at[to % 2, dp], w_mine.at[col, dp], q_sem.at[step], {"col": to})
    local(x.at[col // 2], my_x)
    local(w_qkv.at[col % 2], w_mine.at[col])
    for half in range(2):
        local(w_out.at[half], out_at(row, 0, half))
    pass_on(x.at[col // 2], my_x, x_sem.at[cols], {"row": across})
    pass_on(x.at[col // 2], my_x, x_sem.at[2 * cols], {"row": beside})
    for step in range(1, cols):
        to = (col + step) % cols
        pass_on(w_out.at[dp], out_at(row, 0, dp), o_sem.at[step], {"col": to})
        first = pl.multiple_of(to * quarter, quarter)
        for m in range(micro):
            pass_on(
                x.at[m, pl.ds(first, quarter)],
                own_at(m, 0),
                own_sem.at[m * cols + step],
                {"col": to},
            )
    for m in range(micro):
        local(x.at[m, pl.ds(pl.multiple_of(col * quarter, quarter), quarter)], own_at(m, 0))
    for half in range(2):
        pass_on(w_out.at[half], out_at(row, 0, half), o_sem.at[(2 + half) * cols], {"row": across})
        pass_on(w_out.at[half], out_at(row, 0, half), o_sem.at[(4 + half) * cols], {"row": beside})
    for step in range(1, cols):
        part = x_at(row, step)
        arrival(part, x_sem.at[step])
        pass_on(part, part, x_sem.at[cols + step], {"row": across})
        pass_on(part, part, x_sem.at[2 * cols + step], {"row": beside})
        part = w_mine.at[origin(step), dp]
        arrival(part, q_sem.at[step])
        pass_on(part, part, q_sem.at[cols + step], {"dp": other})
    for step in range(cols):
        part = x_at(across, step)
        arrival(part, x_sem.at[cols + step])
        pass_on(part, part, x_sem.at[3 * cols + step], {"row": beside})
    for step in range(1, cols):
        part = out_at(row, step, dp)
        arrival(part, o_sem.at[step])
        pass_on(part, part, o_sem.at[cols + step], {"dp": other})
        pass_on(part, part, o_sem.at[2 * cols + step], {"row": across})
        pass_on(part, part, o_sem.at[4 * cols + step], {"row": beside})
    picks_line[0]()
    cot_line[0]()
    own = pltpu.make_async_copy(weights.at[me], weights_own.at[me], ship_local)
    own.start()
    for step in range(1, cols):
        arrival(w_mine.at[origin(step), other], q_sem.at[cols + step])
    for at, row_from in enumerate((beside, far)):
        for step in range(cols):
            arrival(x_at(row_from, step), x_sem.at[(2 + at) * cols + step])
    for copy in locals_:
        copy.wait()

    tokens, model_width = x_all.shape
    projection = w_mine[...].reshape(model_width, w_mine.shape[3])
    for block in range(rows):
        part = slice(block * depth, (block + 1) * depth)
        _, normed = norm_rows(x_all[part, :].astype(jnp.float32), gain_one[...])
        values = project(normed, projection)
        cosine, sine = cos_table[part, :], sin_table[part, :]
        for at in range(2):
            piece = slice(at * 128, (at + 1) * 128)
            qkv[part, piece] = turn(values[:, piece], cosine, sine).astype(low)
        qkv[part, 256:] = values[:, 256:].astype(low)
    heads = attended.shape[2] // HEAD_DIM
    kv_at = heads * HEAD_DIM
    for block in range(rows):
        extent = key_extent(block, depth, tokens)
        allowed = visible(doc_col, doc_row, block, depth, extent)
        key = qkv[0:extent, kv_at : kv_at + HEAD_DIM]
        value = qkv[0:extent, kv_at + HEAD_DIM : kv_at + 2 * HEAD_DIM]
        outs = []
        for head in range(heads):
            query = qkv[
                block * depth : (block + 1) * depth, head * HEAD_DIM : (head + 1) * HEAD_DIM
            ]
            outs.append(project(attend(query, key, allowed).astype(low), value))
        out = jnp.concatenate(outs, axis=1).astype(low)
        attended[block * cols : (block + 1) * cols] = out.reshape(cols, quarter, out.shape[1])
    for step in range(1, size):
        to = (me + step) % size
        moved.append(
            send(
                attended.at[to],
                att_own.at[me],
                att_send.at[step],
                att_recv.at[step],
                device_at(plane, to),
            )
        )
    stay = pltpu.make_async_copy(attended.at[me], att_own.at[me], att_send.at[0])
    stay.start()
    ship(1, 5)
    for step in range(cols):
        picks_line[1](step)
        cot_line[1](step)
    for step in range(1, cols):
        part = out_at(row, step, other)
        arrival(part, o_sem.at[cols + step])
        pass_on(part, part, o_sem.at[3 * cols + step], {"row": across})
        pass_on(part, part, o_sem.at[5 * cols + step], {"row": beside})
    for at in range(2):
        for step in range(cols):
            half = at if step == 0 else (dp if at == 0 else other)
            part = out_at(across, step, half)
            arrival(part, o_sem.at[(2 + at) * cols + step])
            pass_on(part, part, o_sem.at[(6 + at) * cols + step], {"row": beside})
    for at, row_from in enumerate((beside, far)):
        for step in range(cols):
            for part in range(2):
                half = part if step == 0 else (dp if part == 0 else other)
                arrival(out_at(row_from, step, half), o_sem.at[(4 + 2 * at + part) * cols + step])
    for step in range(1, cols):
        for m in range(micro):
            arrival(own_at(m, step), own_sem.at[m * cols + step])
    stay.wait()
    for step in range(1, size):
        arrival(att_own.at[(me + size - step) % size], att_recv.at[step])
    pairs = cols // micro
    for m in range(micro):
        total = jnp.zeros((quarter, model_width), jnp.float32)
        for row_from in range(rows):
            for pair in range(pairs):
                first = (row_from * pairs + pair) * kv_at
                total = total + project(
                    att_own[row_from * cols + m * pairs + pair],
                    w_out_all[first : first + kv_at, :],
                )
        part = slice(m * quarter, (m + 1) * quarter)
        value = x_own[part, :].astype(jnp.float32) + resid_scale * total
        mixed[part, :] = value
        normed_two[0, part, :] = norm_rows(value, gain_two[...])[1]

    begin, line, side, corner, finish = norm_line
    begin()
    for step in range(cols):
        picks_line[2](step)
        cot_line[2](step)
        ship(5 + 2 * step, 7 + 2 * step)
    for step in range(cols):
        line(step)
    ship(5 + 2 * cols, size)
    for step in range(cols):
        picks_line[3](step)
        cot_line[3](step)
        side(step)
    for step in range(cols):
        corner(step)
    picks_line[4]()
    cot_line[4]()
    finish()
    own.wait()
    for copy in moved[: size - 1]:
        copy.wait_send()
    for copy in moved[size - 1 :]:
        copy.wait()
    for copy in copies + sent:
        copy.wait_send()


def front(number, x, w_qkv, w_out, picks, cot, weights, gains, tables, docs, heads_width):
    cols, rows = lax.axis_size("col"), lax.axis_size("row")
    total, plane = group_size_of(("dp", "row", "col")), group_size_of(("row", "col"))
    micro, depth, part_width = x.shape
    width, tokens, low = part_width * cols, depth * rows, jnp.bfloat16
    quarter = depth // cols
    vmem = pl.BlockSpec(memory_space=pltpu.VMEM)
    shape = jax.ShapeDtypeStruct
    return pl.pallas_call(
        front_kernel,
        out_shape=[
            shape((tokens, width), low),
            shape((cols,) + w_qkv.shape[1:], low),
            shape((rows * 2 * w_out.shape[1], width), low),
            shape((total,) + picks.shape, picks.dtype),
            shape((total,) + cot.shape, low),
            shape((total,) + cot.shape, low),
            shape(weights.shape, low),
            shape((tokens, w_qkv.shape[3]), low),
            shape((plane, quarter, heads_width), low),
            shape((micro * quarter, width), jnp.float32),
        ],
        in_specs=[ANYWHERE] * 6 + [vmem] * 6,
        out_specs=[vmem] * 3 + [ANYWHERE] * 4 + [vmem] * 3,
        scratch_shapes=[
            pltpu.VMEM((micro * quarter, width), low),
            pltpu.VMEM((plane, quarter, heads_width), low),
            pltpu.VMEM((1, micro * quarter, width), low),
            pltpu.SemaphoreType.DMA((8,)),
            pltpu.SemaphoreType.DMA((72,)),
            pltpu.SemaphoreType.DMA((4 * cols,)),
            pltpu.SemaphoreType.DMA((2 * cols,)),
            pltpu.SemaphoreType.DMA((8 * cols,)),
            pltpu.SemaphoreType.DMA((micro * cols,)),
            pltpu.SemaphoreType.DMA((plane,)),
            pltpu.SemaphoreType.DMA((plane,)),
            pltpu.SemaphoreType.DMA,
            pltpu.SemaphoreType.DMA((plane,)),
            pltpu.SemaphoreType.DMA((plane,)),
        ]
        + gather_sems() * 3,
        compiler_params=pltpu.CompilerParams(
            collective_id=number, has_side_effects=True, vmem_limit_bytes=56 * 2**20
        ),
        name="front" + str(number),
    )(x, w_qkv, w_out, picks[None], cot[None], weights, *gains, *tables, *docs)


def sum_body(
    more,
    between,
    partial,
    total_out,
    near,
    mine,
    passed,
    stage,
    last,
    local_sem,
    send_sem,
    beside_sem,
    first_sem,
    second_sem,
    col_sem,
):
    row, across, beside = row_peers()
    rows, cols = lax.axis_size("row"), lax.axis_size("col")
    col, dp = lax.axis_index("col"), lax.axis_index("dp")
    other = 1 - dp
    copies, loads = [], []

    def pass_on(src, dst, sem, peer):
        copies.append(send(src, dst, send_sem.at[len(copies)], sem, peer))

    def arrival(ref, sem):
        pltpu.make_async_copy(ref, ref, sem).wait()

    def block_of(dp_to, row_to, col_to):
        return (dp_to * rows + row_to) * cols + col_to

    far = (beside + rows // 2) % rows
    theirs = ((other, far), (other, beside), (dp, far), (dp, beside))
    ours = ((other, across), (other, row), (dp, across), (dp, row))
    for turn, (dp_to, row_to) in enumerate(theirs):
        for z in range(cols):
            at = turn * cols + z
            pass_on(
                partial.at[block_of(dp_to, row_to, z)],
                near.at[at],
                beside_sem.at[at],
                {"row": beside},
            )
            load = pltpu.make_async_copy(
                partial.at[block_of(*ours[turn], z)], mine.at[at], local_sem.at[at]
            )
            load.start()
            loads.append(load)

    def chip_sum(turn, z):
        at = turn * cols + z
        loads[at].wait()
        arrival(near.at[at], beside_sem.at[at])
        return mine[at].astype(jnp.float32) + near[at].astype(jnp.float32)

    low = jnp.bfloat16
    more(5)
    for z in range(cols):
        passed[z] = chip_sum(0, z).astype(low)
        peer = {"dp": other} if z < 2 else {"row": across}
        pass_on(passed.at[z], stage.at[z], first_sem.at[z], peer)
    more(5)
    if between:
        between[0]()
    for z in range(cols):
        value = chip_sum(1, z)
        if z >= 2:
            arrival(stage.at[z], first_sem.at[z])
            value = value + stage[z].astype(jnp.float32)
        passed[cols + z] = value.astype(low)
        pass_on(passed.at[cols + z], stage.at[cols + z], second_sem.at[z], {"dp": other})
        value = chip_sum(2, z)
        if z < 2:
            arrival(stage.at[z], first_sem.at[z])
            value = value + stage[z].astype(jnp.float32)
        passed[2 * cols + z] = value.astype(low)
        pass_on(
            passed.at[2 * cols + z],
            stage.at[2 * cols + z],
            second_sem.at[cols + z],
            {"row": across},
        )
    more(99)
    if between:
        between[1]()
    for step in range(cols - 1, -1, -1):
        z = (col + step) % cols
        at = 3 * cols + z
        pltpu.make_async_copy(mine.at[at], mine.at[at], local_sem.at[at]).wait()
        arrival(near.at[at], beside_sem.at[at])
        value = mine[at].astype(jnp.float32) + near[at].astype(jnp.float32)
        arrival(stage.at[cols + z], second_sem.at[z])
        arrival(stage.at[2 * cols + z], second_sem.at[cols + z])
        value = (
            value + stage[cols + z].astype(jnp.float32) + stage[2 * cols + z].astype(jnp.float32)
        )
        if step > 0:
            passed[at] = value.astype(low)
            pass_on(passed.at[at], last.at[step], col_sem.at[step], {"col": z})
    for step in range(1, cols):
        arrival(last.at[step], col_sem.at[step])
        value = value + last[step].astype(jnp.float32)
    total_out[...] = value
    for copy in copies:
        copy.wait_send()


def sum_scratch(block):
    cols = lax.axis_size("col")
    low = jnp.bfloat16
    return [
        pltpu.VMEM((4 * cols,) + block, low),
        pltpu.VMEM((4 * cols,) + block, low),
        pltpu.VMEM((4 * cols,) + block, low),
        pltpu.VMEM((3 * cols,) + block, low),
        pltpu.VMEM((cols,) + block, low),
        pltpu.SemaphoreType.DMA((4 * cols,)),
        pltpu.SemaphoreType.DMA((48,)),
        pltpu.SemaphoreType.DMA((4 * cols,)),
        pltpu.SemaphoreType.DMA((cols,)),
        pltpu.SemaphoreType.DMA((2 * cols,)),
        pltpu.SemaphoreType.DMA((cols,)),
    ]


def heads_body(
    partial, total_out, near, across_buf, pair_buf, passed, send_sem, near_sem, across_sem, pair_sem
):
    row, across, beside = row_peers()
    rows = lax.axis_size("row")
    col = lax.axis_index("col")
    half = col % 2
    pair = col + 1 - 2 * half
    far = (beside + rows // 2) % rows
    copies = []

    def pass_on(src, dst, sem, peer):
        copies.append(send(src, dst, send_sem.at[len(copies)], sem, peer))

    def arrival(ref, sem):
        pltpu.make_async_copy(ref, ref, sem).wait()

    def block(row_to, part):
        return partial.at[row_to * 2 + part]

    low = jnp.bfloat16
    parts = (1 - half, half)
    theirs, ours = (far, beside), (across, row)
    for turn in range(2):
        for at, part in enumerate(parts):
            slot = 2 * turn + at
            pass_on(
                block(theirs[turn], part), near.at[slot], near_sem.at[slot], {"row": beside}
            )

    def chip_sum(turn, at):
        slot = 2 * turn + at
        arrival(near.at[slot], near_sem.at[slot])
        return block(ours[turn], parts[at])[...].astype(jnp.float32) + near[slot].astype(
            jnp.float32
        )

    def first():
        for at in range(2):
            passed[at] = chip_sum(0, at).astype(low)
            pass_on(passed.at[at], across_buf.at[at], across_sem.at[at], {"row": across})

    def second():
        for at in range(2):
            value = chip_sum(1, at)
            arrival(across_buf.at[at], across_sem.at[at])
            value = value + across_buf[at].astype(jnp.float32)
            if at == 0:
                passed[2] = value.astype(low)
                pass_on(passed.at[2], pair_buf, pair_sem, {"col": pair})
        arrival(pair_buf, pair_sem)
        total_out[...] = value + pair_buf[...].astype(jnp.float32)
        for copy in copies:
            copy.wait_send()

    return first, second


def heads_scratch(block):
    low = jnp.bfloat16
    return [
        pltpu.VMEM((4,) + block, low),
        pltpu.VMEM((2,) + block, low),
        pltpu.VMEM(block, low),
        pltpu.VMEM((3,) + block, low),
        pltpu.SemaphoreType.DMA((8,)),
        pltpu.SemaphoreType.DMA((4,)),
        pltpu.SemaphoreType.DMA((2,)),
        pltpu.SemaphoreType.DMA,
    ]


def sum_trade_kernel(plans, with_heads, *refs):
    count = len(plans)
    refs = list(refs)

    def take(number):
        out = refs[:number]
        del refs[:number]
        return out

    sources, (partial,) = take(count), take(1)
    heads = take(1) if with_heads else []
    targets, (total_out,) = take(count), take(1)
    heads += take(1) if with_heads else []
    sems = take(3 * count)
    everyone = ("dp", "row", "col")
    size, me = group_size_of(everyone), place_in(everyone)
    meet([device_at(everyone, (me + step) % size) for step in range(1, size)])
    locals_, copies, more = trade_start(plans, sources, targets, sems)
    between = ()
    if with_heads:
        between = heads_body(*heads, *refs[11:])
    sum_body(more, between, partial, total_out, *refs[:11])
    for own in locals_:
        own.wait()
    for copy in copies:
        copy.wait()


def sum_trade(number, partial, *pairs, heads=None):
    arrays = [array for array, _ in pairs] + [partial]
    plans = [(axes, array.shape[0] == 1, array.size > 2**21) for array, axes in pairs]
    scratch, shapes = trade_shapes(pairs)
    block = partial.shape[1:]
    vmem = pl.BlockSpec(memory_space=pltpu.VMEM)
    in_specs, out_specs = [ANYWHERE] * len(arrays), [ANYWHERE] * len(pairs) + [vmem]
    shapes, scratch = shapes + [jax.ShapeDtypeStruct(block, jnp.float32)], scratch + sum_scratch(block)
    if heads is not None:
        arrays, in_specs, out_specs = arrays + [heads], in_specs + [vmem], out_specs + [vmem]
        shapes.append(jax.ShapeDtypeStruct(heads.shape[1:], jnp.float32))
        scratch = scratch + heads_scratch(heads.shape[1:])
    return pl.pallas_call(
        functools.partial(sum_trade_kernel, plans, heads is not None),
        out_shape=shapes,
        in_specs=in_specs,
        out_specs=out_specs,
        scratch_shapes=scratch,
        compiler_params=pltpu.CompilerParams(
            collective_id=number, has_side_effects=True, vmem_limit_bytes=48 * 2**20
        ),
        name="sum_trade" + str(number),
    )(*arrays)


def expert_kernel(
    normed,
    cot,
    table,
    rank,
    mark,
    router,
    weights,
    mix_out,
    rows_out,
    score_out,
    grads_out,
    down_out,
    kept_in,
    kept_dye,
    kept_act,
    kept_gate,
    kept_up,
):
    low = jnp.bfloat16
    step = pl.program_id(0)
    slots = kept_in.shape[1]
    parts, _, ff_width = weights.shape
    depth = normed.shape[1] // parts
    down_depth = ff_width // parts

    gate_w = weights[:, 0:depth, :].reshape(parts * depth, ff_width)
    up_w = weights[:, depth : 2 * depth, :].reshape(parts * depth, ff_width)

    def down_w(chunk):
        at = 2 * depth + chunk * down_depth
        return weights[:, at : at + down_depth, :].reshape(ff_width, ff_width)

    chunks = normed.shape[1] // ff_width
    tokens = normed[...]
    cots = cot[...]
    logits = jnp.where(
        table[...] > 0, project(tokens, router[...]), -jnp.inf
    )
    top = jnp.max(logits, axis=1, keepdims=True)
    raised = jnp.exp(logits - top)
    gates = raised / jnp.sum(raised, axis=1, keepdims=True)
    slot = lax.broadcasted_iota(jnp.int32, (slots, normed.shape[0]), 0)
    picked = slot == rank[0, 0:1, :]
    chosen = picked.astype(jnp.float32)
    select = chosen.astype(low)
    gate = jnp.sum(
        jnp.dot(chosen, gates, precision=highest, preferred_element_type=jnp.float32) * mark[...],
        axis=1,
        keepdims=True,
    )
    expert_in = project(select, tokens).astype(low)
    grad_mix = resid_scale * project(select, cots)
    grad_out = (gate * grad_mix).astype(low)
    gate_proj = project(expert_in, gate_w)
    up_proj = project(expert_in, up_w)
    sigmoid = 1.0 / (1.0 + jnp.exp(-gate_proj))
    silu = gate_proj * sigmoid
    act = (silu * up_proj).astype(low)
    score = jnp.zeros((slots, 1), jnp.float32)
    grad_act = jnp.zeros((slots, ff_width), jnp.float32)
    for chunk in range(chunks):
        lanes = slice(chunk * ff_width, (chunk + 1) * ff_width)
        part = down_w(chunk)
        out = project(act, part).astype(low).astype(jnp.float32)
        score = score + jnp.sum(grad_mix[:, lanes] * out, axis=1, keepdims=True)
        mix_out[:, lanes] = tn(select, (gate * out).astype(low)).astype(low)
        grad_act = grad_act + nt(grad_out[:, lanes], part)
    grad_gate = (grad_act * up_proj * (sigmoid + gate_proj * sigmoid * (1.0 - sigmoid))).astype(low)
    grad_up = (grad_act * silu).astype(low)
    grad_in = (nt(grad_gate, gate_w) + nt(grad_up, up_w)).astype(low)
    rows_out[...] = tn(select, grad_in).astype(low)
    score_row = jnp.sum(chosen * score, axis=0, keepdims=True)
    score_out[0] = jnp.broadcast_to(score_row, score_out.shape[1:])
    kept_in[step] = expert_in
    kept_dye[step] = grad_out
    kept_act[step] = act
    kept_gate[step] = grad_gate
    kept_up[step] = grad_up

    @pl.when(step == pl.num_programs(0) - 1)
    def _():
        def all_of(kept):
            return kept[...].reshape(kept.shape[0] * slots, kept.shape[2])

        rows = all_of(kept_in)
        for at, kept in ((0, kept_gate), (depth, kept_up)):
            grad = tn(rows, all_of(kept)).astype(low)
            grads_out[:, at : at + depth, :] = grad.reshape(parts, depth, ff_width)
        act_all = all_of(kept_act)
        for chunk in range(chunks):
            lanes = slice(chunk * ff_width, (chunk + 1) * ff_width)
            grad = tn(act_all, all_of(kept_dye.at[:, :, lanes])).astype(low)
            at = chunk * down_depth
            down_out[:, at : at + down_depth, :] = grad.reshape(parts, down_depth, ff_width)


def expert_pass(normed, cot, table, rank, mark, router, weights, slots):
    tiles, tile = rank.shape[0], rank.shape[2]
    tokens, width = normed.shape
    low = jnp.bfloat16
    ff_width = weights.shape[2]
    parts, depth, _ = weights.shape
    gate_up = jax.ShapeDtypeStruct((parts, 2 * (width // parts), ff_width), low)
    down = jax.ShapeDtypeStruct((parts, depth - gate_up.shape[1], ff_width), low)
    rows = pl.BlockSpec((tile, width), lambda i: (i, 0))
    whole = lambda a: pl.BlockSpec(
        a.shape, lambda i: (0,) * len(a.shape), pipeline_mode=pl.Buffered(1)
    )
    return pl.pallas_call(
        expert_kernel,
        grid=(tiles,),
        out_shape=[
            jax.ShapeDtypeStruct((tokens, width), low),
            jax.ShapeDtypeStruct((tokens, width), low),
            jax.ShapeDtypeStruct((tiles, 8, tile), jnp.float32),
            gate_up,
            down,
        ],
        in_specs=[
            rows,
            rows,
            pl.BlockSpec((tile, table.shape[1]), lambda i: (i, 0)),
            pl.BlockSpec((1,) + rank.shape[1:], lambda i: (i, 0, 0)),
            whole(mark),
            whole(router),
            whole(weights),
        ],
        out_specs=[
            rows,
            rows,
            pl.BlockSpec((1, 8, tile), lambda i: (i, 0, 0)),
            whole(gate_up),
            whole(down),
        ],
        scratch_shapes=[
            pltpu.VMEM((tiles, slots, width), low),
            pltpu.VMEM((tiles, slots, width), low),
            pltpu.VMEM((tiles, slots, ff_width), low),
            pltpu.VMEM((tiles, slots, ff_width), low),
            pltpu.VMEM((tiles, slots, ff_width), low),
        ],
        compiler_params=pltpu.CompilerParams(vmem_limit_bytes=56 * 2**20),
        cost_estimate=pl.CostEstimate(
            flops=22 * 10**9, bytes_accessed=50 * 10**6, transcendentals=10**6
        ),
        name="expert_pass",
    )(normed, cot, table, rank, mark, router, weights)


def owned(
    hidden_in,
    norm_gain,
    w_query,
    w_key,
    w_value,
    w_out,
    mix_gain,
    w_router,
    w_gate,
    w_up,
    w_down,
    lengths,
    routes,
    mask,
    cotangent,
):
    everyone = ("dp", "row", "col")
    plane = ("row", "col")
    micro_count, tok_row, width_part = hidden_in.shape
    row_count = lax.axis_size("row")
    col_count = lax.axis_size("col")
    dp_count = lax.axis_size("dp")
    row_at = lax.axis_index("row")
    col_at = lax.axis_index("col")
    dp_at = lax.axis_index("dp")
    plane_count = row_count * col_count
    device_count = plane_count * dp_count
    plane_at = row_at * col_count + col_at
    model_width = width_part * col_count
    kv_here = w_key.shape[1] // HEAD_DIM
    group_size = w_query.shape[1] // w_key.shape[1]
    q_width = group_size * HEAD_DIM
    group_tokens = tok_row * row_count
    quarter = tok_row // col_count
    own_rows = micro_count * quarter
    experts_here, slice_width, ff_width = w_gate.shape
    down_slice = w_down.shape[1]
    experts_all = experts_here * dp_count
    expert_at = dp_at * plane_count + plane_at
    micro_at = col_at // kv_here
    half_at = col_at % kv_here

    masked_cot = cotangent * mask[:, :, None].astype(cotangent.dtype)

    w_qkv = jnp.concatenate(
        [
            w_query.reshape(width_part, kv_here, q_width),
            w_key.reshape(width_part, kv_here, HEAD_DIM),
            w_value.reshape(width_part, kv_here, HEAD_DIM),
        ],
        axis=2,
    ).transpose(1, 0, 2)
    qkv_width = q_width + 2 * HEAD_DIM
    picks = jnp.pad(routes.reshape(own_rows, TOP).T, ((0, 0), (0, 128 - own_rows)))
    weights = jnp.concatenate(
        [w_gate, w_up]
        + [w_down[:, :, at : at + ff_width] for at in range(0, model_width, ff_width)],
        axis=1,
    )
    doc_id, position = documents(lengths[:, 0][micro_at], group_tokens)
    sin_table, cos_table = (
        table[:, 0] for table in angles(position.astype(jnp.float32), HEAD_DIM)
    )
    cos_lanes = jnp.tile(cos_table, (1, 4))
    sin_lanes = jnp.tile(jnp.concatenate([-sin_table, sin_table], axis=1), (1, 2))
    (
        x_micro,
        w_mine,
        w_out_all,
        routes_all,
        cot_all,
        normed_all,
        weights,
        qkv,
        attended,
        mixed,
    ) = front(
        0,
        hidden_in,
        w_qkv.reshape(kv_here, dp_count, width_part // dp_count, qkv_width),
        w_out.reshape(dp_count, w_out.shape[0] // dp_count, w_out.shape[1]),
        picks,
        masked_cot.reshape(own_rows, model_width),
        weights,
        (norm_gain[None], mix_gain[None]),
        (cos_lanes, sin_lanes),
        (
            jnp.broadcast_to(doc_id[:, None], (group_tokens, 128)),
            jnp.broadcast_to(doc_id[None, :], (8, group_tokens)),
        ),
        q_width,
    )
    x_micro = x_micro.astype(jnp.float32)
    w_mine = w_mine.reshape(model_width, qkv_width)
    scale_m = lax.rsqrt(jnp.mean(x_micro * x_micro, axis=1, keepdims=True) + eps_norm)
    normed_m = (x_micro * scale_m * norm_gain).astype(jnp.bfloat16)
    sin_table, cos_table = sin_table[:, None], cos_table[:, None]
    query = qkv[:, :q_width].reshape(group_tokens, group_size, HEAD_DIM)
    key = qkv[:, q_width : q_width + HEAD_DIM]
    value = qkv[:, q_width + HEAD_DIM :]
    order = jnp.arange(group_tokens, dtype=jnp.int32)
    allowed = (doc_id[:, None] == doc_id[None, :]) & (order[None, :] <= order[:, None])
    raw_scores = jnp.einsum("qgd,kd->gqk", query, key, preferred_element_type=jnp.float32)
    scores = jnp.where(allowed[None], raw_scores * attn_scale, -1e30)
    probs = jax.nn.softmax(scores, axis=-1)
    probs_low = probs.astype(jnp.bfloat16)
    attended = attended.reshape(group_tokens, q_width)
    routes_all = (
        routes_all[:, :, :own_rows].transpose(0, 2, 1).reshape(device_count * own_rows, TOP)
    )
    scale_two = lax.rsqrt(jnp.mean(mixed * mixed, axis=1, keepdims=True) + eps_norm)
    unit_two = mixed * scale_two
    normed_two = (unit_two * mix_gain).astype(jnp.bfloat16)
    expert_ids = jnp.arange(experts_all, dtype=jnp.int32)

    def gating(normed_rows, picks):
        chosen = jnp.any(picks[:, :, None] == expert_ids[None, None, :], axis=1)
        logits = jnp.where(chosen, project(normed_rows, w_router), -jnp.inf)
        return jax.nn.softmax(logits, axis=-1)

    normed_all = normed_all.reshape(device_count * own_rows, model_width)
    cot_all = cot_all.reshape(device_count * own_rows, model_width)
    gates_own = gating(normed_two, routes.reshape(own_rows, TOP))

    tile = col_count * own_rows
    slots = col_count * micro_count * (quarter * 3 // 8)
    table = jnp.any(routes_all[:, :, None] == expert_ids[None, None, :], axis=1)
    here = jnp.any(routes_all == expert_at, axis=1).astype(jnp.int32).reshape(-1, tile)
    rank = jnp.where(here > 0, jnp.cumsum(here, axis=1, dtype=jnp.int32) - 1, -1)
    pad_experts = 128 - experts_all
    mix_part, grad_rows_part, grad_gate_mine, grads, grads_down = expert_pass(
        normed_all,
        cot_all,
        jnp.pad(table.astype(jnp.float32), ((0, 0), (0, pad_experts))),
        jnp.broadcast_to(rank[:, None, :], (rank.shape[0], 8, tile)),
        (jnp.arange(128, dtype=jnp.int32) == expert_at).astype(jnp.float32)[None],
        jnp.pad(w_router, ((0, 0), (0, pad_experts))),
        weights,
        slots,
    )
    grad_gate_mine = grad_gate_mine[:, 0, :].reshape(-1)
    scores_send = jnp.broadcast_to(
        jnp.pad(
            grad_gate_mine.reshape(device_count, 1, own_rows),
            ((0, 0), (0, 0), (0, 128 - own_rows)),
        ),
        (device_count, 8, 128),
    )
    grad_gates, grads, grad_normed = sum_trade(
        3,
        grad_rows_part.reshape(device_count, own_rows, model_width),
        (scores_send, everyone),
        (grads, plane),
    )
    grad_gates = grad_gates[:, 0, :own_rows].T
    chosen_own = jnp.any(
        routes.reshape(own_rows, TOP)[:, :, None] == expert_ids[None, None, :], axis=1
    )
    grad_gates = jnp.where(chosen_own, grad_gates, 0.0)
    grad_logits = gates_own * (
        grad_gates - jnp.sum(gates_own * grad_gates, axis=1, keepdims=True)
    )
    grad_normed = grad_normed + jnp.dot(
        grad_logits, w_router.astype(jnp.float32).T, precision=highest
    )
    mix_part_grad = jnp.sum(grad_normed * unit_two, axis=0)
    grad_scaled = grad_normed * mix_gain
    grad_mixed = masked_cot.reshape(own_rows, model_width).astype(jnp.float32) + scale_two * (
        grad_scaled - unit_two * jnp.mean(grad_scaled * unit_two, axis=1, keepdims=True)
    )
    grad_branch = (resid_scale * grad_mixed).astype(jnp.bfloat16)

    lines = lambda row: jnp.pad(row.reshape(-1, 128), ((0, 4), (0, 0)))[None]
    branch_m, logits_plane, mix_parts = gather_plane(
        4,
        (grad_branch.reshape(micro_count, quarter, model_width), "micro", True),
        (jnp.pad(grad_logits.T, ((0, 0), (0, 128 - own_rows)))[None], "all", True),
        (lines(mix_part_grad), "all", True),
    )
    branch_m, grads_down = lax.optimization_barrier((branch_m, grads_down))
    grads_down = spread_plane(grads_down)
    out_gate = grads[:, :slice_width].astype(jnp.float32)
    out_up = grads[:, slice_width : 2 * slice_width].astype(jnp.float32)
    out_down = jnp.concatenate(
        [
            grads_down[:, at : at + down_slice]
            for at in range(0, grads_down.shape[1], down_slice)
        ],
        axis=2,
    ).astype(jnp.float32)
    low = jnp.bfloat16
    left = logits_plane[:, :, :own_rows].transpose(1, 0, 2).reshape(experts_all, -1)
    parts = []
    for _ in range(3):
        parts.append(left.astype(low))
        left = left - parts[-1].astype(jnp.float32)
    normed_plane = lax.dynamic_slice_in_dim(
        normed_all, dp_at * plane_count * own_rows, plane_count * own_rows
    )
    router_part = jnp.sum(
        jnp.dot(
            jnp.concatenate(parts, axis=0), normed_plane, preferred_element_type=jnp.float32
        ).reshape(3, experts_all, model_width),
        axis=0,
    )
    mix_part_grad = jnp.sum(mix_parts, axis=0)
    branch_m = branch_m.reshape(group_tokens, model_width)
    w_out_mine = lax.dynamic_slice_in_dim(
        w_out_all, (row_at * kv_here + half_at) * q_width, q_width
    )
    grad_att = (
        jnp.dot(branch_m, w_out_mine.T, preferred_element_type=jnp.float32)
        .astype(jnp.bfloat16)
        .reshape(group_tokens, group_size, HEAD_DIM)
    )
    out_part = jnp.dot(attended.T, branch_m, preferred_element_type=jnp.float32)
    grad_probs = jnp.einsum("qgd,kd->gqk", grad_att, value, preferred_element_type=jnp.float32)
    grad_scores = probs * (grad_probs - jnp.sum(probs * grad_probs, axis=-1, keepdims=True))
    grad_raw = (grad_scores * attn_scale).astype(jnp.bfloat16)
    grad_query = jnp.einsum("gqk,kd->qgd", grad_raw, key, preferred_element_type=jnp.float32)
    grad_key = jnp.einsum("gqk,qgd->kd", grad_raw, query, preferred_element_type=jnp.float32)
    grad_value = jnp.einsum("gqk,qgd->kd", probs_low, grad_att, preferred_element_type=jnp.float32)
    grad_qkv = jnp.concatenate(
        [
            rotate(grad_query, -sin_table, cos_table).reshape(group_tokens, q_width),
            rotate(grad_key[:, None], -sin_table, cos_table)[:, 0],
            grad_value,
        ],
        axis=1,
    ).astype(jnp.bfloat16)
    qkv_part = jnp.dot(grad_qkv.T, normed_m, preferred_element_type=jnp.float32)
    heads_part = nt(grad_qkv, w_mine).astype(low)
    qkv_part, out_part, router_grad, mix_grad, expert_mix, grad_normed_one = sum_trade(
        5,
        mix_part.reshape(device_count, own_rows, model_width),
        (
            qkv_part.astype(low).reshape(qkv_width, col_count, width_part).transpose(1, 0, 2),
            ("col",),
        ),
        (
            out_part.astype(low).reshape(q_width, col_count, width_part).transpose(1, 0, 2),
            ("col",),
        ),
        (router_part[None], ("dp",)),
        (mix_part_grad[None], ("dp",)),
        heads=heads_part.reshape(2 * row_count, -1, model_width),
    )
    layer_out = (mixed + resid_scale * expert_mix).astype(jnp.bfloat16)
    rows_each = grad_normed_one.shape[0]
    first = (row_at * kv_here + half_at) * rows_each

    def part_of(array):
        return lax.dynamic_slice_in_dim(array, first, rows_each)

    scale_one = part_of(scale_m)
    unit_one = part_of(x_micro) * scale_one
    norm_part = jnp.sum(grad_normed_one * unit_one, axis=0)
    grad_scaled_one = grad_normed_one * norm_gain
    grad_x = part_of(branch_m).astype(jnp.float32) * (1.0 / resid_scale) + scale_one * (
        grad_scaled_one
        - unit_one * jnp.mean(grad_scaled_one * unit_one, axis=1, keepdims=True)
    )

    def halves(part):
        part = part.astype(jnp.float32)
        return jnp.sum(part.reshape((micro_count, kv_here) + part.shape[1:]), axis=0).astype(low)

    grad_input, qkv_sum, out_sum, norm_grad = trade(
        6,
        (
            grad_x.astype(low).reshape(rows_each, col_count, width_part).transpose(1, 0, 2),
            ("col",),
        ),
        (halves(qkv_part)[None], ("dp",)),
        (halves(out_part)[None], ("dp",)),
        (lines(norm_part), everyone),
    )
    grad_input = grad_input.reshape(micro_count, tok_row, width_part).astype(jnp.float32)
    qkv_sum = jnp.sum(qkv_sum.astype(jnp.float32), axis=0)
    out_sum = jnp.sum(out_sum.astype(jnp.float32), axis=0)
    router_grad = jnp.sum(router_grad, axis=0).T
    mix_grad = jnp.sum(mix_grad, axis=0).reshape(-1)[:model_width]
    norm_grad = jnp.sum(norm_grad, axis=0).reshape(-1)[:model_width]
    grad_wq = qkv_sum[:, :q_width].reshape(-1, width_part).T
    grad_wk = qkv_sum[:, q_width : q_width + HEAD_DIM].reshape(-1, width_part).T
    grad_wv = qkv_sum[:, q_width + HEAD_DIM :].reshape(-1, width_part).T
    grad_wo = out_sum.reshape(w_out.shape)
    return (
        layer_out.reshape(micro_count, quarter, model_width),
        grad_input,
        norm_grad,
        grad_wq,
        grad_wk,
        grad_wv,
        grad_wo,
        mix_grad,
        router_grad,
        out_gate,
        out_up,
        out_down,
    )


def solution(mesh):
    dp_count, row_count, col_count = (mesh.shape[name] for name in ("dp", "row", "col"))

    def body(*args):
        hidden_in, w_key, w_gate = args[0], args[3], args[8]
        kv_here = w_key.shape[1] // HEAD_DIM
        one_each = w_gate.shape[0] == row_count * col_count
        pairs = hidden_in.shape[0] * kv_here == col_count
        sizes = (dp_count, row_count, col_count, kv_here) == (2, 4, 4, 2)
        return (owned if sizes and one_each and pairs else shards)(*args)

    placed = (
        P(None, ("dp", "row"), "col"),
        P(),
        P("col", "row"),
        P("col", "row"),
        P("col", "row"),
        P("row", "col"),
        P(),
        P(),
        P("dp", ("row", "col"), None),
        P("dp", ("row", "col"), None),
        P("dp", ("row", "col"), None),
        P(None, "dp", None),
        P(None, ("dp", "row", "col"), None),
        P(None, ("dp", "row", "col")),
        P(None, ("dp", "row", "col"), None),
    )
    return jax.shard_map(
        body,
        mesh=mesh,
        in_specs=placed,
        out_specs=(
            P(None, ("dp", "row", "col"), None),
            P(None, ("dp", "row"), "col"),
            P(),
            P("col", "row"),
            P("col", "row"),
            P("col", "row"),
            P("row", "col"),
            P(),
            P(),
            P("dp", ("row", "col"), None),
            P("dp", ("row", "col"), None),
            P("dp", ("row", "col"), None),
        ),
        check_vma=False,
    )
```

```python
import functools

import jax
import jax.numpy as jnp
from jax import lax
from jax.experimental import pallas as pl
from jax.experimental.pallas import tpu as pltpu
from jax.sharding import PartitionSpec as P

D = 1536
HEAD_DIM = 64
TOP = 8


eps_norm = 1e-06
resid_scale = 0.22
attn_scale = 0.015625
rope_base = 10000.0
highest = lax.Precision.HIGHEST


def shortened(shard):
    return jax.tree.map(lambda a: a.astype(jnp.bfloat16) if a.dtype == jnp.float32 else a, shard)


def documents(doc_lengths, length_all):
    doc_ends = jnp.cumsum(doc_lengths, dtype=jnp.int32)
    doc_starts = doc_ends - doc_lengths
    positions = jnp.arange(length_all, dtype=jnp.int32)
    doc_id = jnp.sum(
        (positions[:, None] >= doc_ends[None, :]).astype(jnp.int32), axis=1, dtype=jnp.int32
    )
    member = doc_id[:, None] == jnp.arange(doc_lengths.shape[0], dtype=jnp.int32)[None, :]
    doc_start = jnp.sum(jnp.where(member, doc_starts[None, :], 0), axis=1, dtype=jnp.int32)
    return (doc_id, positions - doc_start)


def angles(position, head_width):
    half_width = head_width // 2
    frequency = rope_base ** (-2.0 * jnp.arange(half_width, dtype=jnp.float32) / head_width)
    turned = position[:, None] * frequency[None, :]
    return (jnp.sin(turned)[:, None, :], jnp.cos(turned)[:, None, :])


def rotate(values, sin_table, cos_table):
    half_width = values.shape[-1] // 2
    front_half = values[..., :half_width]
    back_half = values[..., half_width:]
    return jnp.concatenate(
        [
            front_half * cos_table - back_half * sin_table,
            back_half * cos_table + front_half * sin_table,
        ],
        axis=-1,
    )


def gather_rows(value):
    return lax.all_gather(value, "row", axis=0, tiled=True)


def gather_cols(value):
    return jax.tree.map(
        lambda part, own: part.astype(own.dtype),
        lax.all_gather(shortened(value), "col", axis=0, tiled=True),
        value,
    )


def sum_cols(pieces):
    return lax.psum_scatter(pieces, "col", scatter_dimension=0, tiled=True)


def sum_rows(pieces):
    return lax.psum_scatter(pieces, "row", scatter_dimension=0, tiled=True)


def width_total(value):
    return lax.psum(value, "col")


def expert_trade(value):
    return lax.all_to_all(value, "dp", split_axis=1, concat_axis=1, tiled=True)


def attn_total(value):
    return jax.tree.map(lambda part: part.astype(jnp.float32), lax.psum(shortened(value), "dp"))


def expert_total(value):
    return jax.tree.map(
        lambda part: part.astype(jnp.float32),
        lax.psum_scatter(shortened(value), ("row", "col"), scatter_dimension=1, tiled=True),
    )


def add_all(first_set, second_set):
    return tuple((left_one + right_one for left_one, right_one in zip(first_set, second_set)))


def project(left_side, right_side):
    return jnp.dot(left_side, right_side, preferred_element_type=jnp.float32)


def shards(
    hidden_in,
    norm_gain,
    w_query,
    w_key,
    w_value,
    w_out,
    mix_gain,
    w_router,
    w_gate,
    w_up,
    w_down,
    lengths,
    routes,
    mask,
    cotangent,
):
    micro_count = hidden_in.shape[0]
    tok_dev = hidden_in.shape[1]
    width_part = hidden_in.shape[2]
    col_count = lax.axis_size("col")
    row_count = lax.axis_size("row")
    dp_count = lax.axis_size("dp")
    col_at = lax.axis_index("col")
    model_width = D
    heads_here = w_query.shape[1] // HEAD_DIM
    kv_here = w_key.shape[1] // HEAD_DIM
    group_size = heads_here // kv_here
    group_tokens = tok_dev * row_count
    quarter = tok_dev // col_count
    experts_here = w_gate.shape[0]
    experts_all = experts_here * dp_count
    capacity = quarter * 3 // 8
    slot_count = experts_all * capacity
    gain_part = lax.dynamic_slice_in_dim(norm_gain, col_at * width_part, width_part)
    router_wide = w_router.astype(jnp.float32)
    full_gate, full_up, full_down = (
        lax.all_gather(w_gate, ("row", "col"), axis=1, tiled=True),
        lax.all_gather(w_up, ("row", "col"), axis=1, tiled=True),
        lax.all_gather(w_down, ("row", "col"), axis=1, tiled=True),
    )
    expert_ids = jnp.arange(experts_all, dtype=jnp.int32)
    group_index = jnp.arange(group_tokens, dtype=jnp.int32)
    query_start = col_at * tok_dev
    query_index = query_start + jnp.arange(tok_dev, dtype=jnp.int32)
    attn_local = (
        jnp.zeros(w_query.shape, jnp.float32),
        jnp.zeros(w_key.shape, jnp.float32),
        jnp.zeros(w_value.shape, jnp.float32),
        jnp.zeros(w_out.shape, jnp.float32),
    )
    expert_local = (
        jnp.zeros(full_gate.shape, jnp.float32),
        jnp.zeros(full_up.shape, jnp.float32),
        jnp.zeros(full_down.shape, jnp.float32),
    )
    router_acc = jnp.zeros(w_router.shape, jnp.float32)
    norm_acc = jnp.zeros((width_part,), jnp.float32)
    mix_acc = jnp.zeros((model_width,), jnp.float32)
    layer_rows = []
    input_grads = []
    for step in range(micro_count):
        x_full = hidden_in[step].astype(jnp.float32)
        squares = width_total(jnp.sum(x_full * x_full, axis=1))
        scale_one = lax.rsqrt(squares / model_width + eps_norm)[:, None]
        unit_one = x_full * scale_one
        normed = (unit_one * gain_part).astype(jnp.bfloat16)
        normed_all = gather_rows(normed)
        query_p, key_p, value_p = sum_cols(
            (project(normed_all, w_query), project(normed_all, w_key), project(normed_all, w_value))
        )
        doc_all, pos_all = documents(lengths[step, 0], group_tokens)
        doc_query = lax.dynamic_slice_in_dim(doc_all, query_start, tok_dev)
        pos_query = lax.dynamic_slice_in_dim(pos_all, query_start, tok_dev).astype(jnp.float32)
        sin_table, cos_table = angles(pos_query, HEAD_DIM)
        query_rot = rotate(
            query_p.reshape(tok_dev, heads_here, HEAD_DIM), sin_table, cos_table
        ).astype(jnp.bfloat16)
        key_rot = rotate(key_p.reshape(tok_dev, kv_here, HEAD_DIM), sin_table, cos_table).astype(
            jnp.bfloat16
        )
        value_low = value_p.astype(jnp.bfloat16).reshape(tok_dev, kv_here, HEAD_DIM)
        keys_all, values_all = (
            lax.all_gather(key_rot, "col", axis=0, tiled=True),
            lax.all_gather(value_low, "col", axis=0, tiled=True),
        )
        allowed = (doc_query[:, None] == doc_all[None, :]) & (
            group_index[None, :] <= query_index[:, None]
        )
        query_grp = query_rot.reshape(tok_dev, kv_here, group_size, HEAD_DIM)
        raw_scores = jnp.einsum(
            "qhgd,khd->hgqk", query_grp, keys_all, preferred_element_type=jnp.float32
        )
        scores = jnp.where(allowed[None, None], raw_scores * attn_scale, -1e30)
        top_score = jnp.max(scores, axis=-1, keepdims=True)
        expd = jnp.exp(scores - top_score)
        row_total = jnp.sum(expd, axis=-1, keepdims=True)
        attn_probs = expd / row_total
        log_total = top_score + jnp.log(row_total)
        probs_low = attn_probs.astype(jnp.bfloat16)
        attended = jnp.einsum(
            "hgqk,khd->qhgd", probs_low, values_all, preferred_element_type=jnp.float32
        )
        attended_low = attended.reshape(tok_dev, heads_here * HEAD_DIM).astype(jnp.bfloat16)
        attended_all = gather_cols(attended_low)
        attn_branch = sum_rows(project(attended_all, w_out))
        mixed = x_full + resid_scale * attn_branch
        mixed_rows = lax.all_to_all(
            mixed.reshape(col_count, quarter, width_part),
            "col",
            split_axis=0,
            concat_axis=2,
            tiled=True,
        ).reshape(quarter, model_width)
        scale_two = lax.rsqrt(jnp.mean(mixed_rows * mixed_rows, axis=1, keepdims=True) + eps_norm)
        unit_two = mixed_rows * scale_two
        normed_two = (unit_two * mix_gain).astype(jnp.bfloat16)
        logits = project(normed_two, w_router)
        picks = routes[step]
        choose = (picks[:, :, None] == expert_ids[None, None, :]).astype(jnp.float32)
        chosen = jnp.sum(choose * logits[:, None, :], axis=-1)
        gate_weights = jax.nn.softmax(chosen, axis=-1)
        flat_picks = picks.reshape(-1)
        hit_table = (flat_picks[:, None] == expert_ids[None, :]).astype(jnp.int32)
        slot_rank = jnp.sum(
            hit_table * (jnp.cumsum(hit_table, axis=0, dtype=jnp.int32) - 1),
            axis=1,
            dtype=jnp.int32,
        )
        owner_dp = flat_picks // experts_here
        local_expert = flat_picks % experts_here
        slot_index = local_expert * (dp_count * capacity) + owner_dp * capacity + slot_rank
        token_of = (
            jnp.full((slot_count,), quarter, jnp.int32)
            .at[slot_index]
            .set(jnp.arange(quarter * TOP, dtype=jnp.int32) // TOP)
        )
        padded = jnp.concatenate([normed_two, jnp.zeros((1, model_width), jnp.bfloat16)], axis=0)
        send_rows = padded[token_of].reshape(experts_here, dp_count * capacity, model_width)
        expert_in = expert_trade(send_rows)
        gate_proj = jnp.einsum(
            "ecd,edf->ecf", expert_in, full_gate, preferred_element_type=jnp.float32
        )
        up_proj = jnp.einsum("ecd,edf->ecf", expert_in, full_up, preferred_element_type=jnp.float32)
        activated = (jax.nn.silu(gate_proj) * up_proj).astype(jnp.bfloat16)
        expert_out = jnp.einsum(
            "ecf,efd->ecd", activated, full_down, preferred_element_type=jnp.float32
        ).astype(jnp.bfloat16)
        returned = expert_trade(expert_out).reshape(slot_count, model_width)
        combined = returned[slot_index].reshape(quarter, TOP, model_width).astype(jnp.float32)
        expert_mix = jnp.sum(gate_weights[:, :, None] * combined, axis=1)
        layer_rows.append((mixed_rows + resid_scale * expert_mix).astype(jnp.bfloat16))
        grad_rows = cotangent[step].astype(jnp.float32) * mask[step][:, None].astype(jnp.float32)
        grad_mix = resid_scale * grad_rows
        grad_gates = jnp.sum(grad_mix[:, None, :] * combined, axis=-1)
        grad_chosen = gate_weights * (
            grad_gates - jnp.sum(gate_weights * grad_gates, axis=-1, keepdims=True)
        )
        grad_logits = jnp.sum(choose * grad_chosen[:, :, None], axis=1)
        gate_slots = (
            jnp.zeros((slot_count,), jnp.float32).at[slot_index].set(gate_weights.reshape(-1))
        )
        grad_pad = jnp.concatenate([grad_mix, jnp.zeros((1, model_width), jnp.float32)], axis=0)
        grad_send = (gate_slots[:, None] * grad_pad[token_of]).astype(jnp.bfloat16)
        grad_expert = expert_trade(
            grad_send.reshape(experts_here, dp_count * capacity, model_width)
        )
        grad_act = jnp.einsum(
            "ecd,efd->ecf", grad_expert, full_down, preferred_element_type=jnp.float32
        )
        micro_down = jnp.einsum(
            "ecf,ecd->efd", activated, grad_expert, preferred_element_type=jnp.float32
        )
        sigmoid_gate = jax.nn.sigmoid(gate_proj)
        silu_gate = gate_proj * sigmoid_gate
        grad_gate_p = (
            grad_act * up_proj * (sigmoid_gate + gate_proj * sigmoid_gate * (1.0 - sigmoid_gate))
        ).astype(jnp.bfloat16)
        grad_up_p = (grad_act * silu_gate).astype(jnp.bfloat16)
        grad_in = jnp.einsum(
            "ecf,edf->ecd", grad_gate_p, full_gate, preferred_element_type=jnp.float32
        ) + jnp.einsum("ecf,edf->ecd", grad_up_p, full_up, preferred_element_type=jnp.float32)
        micro_gate = jnp.einsum(
            "ecd,ecf->edf", expert_in, grad_gate_p, preferred_element_type=jnp.float32
        )
        micro_up = jnp.einsum(
            "ecd,ecf->edf", expert_in, grad_up_p, preferred_element_type=jnp.float32
        )
        expert_local = add_all(expert_local, (micro_gate, micro_up, micro_down))
        grad_back = expert_trade(grad_in.astype(jnp.bfloat16)).reshape(slot_count, model_width)
        grad_normed = jnp.sum(
            grad_back[slot_index].reshape(quarter, TOP, model_width).astype(jnp.float32), axis=1
        ) + jnp.dot(grad_logits, router_wide.T, precision=highest)
        router_acc = router_acc + jnp.dot(
            normed_two.astype(jnp.float32).T, grad_logits, precision=highest
        )
        mix_acc = mix_acc + jnp.sum(grad_normed * unit_two, axis=0)
        grad_scaled = grad_normed * mix_gain
        grad_mixed_rows = grad_rows + scale_two * (
            grad_scaled - unit_two * jnp.mean(grad_scaled * unit_two, axis=1, keepdims=True)
        )
        grad_mixed = lax.all_to_all(
            grad_mixed_rows.reshape(1, quarter, model_width),
            "col",
            split_axis=2,
            concat_axis=0,
            tiled=True,
        ).reshape(tok_dev, width_part)
        grad_branch = (resid_scale * grad_mixed).astype(jnp.bfloat16)
        grad_branch_all = gather_rows(grad_branch)
        micro_out = jnp.dot(attended_all.T, grad_branch_all, preferred_element_type=jnp.float32)
        grad_attended = sum_cols(
            jnp.dot(grad_branch_all, w_out.T, preferred_element_type=jnp.float32)
        )
        grad_att_low = grad_attended.astype(jnp.bfloat16).reshape(
            tok_dev, kv_here, group_size, HEAD_DIM
        )
        probs_again = jnp.exp(scores - log_total)
        grad_probs = jnp.einsum(
            "qhgd,khd->hgqk", grad_att_low, values_all, preferred_element_type=jnp.float32
        )
        grad_scores = probs_again * (
            grad_probs - jnp.sum(probs_again * grad_probs, axis=-1, keepdims=True)
        )
        grad_raw = (grad_scores * attn_scale).astype(jnp.bfloat16)
        probs_again_low = probs_again.astype(jnp.bfloat16)
        grad_query = jnp.einsum(
            "hgqk,khd->qhgd", grad_raw, keys_all, preferred_element_type=jnp.float32
        )
        grad_key_part = jnp.einsum(
            "hgqk,qhgd->khd", grad_raw, query_grp, preferred_element_type=jnp.float32
        )
        grad_value_part = jnp.einsum(
            "hgqk,qhgd->khd", probs_again_low, grad_att_low, preferred_element_type=jnp.float32
        )
        grad_key, grad_value = sum_cols(
            (
                grad_key_part.reshape(group_tokens, kv_here * HEAD_DIM),
                grad_value_part.reshape(group_tokens, kv_here * HEAD_DIM),
            )
        )
        grad_query_p = (
            rotate(grad_query.reshape(tok_dev, heads_here, HEAD_DIM), -sin_table, cos_table)
            .astype(jnp.bfloat16)
            .reshape(tok_dev, heads_here * HEAD_DIM)
        )
        grad_key_p = (
            rotate(grad_key.reshape(tok_dev, kv_here, HEAD_DIM), -sin_table, cos_table)
            .astype(jnp.bfloat16)
            .reshape(tok_dev, kv_here * HEAD_DIM)
        )
        grad_value_p = grad_value.astype(jnp.bfloat16)
        query_all, key_all, value_all = gather_cols((grad_query_p, grad_key_p, grad_value_p))
        micro_query = jnp.dot(normed_all.T, query_all, preferred_element_type=jnp.float32)
        micro_key = jnp.dot(normed_all.T, key_all, preferred_element_type=jnp.float32)
        micro_value = jnp.dot(normed_all.T, value_all, preferred_element_type=jnp.float32)
        grad_normed_one = sum_rows(
            jnp.dot(query_all, w_query.T, preferred_element_type=jnp.float32)
            + jnp.dot(key_all, w_key.T, preferred_element_type=jnp.float32)
            + jnp.dot(value_all, w_value.T, preferred_element_type=jnp.float32)
        )
        grad_scaled_one = grad_normed_one * gain_part
        inner_sum = width_total(jnp.sum(grad_scaled_one * unit_one, axis=1))
        norm_acc = norm_acc + jnp.sum(grad_normed_one * unit_one, axis=0)
        input_grads.append(
            grad_mixed
            + scale_one * (grad_scaled_one - unit_one * (inner_sum / model_width)[:, None])
        )
        attn_local = add_all(attn_local, (micro_query, micro_key, micro_value, micro_out))
    attn_summed = attn_total(attn_local)
    expert_summed = expert_total(expert_local)
    gain_full = lax.dynamic_update_slice_in_dim(
        jnp.zeros((model_width,), jnp.float32), norm_acc, col_at * width_part, 0
    )
    router_grad, gain_grad, mix_grad = lax.psum(
        (router_acc, gain_full, mix_acc), ("dp", "row", "col")
    )
    return (
        jnp.stack(layer_rows),
        jnp.stack(input_grads),
        gain_grad,
        attn_summed[0],
        attn_summed[1],
        attn_summed[2],
        attn_summed[3],
        mix_grad,
        router_grad,
        expert_summed[0],
        expert_summed[1],
        expert_summed[2],
    )


MESH = pl.DeviceIdType.MESH
ANYWHERE = pl.BlockSpec(memory_space=pl.ANY)


def group_size_of(axes):
    total = 1
    for axis in axes:
        total = total * lax.axis_size(axis)
    return total


def place_in(axes):
    at = 0
    for axis in axes:
        at = at * lax.axis_size(axis) + lax.axis_index(axis)
    return at


def device_at(axes, index):
    place = {}
    for axis in reversed(axes):
        place[axis] = index % lax.axis_size(axis)
        index = index // lax.axis_size(axis)
    return place


def meet(peers):
    barrier = pltpu.get_barrier_semaphore()
    for peer in peers:
        pl.semaphore_signal(barrier, inc=1, device_id=peer, device_id_type=MESH)
    pl.semaphore_wait(barrier, len(peers))


def send(src, dst, send_sem, recv_sem, peer):
    copy = pltpu.make_async_remote_copy(
        src_ref=src,
        dst_ref=dst,
        send_sem=send_sem,
        recv_sem=recv_sem,
        device_id=peer,
        device_id_type=MESH,
    )
    copy.start()
    return copy


def row_peers():
    row = lax.axis_index("row")
    rows = lax.axis_size("row")
    across = (row + rows // 2) % rows
    beside = row + 1 - 2 * (row % 2)
    return row, across, beside


def gather_line(source, target, sems, copies):
    local_sem, send_sem, col_sem, dp_sem, across_sem, beside_sem = sems
    row, across, beside = row_peers()
    rows, cols = lax.axis_size("row"), lax.axis_size("col")
    col, dp = lax.axis_index("col"), lax.axis_index("dp")
    other = 1 - dp
    far = (beside + rows // 2) % rows
    sent = []

    def block_of(dp_from, row_from, step):
        return (dp_from * rows + row_from) * cols + (col + cols - step) % cols

    def arrival(block, sem):
        pltpu.make_async_copy(target.at[block], target.at[block], sem).wait()

    def pass_on(part, block, sem, peer):
        copy = send(part, target.at[block], send_sem.at[len(sent)], sem, peer)
        sent.append(copy)
        copies.append(copy)

    me = block_of(dp, row, 0)
    own = pltpu.make_async_copy(source.at[0], target.at[me], local_sem)

    def begin():
        own.start()
        for step in range(1, cols):
            pass_on(source.at[0], me, col_sem.at[step], {"col": (col + step) % cols})

    def line(step):
        block = block_of(dp, row, step)
        part = source.at[0] if step == 0 else target.at[block]
        if step > 0:
            arrival(block, col_sem.at[step])
        pass_on(part, block, dp_sem.at[step], {"dp": other})
        pass_on(part, block, across_sem.at[step], {"row": across})
        pass_on(part, block, beside_sem.at[step], {"row": beside})

    def side(step):
        block = block_of(other, row, step)
        arrival(block, dp_sem.at[step])
        if step < 2:
            pass_on(target.at[block], block, across_sem.at[cols + step], {"row": across})
        pass_on(target.at[block], block, beside_sem.at[cols + step], {"row": beside})
        block = block_of(dp, across, step)
        arrival(block, across_sem.at[step])
        if step >= 2:
            pass_on(target.at[block], block, dp_sem.at[cols + step], {"dp": other})
        pass_on(target.at[block], block, beside_sem.at[2 * cols + step], {"row": beside})

    def corner(step):
        block = block_of(other, across, step)
        arrival(block, (across_sem if step < 2 else dp_sem).at[cols + step])
        pass_on(target.at[block], block, beside_sem.at[3 * cols + step], {"row": beside})

    def finish():
        for turn, (dp_from, row_from) in enumerate(
            ((dp, beside), (other, beside), (dp, far), (other, far))
        ):
            for step in range(cols):
                arrival(block_of(dp_from, row_from, step), beside_sem.at[turn * cols + step])
        own.wait()

    return begin, line, side, corner, finish


def gather_sems():
    cols = lax.axis_size("col")
    return [
        pltpu.SemaphoreType.DMA,
        pltpu.SemaphoreType.DMA((40,)),
        pltpu.SemaphoreType.DMA((cols,)),
        pltpu.SemaphoreType.DMA((2 * cols,)),
        pltpu.SemaphoreType.DMA((2 * cols,)),
        pltpu.SemaphoreType.DMA((4 * cols,)),
    ]


def nt(left, right):
    return lax.dot_general(
        left, right, (((1,), (1,)), ((), ())), preferred_element_type=jnp.float32
    )


def tn(left, right):
    return lax.dot_general(
        left, right, (((0,), (0,)), ((), ())), preferred_element_type=jnp.float32
    )


def norm_rows(x, gain):
    scale = lax.rsqrt(jnp.mean(x * x, axis=1, keepdims=True) + eps_norm)
    return scale, (x * scale * gain).astype(jnp.bfloat16)


def turn(values, cos_table, sin_table):
    lane = lax.broadcasted_iota(jnp.int32, values.shape, 1)
    ahead = pltpu.roll(values, values.shape[1] - HEAD_DIM // 2, 1)
    behind = pltpu.roll(values, HEAD_DIM // 2, 1)
    return values * cos_table + jnp.where(lane % HEAD_DIM < HEAD_DIM // 2, ahead, behind) * sin_table


def key_extent(block, rows, total):
    return min(total, -(-(block + 1) * rows // 128) * 128)


def visible(doc_col, doc_row, block, rows, extent):
    query = block * rows + lax.broadcasted_iota(jnp.int32, (rows, extent), 0)
    keys = lax.broadcasted_iota(jnp.int32, (rows, extent), 1)
    same = doc_col[block * rows : (block + 1) * rows, 0:1] == doc_row[0:1, 0:extent]
    return same & (keys <= query)


def attend(query, key, allowed):
    scores = jnp.where(allowed, nt(query, key) * attn_scale, -1e30)
    raised = jnp.exp(scores - jnp.max(scores, axis=1, keepdims=True))
    return raised / jnp.sum(raised, axis=1, keepdims=True)


def front_kernel(
    x,
    w_qkv,
    w_out,
    picks,
    cot,
    weights,
    gain_one,
    gain_two,
    cos_table,
    sin_table,
    doc_col,
    doc_row,
    x_all,
    w_mine,
    w_out_all,
    picks_all,
    cot_all,
    normed_all,
    weights_own,
    qkv,
    attended,
    mixed,
    x_own,
    att_own,
    normed_two,
    local_sem,
    send_sem,
    x_sem,
    q_sem,
    o_sem,
    own_sem,
    att_send,
    att_recv,
    ship_local,
    ship_send,
    ship_recv,
    *line_sems,
):
    row, across, beside = row_peers()
    rows, cols = lax.axis_size("row"), lax.axis_size("col")
    col, dp = lax.axis_index("col"), lax.axis_index("dp")
    other = 1 - dp
    far = (beside + rows // 2) % rows
    plane = ("row", "col")
    size, me = group_size_of(plane), place_in(plane)
    low = jnp.bfloat16
    meet(
        [device_at(plane, (me + step) % size) for step in range(1, size)] + [{"dp": other}]
    )
    copies, locals_, sent, moved = [], [], [], []
    picks_line = gather_line(picks, picks_all, line_sems[0:6], copies)
    cot_line = gather_line(cot, cot_all, line_sems[6:12], copies)
    norm_line = gather_line(normed_two, normed_all, line_sems[12:18], copies)

    def pass_on(src, dst, sem, peer):
        sent.append(send(src, dst, send_sem.at[len(sent)], sem, peer))

    def arrival(ref, sem):
        pltpu.make_async_copy(ref, ref, sem).wait()

    def local(src, dst):
        copy = pltpu.make_async_copy(src, dst, local_sem.at[len(locals_)])
        copy.start()
        locals_.append(copy)

    def ship(first, last):
        for step in range(first, last):
            to = (me + step) % size
            moved.append(
                send(
                    weights.at[to],
                    weights_own.at[me],
                    ship_send.at[step],
                    ship_recv.at[step],
                    device_at(plane, to),
                )
            )

    def origin(step):
        return (col + cols - step) % cols

    micro, depth, width = x.shape
    quarter = depth // cols
    half_depth = w_out.shape[1]

    def lanes(step):
        return pl.ds(pl.multiple_of(origin(step) * width, width), width)

    def x_at(row_from, step):
        return x_all.at[pl.ds(pl.multiple_of(row_from * depth, depth), depth), lanes(step)]

    def out_at(row_from, step, half):
        first = pl.multiple_of((row_from * 2 + half) * half_depth, half_depth)
        return w_out_all.at[pl.ds(first, half_depth), lanes(step)]

    def own_at(m, step):
        return x_own.at[pl.ds(m * quarter, quarter), lanes(step)]

    my_x = x_at(row, 0)
    for step in range(1, cols):
        to = (col + step) % cols
        pass_on(x.at[to // 2], my_x, x_sem.at[step], {"col": to})
        pass_on(w_qkv.at[to % 2, dp], w_mine.at[col, dp], q_sem.at[step], {"col": to})
    local(x.at[col // 2], my_x)
    local(w_qkv.at[col % 2], w_mine.at[col])
    for half in range(2):
        local(w_out.at[half], out_at(row, 0, half))
    pass_on(x.at[col // 2], my_x, x_sem.at[cols], {"row": across})
    pass_on(x.at[col // 2], my_x, x_sem.at[2 * cols], {"row": beside})
    for step in range(1, cols):
        to = (col + step) % cols
        pass_on(w_out.at[dp], out_at(row, 0, dp), o_sem.at[step], {"col": to})
        first = pl.multiple_of(to * quarter, quarter)
        for m in range(micro):
            pass_on(
                x.at[m, pl.ds(first, quarter)],
                own_at(m, 0),
                own_sem.at[m * cols + step],
                {"col": to},
            )
    for m in range(micro):
        local(x.at[m, pl.ds(pl.multiple_of(col * quarter, quarter), quarter)], own_at(m, 0))
    for half in range(2):
        pass_on(w_out.at[half], out_at(row, 0, half), o_sem.at[(2 + half) * cols], {"row": across})
        pass_on(w_out.at[half], out_at(row, 0, half), o_sem.at[(4 + half) * cols], {"row": beside})
    for step in range(1, cols):
        part = x_at(row, step)
        arrival(part, x_sem.at[step])
        pass_on(part, part, x_sem.at[cols + step], {"row": across})
        pass_on(part, part, x_sem.at[2 * cols + step], {"row": beside})
        part = w_mine.at[origin(step), dp]
        arrival(part, q_sem.at[step])
        pass_on(part, part, q_sem.at[cols + step], {"dp": other})
    for step in range(cols):
        part = x_at(across, step)
        arrival(part, x_sem.at[cols + step])
        pass_on(part, part, x_sem.at[3 * cols + step], {"row": beside})
    for step in range(1, cols):
        part = out_at(row, step, dp)
        arrival(part, o_sem.at[step])
        pass_on(part, part, o_sem.at[cols + step], {"dp": other})
        pass_on(part, part, o_sem.at[2 * cols + step], {"row": across})
        pass_on(part, part, o_sem.at[4 * cols + step], {"row": beside})
    picks_line[0]()
    cot_line[0]()
    own = pltpu.make_async_copy(weights.at[me], weights_own.at[me], ship_local)
    own.start()
    for step in range(1, cols):
        arrival(w_mine.at[origin(step), other], q_sem.at[cols + step])
    for at, row_from in enumerate((beside, far)):
        for step in range(cols):
            arrival(x_at(row_from, step), x_sem.at[(2 + at) * cols + step])
    for copy in locals_:
        copy.wait()

    tokens, model_width = x_all.shape
    projection = w_mine[...].reshape(model_width, w_mine.shape[3])
    for block in range(rows):
        part = slice(block * depth, (block + 1) * depth)
        _, normed = norm_rows(x_all[part, :].astype(jnp.float32), gain_one[...])
        values = project(normed, projection)
        cosine, sine = cos_table[part, :], sin_table[part, :]
        for at in range(2):
            piece = slice(at * 128, (at + 1) * 128)
            qkv[part, piece] = turn(values[:, piece], cosine, sine).astype(low)
        qkv[part, 256:] = values[:, 256:].astype(low)
    heads = attended.shape[2] // HEAD_DIM
    kv_at = heads * HEAD_DIM
    for block in range(rows):
        extent = key_extent(block, depth, tokens)
        allowed = visible(doc_col, doc_row, block, depth, extent)
        key = qkv[0:extent, kv_at : kv_at + HEAD_DIM]
        value = qkv[0:extent, kv_at + HEAD_DIM : kv_at + 2 * HEAD_DIM]
        outs = []
        for head in range(heads):
            query = qkv[
                block * depth : (block + 1) * depth, head * HEAD_DIM : (head + 1) * HEAD_DIM
            ]
            outs.append(project(attend(query, key, allowed).astype(low), value))
        out = jnp.concatenate(outs, axis=1).astype(low)
        attended[block * cols : (block + 1) * cols] = out.reshape(cols, quarter, out.shape[1])
    for step in range(1, size):
        to = (me + step) % size
        moved.append(
            send(
                attended.at[to],
                att_own.at[me],
                att_send.at[step],
                att_recv.at[step],
                device_at(plane, to),
            )
        )
    stay = pltpu.make_async_copy(attended.at[me], att_own.at[me], att_send.at[0])
    stay.start()
    ship(1, 5)
    for step in range(cols):
        picks_line[1](step)
        cot_line[1](step)
    for step in range(1, cols):
        part = out_at(row, step, other)
        arrival(part, o_sem.at[cols + step])
        pass_on(part, part, o_sem.at[3 * cols + step], {"row": across})
        pass_on(part, part, o_sem.at[5 * cols + step], {"row": beside})
    for at in range(2):
        for step in range(cols):
            half = at if step == 0 else (dp if at == 0 else other)
            part = out_at(across, step, half)
            arrival(part, o_sem.at[(2 + at) * cols + step])
            pass_on(part, part, o_sem.at[(6 + at) * cols + step], {"row": beside})
    for at, row_from in enumerate((beside, far)):
        for step in range(cols):
            for part in range(2):
                half = part if step == 0 else (dp if part == 0 else other)
                arrival(out_at(row_from, step, half), o_sem.at[(4 + 2 * at + part) * cols + step])
    for step in range(1, cols):
        for m in range(micro):
            arrival(own_at(m, step), own_sem.at[m * cols + step])
    stay.wait()
    for step in range(1, size):
        arrival(att_own.at[(me + size - step) % size], att_recv.at[step])
    pairs = cols // micro
    for m in range(micro):
        total = jnp.zeros((quarter, model_width), jnp.float32)
        for row_from in range(rows):
            for pair in range(pairs):
                first = (row_from * pairs + pair) * kv_at
                total = total + project(
                    att_own[row_from * cols + m * pairs + pair],
                    w_out_all[first : first + kv_at, :],
                )
        part = slice(m * quarter, (m + 1) * quarter)
        value = x_own[part, :].astype(jnp.float32) + resid_scale * total
        mixed[part, :] = value
        normed_two[0, part, :] = norm_rows(value, gain_two[...])[1]

    begin, line, side, corner, finish = norm_line
    begin()
    for step in range(cols):
        picks_line[2](step)
        cot_line[2](step)
        ship(5 + 2 * step, 7 + 2 * step)
    for step in range(cols):
        line(step)
    ship(5 + 2 * cols, size)
    for step in range(cols):
        picks_line[3](step)
        cot_line[3](step)
        side(step)
    for step in range(cols):
        corner(step)
    picks_line[4]()
    cot_line[4]()
    finish()
    own.wait()
    for copy in moved[: size - 1]:
        copy.wait_send()
    for copy in moved[size - 1 :]:
        copy.wait()
    for copy in copies + sent:
        copy.wait_send()


def front(number, x, w_qkv, w_out, picks, cot, weights, gains, tables, docs, heads_width):
    cols, rows = lax.axis_size("col"), lax.axis_size("row")
    total, plane = group_size_of(("dp", "row", "col")), group_size_of(("row", "col"))
    micro, depth, part_width = x.shape
    width, tokens, low = part_width * cols, depth * rows, jnp.bfloat16
    quarter = depth // cols
    vmem = pl.BlockSpec(memory_space=pltpu.VMEM)
    shape = jax.ShapeDtypeStruct
    return pl.pallas_call(
        front_kernel,
        out_shape=[
            shape((tokens, width), low),
            shape((cols,) + w_qkv.shape[1:], low),
            shape((rows * 2 * w_out.shape[1], width), low),
            shape((total,) + picks.shape, picks.dtype),
            shape((total,) + cot.shape, low),
            shape((total,) + cot.shape, low),
            shape(weights.shape, low),
            shape((tokens, w_qkv.shape[3]), low),
            shape((plane, quarter, heads_width), low),
            shape((micro * quarter, width), jnp.float32),
        ],
        in_specs=[ANYWHERE] * 6 + [vmem] * 6,
        out_specs=[vmem] * 3 + [ANYWHERE] * 4 + [vmem] * 3,
        scratch_shapes=[
            pltpu.VMEM((micro * quarter, width), low),
            pltpu.VMEM((plane, quarter, heads_width), low),
            pltpu.VMEM((1, micro * quarter, width), low),
            pltpu.SemaphoreType.DMA((8,)),
            pltpu.SemaphoreType.DMA((72,)),
            pltpu.SemaphoreType.DMA((4 * cols,)),
            pltpu.SemaphoreType.DMA((2 * cols,)),
            pltpu.SemaphoreType.DMA((8 * cols,)),
            pltpu.SemaphoreType.DMA((micro * cols,)),
            pltpu.SemaphoreType.DMA((plane,)),
            pltpu.SemaphoreType.DMA((plane,)),
            pltpu.SemaphoreType.DMA,
            pltpu.SemaphoreType.DMA((plane,)),
            pltpu.SemaphoreType.DMA((plane,)),
        ]
        + gather_sems() * 3,
        compiler_params=pltpu.CompilerParams(
            collective_id=number, has_side_effects=True, vmem_limit_bytes=56 * 2**20
        ),
        name="front" + str(number),
    )(x, w_qkv, w_out, picks[None], cot[None], weights, *gains, *tables, *docs)


def sum_scratch(block):
    cols = lax.axis_size("col")
    low = jnp.bfloat16
    return [
        pltpu.VMEM((4 * cols,) + block, low),
        pltpu.VMEM((4 * cols,) + block, low),
        pltpu.VMEM((4 * cols,) + block, low),
        pltpu.VMEM((3 * cols,) + block, low),
        pltpu.VMEM((cols,) + block, low),
        pltpu.SemaphoreType.DMA((4 * cols,)),
        pltpu.SemaphoreType.DMA((48,)),
        pltpu.SemaphoreType.DMA((4 * cols,)),
        pltpu.SemaphoreType.DMA((cols,)),
        pltpu.SemaphoreType.DMA((2 * cols,)),
        pltpu.SemaphoreType.DMA((cols,)),
    ]


def sum_steps(partial, sems, copies):
    (
        near,
        mine,
        passed,
        stage,
        last,
        local_sem,
        send_sem,
        beside_sem,
        first_sem,
        second_sem,
        col_sem,
    ) = sems
    row, across, beside = row_peers()
    rows, cols = lax.axis_size("row"), lax.axis_size("col")
    col, dp = lax.axis_index("col"), lax.axis_index("dp")
    other = 1 - dp
    low = jnp.bfloat16
    sent = []

    def pass_on(src, dst, sem, peer):
        copy = send(src, dst, send_sem.at[len(sent)], sem, peer)
        sent.append(copy)
        copies.append(copy)

    def arrival(ref, sem):
        pltpu.make_async_copy(ref, ref, sem).wait()

    def block_of(dp_to, row_to, col_to):
        return (dp_to * rows + row_to) * cols + col_to

    far = (beside + rows // 2) % rows
    theirs = ((other, far), (other, beside), (dp, far), (dp, beside))
    ours = ((other, across), (other, row), (dp, across), (dp, row))

    def start():
        for turn in range(4):
            for z in range(cols):
                at = turn * cols + z
                pass_on(
                    partial.at[block_of(*theirs[turn], z)],
                    near.at[at],
                    beside_sem.at[at],
                    {"row": beside},
                )
                pltpu.make_async_copy(
                    partial.at[block_of(*ours[turn], z)], mine.at[at], local_sem.at[at]
                ).start()

    def chip_sum(at):
        arrival(mine.at[at], local_sem.at[at])
        arrival(near.at[at], beside_sem.at[at])
        return mine[at].astype(jnp.float32) + near[at].astype(jnp.float32)

    def diagonal():
        for z in range(cols):
            passed[z] = chip_sum(z).astype(low)
            peer = {"dp": other} if z < 2 else {"row": across}
            pass_on(passed.at[z], stage.at[z], first_sem.at[z], peer)

    def middle():
        for z in range(cols):
            for turn, here, peer in ((1, z >= 2, {"dp": other}), (2, z < 2, {"row": across})):
                at = turn * cols + z
                value = chip_sum(at)
                if here:
                    arrival(stage.at[z], first_sem.at[z])
                    value = value + stage[z].astype(jnp.float32)
                passed[at] = value.astype(low)
                pass_on(passed.at[at], stage.at[at], second_sem.at[at - cols], peer)

    def chip_total(z):
        value = chip_sum(3 * cols + z)
        for turn in (1, 2):
            arrival(stage.at[turn * cols + z], second_sem.at[(turn - 1) * cols + z])
            value = value + stage[turn * cols + z].astype(jnp.float32)
        return value

    def spread():
        for step in range(cols - 1, 0, -1):
            z = (col + step) % cols
            passed[3 * cols + z] = chip_total(z).astype(low)
            pass_on(passed.at[3 * cols + z], last.at[step], col_sem.at[step], {"col": z})

    def total():
        value = chip_total(col)
        for step in range(1, cols):
            arrival(last.at[step], col_sem.at[step])
            value = value + last[step].astype(jnp.float32)
        return value

    return start, diagonal, middle, spread, total


def back_kernel(
    partial,
    mix_part,
    grads,
    scores,
    normed_all,
    mixed,
    cot,
    gates,
    router_t,
    gain_one,
    gain_two,
    x_all,
    w_mine,
    w_out_mine,
    qkv,
    attended,
    cos_table,
    sin_table,
    doc_col,
    doc_row,
    mix_out,
    grads_own,
    dw_pair,
    do_pair,
    router_pair,
    x_grads,
    lines_all,
    scores_in,
    branch,
    branch_all,
    logits,
    logits_all,
    plane_rows,
    rotated,
    values_grad,
    grad_att,
    grad_qkv,
    normed,
    heads,
    heads_near,
    heads_across,
    heads_pair,
    heads_passed,
    dw_send,
    dw_in,
    do_send,
    do_in,
    x_send,
    lines,
    score_local,
    score_send,
    score_recv,
    ship_local,
    ship_send,
    ship_recv,
    plane_sem,
    gather_send,
    branch_col,
    branch_across,
    branch_beside,
    logits_col,
    logits_across,
    logits_beside,
    heads_send,
    near_sem,
    across_sem,
    pair_sem,
    part_local,
    part_send,
    dw_sem,
    do_sem,
    x_sem,
    swap_sem,
    *groups,
):
    row, across, beside = row_peers()
    rows, cols = lax.axis_size("row"), lax.axis_size("col")
    col, dp = lax.axis_index("col"), lax.axis_index("dp")
    other = 1 - dp
    far = (beside + rows // 2) % rows
    half = col % 2
    pair = col + 1 - 2 * half
    everyone, plane = ("dp", "row", "col"), ("row", "col")
    size, me = group_size_of(everyone), place_in(everyone)
    plane_size, plane_me = group_size_of(plane), place_in(plane)
    low, wide = jnp.bfloat16, jnp.float32
    copies, moved, parts, small, locals_ = [], [], [], [], []
    meet([device_at(everyone, (me + step) % size) for step in range(1, size)])

    def arrival(ref, sem):
        pltpu.make_async_copy(ref, ref, sem).wait()

    def ship(first, last):
        for step in range(first, last):
            to = (plane_me + step) % plane_size
            moved.append(
                send(
                    grads.at[to],
                    grads_own.at[plane_me],
                    ship_send.at[step],
                    ship_recv.at[step],
                    device_at(plane, to),
                )
            )

    def keep(src, dst):
        copy = pltpu.make_async_copy(src, dst, part_local.at[len(locals_)])
        copy.start()
        locals_.append(copy)

    rows_sum = sum_steps(partial, groups[0:11], copies)
    mix_sum = sum_steps(
        mix_part, groups[0:3] + groups[11:12] + groups[4:5] + groups[12:18], copies
    )
    lines_line = gather_line(lines, lines_all, groups[18:24], copies)

    score_own = pltpu.make_async_copy(scores.at[me], scores_in.at[me], score_local)
    score_own.start()
    for step in range(1, size):
        to = (me + step) % size
        small.append(
            send(
                scores.at[to],
                scores_in.at[me],
                score_send.at[step],
                score_recv.at[step],
                device_at(everyone, to),
            )
        )
    rows_sum[0]()
    keep(grads.at[plane_me], grads_own.at[plane_me])
    ship(1, 5)
    tokens, model_width = x_all.shape
    depth = tokens // rows
    for block in range(rows):
        part = slice(block * depth, (block + 1) * depth)
        normed[part, :] = norm_rows(x_all[part, :].astype(wide), gain_one[...])[1]
    rows_sum[1]()
    rows_sum[2]()
    rows_sum[3]()
    score_own.wait()
    for copy in small:
        copy.wait()
    gate = gates[...]
    scored = jnp.concatenate(
        [scores_in[:, 0, :], jnp.zeros((128 - size, 128), wide)], axis=0
    ).T[: gate.shape[0], :]
    grad_logits = gate * (scored - jnp.sum(gate * scored, axis=1, keepdims=True))
    routed = jnp.dot(
        grad_logits, router_t[...].astype(wide), precision=highest, preferred_element_type=wide
    )
    logits[0] = jnp.concatenate(
        [grad_logits, jnp.zeros((128 - gate.shape[0], 128), wide)], axis=0
    ).T[: logits.shape[1], :]
    value = mixed[...]
    scale_two = lax.rsqrt(jnp.mean(value * value, axis=1, keepdims=True) + eps_norm)
    unit_two = value * scale_two
    grad_normed = rows_sum[4]() + routed
    mix_row = jnp.sum(grad_normed * unit_two, axis=0, keepdims=True)
    grad_scaled = grad_normed * gain_two[...]
    grad_mixed = cot[...].astype(wide) + scale_two * (
        grad_scaled - unit_two * jnp.mean(grad_scaled * unit_two, axis=1, keepdims=True)
    )
    quarter = branch.shape[1]
    for m in range(2):
        branch[m] = (resid_scale * grad_mixed[m * quarter : (m + 1) * quarter, :]).astype(low)

    sent = []

    def pass_on(src, dst, sem, peer):
        sent.append(send(src, dst, gather_send.at[len(sent)], sem, peer))

    def origin(step):
        return (col + cols - step) % cols

    for step in range(1, cols):
        to = (col + step) % cols
        pass_on(branch.at[to // 2], branch_all.at[plane_me], branch_col.at[step], {"col": to})
        pass_on(logits.at[0], logits_all.at[plane_me], logits_col.at[step], {"col": to})
    keep(branch.at[col // 2], branch_all.at[plane_me])
    keep(logits.at[0], logits_all.at[plane_me])
    plans = (
        (branch.at[col // 2], branch_all, branch_col, branch_across, branch_beside),
        (logits.at[0], logits_all, logits_col, logits_across, logits_beside),
    )
    for step in range(cols):
        for mine, target, col_sem, side_sem, core_sem in plans:
            part = target.at[row * cols + origin(step)]
            if step > 0:
                arrival(part, col_sem.at[step])
            source = mine if step == 0 else part
            pass_on(source, part, side_sem.at[step], {"row": across})
            pass_on(source, part, core_sem.at[step], {"row": beside})
    ship(5, 11)
    for step in range(cols):
        for mine, target, col_sem, side_sem, core_sem in plans:
            part = target.at[across * cols + origin(step)]
            arrival(part, side_sem.at[step])
            pass_on(part, part, core_sem.at[cols + step], {"row": beside})
    for at, row_from in enumerate((beside, far)):
        for step in range(cols):
            for mine, target, col_sem, side_sem, core_sem in plans:
                arrival(target.at[row_from * cols + origin(step)], core_sem.at[at * cols + step])
    for copy in locals_:
        copy.wait()
    for copy in copies:
        copy.wait_send()
    done = len(copies)
    mix_sum[0]()

    branch_rows = branch_all[...].reshape(tokens, model_width)
    kv_at = attended.shape[2]
    count = kv_at // HEAD_DIM
    grad_att[...] = nt(branch_rows, w_out_mine[...]).astype(low)
    rotated[:, kv_at : kv_at + HEAD_DIM] = jnp.zeros((tokens, HEAD_DIM), wide)
    values_grad[...] = jnp.zeros_like(values_grad)
    for block in range(rows):
        part = slice(block * depth, (block + 1) * depth)
        extent = key_extent(block, depth, tokens)
        allowed = visible(doc_col, doc_row, block, depth, extent)
        key = qkv[0:extent, kv_at : kv_at + HEAD_DIM]
        value_rows = qkv[0:extent, kv_at + HEAD_DIM : kv_at + 2 * HEAD_DIM]
        key_sum = jnp.zeros((extent, HEAD_DIM), wide)
        value_sum = jnp.zeros((extent, HEAD_DIM), wide)
        for head in range(count):
            lanes = slice(head * HEAD_DIM, (head + 1) * HEAD_DIM)
            query = qkv[part, lanes]
            probs = attend(query, key, allowed)
            grad_out = grad_att[part, lanes]
            grad_probs = nt(grad_out, value_rows)
            grad_scores = probs * (
                grad_probs - jnp.sum(probs * grad_probs, axis=1, keepdims=True)
            )
            grad_raw = (grad_scores * attn_scale).astype(low)
            rotated[part, lanes] = project(grad_raw, key)
            key_sum = key_sum + tn(grad_raw, query)
            value_sum = value_sum + tn(probs.astype(low), grad_out)
        rotated[0:extent, kv_at : kv_at + HEAD_DIM] += key_sum
        values_grad[0:extent, :] += value_sum
        if block == 1:
            mix_sum[1]()
    for at in range(2):
        piece = slice(at * 128, (at + 1) * 128)
        grad_qkv[:, piece] = turn(rotated[:, piece], cos_table[...], -sin_table[...]).astype(low)
    grad_qkv[:, 256:] = values_grad[...].astype(low)

    rows_each = heads.shape[1]
    projection = w_mine[...].reshape(model_width, w_mine.shape[3])
    heads_sent = []

    def heads_on(src, dst, sem, peer):
        heads_sent.append(send(src, dst, heads_send.at[len(heads_sent)], sem, peer))

    halves = (1 - half, half)
    for at, row_to in enumerate((far, beside, across, row)):
        for which, part in enumerate(halves):
            slot = 2 * at + which
            first = pl.multiple_of((row_to * 2 + part) * rows_each, rows_each)
            heads[slot] = nt(grad_qkv[pl.ds(first, rows_each), :], projection).astype(low)
            if at < 2:
                heads_on(heads.at[slot], heads_near.at[slot], near_sem.at[slot], {"row": beside})
    width = model_width // cols
    heads_out = attended[...].reshape(tokens, kv_at)
    for step in range(cols - 1, -1, -1):
        to = (col + step) % cols
        lanes = pl.ds(pl.multiple_of(to * width, width), width)
        dw_send[to] = tn(grad_qkv[...], normed[:, lanes]).astype(low)
        chunk = branch_all[:, :, lanes].reshape(tokens, width)
        do_send[to] = tn(heads_out, chunk).astype(low)
        if step > 0:
            parts.append(
                send(dw_send.at[to], dw_in.at[col], part_send.at[step], dw_sem.at[step], {"col": to})
            )
            parts.append(
                send(
                    do_send.at[to],
                    do_in.at[col],
                    part_send.at[cols + step],
                    do_sem.at[step],
                    {"col": to},
                )
            )
    keep(dw_send.at[col], dw_in.at[col])
    keep(do_send.at[col], do_in.at[col])

    def heads_sum(slot):
        arrival(heads_near.at[slot - 4], near_sem.at[slot - 4])
        return heads[slot].astype(wide) + heads_near[slot - 4].astype(wide)

    for which in range(2):
        heads_passed[which] = heads_sum(4 + which).astype(low)
        heads_on(
            heads_passed.at[which], heads_across.at[which], across_sem.at[which], {"row": across}
        )
    mix_sum[2]()
    ship(11, plane_size)
    router_sum = jnp.zeros((logits.shape[1], model_width), wide)
    group = plane_rows.shape[0]
    for first in range(0, plane_size, group):
        load = pltpu.make_async_copy(
            normed_all.at[pl.ds(dp * plane_size + first, group)], plane_rows, score_local
        )
        load.start()
        load.wait()
        for at in range(group):
            left = logits_all[first + at, :, 0 : 2 * quarter]
            for _ in range(3):
                piece = left.astype(low)
                left = left - piece.astype(wide)
                router_sum = router_sum + project(piece, plane_rows[at])
    router_pair[dp] = router_sum
    swaps = [
        send(router_pair.at[dp], router_pair.at[dp], swap_sem.at[0], swap_sem.at[1], {"dp": other})
    ]
    for which in range(2):
        grad_one = heads_sum(6 + which)
        arrival(heads_across.at[which], across_sem.at[which])
        grad_one = grad_one + heads_across[which].astype(wide)
        if which == 0:
            heads_passed[2] = grad_one.astype(low)
            heads_on(heads_passed.at[2], heads_pair, pair_sem, {"col": pair})
    arrival(heads_pair, pair_sem)
    grad_one = grad_one + heads_pair[...].astype(wide)
    first = (row * 2 + half) * rows_each
    x_rows = x_all[pl.ds(pl.multiple_of(first, rows_each), rows_each), :].astype(wide)
    scale_one = lax.rsqrt(jnp.mean(x_rows * x_rows, axis=1, keepdims=True) + eps_norm)
    unit_one = x_rows * scale_one
    norm_row = jnp.sum(grad_one * unit_one, axis=0, keepdims=True)
    each = rows_each // quarter
    grad_h = branch_all[pl.ds((row * 2 + half) * each, each)].reshape(rows_each, model_width)
    grad_scaled = grad_one * gain_one[...]
    grad_x = grad_h.astype(wide) * (1.0 / resid_scale) + scale_one * (
        grad_scaled - unit_one * jnp.mean(grad_scaled * unit_one, axis=1, keepdims=True)
    )
    for to in range(cols):
        x_send[to] = grad_x[:, to * width : (to + 1) * width].astype(low)
    for step in range(1, cols):
        to = (col + step) % cols
        swaps.append(
            send(
                x_send.at[to], x_grads.at[col], x_sem.at[step], x_sem.at[cols + step], {"col": to}
            )
        )
    keep(x_send.at[col], x_grads.at[col])
    steps = model_width // 128
    for at in range(steps):
        piece = slice(at * 128, (at + 1) * 128)
        lines[0, at : at + 1, :] = norm_row[:, piece]
        lines[0, steps + at : steps + at + 1, :] = mix_row[:, piece]
    lines_line[0]()
    for copy in locals_[3:]:
        copy.wait()
    for step in range(1, cols):
        arrival(dw_in.at[origin(step)], dw_sem.at[step])
        arrival(do_in.at[origin(step)], do_sem.at[step])
    for h in range(2):
        dw_pair[dp, h] = (dw_in[h].astype(wide) + dw_in[2 + h].astype(wide)).astype(low)
        do_pair[dp, h] = (do_in[h].astype(wide) + do_in[2 + h].astype(wide)).astype(low)
    swaps.append(
        send(dw_pair.at[dp], dw_pair.at[dp], swap_sem.at[2], swap_sem.at[3], {"dp": other})
    )
    swaps.append(
        send(do_pair.at[dp], do_pair.at[dp], swap_sem.at[4], swap_sem.at[5], {"dp": other})
    )
    mix_sum[3]()
    for at in range(1, 4):
        for step in range(cols):
            lines_line[at](step)
    mix_out[...] = mix_sum[4]()
    lines_line[4]()
    for copy in swaps:
        copy.wait()
    for copy in moved:
        copy.wait()
    for copy in copies[done:] + parts + sent + heads_sent:
        copy.wait_send()


def back(number, partial, mix_part, grads, scores, normed_all, *rest):
    mixed, _, _, _, _, _, x_all, w_mine, _, qkv, attended = rest[:11]
    cols, rows = lax.axis_size("col"), lax.axis_size("row")
    total, plane = group_size_of(("dp", "row", "col")), group_size_of(("row", "col"))
    low, wide = jnp.bfloat16, jnp.float32
    vmem = pl.BlockSpec(memory_space=pltpu.VMEM)
    shape, dma = jax.ShapeDtypeStruct, pltpu.SemaphoreType.DMA
    tokens, width = x_all.shape
    quarter, heads_width = attended.shape[1:]
    block = partial.shape[1:]
    part = width // cols
    qkv_width = w_mine.shape[3]
    lines = -(-2 * (width // 128) // 8) * 8
    return pl.pallas_call(
        back_kernel,
        out_shape=[
            shape(block, wide),
            shape(grads.shape, low),
            shape((2, 2, qkv_width, part), low),
            shape((2, 2, heads_width, part), low),
            shape((2, total, width), wide),
            shape((cols, tokens // (2 * rows), part), low),
            shape((total, lines, 128), wide),
        ],
        in_specs=[ANYWHERE] * 5 + [vmem] * len(rest),
        out_specs=[vmem, ANYWHERE, vmem, vmem, vmem, vmem, ANYWHERE],
        scratch_shapes=[
            pltpu.VMEM(scores.shape, wide),
            pltpu.VMEM((2, quarter, width), low),
            pltpu.VMEM((plane, quarter, width), low),
            pltpu.VMEM((1, total, 128), wide),
            pltpu.VMEM((plane, total, 128), wide),
            pltpu.VMEM((4,) + block, low),
            pltpu.VMEM((tokens, 256), wide),
            pltpu.VMEM((tokens, HEAD_DIM), wide),
            pltpu.VMEM((tokens, heads_width), low),
            pltpu.VMEM((tokens, qkv_width), low),
            pltpu.VMEM((tokens, width), low),
            pltpu.VMEM((8, tokens // (2 * rows), width), low),
            pltpu.VMEM((4, tokens // (2 * rows), width), low),
            pltpu.VMEM((2, tokens // (2 * rows), width), low),
            pltpu.VMEM((tokens // (2 * rows), width), low),
            pltpu.VMEM((3, tokens // (2 * rows), width), low),
            pltpu.VMEM((cols, qkv_width, part), low),
            pltpu.VMEM((cols, qkv_width, part), low),
            pltpu.VMEM((cols, heads_width, part), low),
            pltpu.VMEM((cols, heads_width, part), low),
            pltpu.VMEM((cols, tokens // (2 * rows), part), low),
            pltpu.VMEM((1, lines, 128), wide),
            dma,
            dma((total,)),
            dma((total,)),
            dma,
            dma((plane,)),
            dma((plane,)),
            dma,
            dma((40,)),
            dma((cols,)),
            dma((cols,)),
            dma((2 * cols,)),
            dma((cols,)),
            dma((cols,)),
            dma((2 * cols,)),
            dma((8,)),
            dma((4,)),
            dma((2,)),
            dma,
            dma((8,)),
            dma((2 * cols,)),
            dma((cols,)),
            dma((cols,)),
            dma((2 * cols,)),
            dma((6,)),
        ]
        + sum_scratch(block)
        + [pltpu.VMEM((3 * cols,) + block, low)]
        + sum_scratch(block)[5:]
        + gather_sems(),
        compiler_params=pltpu.CompilerParams(
            collective_id=number, has_side_effects=True, vmem_limit_bytes=62 * 2**20
        ),
        name="back" + str(number),
    )(partial, mix_part, grads, scores, normed_all, *rest)


def expert_kernel(
    normed,
    cot,
    table,
    rank,
    mark,
    router,
    weights,
    mix_out,
    rows_out,
    score_out,
    grads_out,
    kept_in,
    kept_dye,
    kept_act,
    kept_gate,
    kept_up,
):
    low = jnp.bfloat16
    step = pl.program_id(0)
    slots = kept_in.shape[1]
    parts, _, ff_width = weights.shape
    depth = normed.shape[1] // parts
    down_depth = ff_width // parts

    gate_w = weights[:, 0:depth, :].reshape(parts * depth, ff_width)
    up_w = weights[:, depth : 2 * depth, :].reshape(parts * depth, ff_width)

    def down_w(chunk):
        at = 2 * depth + chunk * down_depth
        return weights[:, at : at + down_depth, :].reshape(ff_width, ff_width)

    chunks = normed.shape[1] // ff_width
    tokens = normed[...]
    cots = cot[...]
    logits = jnp.where(
        table[...] > 0, project(tokens, router[...]), -jnp.inf
    )
    top = jnp.max(logits, axis=1, keepdims=True)
    raised = jnp.exp(logits - top)
    gates = raised / jnp.sum(raised, axis=1, keepdims=True)
    slot = lax.broadcasted_iota(jnp.int32, (slots, normed.shape[0]), 0)
    picked = slot == rank[0, 0:1, :]
    chosen = picked.astype(jnp.float32)
    select = chosen.astype(low)
    gate = jnp.sum(
        jnp.dot(chosen, gates, precision=highest, preferred_element_type=jnp.float32) * mark[...],
        axis=1,
        keepdims=True,
    )
    expert_in = project(select, tokens).astype(low)
    grad_mix = resid_scale * project(select, cots)
    grad_out = (gate * grad_mix).astype(low)
    gate_proj = project(expert_in, gate_w)
    up_proj = project(expert_in, up_w)
    sigmoid = 1.0 / (1.0 + jnp.exp(-gate_proj))
    silu = gate_proj * sigmoid
    act = (silu * up_proj).astype(low)
    score = jnp.zeros((slots, 1), jnp.float32)
    grad_act = jnp.zeros((slots, ff_width), jnp.float32)
    for chunk in range(chunks):
        lanes = slice(chunk * ff_width, (chunk + 1) * ff_width)
        part = down_w(chunk)
        out = project(act, part).astype(low).astype(jnp.float32)
        score = score + jnp.sum(grad_mix[:, lanes] * out, axis=1, keepdims=True)
        mix_out[:, lanes] = tn(select, (gate * out).astype(low)).astype(low)
        grad_act = grad_act + nt(grad_out[:, lanes], part)
    grad_gate = (grad_act * up_proj * (sigmoid + gate_proj * sigmoid * (1.0 - sigmoid))).astype(low)
    grad_up = (grad_act * silu).astype(low)
    grad_in = (nt(grad_gate, gate_w) + nt(grad_up, up_w)).astype(low)
    rows_out[...] = tn(select, grad_in).astype(low)
    score_row = jnp.sum(chosen * score, axis=0, keepdims=True)
    score_out[0] = jnp.broadcast_to(score_row, score_out.shape[1:])
    kept_in[step] = expert_in
    kept_dye[step] = grad_out
    kept_act[step] = act
    kept_gate[step] = grad_gate
    kept_up[step] = grad_up

    @pl.when(step == pl.num_programs(0) - 1)
    def _():
        def all_of(kept):
            return kept[...].reshape(kept.shape[0] * slots, kept.shape[2])

        rows = all_of(kept_in)
        for at, kept in ((0, kept_gate), (depth, kept_up)):
            grad = tn(rows, all_of(kept)).astype(low)
            grads_out[:, at : at + depth, :] = grad.reshape(parts, depth, ff_width)
        act_all = all_of(kept_act)
        for chunk in range(chunks):
            lanes = slice(chunk * ff_width, (chunk + 1) * ff_width)
            grad = tn(act_all, all_of(kept_dye.at[:, :, lanes])).astype(low)
            at = 2 * depth + chunk * down_depth
            grads_out[:, at : at + down_depth, :] = grad.reshape(parts, down_depth, ff_width)


def expert_pass(normed, cot, table, rank, mark, router, weights, slots):
    tiles, tile = rank.shape[0], rank.shape[2]
    tokens, width = normed.shape
    low = jnp.bfloat16
    ff_width = weights.shape[2]
    rows = pl.BlockSpec((tile, width), lambda i: (i, 0))
    whole = lambda a: pl.BlockSpec(
        a.shape, lambda i: (0,) * len(a.shape), pipeline_mode=pl.Buffered(1)
    )
    return pl.pallas_call(
        expert_kernel,
        grid=(tiles,),
        out_shape=[
            jax.ShapeDtypeStruct((tokens, width), low),
            jax.ShapeDtypeStruct((tokens, width), low),
            jax.ShapeDtypeStruct((tiles, 8, tile), jnp.float32),
            jax.ShapeDtypeStruct(weights.shape, low),
        ],
        in_specs=[
            rows,
            rows,
            pl.BlockSpec((tile, table.shape[1]), lambda i: (i, 0)),
            pl.BlockSpec((1,) + rank.shape[1:], lambda i: (i, 0, 0)),
            whole(mark),
            whole(router),
            whole(weights),
        ],
        out_specs=[
            rows,
            rows,
            pl.BlockSpec((1, 8, tile), lambda i: (i, 0, 0)),
            whole(weights),
        ],
        scratch_shapes=[
            pltpu.VMEM((tiles, slots, width), low),
            pltpu.VMEM((tiles, slots, width), low),
            pltpu.VMEM((tiles, slots, ff_width), low),
            pltpu.VMEM((tiles, slots, ff_width), low),
            pltpu.VMEM((tiles, slots, ff_width), low),
        ],
        compiler_params=pltpu.CompilerParams(vmem_limit_bytes=56 * 2**20),
        cost_estimate=pl.CostEstimate(
            flops=22 * 10**9, bytes_accessed=50 * 10**6, transcendentals=10**6
        ),
        name="expert_pass",
    )(normed, cot, table, rank, mark, router, weights)


def owned(
    hidden_in,
    norm_gain,
    w_query,
    w_key,
    w_value,
    w_out,
    mix_gain,
    w_router,
    w_gate,
    w_up,
    w_down,
    lengths,
    routes,
    mask,
    cotangent,
):
    everyone = ("dp", "row", "col")
    plane = ("row", "col")
    micro_count, tok_row, width_part = hidden_in.shape
    row_count = lax.axis_size("row")
    col_count = lax.axis_size("col")
    dp_count = lax.axis_size("dp")
    row_at = lax.axis_index("row")
    col_at = lax.axis_index("col")
    dp_at = lax.axis_index("dp")
    plane_count = row_count * col_count
    device_count = plane_count * dp_count
    plane_at = row_at * col_count + col_at
    model_width = width_part * col_count
    kv_here = w_key.shape[1] // HEAD_DIM
    group_size = w_query.shape[1] // w_key.shape[1]
    q_width = group_size * HEAD_DIM
    group_tokens = tok_row * row_count
    quarter = tok_row // col_count
    own_rows = micro_count * quarter
    experts_here, slice_width, ff_width = w_gate.shape
    down_slice = w_down.shape[1]
    experts_all = experts_here * dp_count
    expert_at = dp_at * plane_count + plane_at
    micro_at = col_at // kv_here
    half_at = col_at % kv_here

    masked_cot = cotangent * mask[:, :, None].astype(cotangent.dtype)

    w_qkv = jnp.concatenate(
        [
            w_query.reshape(width_part, kv_here, q_width),
            w_key.reshape(width_part, kv_here, HEAD_DIM),
            w_value.reshape(width_part, kv_here, HEAD_DIM),
        ],
        axis=2,
    ).transpose(1, 0, 2)
    qkv_width = q_width + 2 * HEAD_DIM
    picks = jnp.pad(routes.reshape(own_rows, TOP).T, ((0, 0), (0, 128 - own_rows)))
    weights = jnp.concatenate(
        [w_gate, w_up]
        + [w_down[:, :, at : at + ff_width] for at in range(0, model_width, ff_width)],
        axis=1,
    )
    doc_id, position = documents(lengths[:, 0][micro_at], group_tokens)
    sin_table, cos_table = (
        table[:, 0] for table in angles(position.astype(jnp.float32), HEAD_DIM)
    )
    doc_col = jnp.broadcast_to(doc_id[:, None], (group_tokens, 128))
    doc_row = jnp.broadcast_to(doc_id[None, :], (8, group_tokens))
    cos_lanes = jnp.tile(cos_table, (1, 4))
    sin_lanes = jnp.tile(jnp.concatenate([-sin_table, sin_table], axis=1), (1, 2))
    (
        x_micro,
        w_mine,
        w_out_all,
        routes_all,
        cot_all,
        normed_all,
        weights,
        qkv,
        attended,
        mixed,
    ) = front(
        0,
        hidden_in,
        w_qkv.reshape(kv_here, dp_count, width_part // dp_count, qkv_width),
        w_out.reshape(dp_count, w_out.shape[0] // dp_count, w_out.shape[1]),
        picks,
        masked_cot.reshape(own_rows, model_width),
        weights,
        (norm_gain[None], mix_gain[None]),
        (cos_lanes, sin_lanes),
        (doc_col, doc_row),
        q_width,
    )
    routes_all = (
        routes_all[:, :, :own_rows].transpose(0, 2, 1).reshape(device_count * own_rows, TOP)
    )
    expert_ids = jnp.arange(experts_all, dtype=jnp.int32)

    def gating(normed_rows, picks):
        chosen = jnp.any(picks[:, :, None] == expert_ids[None, None, :], axis=1)
        logits = jnp.where(chosen, project(normed_rows, w_router), -jnp.inf)
        return jax.nn.softmax(logits, axis=-1)

    normed_two = lax.dynamic_index_in_dim(normed_all, expert_at, 0, keepdims=False)
    gates_own = gating(normed_two, routes.reshape(own_rows, TOP))

    tile = col_count * own_rows
    slots = col_count * micro_count * (quarter * 3 // 8)
    table = jnp.any(routes_all[:, :, None] == expert_ids[None, None, :], axis=1)
    here = jnp.any(routes_all == expert_at, axis=1).astype(jnp.int32).reshape(-1, tile)
    rank = jnp.where(here > 0, jnp.cumsum(here, axis=1, dtype=jnp.int32) - 1, -1)
    pad_experts = 128 - experts_all
    mix_part, grad_rows_part, grad_gate_mine, grads = expert_pass(
        normed_all.reshape(device_count * own_rows, model_width),
        cot_all.reshape(device_count * own_rows, model_width),
        jnp.pad(table.astype(jnp.float32), ((0, 0), (0, pad_experts))),
        jnp.broadcast_to(rank[:, None, :], (rank.shape[0], 8, tile)),
        (jnp.arange(128, dtype=jnp.int32) == expert_at).astype(jnp.float32)[None],
        jnp.pad(w_router, ((0, 0), (0, pad_experts))),
        weights,
        slots,
    )
    grad_gate_mine = grad_gate_mine[:, 0, :].reshape(-1)
    scores_send = jnp.broadcast_to(
        jnp.pad(
            grad_gate_mine.reshape(device_count, 1, own_rows),
            ((0, 0), (0, 0), (0, 128 - own_rows)),
        ),
        (device_count, 8, 128),
    )
    w_out_mine = lax.dynamic_slice_in_dim(
        w_out_all, (row_at * kv_here + half_at) * q_width, q_width
    )
    expert_mix, grads, qkv_sum, out_sum, router_grad, grad_input, lines = back(
        1,
        grad_rows_part.reshape(device_count, own_rows, model_width),
        mix_part.reshape(device_count, own_rows, model_width),
        grads,
        scores_send,
        normed_all,
        mixed,
        masked_cot.reshape(own_rows, model_width),
        jnp.pad(gates_own, ((0, 0), (0, pad_experts))),
        jnp.pad(w_router.T, ((0, pad_experts), (0, 0))),
        norm_gain[None],
        mix_gain[None],
        x_micro,
        w_mine,
        w_out_mine,
        qkv,
        attended,
        cos_lanes,
        sin_lanes,
        doc_col,
        doc_row,
    )
    layer_out = (mixed + resid_scale * expert_mix).astype(jnp.bfloat16)
    out_gate = grads[:, :slice_width].astype(jnp.float32)
    out_up = grads[:, slice_width : 2 * slice_width].astype(jnp.float32)
    out_down = jnp.concatenate(
        [
            grads[:, at : at + down_slice]
            for at in range(2 * slice_width, grads.shape[1], down_slice)
        ],
        axis=2,
    ).astype(jnp.float32)
    grad_input = grad_input.reshape(micro_count, tok_row, width_part).astype(jnp.float32)
    qkv_sum = jnp.sum(qkv_sum.astype(jnp.float32), axis=0)
    out_sum = jnp.sum(out_sum.astype(jnp.float32), axis=0)
    router_grad = jnp.sum(router_grad, axis=0).T
    lines = jnp.sum(lines, axis=0)
    norm_grad = lines[: model_width // 128].reshape(-1)
    mix_grad = lines[model_width // 128 : 2 * (model_width // 128)].reshape(-1)
    grad_wq = qkv_sum[:, :q_width].reshape(-1, width_part).T
    grad_wk = qkv_sum[:, q_width : q_width + HEAD_DIM].reshape(-1, width_part).T
    grad_wv = qkv_sum[:, q_width + HEAD_DIM :].reshape(-1, width_part).T
    grad_wo = out_sum.reshape(w_out.shape)
    return (
        layer_out.reshape(micro_count, quarter, model_width),
        grad_input,
        norm_grad,
        grad_wq,
        grad_wk,
        grad_wv,
        grad_wo,
        mix_grad,
        router_grad,
        out_gate,
        out_up,
        out_down,
    )


def solution(mesh):
    dp_count, row_count, col_count = (mesh.shape[name] for name in ("dp", "row", "col"))

    def body(*args):
        hidden_in, w_key, w_gate = args[0], args[3], args[8]
        kv_here = w_key.shape[1] // HEAD_DIM
        one_each = w_gate.shape[0] == row_count * col_count
        pairs = hidden_in.shape[0] * kv_here == col_count
        sizes = (dp_count, row_count, col_count, kv_here) == (2, 4, 4, 2)
        return (owned if sizes and one_each and pairs else shards)(*args)

    placed = (
        P(None, ("dp", "row"), "col"),
        P(),
        P("col", "row"),
        P("col", "row"),
        P("col", "row"),
        P("row", "col"),
        P(),
        P(),
        P("dp", ("row", "col"), None),
        P("dp", ("row", "col"), None),
        P("dp", ("row", "col"), None),
        P(None, "dp", None),
        P(None, ("dp", "row", "col"), None),
        P(None, ("dp", "row", "col")),
        P(None, ("dp", "row", "col"), None),
    )
    return jax.shard_map(
        body,
        mesh=mesh,
        in_specs=placed,
        out_specs=(
            P(None, ("dp", "row", "col"), None),
            P(None, ("dp", "row"), "col"),
            P(),
            P("col", "row"),
            P("col", "row"),
            P("col", "row"),
            P("row", "col"),
            P(),
            P(),
            P("dp", ("row", "col"), None),
            P("dp", ("row", "col"), None),
            P("dp", ("row", "col"), None),
        ),
        check_vma=False,
    )
```

```python
import functools

import jax
import jax.numpy as jnp
from jax import lax
from jax.experimental import pallas as pl
from jax.experimental.pallas import tpu as pltpu
from jax.sharding import PartitionSpec as P

D = 1536
HEAD_DIM = 64
TOP = 8


eps_norm = 1e-06
resid_scale = 0.22
attn_scale = 0.015625
rope_base = 10000.0
highest = lax.Precision.HIGHEST


def shortened(shard):
    return jax.tree.map(lambda a: a.astype(jnp.bfloat16) if a.dtype == jnp.float32 else a, shard)


def documents(doc_lengths, length_all):
    doc_ends = jnp.cumsum(doc_lengths, dtype=jnp.int32)
    doc_starts = doc_ends - doc_lengths
    positions = jnp.arange(length_all, dtype=jnp.int32)
    doc_id = jnp.sum(
        (positions[:, None] >= doc_ends[None, :]).astype(jnp.int32), axis=1, dtype=jnp.int32
    )
    member = doc_id[:, None] == jnp.arange(doc_lengths.shape[0], dtype=jnp.int32)[None, :]
    doc_start = jnp.sum(jnp.where(member, doc_starts[None, :], 0), axis=1, dtype=jnp.int32)
    return (doc_id, positions - doc_start)


def angles(position, head_width):
    half_width = head_width // 2
    frequency = rope_base ** (-2.0 * jnp.arange(half_width, dtype=jnp.float32) / head_width)
    turned = position[:, None] * frequency[None, :]
    return (jnp.sin(turned)[:, None, :], jnp.cos(turned)[:, None, :])


def rotate(values, sin_table, cos_table):
    half_width = values.shape[-1] // 2
    front_half = values[..., :half_width]
    back_half = values[..., half_width:]
    return jnp.concatenate(
        [
            front_half * cos_table - back_half * sin_table,
            back_half * cos_table + front_half * sin_table,
        ],
        axis=-1,
    )


def gather_rows(value):
    return lax.all_gather(value, "row", axis=0, tiled=True)


def gather_cols(value):
    return jax.tree.map(
        lambda part, own: part.astype(own.dtype),
        lax.all_gather(shortened(value), "col", axis=0, tiled=True),
        value,
    )


def sum_cols(pieces):
    return lax.psum_scatter(pieces, "col", scatter_dimension=0, tiled=True)


def sum_rows(pieces):
    return lax.psum_scatter(pieces, "row", scatter_dimension=0, tiled=True)


def width_total(value):
    return lax.psum(value, "col")


def expert_trade(value):
    return lax.all_to_all(value, "dp", split_axis=1, concat_axis=1, tiled=True)


def attn_total(value):
    return jax.tree.map(lambda part: part.astype(jnp.float32), lax.psum(shortened(value), "dp"))


def expert_total(value):
    return jax.tree.map(
        lambda part: part.astype(jnp.float32),
        lax.psum_scatter(shortened(value), ("row", "col"), scatter_dimension=1, tiled=True),
    )


def add_all(first_set, second_set):
    return tuple((left_one + right_one for left_one, right_one in zip(first_set, second_set)))


def project(left_side, right_side):
    return jnp.dot(left_side, right_side, preferred_element_type=jnp.float32)


def shards(
    hidden_in,
    norm_gain,
    w_query,
    w_key,
    w_value,
    w_out,
    mix_gain,
    w_router,
    w_gate,
    w_up,
    w_down,
    lengths,
    routes,
    mask,
    cotangent,
):
    micro_count = hidden_in.shape[0]
    tok_dev = hidden_in.shape[1]
    width_part = hidden_in.shape[2]
    col_count = lax.axis_size("col")
    row_count = lax.axis_size("row")
    dp_count = lax.axis_size("dp")
    col_at = lax.axis_index("col")
    model_width = D
    heads_here = w_query.shape[1] // HEAD_DIM
    kv_here = w_key.shape[1] // HEAD_DIM
    group_size = heads_here // kv_here
    group_tokens = tok_dev * row_count
    quarter = tok_dev // col_count
    experts_here = w_gate.shape[0]
    experts_all = experts_here * dp_count
    capacity = quarter * 3 // 8
    slot_count = experts_all * capacity
    gain_part = lax.dynamic_slice_in_dim(norm_gain, col_at * width_part, width_part)
    router_wide = w_router.astype(jnp.float32)
    full_gate, full_up, full_down = (
        lax.all_gather(w_gate, ("row", "col"), axis=1, tiled=True),
        lax.all_gather(w_up, ("row", "col"), axis=1, tiled=True),
        lax.all_gather(w_down, ("row", "col"), axis=1, tiled=True),
    )
    expert_ids = jnp.arange(experts_all, dtype=jnp.int32)
    group_index = jnp.arange(group_tokens, dtype=jnp.int32)
    query_start = col_at * tok_dev
    query_index = query_start + jnp.arange(tok_dev, dtype=jnp.int32)
    attn_local = (
        jnp.zeros(w_query.shape, jnp.float32),
        jnp.zeros(w_key.shape, jnp.float32),
        jnp.zeros(w_value.shape, jnp.float32),
        jnp.zeros(w_out.shape, jnp.float32),
    )
    expert_local = (
        jnp.zeros(full_gate.shape, jnp.float32),
        jnp.zeros(full_up.shape, jnp.float32),
        jnp.zeros(full_down.shape, jnp.float32),
    )
    router_acc = jnp.zeros(w_router.shape, jnp.float32)
    norm_acc = jnp.zeros((width_part,), jnp.float32)
    mix_acc = jnp.zeros((model_width,), jnp.float32)
    layer_rows = []
    input_grads = []
    for step in range(micro_count):
        x_full = hidden_in[step].astype(jnp.float32)
        squares = width_total(jnp.sum(x_full * x_full, axis=1))
        scale_one = lax.rsqrt(squares / model_width + eps_norm)[:, None]
        unit_one = x_full * scale_one
        normed = (unit_one * gain_part).astype(jnp.bfloat16)
        normed_all = gather_rows(normed)
        query_p, key_p, value_p = sum_cols(
            (project(normed_all, w_query), project(normed_all, w_key), project(normed_all, w_value))
        )
        doc_all, pos_all = documents(lengths[step, 0], group_tokens)
        doc_query = lax.dynamic_slice_in_dim(doc_all, query_start, tok_dev)
        pos_query = lax.dynamic_slice_in_dim(pos_all, query_start, tok_dev).astype(jnp.float32)
        sin_table, cos_table = angles(pos_query, HEAD_DIM)
        query_rot = rotate(
            query_p.reshape(tok_dev, heads_here, HEAD_DIM), sin_table, cos_table
        ).astype(jnp.bfloat16)
        key_rot = rotate(key_p.reshape(tok_dev, kv_here, HEAD_DIM), sin_table, cos_table).astype(
            jnp.bfloat16
        )
        value_low = value_p.astype(jnp.bfloat16).reshape(tok_dev, kv_here, HEAD_DIM)
        keys_all, values_all = (
            lax.all_gather(key_rot, "col", axis=0, tiled=True),
            lax.all_gather(value_low, "col", axis=0, tiled=True),
        )
        allowed = (doc_query[:, None] == doc_all[None, :]) & (
            group_index[None, :] <= query_index[:, None]
        )
        query_grp = query_rot.reshape(tok_dev, kv_here, group_size, HEAD_DIM)
        raw_scores = jnp.einsum(
            "qhgd,khd->hgqk", query_grp, keys_all, preferred_element_type=jnp.float32
        )
        scores = jnp.where(allowed[None, None], raw_scores * attn_scale, -1e30)
        top_score = jnp.max(scores, axis=-1, keepdims=True)
        expd = jnp.exp(scores - top_score)
        row_total = jnp.sum(expd, axis=-1, keepdims=True)
        attn_probs = expd / row_total
        log_total = top_score + jnp.log(row_total)
        probs_low = attn_probs.astype(jnp.bfloat16)
        attended = jnp.einsum(
            "hgqk,khd->qhgd", probs_low, values_all, preferred_element_type=jnp.float32
        )
        attended_low = attended.reshape(tok_dev, heads_here * HEAD_DIM).astype(jnp.bfloat16)
        attended_all = gather_cols(attended_low)
        attn_branch = sum_rows(project(attended_all, w_out))
        mixed = x_full + resid_scale * attn_branch
        mixed_rows = lax.all_to_all(
            mixed.reshape(col_count, quarter, width_part),
            "col",
            split_axis=0,
            concat_axis=2,
            tiled=True,
        ).reshape(quarter, model_width)
        scale_two = lax.rsqrt(jnp.mean(mixed_rows * mixed_rows, axis=1, keepdims=True) + eps_norm)
        unit_two = mixed_rows * scale_two
        normed_two = (unit_two * mix_gain).astype(jnp.bfloat16)
        logits = project(normed_two, w_router)
        picks = routes[step]
        choose = (picks[:, :, None] == expert_ids[None, None, :]).astype(jnp.float32)
        chosen = jnp.sum(choose * logits[:, None, :], axis=-1)
        gate_weights = jax.nn.softmax(chosen, axis=-1)
        flat_picks = picks.reshape(-1)
        hit_table = (flat_picks[:, None] == expert_ids[None, :]).astype(jnp.int32)
        slot_rank = jnp.sum(
            hit_table * (jnp.cumsum(hit_table, axis=0, dtype=jnp.int32) - 1),
            axis=1,
            dtype=jnp.int32,
        )
        owner_dp = flat_picks // experts_here
        local_expert = flat_picks % experts_here
        slot_index = local_expert * (dp_count * capacity) + owner_dp * capacity + slot_rank
        token_of = (
            jnp.full((slot_count,), quarter, jnp.int32)
            .at[slot_index]
            .set(jnp.arange(quarter * TOP, dtype=jnp.int32) // TOP)
        )
        padded = jnp.concatenate([normed_two, jnp.zeros((1, model_width), jnp.bfloat16)], axis=0)
        send_rows = padded[token_of].reshape(experts_here, dp_count * capacity, model_width)
        expert_in = expert_trade(send_rows)
        gate_proj = jnp.einsum(
            "ecd,edf->ecf", expert_in, full_gate, preferred_element_type=jnp.float32
        )
        up_proj = jnp.einsum("ecd,edf->ecf", expert_in, full_up, preferred_element_type=jnp.float32)
        activated = (jax.nn.silu(gate_proj) * up_proj).astype(jnp.bfloat16)
        expert_out = jnp.einsum(
            "ecf,efd->ecd", activated, full_down, preferred_element_type=jnp.float32
        ).astype(jnp.bfloat16)
        returned = expert_trade(expert_out).reshape(slot_count, model_width)
        combined = returned[slot_index].reshape(quarter, TOP, model_width).astype(jnp.float32)
        expert_mix = jnp.sum(gate_weights[:, :, None] * combined, axis=1)
        layer_rows.append((mixed_rows + resid_scale * expert_mix).astype(jnp.bfloat16))
        grad_rows = cotangent[step].astype(jnp.float32) * mask[step][:, None].astype(jnp.float32)
        grad_mix = resid_scale * grad_rows
        grad_gates = jnp.sum(grad_mix[:, None, :] * combined, axis=-1)
        grad_chosen = gate_weights * (
            grad_gates - jnp.sum(gate_weights * grad_gates, axis=-1, keepdims=True)
        )
        grad_logits = jnp.sum(choose * grad_chosen[:, :, None], axis=1)
        gate_slots = (
            jnp.zeros((slot_count,), jnp.float32).at[slot_index].set(gate_weights.reshape(-1))
        )
        grad_pad = jnp.concatenate([grad_mix, jnp.zeros((1, model_width), jnp.float32)], axis=0)
        grad_send = (gate_slots[:, None] * grad_pad[token_of]).astype(jnp.bfloat16)
        grad_expert = expert_trade(
            grad_send.reshape(experts_here, dp_count * capacity, model_width)
        )
        grad_act = jnp.einsum(
            "ecd,efd->ecf", grad_expert, full_down, preferred_element_type=jnp.float32
        )
        micro_down = jnp.einsum(
            "ecf,ecd->efd", activated, grad_expert, preferred_element_type=jnp.float32
        )
        sigmoid_gate = jax.nn.sigmoid(gate_proj)
        silu_gate = gate_proj * sigmoid_gate
        grad_gate_p = (
            grad_act * up_proj * (sigmoid_gate + gate_proj * sigmoid_gate * (1.0 - sigmoid_gate))
        ).astype(jnp.bfloat16)
        grad_up_p = (grad_act * silu_gate).astype(jnp.bfloat16)
        grad_in = jnp.einsum(
            "ecf,edf->ecd", grad_gate_p, full_gate, preferred_element_type=jnp.float32
        ) + jnp.einsum("ecf,edf->ecd", grad_up_p, full_up, preferred_element_type=jnp.float32)
        micro_gate = jnp.einsum(
            "ecd,ecf->edf", expert_in, grad_gate_p, preferred_element_type=jnp.float32
        )
        micro_up = jnp.einsum(
            "ecd,ecf->edf", expert_in, grad_up_p, preferred_element_type=jnp.float32
        )
        expert_local = add_all(expert_local, (micro_gate, micro_up, micro_down))
        grad_back = expert_trade(grad_in.astype(jnp.bfloat16)).reshape(slot_count, model_width)
        grad_normed = jnp.sum(
            grad_back[slot_index].reshape(quarter, TOP, model_width).astype(jnp.float32), axis=1
        ) + jnp.dot(grad_logits, router_wide.T, precision=highest)
        router_acc = router_acc + jnp.dot(
            normed_two.astype(jnp.float32).T, grad_logits, precision=highest
        )
        mix_acc = mix_acc + jnp.sum(grad_normed * unit_two, axis=0)
        grad_scaled = grad_normed * mix_gain
        grad_mixed_rows = grad_rows + scale_two * (
            grad_scaled - unit_two * jnp.mean(grad_scaled * unit_two, axis=1, keepdims=True)
        )
        grad_mixed = lax.all_to_all(
            grad_mixed_rows.reshape(1, quarter, model_width),
            "col",
            split_axis=2,
            concat_axis=0,
            tiled=True,
        ).reshape(tok_dev, width_part)
        grad_branch = (resid_scale * grad_mixed).astype(jnp.bfloat16)
        grad_branch_all = gather_rows(grad_branch)
        micro_out = jnp.dot(attended_all.T, grad_branch_all, preferred_element_type=jnp.float32)
        grad_attended = sum_cols(
            jnp.dot(grad_branch_all, w_out.T, preferred_element_type=jnp.float32)
        )
        grad_att_low = grad_attended.astype(jnp.bfloat16).reshape(
            tok_dev, kv_here, group_size, HEAD_DIM
        )
        probs_again = jnp.exp(scores - log_total)
        grad_probs = jnp.einsum(
            "qhgd,khd->hgqk", grad_att_low, values_all, preferred_element_type=jnp.float32
        )
        grad_scores = probs_again * (
            grad_probs - jnp.sum(probs_again * grad_probs, axis=-1, keepdims=True)
        )
        grad_raw = (grad_scores * attn_scale).astype(jnp.bfloat16)
        probs_again_low = probs_again.astype(jnp.bfloat16)
        grad_query = jnp.einsum(
            "hgqk,khd->qhgd", grad_raw, keys_all, preferred_element_type=jnp.float32
        )
        grad_key_part = jnp.einsum(
            "hgqk,qhgd->khd", grad_raw, query_grp, preferred_element_type=jnp.float32
        )
        grad_value_part = jnp.einsum(
            "hgqk,qhgd->khd", probs_again_low, grad_att_low, preferred_element_type=jnp.float32
        )
        grad_key, grad_value = sum_cols(
            (
                grad_key_part.reshape(group_tokens, kv_here * HEAD_DIM),
                grad_value_part.reshape(group_tokens, kv_here * HEAD_DIM),
            )
        )
        grad_query_p = (
            rotate(grad_query.reshape(tok_dev, heads_here, HEAD_DIM), -sin_table, cos_table)
            .astype(jnp.bfloat16)
            .reshape(tok_dev, heads_here * HEAD_DIM)
        )
        grad_key_p = (
            rotate(grad_key.reshape(tok_dev, kv_here, HEAD_DIM), -sin_table, cos_table)
            .astype(jnp.bfloat16)
            .reshape(tok_dev, kv_here * HEAD_DIM)
        )
        grad_value_p = grad_value.astype(jnp.bfloat16)
        query_all, key_all, value_all = gather_cols((grad_query_p, grad_key_p, grad_value_p))
        micro_query = jnp.dot(normed_all.T, query_all, preferred_element_type=jnp.float32)
        micro_key = jnp.dot(normed_all.T, key_all, preferred_element_type=jnp.float32)
        micro_value = jnp.dot(normed_all.T, value_all, preferred_element_type=jnp.float32)
        grad_normed_one = sum_rows(
            jnp.dot(query_all, w_query.T, preferred_element_type=jnp.float32)
            + jnp.dot(key_all, w_key.T, preferred_element_type=jnp.float32)
            + jnp.dot(value_all, w_value.T, preferred_element_type=jnp.float32)
        )
        grad_scaled_one = grad_normed_one * gain_part
        inner_sum = width_total(jnp.sum(grad_scaled_one * unit_one, axis=1))
        norm_acc = norm_acc + jnp.sum(grad_normed_one * unit_one, axis=0)
        input_grads.append(
            grad_mixed
            + scale_one * (grad_scaled_one - unit_one * (inner_sum / model_width)[:, None])
        )
        attn_local = add_all(attn_local, (micro_query, micro_key, micro_value, micro_out))
    attn_summed = attn_total(attn_local)
    expert_summed = expert_total(expert_local)
    gain_full = lax.dynamic_update_slice_in_dim(
        jnp.zeros((model_width,), jnp.float32), norm_acc, col_at * width_part, 0
    )
    router_grad, gain_grad, mix_grad = lax.psum(
        (router_acc, gain_full, mix_acc), ("dp", "row", "col")
    )
    return (
        jnp.stack(layer_rows),
        jnp.stack(input_grads),
        gain_grad,
        attn_summed[0],
        attn_summed[1],
        attn_summed[2],
        attn_summed[3],
        mix_grad,
        router_grad,
        expert_summed[0],
        expert_summed[1],
        expert_summed[2],
    )


MESH = pl.DeviceIdType.MESH
ANYWHERE = pl.BlockSpec(memory_space=pl.ANY)


def group_size_of(axes):
    total = 1
    for axis in axes:
        total = total * lax.axis_size(axis)
    return total


def place_in(axes):
    at = 0
    for axis in axes:
        at = at * lax.axis_size(axis) + lax.axis_index(axis)
    return at


def device_at(axes, index):
    place = {}
    for axis in reversed(axes):
        place[axis] = index % lax.axis_size(axis)
        index = index // lax.axis_size(axis)
    return place


def meet(peers):
    barrier = pltpu.get_barrier_semaphore()
    for peer in peers:
        pl.semaphore_signal(barrier, inc=1, device_id=peer, device_id_type=MESH)
    pl.semaphore_wait(barrier, len(peers))


def send(src, dst, send_sem, recv_sem, peer):
    copy = pltpu.make_async_remote_copy(
        src_ref=src,
        dst_ref=dst,
        send_sem=send_sem,
        recv_sem=recv_sem,
        device_id=peer,
        device_id_type=MESH,
    )
    copy.start()
    return copy


def row_peers():
    row = lax.axis_index("row")
    rows = lax.axis_size("row")
    across = (row + rows // 2) % rows
    beside = row + 1 - 2 * (row % 2)
    return row, across, beside


def col_peers():
    col, cols = lax.axis_index("col"), lax.axis_size("col")
    two_on = (col + 2) % cols
    near = col + 1 - 2 * (col % 2)
    return two_on, near, (col, two_on, near, (near + 2) % cols)


def gather_line(source, target, sems, copies):
    local_sem, send_sem, col_sem, dp_sem, across_sem, beside_sem = sems
    row, across, beside = row_peers()
    rows, cols = lax.axis_size("row"), lax.axis_size("col")
    dp = lax.axis_index("dp")
    other = 1 - dp
    two_on, near, order = col_peers()
    far = (beside + rows // 2) % rows
    sent = []

    def block_of(dp_from, row_from, step):
        return (dp_from * rows + row_from) * cols + order[step]

    def arrival(block, sem):
        pltpu.make_async_copy(target.at[block], target.at[block], sem).wait()

    def pass_on(part, block, sem, peer):
        copy = send(part, target.at[block], send_sem.at[len(sent)], sem, peer)
        sent.append(copy)
        copies.append(copy)

    me = block_of(dp, row, 0)
    own = pltpu.make_async_copy(source.at[0], target.at[me], local_sem)

    def begin():
        own.start()
        pass_on(source.at[0], me, col_sem.at[1], {"col": two_on})
        pass_on(source.at[0], me, col_sem.at[2], {"col": near})

    def line(step):
        block = block_of(dp, row, step)
        part = source.at[0] if step == 0 else target.at[block]
        if step > 0:
            arrival(block, col_sem.at[step])
        if step == 1:
            pass_on(part, block, col_sem.at[3], {"col": near})
        pass_on(part, block, dp_sem.at[step], {"dp": other})
        pass_on(part, block, across_sem.at[step], {"row": across})
        pass_on(part, block, beside_sem.at[step], {"row": beside})

    def side(step):
        block = block_of(other, row, step)
        arrival(block, dp_sem.at[step])
        pass_on(target.at[block], block, beside_sem.at[cols + step], {"row": beside})
        block = block_of(dp, across, step)
        arrival(block, across_sem.at[step])
        pass_on(target.at[block], block, dp_sem.at[cols + step], {"dp": other})
        pass_on(target.at[block], block, beside_sem.at[2 * cols + step], {"row": beside})

    def corner(step):
        block = block_of(other, across, step)
        arrival(block, dp_sem.at[cols + step])
        pass_on(target.at[block], block, beside_sem.at[3 * cols + step], {"row": beside})

    def finish():
        for turn, (dp_from, row_from) in enumerate(
            ((dp, beside), (other, beside), (dp, far), (other, far))
        ):
            for step in range(cols):
                arrival(block_of(dp_from, row_from, step), beside_sem.at[turn * cols + step])
        own.wait()

    return begin, line, side, corner, finish


def gather_sems():
    cols = lax.axis_size("col")
    return [
        pltpu.SemaphoreType.DMA,
        pltpu.SemaphoreType.DMA((40,)),
        pltpu.SemaphoreType.DMA((cols,)),
        pltpu.SemaphoreType.DMA((2 * cols,)),
        pltpu.SemaphoreType.DMA((2 * cols,)),
        pltpu.SemaphoreType.DMA((4 * cols,)),
    ]


def nt(left, right):
    return lax.dot_general(
        left, right, (((1,), (1,)), ((), ())), preferred_element_type=jnp.float32
    )


def tn(left, right):
    return lax.dot_general(
        left, right, (((0,), (0,)), ((), ())), preferred_element_type=jnp.float32
    )


def norm_rows(x, gain):
    scale = lax.rsqrt(jnp.mean(x * x, axis=1, keepdims=True) + eps_norm)
    return scale, (x * scale * gain).astype(jnp.bfloat16)


def turn(values, cos_table, sin_table):
    lane = lax.broadcasted_iota(jnp.int32, values.shape, 1)
    ahead = pltpu.roll(values, values.shape[1] - HEAD_DIM // 2, 1)
    behind = pltpu.roll(values, HEAD_DIM // 2, 1)
    return values * cos_table + jnp.where(lane % HEAD_DIM < HEAD_DIM // 2, ahead, behind) * sin_table


def key_extent(block, rows, total):
    return min(total, -(-(block + 1) * rows // 128) * 128)


def visible(doc_col, doc_row, block, rows, extent):
    query = block * rows + lax.broadcasted_iota(jnp.int32, (rows, extent), 0)
    keys = lax.broadcasted_iota(jnp.int32, (rows, extent), 1)
    same = doc_col[block * rows : (block + 1) * rows, 0:1] == doc_row[0:1, 0:extent]
    return same & (keys <= query)


def attend(query, key, allowed):
    scores = jnp.where(allowed, nt(query, key) * attn_scale, -1e30)
    raised = jnp.exp(scores - jnp.max(scores, axis=1, keepdims=True))
    return raised / jnp.sum(raised, axis=1, keepdims=True)


def front_kernel(
    x,
    w_qkv,
    w_out,
    picks,
    cot,
    w_gate,
    w_up,
    w_down,
    gain_one,
    gain_two,
    cos_table,
    sin_table,
    doc_col,
    doc_row,
    router_t,
    table,
    x_all,
    w_mine,
    w_out_mine,
    cot_all,
    normed_all,
    qkv,
    attended,
    mixed,
    gates_own,
    rows_part,
    mix_part,
    scores,
    grads_gu,
    grads_down,
    w_out_all,
    picks_all,
    x_own,
    att_own,
    normed_two,
    gate_up,
    down,
    down_grad,
    pool_rows,
    pool_cots,
    kept_in,
    kept_dy,
    kept_dye,
    kept_act,
    kept_gate,
    kept_up,
    gate_proj,
    up_proj,
    kept_weight,
    ranks,
    upper,
    load_sem,
    store_sem,
    grad_local,
    grad_send,
    grad_recv,
    local_sem,
    send_sem,
    x_sem,
    q_sem,
    o_sem,
    own_sem,
    att_send,
    att_recv,
    ship_local,
    ship_send,
    ship_recv,
    *line_sems,
):
    row, across, beside = row_peers()
    rows, cols = lax.axis_size("row"), lax.axis_size("col")
    col, dp = lax.axis_index("col"), lax.axis_index("dp")
    other = 1 - dp
    far = (beside + rows // 2) % rows
    plane = ("row", "col")
    size, me = group_size_of(plane), place_in(plane)
    low = jnp.bfloat16
    meet(
        [device_at(plane, (me + step) % size) for step in range(1, size)] + [{"dp": other}]
    )
    copies, locals_, sent, moved = [], [], [], []
    picks_line = gather_line(picks, picks_all, line_sems[0:6], copies)
    cot_line = gather_line(cot, cot_all, line_sems[6:12], copies)
    norm_line = gather_line(normed_two, normed_all, line_sems[12:18], copies)

    def pass_on(src, dst, sem, peer):
        sent.append(send(src, dst, send_sem.at[len(sent)], sem, peer))

    def arrival(ref, sem):
        pltpu.make_async_copy(ref, ref, sem).wait()

    def local(src, dst):
        copy = pltpu.make_async_copy(src, dst, local_sem.at[len(locals_)])
        copy.start()
        locals_.append(copy)

    slice_rows, ff_width = w_gate.shape[1:]
    down_rows = w_down.shape[1]
    chunks = w_down.shape[2] // ff_width

    def weight_parts(to, at):
        parts = [
            (w_gate.at[to], gate_up.at[at, 0:slice_rows]),
            (w_up.at[to], gate_up.at[at, slice_rows : 2 * slice_rows]),
        ]
        for chunk in range(chunks):
            parts.append(
                (
                    w_down.at[to, :, chunk * ff_width : (chunk + 1) * ff_width],
                    down.at[at, chunk * down_rows : (chunk + 1) * down_rows],
                )
            )
        return parts

    def ship(first, last, which=range(2)):
        for step in range(first, last):
            to = (me + step) % size
            for part in which:
                source, target = weight_parts(to, me)[part]
                moved.append(
                    send(
                        source,
                        target,
                        ship_send.at[part, step],
                        ship_recv.at[part, step],
                        device_at(plane, to),
                    )
                )

    def shipped(which):
        for step in range(1, size):
            for part in which:
                arrival(
                    weight_parts(me, (me + size - step) % size)[part][1], ship_recv.at[part, step]
                )

    def origin(step):
        return (col + cols - step) % cols

    two_on, near, order = col_peers()

    micro, depth, width = x.shape
    quarter = depth // cols
    half_depth = w_out.shape[1]

    def lanes_of(at):
        return pl.ds(pl.multiple_of(at * width, width), width)

    def lanes(step):
        return lanes_of(order[step])

    def x_at(row_from, step):
        return x_all.at[pl.ds(pl.multiple_of(row_from * depth, depth), depth), lanes(step)]

    def out_at(row_from, step, half):
        first = pl.multiple_of((row_from * 2 + half) * half_depth, half_depth)
        return w_out_all.at[pl.ds(first, half_depth), lanes(step)]

    def own_at(m, step):
        return x_own.at[pl.ds(m * quarter, quarter), lanes_of(origin(step))]

    my_x = x_at(row, 0)
    for step in range(1, cols):
        to = (col + step) % cols
        if step < 3:
            peer = (two_on, near)[step - 1]
            pass_on(x.at[peer // 2], my_x, x_sem.at[step], {"col": peer})
        pass_on(w_qkv.at[to % 2, dp], w_mine.at[col, dp], q_sem.at[step], {"col": to})
    local(x.at[col // 2], my_x)
    local(w_qkv.at[col % 2], w_mine.at[col])
    for half in range(2):
        local(w_out.at[half], out_at(row, 0, half))
    pass_on(x.at[col // 2], my_x, x_sem.at[cols], {"row": across})
    pass_on(x.at[col // 2], my_x, x_sem.at[2 * cols], {"row": beside})
    for step in range(1, cols):
        to = (col + step) % cols
        if step < 3:
            peer = (two_on, near)[step - 1]
            pass_on(w_out.at[dp], out_at(row, 0, dp), o_sem.at[step], {"col": peer})
        first = pl.multiple_of(to * quarter, quarter)
        for m in range(micro):
            pass_on(
                x.at[m, pl.ds(first, quarter)],
                own_at(m, 0),
                own_sem.at[m * cols + step],
                {"col": to},
            )
    for m in range(micro):
        local(x.at[m, pl.ds(pl.multiple_of(col * quarter, quarter), quarter)], own_at(m, 0))
    for half in range(2):
        pass_on(w_out.at[half], out_at(row, 0, half), o_sem.at[(2 + half) * cols], {"row": across})
        pass_on(w_out.at[half], out_at(row, 0, half), o_sem.at[(4 + half) * cols], {"row": beside})
    for step in range(1, cols):
        part = x_at(row, step)
        arrival(part, x_sem.at[step])
        if step == 1:
            pass_on(part, part, x_sem.at[3], {"col": near})
        pass_on(part, part, x_sem.at[cols + step], {"row": across})
        pass_on(part, part, x_sem.at[2 * cols + step], {"row": beside})
        part = w_mine.at[origin(step), dp]
        arrival(part, q_sem.at[step])
        pass_on(part, part, q_sem.at[cols + step], {"dp": other})
    for step in range(cols):
        part = x_at(across, step)
        arrival(part, x_sem.at[cols + step])
        pass_on(part, part, x_sem.at[3 * cols + step], {"row": beside})
    for step in range(1, cols):
        part = out_at(row, step, dp)
        arrival(part, o_sem.at[step])
        if step == 1:
            pass_on(part, part, o_sem.at[3], {"col": near})
        pass_on(part, part, o_sem.at[cols + step], {"dp": other})
        pass_on(part, part, o_sem.at[2 * cols + step], {"row": across})
        pass_on(part, part, o_sem.at[4 * cols + step], {"row": beside})
    picks_line[0]()
    cot_line[0]()
    for source, target in weight_parts(me, me):
        local(source, target)
    for step in range(1, cols):
        arrival(w_mine.at[origin(step), other], q_sem.at[cols + step])
    for at, row_from in enumerate((beside, far)):
        for step in range(cols):
            arrival(x_at(row_from, step), x_sem.at[(2 + at) * cols + step])
    for copy in locals_[:6]:
        copy.wait()

    tokens, model_width = x_all.shape
    projection = w_mine[...].reshape(model_width, w_mine.shape[3])
    for block in range(rows):
        part = slice(block * depth, (block + 1) * depth)
        _, normed = norm_rows(x_all[part, :].astype(jnp.float32), gain_one[...])
        values = project(normed, projection)
        cosine, sine = cos_table[part, :], sin_table[part, :]
        for at in range(2):
            piece = slice(at * 128, (at + 1) * 128)
            qkv[part, piece] = turn(values[:, piece], cosine, sine).astype(low)
        qkv[part, 256:] = values[:, 256:].astype(low)
    heads = attended.shape[2] // HEAD_DIM
    kv_at = heads * HEAD_DIM
    for block in range(rows):
        extent = key_extent(block, depth, tokens)
        allowed = visible(doc_col, doc_row, block, depth, extent)
        key = qkv[0:extent, kv_at : kv_at + HEAD_DIM]
        value = qkv[0:extent, kv_at + HEAD_DIM : kv_at + 2 * HEAD_DIM]
        outs = []
        for head in range(heads):
            query = qkv[
                block * depth : (block + 1) * depth, head * HEAD_DIM : (head + 1) * HEAD_DIM
            ]
            outs.append(project(attend(query, key, allowed).astype(low), value))
        out = jnp.concatenate(outs, axis=1).astype(low)
        attended[block * cols : (block + 1) * cols] = out.reshape(cols, quarter, out.shape[1])
    for step in range(1, size):
        to = (me + step) % size
        moved.append(
            send(
                attended.at[to],
                att_own.at[me],
                att_send.at[step],
                att_recv.at[step],
                device_at(plane, to),
            )
        )
    stay = pltpu.make_async_copy(attended.at[me], att_own.at[me], att_send.at[0])
    stay.start()
    ship(1, 5)
    for step in range(cols):
        picks_line[1](step)
        cot_line[1](step)
    for step in range(1, cols):
        part = out_at(row, step, other)
        arrival(part, o_sem.at[cols + step])
        pass_on(part, part, o_sem.at[3 * cols + step], {"row": across})
        pass_on(part, part, o_sem.at[5 * cols + step], {"row": beside})
    for at in range(2):
        for step in range(cols):
            half = at if step == 0 else (dp if at == 0 else other)
            part = out_at(across, step, half)
            arrival(part, o_sem.at[(2 + at) * cols + step])
            pass_on(part, part, o_sem.at[(6 + at) * cols + step], {"row": beside})
    for at, row_from in enumerate((beside, far)):
        for step in range(cols):
            for part in range(2):
                half = part if step == 0 else (dp if part == 0 else other)
                arrival(out_at(row_from, step, half), o_sem.at[(4 + 2 * at + part) * cols + step])
    for step in range(1, cols):
        for m in range(micro):
            arrival(own_at(m, step), own_sem.at[m * cols + step])
    stay.wait()
    for step in range(1, size):
        arrival(att_own.at[(me + size - step) % size], att_recv.at[step])
    pairs = cols // micro
    for m in range(micro):
        total = jnp.zeros((quarter, model_width), jnp.float32)
        for row_from in range(rows):
            for pair in range(pairs):
                first = (row_from * pairs + pair) * kv_at
                total = total + project(
                    att_own[row_from * cols + m * pairs + pair],
                    w_out_all[first : first + kv_at, :],
                )
        part = slice(m * quarter, (m + 1) * quarter)
        value = x_own[part, :].astype(jnp.float32) + resid_scale * total
        mixed[part, :] = value
        normed_two[0, part, :] = norm_rows(value, gain_two[...])[1]

    begin, line, side, corner, finish = norm_line
    begin()
    for step in range(cols):
        picks_line[2](step)
        cot_line[2](step)
        ship(5 + 2 * step, 7 + 2 * step)
    for step in range(cols):
        line(step)
    ship(5 + 2 * cols, size)
    ship(1, size, range(2, 2 + chunks))
    logits = jnp.where(table[...] > 0, nt(normed_two[0], router_t[...]), -jnp.inf)
    raised = jnp.exp(logits - jnp.max(logits, axis=1, keepdims=True))
    gates_own[...] = raised / jnp.sum(raised, axis=1, keepdims=True)
    w_out_mine[...] = w_out_all[
        pl.ds(pl.multiple_of((row * 2 + col % 2) * kv_at, kv_at), kv_at), :
    ]
    for step in range(cols):
        picks_line[3](step)
        cot_line[3](step)
        side(step)
    for step in range(cols):
        corner(step)
    picks_line[4]()
    cot_line[4]()
    finish()

    everyone = ("dp", "row", "col")
    expert = place_in(everyone)
    tiles, slots = kept_in.shape[0], kept_in.shape[1]
    padded = pool_rows.shape[2]
    block_rows = micro * quarter
    span = cols * padded
    pool_rows[...] = jnp.zeros_like(pool_rows)
    pool_cots[...] = jnp.zeros_like(pool_cots)
    upper[...] = (
        lax.broadcasted_iota(jnp.int32, upper.shape, 0)
        < lax.broadcasted_iota(jnp.int32, upper.shape, 1)
    ).astype(low)

    def pool(tile, slot):
        for at, (source, target) in enumerate(((normed_all, pool_rows), (cot_all, pool_cots))):
            yield pltpu.make_async_copy(
                source.at[pl.ds(tile * cols, cols)],
                target.at[slot, :, 0:block_rows],
                load_sem.at[at, slot],
            )

    for copy in pool(0, 0):
        copy.start()
    slot_of = lax.broadcasted_iota(jnp.int32, (slots, span), 0)

    def picked(tile):
        return slot_of == ranks[tile][0:1, :]

    @pl.loop(0, tiles)
    def _(tile):
        slot = tile % 2
        for copy in pool(tile, slot):
            copy.wait()

        @pl.when(tile + 1 < tiles)
        def _():
            for copy in pool(tile + 1, 1 - slot):
                copy.start()

        rows_here = pool_rows[slot].reshape(span, model_width)
        logits = nt(router_t[...], rows_here)[0 : picks_all.shape[0], :]
        ids = lax.broadcasted_iota(jnp.int32, logits.shape, 0)
        names = jnp.concatenate([picks_all[tile * cols + at] for at in range(cols)], axis=1)
        chosen = ids == names[0:1, :]
        for choice in range(1, names.shape[0]):
            chosen = chosen | (ids == names[choice : choice + 1, :])
        logits = jnp.where(chosen, logits, -1e30)
        raised = jnp.where(chosen, jnp.exp(logits - jnp.max(logits, axis=0, keepdims=True)), 0.0)
        total = jnp.sum(raised, axis=0, keepdims=True)
        mine = ids == expert
        gate = jnp.sum(jnp.where(mine, raised, 0.0), axis=0, keepdims=True) / jnp.where(
            total > 0, total, 1.0
        )
        here = jnp.max(jnp.where(mine & chosen, 1.0, 0.0), axis=0, keepdims=True)
        before = project(jnp.broadcast_to(here, (16, span)).astype(low), upper[...])[0:1, :]
        rank = jnp.where(here > 0, before.astype(jnp.int32), -1)
        ranks[tile] = jnp.broadcast_to(rank, ranks.shape[1:])
        select = slot_of == rank
        kept_weight[tile] = jnp.broadcast_to(
            jnp.sum(jnp.where(select, gate, 0.0), axis=1, keepdims=True), kept_weight.shape[1:]
        )
        select = select.astype(low)
        kept_in[tile] = project(select, rows_here).astype(low)
        kept_dy[tile] = project(select, pool_cots[slot].reshape(span, model_width)).astype(low)

    shipped(range(2))
    for copy in locals_[6:]:
        copy.wait()
    gate_w = gate_up[:, 0:slice_rows, :].reshape(model_width, ff_width)
    up_w = gate_up[:, slice_rows : 2 * slice_rows, :].reshape(model_width, ff_width)

    def down_w(chunk):
        at = chunk * down_rows
        return down[:, at : at + down_rows, :].reshape(ff_width, ff_width)

    def two(ref, pair):
        part = ref[pl.ds(2 * pair, 2)]
        return part.reshape(2 * slots, part.shape[2])

    def put(ref, pair, value):
        ref[pl.ds(2 * pair, 2)] = value.reshape(2, slots, value.shape[1])

    @pl.loop(0, tiles // 2)
    def _(pair):
        rows_in = two(kept_in, pair)
        gate_value = project(rows_in, gate_w)
        up_value = project(rows_in, up_w)
        put(gate_proj, pair, gate_value)
        put(up_proj, pair, up_value)
        put(kept_act, pair, (gate_value / (1.0 + jnp.exp(-gate_value)) * up_value).astype(low))
        weight = two(kept_weight, pair)[:, 0:1]
        grad_mix = resid_scale * two(kept_dy, pair).astype(jnp.float32)
        put(kept_dye, pair, (weight * grad_mix).astype(low))

    def all_of(ref):
        value = ref[...]
        return value.reshape(tiles * slots, value.shape[2])

    act_all = all_of(kept_act)
    for chunk in range(chunks):
        grad = tn(act_all, all_of(kept_dye.at[:, :, chunk * ff_width : (chunk + 1) * ff_width]))
        at = chunk * down_rows
        down_grad[:, at : at + down_rows, :] = grad.astype(low).reshape(size, down_rows, ff_width)
    home = pltpu.make_async_copy(down_grad.at[me], grads_down.at[me], grad_local)
    home.start()
    given = []
    for step in range(1, size):
        to = (me + step) % size
        given.append(
            send(
                down_grad.at[to],
                grads_down.at[me],
                grad_send.at[step],
                grad_recv.at[step],
                device_at(plane, to),
            )
        )
    shipped(range(2, 2 + chunks))

    def spill(tile, slot):
        for at, (source, target) in enumerate(((pool_rows, rows_part), (pool_cots, mix_part))):
            yield pltpu.make_async_copy(
                source.at[slot, :, 0:block_rows],
                target.at[pl.ds(tile * cols, cols)],
                store_sem.at[at, slot],
            )

    @pl.loop(0, tiles // 2)
    def _(pair):
        act = two(kept_act, pair)
        grad_out = two(kept_dye, pair)
        gate_value, up_value = two(gate_proj, pair), two(up_proj, pair)
        weight = two(kept_weight, pair)[:, 0:1]
        score = jnp.zeros((2 * slots, 1), jnp.float32)
        grad_act = jnp.zeros((2 * slots, ff_width), jnp.float32)

        @pl.when(pair > 0)
        def _():
            for at in range(2):
                for copy in spill(2 * pair - 2 + at, at):
                    copy.wait()

        selects = [picked(2 * pair + at).astype(low) for at in range(2)]
        for chunk in range(chunks):
            lanes = slice(chunk * ff_width, (chunk + 1) * ff_width)
            part = down_w(chunk)
            out = project(act, part).astype(low).astype(jnp.float32)
            grad_mix = resid_scale * kept_dy[pl.ds(2 * pair, 2), :, lanes].reshape(
                2 * slots, ff_width
            ).astype(jnp.float32)
            score = score + jnp.sum(grad_mix * out, axis=1, keepdims=True)
            mixed_rows = (weight * out).astype(low)
            for at in range(2):
                pool_cots[at, :, :, lanes] = (
                    tn(selects[at], mixed_rows[at * slots : (at + 1) * slots])
                    .astype(low)
                    .reshape(cols, padded, ff_width)
                )
            grad_act = grad_act + nt(grad_out[:, lanes], part)
        sigmoid = 1.0 / (1.0 + jnp.exp(-gate_value))
        grad_gate = (
            grad_act * up_value * (sigmoid + gate_value * sigmoid * (1.0 - sigmoid))
        ).astype(low)
        grad_up = (grad_act * (gate_value * sigmoid)).astype(low)
        put(kept_gate, pair, grad_gate)
        put(kept_up, pair, grad_up)
        grad_in = (nt(grad_gate, gate_w) + nt(grad_up, up_w)).astype(low)
        for at in range(2):
            tile = 2 * pair + at
            part = slice(at * slots, (at + 1) * slots)
            pool_rows[at] = (
                tn(selects[at], grad_in[part]).astype(low).reshape(cols, padded, model_width)
            )
            line_of = jnp.sum(jnp.where(picked(tile), score[part], 0.0), axis=0, keepdims=True)
            for block in range(cols):
                scores[tile * cols + block] = jnp.broadcast_to(
                    line_of[:, block * padded : (block + 1) * padded], scores.shape[1:]
                )
            for copy in spill(tile, at):
                copy.start()

    rows_all = all_of(kept_in)
    for at, kept in ((0, kept_gate), (slice_rows, kept_up)):
        grad = tn(rows_all, all_of(kept)).astype(low)
        grads_gu[:, at : at + slice_rows, :] = grad.reshape(size, slice_rows, ff_width)
    for at in range(2):
        for copy in spill(tiles - 2 + at, at):
            copy.wait()
    home.wait()
    for copy in given:
        copy.wait()
    for copy in moved + copies + sent:
        copy.wait_send()


def front(number, x, w_qkv, w_out, picks, cot, experts, gains, tables, docs, routing, heads_width):
    cols, rows = lax.axis_size("col"), lax.axis_size("row")
    total, plane = group_size_of(("dp", "row", "col")), group_size_of(("row", "col"))
    micro, depth, part_width = x.shape
    width, tokens, low = part_width * cols, depth * rows, jnp.bfloat16
    wide = jnp.float32
    quarter = depth // cols
    _, slice_rows, ff_width = experts[0].shape
    down_depth = slice_rows * plane // ff_width * experts[2].shape[1]
    tiles = total // cols
    slots = cols * micro * (quarter * 3 // 8)
    vmem = pl.BlockSpec(memory_space=pltpu.VMEM)
    shape, dma = jax.ShapeDtypeStruct, pltpu.SemaphoreType.DMA
    pool = pltpu.VMEM((2, cols, 128, width), low)
    return pl.pallas_call(
        front_kernel,
        out_shape=[
            shape((tokens, width), low),
            shape((cols,) + w_qkv.shape[1:], low),
            shape((heads_width, width), low),
            shape((total,) + cot.shape, low),
            shape((total,) + cot.shape, low),
            shape((tokens, w_qkv.shape[3]), low),
            shape((plane, quarter, heads_width), low),
            shape((micro * quarter, width), wide),
            shape((micro * quarter, 128), wide),
            shape((total,) + cot.shape, low),
            shape((total,) + cot.shape, low),
            shape((total, 8, 128), wide),
            shape((plane, 2 * slice_rows, ff_width), low),
            shape((plane, down_depth, ff_width), low),
        ],
        in_specs=[ANYWHERE] * 8 + [vmem] * 8,
        out_specs=[vmem] * 3
        + [ANYWHERE] * 2
        + [vmem] * 4
        + [ANYWHERE] * 2
        + [vmem] * 2
        + [ANYWHERE],
        scratch_shapes=[
            pltpu.VMEM((rows * 2 * w_out.shape[1], width), low),
            pltpu.VMEM((total,) + picks.shape, picks.dtype),
            pltpu.VMEM((micro * quarter, width), low),
            pltpu.VMEM((plane, quarter, heads_width), low),
            pltpu.VMEM((1, micro * quarter, width), low),
            pltpu.VMEM((plane, 2 * slice_rows, ff_width), low),
            pltpu.VMEM((plane, down_depth, ff_width), low),
            pltpu.VMEM((plane, down_depth, ff_width), low),
            pool,
            pool,
            pltpu.VMEM((tiles, slots, width), low),
            pltpu.VMEM((tiles, slots, width), low),
            pltpu.VMEM((tiles, slots, width), low),
            pltpu.VMEM((tiles, slots, ff_width), low),
            pltpu.VMEM((tiles, slots, ff_width), low),
            pltpu.VMEM((tiles, slots, ff_width), low),
            pltpu.VMEM((tiles, slots, ff_width), wide),
            pltpu.VMEM((tiles, slots, ff_width), wide),
            pltpu.VMEM((tiles, slots, 128), wide),
            pltpu.VMEM((tiles, 8, cols * 128), jnp.int32),
            pltpu.VMEM((cols * 128, cols * 128), low),
            dma((2, 2)),
            dma((2, 2)),
            dma,
            dma((plane,)),
            dma((plane,)),
            dma((12,)),
            dma((72,)),
            dma((4 * cols,)),
            dma((2 * cols,)),
            dma((8 * cols,)),
            dma((micro * cols,)),
            dma((plane,)),
            dma((plane,)),
            dma,
            dma((8, plane)),
            dma((8, plane)),
        ]
        + gather_sems() * 3,
        compiler_params=pltpu.CompilerParams(
            collective_id=number, has_side_effects=True, vmem_limit_bytes=63 * 2**20
        ),
        name="front" + str(number),
    )(x, w_qkv, w_out, picks[None], cot[None], *experts, *gains, *tables, *docs, *routing)


def sum_scratch(block):
    cols = lax.axis_size("col")
    low = jnp.bfloat16
    return [
        pltpu.VMEM((4 * cols,) + block, low),
        pltpu.VMEM((4 * cols,) + block, low),
        pltpu.VMEM((4 * cols,) + block, low),
        pltpu.VMEM((3 * cols,) + block, low),
        pltpu.VMEM((cols,) + block, low),
        pltpu.SemaphoreType.DMA((4 * cols,)),
        pltpu.SemaphoreType.DMA((48,)),
        pltpu.SemaphoreType.DMA((4 * cols,)),
        pltpu.SemaphoreType.DMA((cols,)),
        pltpu.SemaphoreType.DMA((2 * cols,)),
        pltpu.SemaphoreType.DMA((cols,)),
    ]


def sum_steps(partial, sems, copies):
    (
        near,
        mine,
        passed,
        stage,
        last,
        local_sem,
        send_sem,
        beside_sem,
        first_sem,
        second_sem,
        col_sem,
    ) = sems
    row, across, beside = row_peers()
    rows, cols = lax.axis_size("row"), lax.axis_size("col")
    col, dp = lax.axis_index("col"), lax.axis_index("dp")
    other = 1 - dp
    low = jnp.bfloat16
    two_on, beside_col, _ = col_peers()
    sent = []

    def pass_on(src, dst, sem, peer):
        copy = send(src, dst, send_sem.at[len(sent)], sem, peer)
        sent.append(copy)
        copies.append(copy)

    def arrival(ref, sem):
        pltpu.make_async_copy(ref, ref, sem).wait()

    def block_of(dp_to, row_to, col_to):
        return (dp_to * rows + row_to) * cols + col_to

    far = (beside + rows // 2) % rows
    theirs = ((other, far), (other, beside), (dp, far), (dp, beside))
    ours = ((other, across), (other, row), (dp, across), (dp, row))

    def start():
        for turn in range(4):
            for z in range(cols):
                at = turn * cols + z
                pass_on(
                    partial.at[block_of(*theirs[turn], z)],
                    near.at[at],
                    beside_sem.at[at],
                    {"row": beside},
                )
                pltpu.make_async_copy(
                    partial.at[block_of(*ours[turn], z)], mine.at[at], local_sem.at[at]
                ).start()

    def chip_sum(at):
        arrival(mine.at[at], local_sem.at[at])
        arrival(near.at[at], beside_sem.at[at])
        return mine[at].astype(jnp.float32) + near[at].astype(jnp.float32)

    def diagonal():
        for z in range(cols):
            passed[z] = chip_sum(z).astype(low)
            peer = {"dp": other} if z < 2 else {"row": across}
            pass_on(passed.at[z], stage.at[z], first_sem.at[z], peer)

    def middle():
        for z in range(cols):
            for turn, here, peer in ((1, z >= 2, {"dp": other}), (2, z < 2, {"row": across})):
                at = turn * cols + z
                value = chip_sum(at)
                if here:
                    arrival(stage.at[z], first_sem.at[z])
                    value = value + stage[z].astype(jnp.float32)
                passed[at] = value.astype(low)
                pass_on(passed.at[at], stage.at[at], second_sem.at[at - cols], peer)

    def chip_total(z):
        value = chip_sum(3 * cols + z)
        for turn in (1, 2):
            arrival(stage.at[turn * cols + z], second_sem.at[(turn - 1) * cols + z])
            value = value + stage[turn * cols + z].astype(jnp.float32)
        return value

    def spread():
        for at, z in enumerate((beside_col, (beside_col + 2) % cols)):
            passed[3 * cols + at] = chip_total(z).astype(low)
            pass_on(passed.at[3 * cols + at], last.at[at], col_sem.at[at], {"col": beside_col})
        value = chip_total(two_on)
        arrival(last.at[1], col_sem.at[1])
        passed[3 * cols + 2] = (value + last[1].astype(jnp.float32)).astype(low)
        pass_on(passed.at[3 * cols + 2], last.at[2], col_sem.at[2], {"col": two_on})

    def total():
        value = chip_total(col)
        for at, sem in ((0, 0), (2, 2)):
            arrival(last.at[at], col_sem.at[sem])
            value = value + last[at].astype(jnp.float32)
        return value

    return start, diagonal, middle, spread, total


def back_kernel(
    partial,
    mix_part,
    grads,
    scores,
    normed_all,
    mixed,
    cot,
    gates,
    router_t,
    gain_one,
    gain_two,
    x_all,
    w_mine,
    w_out_mine,
    qkv,
    attended,
    cos_table,
    sin_table,
    doc_col,
    doc_row,
    mix_out,
    grads_own,
    dw_pair,
    do_pair,
    router_pair,
    x_grads,
    lines_all,
    scores_in,
    branch,
    branch_all,
    logits,
    logits_all,
    plane_rows,
    rotated,
    values_grad,
    grad_att,
    grad_qkv,
    normed,
    heads,
    heads_near,
    heads_across,
    heads_pair,
    heads_passed,
    dw_send,
    dw_in,
    do_send,
    do_in,
    x_send,
    lines,
    score_local,
    score_send,
    score_recv,
    ship_local,
    ship_send,
    ship_recv,
    plane_sem,
    gather_send,
    branch_col,
    branch_across,
    branch_beside,
    logits_col,
    logits_across,
    logits_beside,
    heads_send,
    near_sem,
    across_sem,
    pair_sem,
    part_local,
    part_send,
    dw_sem,
    do_sem,
    x_sem,
    swap_sem,
    *groups,
):
    row, across, beside = row_peers()
    rows, cols = lax.axis_size("row"), lax.axis_size("col")
    col, dp = lax.axis_index("col"), lax.axis_index("dp")
    other = 1 - dp
    far = (beside + rows // 2) % rows
    half = col % 2
    pair = col + 1 - 2 * half
    everyone, plane = ("dp", "row", "col"), ("row", "col")
    size, me = group_size_of(everyone), place_in(everyone)
    plane_size, plane_me = group_size_of(plane), place_in(plane)
    low, wide = jnp.bfloat16, jnp.float32
    copies, moved, parts, small, locals_ = [], [], [], [], []
    meet([device_at(everyone, (me + step) % size) for step in range(1, size)])

    def arrival(ref, sem):
        pltpu.make_async_copy(ref, ref, sem).wait()

    def ship(first, last):
        for step in range(first, last):
            to = (plane_me + step) % plane_size
            moved.append(
                send(
                    grads.at[to],
                    grads_own.at[plane_me],
                    ship_send.at[step],
                    ship_recv.at[step],
                    device_at(plane, to),
                )
            )

    def keep(src, dst):
        copy = pltpu.make_async_copy(src, dst, part_local.at[len(locals_)])
        copy.start()
        locals_.append(copy)

    rows_sum = sum_steps(partial, groups[0:11], copies)
    mix_sum = sum_steps(
        mix_part, groups[0:3] + groups[11:12] + groups[4:5] + groups[12:18], copies
    )
    lines_line = gather_line(lines, lines_all, groups[18:24], copies)

    score_own = pltpu.make_async_copy(scores.at[me], scores_in.at[me], score_local)
    score_own.start()
    for step in range(1, size):
        to = (me + step) % size
        small.append(
            send(
                scores.at[to],
                scores_in.at[me],
                score_send.at[step],
                score_recv.at[step],
                device_at(everyone, to),
            )
        )
    rows_sum[0]()
    keep(grads.at[plane_me], grads_own.at[plane_me])
    ship(1, 5)
    tokens, model_width = x_all.shape
    depth = tokens // rows
    for block in range(rows):
        part = slice(block * depth, (block + 1) * depth)
        normed[part, :] = norm_rows(x_all[part, :].astype(wide), gain_one[...])[1]
    rows_sum[1]()
    rows_sum[2]()
    rows_sum[3]()
    score_own.wait()
    for copy in small:
        copy.wait()
    gate = gates[...]
    scored = jnp.concatenate(
        [scores_in[:, 0, :], jnp.zeros((128 - size, 128), wide)], axis=0
    ).T[: gate.shape[0], :]
    grad_logits = gate * (scored - jnp.sum(gate * scored, axis=1, keepdims=True))
    routed = jnp.dot(
        grad_logits, router_t[...].astype(wide), precision=highest, preferred_element_type=wide
    )
    logits[0] = jnp.concatenate(
        [grad_logits, jnp.zeros((128 - gate.shape[0], 128), wide)], axis=0
    ).T[: logits.shape[1], :]
    value = mixed[...]
    scale_two = lax.rsqrt(jnp.mean(value * value, axis=1, keepdims=True) + eps_norm)
    unit_two = value * scale_two
    grad_normed = rows_sum[4]() + routed
    mix_row = jnp.sum(grad_normed * unit_two, axis=0, keepdims=True)
    grad_scaled = grad_normed * gain_two[...]
    grad_mixed = cot[...].astype(wide) + scale_two * (
        grad_scaled - unit_two * jnp.mean(grad_scaled * unit_two, axis=1, keepdims=True)
    )
    quarter = branch.shape[1]
    for m in range(2):
        branch[m] = (resid_scale * grad_mixed[m * quarter : (m + 1) * quarter, :]).astype(low)

    sent = []

    def pass_on(src, dst, sem, peer):
        sent.append(send(src, dst, gather_send.at[len(sent)], sem, peer))

    def origin(step):
        return (col + cols - step) % cols

    two_on, near, order = col_peers()
    for step, to in ((1, two_on), (2, near)):
        pass_on(branch.at[to // 2], branch_all.at[plane_me], branch_col.at[step], {"col": to})
        pass_on(logits.at[0], logits_all.at[plane_me], logits_col.at[step], {"col": to})
    keep(branch.at[col // 2], branch_all.at[plane_me])
    keep(logits.at[0], logits_all.at[plane_me])
    plans = (
        (branch.at[col // 2], branch_all, branch_col, branch_across, branch_beside),
        (logits.at[0], logits_all, logits_col, logits_across, logits_beside),
    )
    for step in range(cols):
        for mine, target, col_sem, side_sem, core_sem in plans:
            part = target.at[row * cols + order[step]]
            if step > 0:
                arrival(part, col_sem.at[step])
            if step == 1:
                pass_on(part, part, col_sem.at[3], {"col": near})
            source = mine if step == 0 else part
            pass_on(source, part, side_sem.at[step], {"row": across})
            pass_on(source, part, core_sem.at[step], {"row": beside})
    ship(5, 11)
    for step in range(cols):
        for mine, target, col_sem, side_sem, core_sem in plans:
            part = target.at[across * cols + order[step]]
            arrival(part, side_sem.at[step])
            pass_on(part, part, core_sem.at[cols + step], {"row": beside})
    for at, row_from in enumerate((beside, far)):
        for step in range(cols):
            for mine, target, col_sem, side_sem, core_sem in plans:
                arrival(target.at[row_from * cols + order[step]], core_sem.at[at * cols + step])
    for copy in locals_:
        copy.wait()
    for copy in copies:
        copy.wait_send()
    done = len(copies)
    mix_sum[0]()

    branch_rows = branch_all[...].reshape(tokens, model_width)
    kv_at = attended.shape[2]
    count = kv_at // HEAD_DIM
    grad_att[...] = nt(branch_rows, w_out_mine[...]).astype(low)
    rotated[:, kv_at : kv_at + HEAD_DIM] = jnp.zeros((tokens, HEAD_DIM), wide)
    values_grad[...] = jnp.zeros_like(values_grad)
    for block in range(rows):
        part = slice(block * depth, (block + 1) * depth)
        extent = key_extent(block, depth, tokens)
        allowed = visible(doc_col, doc_row, block, depth, extent)
        key = qkv[0:extent, kv_at : kv_at + HEAD_DIM]
        value_rows = qkv[0:extent, kv_at + HEAD_DIM : kv_at + 2 * HEAD_DIM]
        key_sum = jnp.zeros((extent, HEAD_DIM), wide)
        value_sum = jnp.zeros((extent, HEAD_DIM), wide)
        for head in range(count):
            lanes = slice(head * HEAD_DIM, (head + 1) * HEAD_DIM)
            query = qkv[part, lanes]
            probs = attend(query, key, allowed)
            grad_out = grad_att[part, lanes]
            grad_probs = nt(grad_out, value_rows)
            grad_scores = probs * (
                grad_probs - jnp.sum(probs * grad_probs, axis=1, keepdims=True)
            )
            grad_raw = (grad_scores * attn_scale).astype(low)
            rotated[part, lanes] = project(grad_raw, key)
            key_sum = key_sum + tn(grad_raw, query)
            value_sum = value_sum + tn(probs.astype(low), grad_out)
        rotated[0:extent, kv_at : kv_at + HEAD_DIM] += key_sum
        values_grad[0:extent, :] += value_sum
        if block == 1:
            mix_sum[1]()
    for at in range(2):
        piece = slice(at * 128, (at + 1) * 128)
        grad_qkv[:, piece] = turn(rotated[:, piece], cos_table[...], -sin_table[...]).astype(low)
    grad_qkv[:, 256:] = values_grad[...].astype(low)

    rows_each = heads.shape[1]
    projection = w_mine[...].reshape(model_width, w_mine.shape[3])
    heads_sent = []

    def heads_on(src, dst, sem, peer):
        heads_sent.append(send(src, dst, heads_send.at[len(heads_sent)], sem, peer))

    halves = (1 - half, half)
    for at, row_to in enumerate((far, beside, across, row)):
        for which, part in enumerate(halves):
            slot = 2 * at + which
            first = pl.multiple_of((row_to * 2 + part) * rows_each, rows_each)
            heads[slot] = nt(grad_qkv[pl.ds(first, rows_each), :], projection).astype(low)
            if at < 2:
                heads_on(heads.at[slot], heads_near.at[slot], near_sem.at[slot], {"row": beside})
    width = model_width // cols
    heads_out = attended[...].reshape(tokens, kv_at)
    for step in range(cols - 1, -1, -1):
        to = (col + step) % cols
        lanes = pl.ds(pl.multiple_of(to * width, width), width)
        dw_send[to] = tn(grad_qkv[...], normed[:, lanes]).astype(low)
        chunk = branch_all[:, :, lanes].reshape(tokens, width)
        do_send[to] = tn(heads_out, chunk).astype(low)
        if step > 0:
            parts.append(
                send(dw_send.at[to], dw_in.at[col], part_send.at[step], dw_sem.at[step], {"col": to})
            )
            parts.append(
                send(
                    do_send.at[to],
                    do_in.at[col],
                    part_send.at[cols + step],
                    do_sem.at[step],
                    {"col": to},
                )
            )
    keep(dw_send.at[col], dw_in.at[col])
    keep(do_send.at[col], do_in.at[col])

    def heads_sum(slot):
        arrival(heads_near.at[slot - 4], near_sem.at[slot - 4])
        return heads[slot].astype(wide) + heads_near[slot - 4].astype(wide)

    for which in range(2):
        heads_passed[which] = heads_sum(4 + which).astype(low)
        heads_on(
            heads_passed.at[which], heads_across.at[which], across_sem.at[which], {"row": across}
        )
    mix_sum[2]()
    ship(11, plane_size)
    router_sum = jnp.zeros((logits.shape[1], model_width), wide)
    group = plane_rows.shape[0]
    for first in range(0, plane_size, group):
        load = pltpu.make_async_copy(
            normed_all.at[pl.ds(dp * plane_size + first, group)], plane_rows, score_local
        )
        load.start()
        load.wait()
        for at in range(group):
            left = logits_all[first + at, :, 0 : 2 * quarter]
            for _ in range(3):
                piece = left.astype(low)
                left = left - piece.astype(wide)
                router_sum = router_sum + project(piece, plane_rows[at])
    router_pair[dp] = router_sum
    swaps = [
        send(router_pair.at[dp], router_pair.at[dp], swap_sem.at[0], swap_sem.at[1], {"dp": other})
    ]
    for which in range(2):
        grad_one = heads_sum(6 + which)
        arrival(heads_across.at[which], across_sem.at[which])
        grad_one = grad_one + heads_across[which].astype(wide)
        if which == 0:
            heads_passed[2] = grad_one.astype(low)
            heads_on(heads_passed.at[2], heads_pair, pair_sem, {"col": pair})
    arrival(heads_pair, pair_sem)
    grad_one = grad_one + heads_pair[...].astype(wide)
    first = (row * 2 + half) * rows_each
    x_rows = x_all[pl.ds(pl.multiple_of(first, rows_each), rows_each), :].astype(wide)
    scale_one = lax.rsqrt(jnp.mean(x_rows * x_rows, axis=1, keepdims=True) + eps_norm)
    unit_one = x_rows * scale_one
    norm_row = jnp.sum(grad_one * unit_one, axis=0, keepdims=True)
    each = rows_each // quarter
    grad_h = branch_all[pl.ds((row * 2 + half) * each, each)].reshape(rows_each, model_width)
    grad_scaled = grad_one * gain_one[...]
    grad_x = grad_h.astype(wide) * (1.0 / resid_scale) + scale_one * (
        grad_scaled - unit_one * jnp.mean(grad_scaled * unit_one, axis=1, keepdims=True)
    )
    for to in range(cols):
        x_send[to] = grad_x[:, to * width : (to + 1) * width].astype(low)
    for step in range(1, cols):
        to = (col + step) % cols
        swaps.append(
            send(
                x_send.at[to], x_grads.at[col], x_sem.at[step], x_sem.at[cols + step], {"col": to}
            )
        )
    keep(x_send.at[col], x_grads.at[col])
    steps = model_width // 128
    for at in range(steps):
        piece = slice(at * 128, (at + 1) * 128)
        lines[0, at : at + 1, :] = norm_row[:, piece]
        lines[0, steps + at : steps + at + 1, :] = mix_row[:, piece]
    lines_line[0]()
    for copy in locals_[3:]:
        copy.wait()
    for step in range(1, cols):
        arrival(dw_in.at[origin(step)], dw_sem.at[step])
        arrival(do_in.at[origin(step)], do_sem.at[step])
    for h in range(2):
        dw_pair[dp, h] = (dw_in[h].astype(wide) + dw_in[2 + h].astype(wide)).astype(low)
        do_pair[dp, h] = (do_in[h].astype(wide) + do_in[2 + h].astype(wide)).astype(low)
    swaps.append(
        send(dw_pair.at[dp], dw_pair.at[dp], swap_sem.at[2], swap_sem.at[3], {"dp": other})
    )
    swaps.append(
        send(do_pair.at[dp], do_pair.at[dp], swap_sem.at[4], swap_sem.at[5], {"dp": other})
    )
    mix_sum[3]()
    for at in range(1, 4):
        for step in range(cols):
            lines_line[at](step)
    mix_out[...] = mix_sum[4]()
    lines_line[4]()
    for copy in swaps:
        copy.wait()
    for copy in moved:
        copy.wait()
    for copy in copies[done:] + parts + sent + heads_sent:
        copy.wait_send()


def back(number, partial, mix_part, grads, scores, normed_all, *rest):
    mixed, _, _, _, _, _, x_all, w_mine, _, qkv, attended = rest[:11]
    cols, rows = lax.axis_size("col"), lax.axis_size("row")
    total, plane = group_size_of(("dp", "row", "col")), group_size_of(("row", "col"))
    low, wide = jnp.bfloat16, jnp.float32
    vmem = pl.BlockSpec(memory_space=pltpu.VMEM)
    shape, dma = jax.ShapeDtypeStruct, pltpu.SemaphoreType.DMA
    tokens, width = x_all.shape
    quarter, heads_width = attended.shape[1:]
    block = partial.shape[1:]
    part = width // cols
    qkv_width = w_mine.shape[3]
    lines = -(-2 * (width // 128) // 8) * 8
    return pl.pallas_call(
        back_kernel,
        out_shape=[
            shape(block, wide),
            shape(grads.shape, low),
            shape((2, 2, qkv_width, part), low),
            shape((2, 2, heads_width, part), low),
            shape((2, total, width), wide),
            shape((cols, tokens // (2 * rows), part), low),
            shape((total, lines, 128), wide),
        ],
        in_specs=[ANYWHERE] * 5 + [vmem] * len(rest),
        out_specs=[vmem, ANYWHERE, vmem, vmem, vmem, vmem, ANYWHERE],
        scratch_shapes=[
            pltpu.VMEM(scores.shape, wide),
            pltpu.VMEM((2, quarter, width), low),
            pltpu.VMEM((plane, quarter, width), low),
            pltpu.VMEM((1, total, 128), wide),
            pltpu.VMEM((plane, total, 128), wide),
            pltpu.VMEM((4,) + block, low),
            pltpu.VMEM((tokens, 256), wide),
            pltpu.VMEM((tokens, HEAD_DIM), wide),
            pltpu.VMEM((tokens, heads_width), low),
            pltpu.VMEM((tokens, qkv_width), low),
            pltpu.VMEM((tokens, width), low),
            pltpu.VMEM((8, tokens // (2 * rows), width), low),
            pltpu.VMEM((4, tokens // (2 * rows), width), low),
            pltpu.VMEM((2, tokens // (2 * rows), width), low),
            pltpu.VMEM((tokens // (2 * rows), width), low),
            pltpu.VMEM((3, tokens // (2 * rows), width), low),
            pltpu.VMEM((cols, qkv_width, part), low),
            pltpu.VMEM((cols, qkv_width, part), low),
            pltpu.VMEM((cols, heads_width, part), low),
            pltpu.VMEM((cols, heads_width, part), low),
            pltpu.VMEM((cols, tokens // (2 * rows), part), low),
            pltpu.VMEM((1, lines, 128), wide),
            dma,
            dma((total,)),
            dma((total,)),
            dma,
            dma((plane,)),
            dma((plane,)),
            dma,
            dma((40,)),
            dma((cols,)),
            dma((cols,)),
            dma((2 * cols,)),
            dma((cols,)),
            dma((cols,)),
            dma((2 * cols,)),
            dma((8,)),
            dma((4,)),
            dma((2,)),
            dma,
            dma((8,)),
            dma((2 * cols,)),
            dma((cols,)),
            dma((cols,)),
            dma((2 * cols,)),
            dma((6,)),
        ]
        + sum_scratch(block)
        + [pltpu.VMEM((3 * cols,) + block, low)]
        + sum_scratch(block)[5:]
        + gather_sems(),
        compiler_params=pltpu.CompilerParams(
            collective_id=number, has_side_effects=True, vmem_limit_bytes=62 * 2**20
        ),
        name="back" + str(number),
    )(partial, mix_part, grads, scores, normed_all, *rest)


def owned(
    hidden_in,
    norm_gain,
    w_query,
    w_key,
    w_value,
    w_out,
    mix_gain,
    w_router,
    w_gate,
    w_up,
    w_down,
    lengths,
    routes,
    mask,
    cotangent,
):
    everyone = ("dp", "row", "col")
    plane = ("row", "col")
    micro_count, tok_row, width_part = hidden_in.shape
    row_count = lax.axis_size("row")
    col_count = lax.axis_size("col")
    dp_count = lax.axis_size("dp")
    row_at = lax.axis_index("row")
    col_at = lax.axis_index("col")
    dp_at = lax.axis_index("dp")
    plane_count = row_count * col_count
    device_count = plane_count * dp_count
    plane_at = row_at * col_count + col_at
    model_width = width_part * col_count
    kv_here = w_key.shape[1] // HEAD_DIM
    group_size = w_query.shape[1] // w_key.shape[1]
    q_width = group_size * HEAD_DIM
    group_tokens = tok_row * row_count
    quarter = tok_row // col_count
    own_rows = micro_count * quarter
    experts_here, slice_width, ff_width = w_gate.shape
    down_slice = w_down.shape[1]
    experts_all = experts_here * dp_count
    expert_at = dp_at * plane_count + plane_at
    micro_at = col_at // kv_here
    half_at = col_at % kv_here

    masked_cot = cotangent * mask[:, :, None].astype(cotangent.dtype)

    w_qkv = jnp.concatenate(
        [
            w_query.reshape(width_part, kv_here, q_width),
            w_key.reshape(width_part, kv_here, HEAD_DIM),
            w_value.reshape(width_part, kv_here, HEAD_DIM),
        ],
        axis=2,
    ).transpose(1, 0, 2)
    qkv_width = q_width + 2 * HEAD_DIM
    picks = jnp.pad(routes.reshape(own_rows, TOP).T, ((0, 0), (0, 128 - own_rows)), constant_values=-1)
    doc_id, position = documents(lengths[:, 0][micro_at], group_tokens)
    sin_table, cos_table = (
        table[:, 0] for table in angles(position.astype(jnp.float32), HEAD_DIM)
    )
    doc_col = jnp.broadcast_to(doc_id[:, None], (group_tokens, 128))
    doc_row = jnp.broadcast_to(doc_id[None, :], (8, group_tokens))
    cos_lanes = jnp.tile(cos_table, (1, 4))
    sin_lanes = jnp.tile(jnp.concatenate([-sin_table, sin_table], axis=1), (1, 2))
    pad_experts = 128 - experts_all
    table = jnp.any(
        routes.reshape(own_rows, TOP)[:, :, None]
        == jnp.arange(experts_all, dtype=jnp.int32)[None, None, :],
        axis=1,
    )
    router_t = jnp.pad(w_router.T, ((0, pad_experts), (0, 0)))
    cot_own = masked_cot.reshape(own_rows, model_width)
    (
        x_micro,
        w_mine,
        w_out_mine,
        cot_all,
        normed_all,
        qkv,
        attended,
        mixed,
        gates_own,
        rows_part,
        mix_part,
        scores,
        grads,
        grads_down,
    ) = front(
        0,
        hidden_in,
        w_qkv.reshape(kv_here, dp_count, width_part // dp_count, qkv_width),
        w_out.reshape(dp_count, w_out.shape[0] // dp_count, w_out.shape[1]),
        picks,
        cot_own,
        (w_gate, w_up, w_down),
        (norm_gain[None], mix_gain[None]),
        (cos_lanes, sin_lanes),
        (doc_col, doc_row),
        (router_t, jnp.pad(table.astype(jnp.float32), ((0, 0), (0, pad_experts)))),
        q_width,
    )
    expert_mix, grads, qkv_sum, out_sum, router_grad, grad_input, lines = back(
        1,
        rows_part,
        mix_part,
        grads,
        scores,
        normed_all,
        mixed,
        cot_own,
        gates_own,
        router_t,
        norm_gain[None],
        mix_gain[None],
        x_micro,
        w_mine,
        w_out_mine,
        qkv,
        attended,
        cos_lanes,
        sin_lanes,
        doc_col,
        doc_row,
    )
    layer_out = (mixed + resid_scale * expert_mix).astype(jnp.bfloat16)
    out_gate = grads[:, :slice_width].astype(jnp.float32)
    out_up = grads[:, slice_width : 2 * slice_width].astype(jnp.float32)
    out_down = jnp.concatenate(
        [
            grads_down[:, at : at + down_slice]
            for at in range(0, grads_down.shape[1], down_slice)
        ],
        axis=2,
    ).astype(jnp.float32)
    grad_input = grad_input.reshape(micro_count, tok_row, width_part).astype(jnp.float32)
    qkv_sum = jnp.sum(qkv_sum.astype(jnp.float32), axis=0)
    out_sum = jnp.sum(out_sum.astype(jnp.float32), axis=0)
    router_grad = jnp.sum(router_grad, axis=0).T
    lines = jnp.sum(lines, axis=0)
    norm_grad = lines[: model_width // 128].reshape(-1)
    mix_grad = lines[model_width // 128 : 2 * (model_width // 128)].reshape(-1)
    grad_wq = qkv_sum[:, :q_width].reshape(-1, width_part).T
    grad_wk = qkv_sum[:, q_width : q_width + HEAD_DIM].reshape(-1, width_part).T
    grad_wv = qkv_sum[:, q_width + HEAD_DIM :].reshape(-1, width_part).T
    grad_wo = out_sum.reshape(w_out.shape)
    return (
        layer_out.reshape(micro_count, quarter, model_width),
        grad_input,
        norm_grad,
        grad_wq,
        grad_wk,
        grad_wv,
        grad_wo,
        mix_grad,
        router_grad,
        out_gate,
        out_up,
        out_down,
    )


def solution(mesh):
    dp_count, row_count, col_count = (mesh.shape[name] for name in ("dp", "row", "col"))

    def body(*args):
        hidden_in, w_key, w_gate = args[0], args[3], args[8]
        kv_here = w_key.shape[1] // HEAD_DIM
        one_each = w_gate.shape[0] == row_count * col_count
        pairs = hidden_in.shape[0] * kv_here == col_count
        sizes = (dp_count, row_count, col_count, kv_here) == (2, 4, 4, 2)
        return (owned if sizes and one_each and pairs else shards)(*args)

    placed = (
        P(None, ("dp", "row"), "col"),
        P(),
        P("col", "row"),
        P("col", "row"),
        P("col", "row"),
        P("row", "col"),
        P(),
        P(),
        P("dp", ("row", "col"), None),
        P("dp", ("row", "col"), None),
        P("dp", ("row", "col"), None),
        P(None, "dp", None),
        P(None, ("dp", "row", "col"), None),
        P(None, ("dp", "row", "col")),
        P(None, ("dp", "row", "col"), None),
    )
    return jax.shard_map(
        body,
        mesh=mesh,
        in_specs=placed,
        out_specs=(
            P(None, ("dp", "row", "col"), None),
            P(None, ("dp", "row"), "col"),
            P(),
            P("col", "row"),
            P("col", "row"),
            P("col", "row"),
            P("row", "col"),
            P(),
            P(),
            P("dp", ("row", "col"), None),
            P("dp", ("row", "col"), None),
            P("dp", ("row", "col"), None),
        ),
        check_vma=False,
    )
```

```python
import functools

import jax
import jax.numpy as jnp
from jax import lax
from jax.experimental import pallas as pl
from jax.experimental.pallas import tpu as pltpu
from jax.sharding import PartitionSpec as P

D = 1536
HEAD_DIM = 64
TOP = 8


eps_norm = 1e-06
resid_scale = 0.22
attn_scale = 0.015625
rope_base = 10000.0
highest = lax.Precision.HIGHEST


def shortened(shard):
    return jax.tree.map(lambda a: a.astype(jnp.bfloat16) if a.dtype == jnp.float32 else a, shard)


def documents(doc_lengths, length_all):
    doc_ends = jnp.cumsum(doc_lengths, dtype=jnp.int32)
    doc_starts = doc_ends - doc_lengths
    positions = jnp.arange(length_all, dtype=jnp.int32)
    doc_id = jnp.sum(
        (positions[:, None] >= doc_ends[None, :]).astype(jnp.int32), axis=1, dtype=jnp.int32
    )
    member = doc_id[:, None] == jnp.arange(doc_lengths.shape[0], dtype=jnp.int32)[None, :]
    doc_start = jnp.sum(jnp.where(member, doc_starts[None, :], 0), axis=1, dtype=jnp.int32)
    return (doc_id, positions - doc_start)


def angles(position, head_width):
    half_width = head_width // 2
    frequency = rope_base ** (-2.0 * jnp.arange(half_width, dtype=jnp.float32) / head_width)
    turned = position[:, None] * frequency[None, :]
    return (jnp.sin(turned)[:, None, :], jnp.cos(turned)[:, None, :])


def rotate(values, sin_table, cos_table):
    half_width = values.shape[-1] // 2
    front_half = values[..., :half_width]
    back_half = values[..., half_width:]
    return jnp.concatenate(
        [
            front_half * cos_table - back_half * sin_table,
            back_half * cos_table + front_half * sin_table,
        ],
        axis=-1,
    )


def gather_rows(value):
    return lax.all_gather(value, "row", axis=0, tiled=True)


def gather_cols(value):
    return jax.tree.map(
        lambda part, own: part.astype(own.dtype),
        lax.all_gather(shortened(value), "col", axis=0, tiled=True),
        value,
    )


def sum_cols(pieces):
    return lax.psum_scatter(pieces, "col", scatter_dimension=0, tiled=True)


def sum_rows(pieces):
    return lax.psum_scatter(pieces, "row", scatter_dimension=0, tiled=True)


def width_total(value):
    return lax.psum(value, "col")


def expert_trade(value):
    return lax.all_to_all(value, "dp", split_axis=1, concat_axis=1, tiled=True)


def attn_total(value):
    return jax.tree.map(lambda part: part.astype(jnp.float32), lax.psum(shortened(value), "dp"))


def expert_total(value):
    return jax.tree.map(
        lambda part: part.astype(jnp.float32),
        lax.psum_scatter(shortened(value), ("row", "col"), scatter_dimension=1, tiled=True),
    )


def add_all(first_set, second_set):
    return tuple((left_one + right_one for left_one, right_one in zip(first_set, second_set)))


def project(left_side, right_side):
    return jnp.dot(left_side, right_side, preferred_element_type=jnp.float32)


def shards(
    hidden_in,
    norm_gain,
    w_query,
    w_key,
    w_value,
    w_out,
    mix_gain,
    w_router,
    w_gate,
    w_up,
    w_down,
    lengths,
    routes,
    mask,
    cotangent,
):
    micro_count = hidden_in.shape[0]
    tok_dev = hidden_in.shape[1]
    width_part = hidden_in.shape[2]
    col_count = lax.axis_size("col")
    row_count = lax.axis_size("row")
    dp_count = lax.axis_size("dp")
    col_at = lax.axis_index("col")
    model_width = D
    heads_here = w_query.shape[1] // HEAD_DIM
    kv_here = w_key.shape[1] // HEAD_DIM
    group_size = heads_here // kv_here
    group_tokens = tok_dev * row_count
    quarter = tok_dev // col_count
    experts_here = w_gate.shape[0]
    experts_all = experts_here * dp_count
    capacity = quarter * 3 // 8
    slot_count = experts_all * capacity
    gain_part = lax.dynamic_slice_in_dim(norm_gain, col_at * width_part, width_part)
    router_wide = w_router.astype(jnp.float32)
    full_gate, full_up, full_down = (
        lax.all_gather(w_gate, ("row", "col"), axis=1, tiled=True),
        lax.all_gather(w_up, ("row", "col"), axis=1, tiled=True),
        lax.all_gather(w_down, ("row", "col"), axis=1, tiled=True),
    )
    expert_ids = jnp.arange(experts_all, dtype=jnp.int32)
    group_index = jnp.arange(group_tokens, dtype=jnp.int32)
    query_start = col_at * tok_dev
    query_index = query_start + jnp.arange(tok_dev, dtype=jnp.int32)
    attn_local = (
        jnp.zeros(w_query.shape, jnp.float32),
        jnp.zeros(w_key.shape, jnp.float32),
        jnp.zeros(w_value.shape, jnp.float32),
        jnp.zeros(w_out.shape, jnp.float32),
    )
    expert_local = (
        jnp.zeros(full_gate.shape, jnp.float32),
        jnp.zeros(full_up.shape, jnp.float32),
        jnp.zeros(full_down.shape, jnp.float32),
    )
    router_acc = jnp.zeros(w_router.shape, jnp.float32)
    norm_acc = jnp.zeros((width_part,), jnp.float32)
    mix_acc = jnp.zeros((model_width,), jnp.float32)
    layer_rows = []
    input_grads = []
    for step in range(micro_count):
        x_full = hidden_in[step].astype(jnp.float32)
        squares = width_total(jnp.sum(x_full * x_full, axis=1))
        scale_one = lax.rsqrt(squares / model_width + eps_norm)[:, None]
        unit_one = x_full * scale_one
        normed = (unit_one * gain_part).astype(jnp.bfloat16)
        normed_all = gather_rows(normed)
        query_p, key_p, value_p = sum_cols(
            (project(normed_all, w_query), project(normed_all, w_key), project(normed_all, w_value))
        )
        doc_all, pos_all = documents(lengths[step, 0], group_tokens)
        doc_query = lax.dynamic_slice_in_dim(doc_all, query_start, tok_dev)
        pos_query = lax.dynamic_slice_in_dim(pos_all, query_start, tok_dev).astype(jnp.float32)
        sin_table, cos_table = angles(pos_query, HEAD_DIM)
        query_rot = rotate(
            query_p.reshape(tok_dev, heads_here, HEAD_DIM), sin_table, cos_table
        ).astype(jnp.bfloat16)
        key_rot = rotate(key_p.reshape(tok_dev, kv_here, HEAD_DIM), sin_table, cos_table).astype(
            jnp.bfloat16
        )
        value_low = value_p.astype(jnp.bfloat16).reshape(tok_dev, kv_here, HEAD_DIM)
        keys_all, values_all = (
            lax.all_gather(key_rot, "col", axis=0, tiled=True),
            lax.all_gather(value_low, "col", axis=0, tiled=True),
        )
        allowed = (doc_query[:, None] == doc_all[None, :]) & (
            group_index[None, :] <= query_index[:, None]
        )
        query_grp = query_rot.reshape(tok_dev, kv_here, group_size, HEAD_DIM)
        raw_scores = jnp.einsum(
            "qhgd,khd->hgqk", query_grp, keys_all, preferred_element_type=jnp.float32
        )
        scores = jnp.where(allowed[None, None], raw_scores * attn_scale, -1e30)
        top_score = jnp.max(scores, axis=-1, keepdims=True)
        expd = jnp.exp(scores - top_score)
        row_total = jnp.sum(expd, axis=-1, keepdims=True)
        attn_probs = expd / row_total
        log_total = top_score + jnp.log(row_total)
        probs_low = attn_probs.astype(jnp.bfloat16)
        attended = jnp.einsum(
            "hgqk,khd->qhgd", probs_low, values_all, preferred_element_type=jnp.float32
        )
        attended_low = attended.reshape(tok_dev, heads_here * HEAD_DIM).astype(jnp.bfloat16)
        attended_all = gather_cols(attended_low)
        attn_branch = sum_rows(project(attended_all, w_out))
        mixed = x_full + resid_scale * attn_branch
        mixed_rows = lax.all_to_all(
            mixed.reshape(col_count, quarter, width_part),
            "col",
            split_axis=0,
            concat_axis=2,
            tiled=True,
        ).reshape(quarter, model_width)
        scale_two = lax.rsqrt(jnp.mean(mixed_rows * mixed_rows, axis=1, keepdims=True) + eps_norm)
        unit_two = mixed_rows * scale_two
        normed_two = (unit_two * mix_gain).astype(jnp.bfloat16)
        logits = project(normed_two, w_router)
        picks = routes[step]
        choose = (picks[:, :, None] == expert_ids[None, None, :]).astype(jnp.float32)
        chosen = jnp.sum(choose * logits[:, None, :], axis=-1)
        gate_weights = jax.nn.softmax(chosen, axis=-1)
        flat_picks = picks.reshape(-1)
        hit_table = (flat_picks[:, None] == expert_ids[None, :]).astype(jnp.int32)
        slot_rank = jnp.sum(
            hit_table * (jnp.cumsum(hit_table, axis=0, dtype=jnp.int32) - 1),
            axis=1,
            dtype=jnp.int32,
        )
        owner_dp = flat_picks // experts_here
        local_expert = flat_picks % experts_here
        slot_index = local_expert * (dp_count * capacity) + owner_dp * capacity + slot_rank
        token_of = (
            jnp.full((slot_count,), quarter, jnp.int32)
            .at[slot_index]
            .set(jnp.arange(quarter * TOP, dtype=jnp.int32) // TOP)
        )
        padded = jnp.concatenate([normed_two, jnp.zeros((1, model_width), jnp.bfloat16)], axis=0)
        send_rows = padded[token_of].reshape(experts_here, dp_count * capacity, model_width)
        expert_in = expert_trade(send_rows)
        gate_proj = jnp.einsum(
            "ecd,edf->ecf", expert_in, full_gate, preferred_element_type=jnp.float32
        )
        up_proj = jnp.einsum("ecd,edf->ecf", expert_in, full_up, preferred_element_type=jnp.float32)
        activated = (jax.nn.silu(gate_proj) * up_proj).astype(jnp.bfloat16)
        expert_out = jnp.einsum(
            "ecf,efd->ecd", activated, full_down, preferred_element_type=jnp.float32
        ).astype(jnp.bfloat16)
        returned = expert_trade(expert_out).reshape(slot_count, model_width)
        combined = returned[slot_index].reshape(quarter, TOP, model_width).astype(jnp.float32)
        expert_mix = jnp.sum(gate_weights[:, :, None] * combined, axis=1)
        layer_rows.append((mixed_rows + resid_scale * expert_mix).astype(jnp.bfloat16))
        grad_rows = cotangent[step].astype(jnp.float32) * mask[step][:, None].astype(jnp.float32)
        grad_mix = resid_scale * grad_rows
        grad_gates = jnp.sum(grad_mix[:, None, :] * combined, axis=-1)
        grad_chosen = gate_weights * (
            grad_gates - jnp.sum(gate_weights * grad_gates, axis=-1, keepdims=True)
        )
        grad_logits = jnp.sum(choose * grad_chosen[:, :, None], axis=1)
        gate_slots = (
            jnp.zeros((slot_count,), jnp.float32).at[slot_index].set(gate_weights.reshape(-1))
        )
        grad_pad = jnp.concatenate([grad_mix, jnp.zeros((1, model_width), jnp.float32)], axis=0)
        grad_send = (gate_slots[:, None] * grad_pad[token_of]).astype(jnp.bfloat16)
        grad_expert = expert_trade(
            grad_send.reshape(experts_here, dp_count * capacity, model_width)
        )
        grad_act = jnp.einsum(
            "ecd,efd->ecf", grad_expert, full_down, preferred_element_type=jnp.float32
        )
        micro_down = jnp.einsum(
            "ecf,ecd->efd", activated, grad_expert, preferred_element_type=jnp.float32
        )
        sigmoid_gate = jax.nn.sigmoid(gate_proj)
        silu_gate = gate_proj * sigmoid_gate
        grad_gate_p = (
            grad_act * up_proj * (sigmoid_gate + gate_proj * sigmoid_gate * (1.0 - sigmoid_gate))
        ).astype(jnp.bfloat16)
        grad_up_p = (grad_act * silu_gate).astype(jnp.bfloat16)
        grad_in = jnp.einsum(
            "ecf,edf->ecd", grad_gate_p, full_gate, preferred_element_type=jnp.float32
        ) + jnp.einsum("ecf,edf->ecd", grad_up_p, full_up, preferred_element_type=jnp.float32)
        micro_gate = jnp.einsum(
            "ecd,ecf->edf", expert_in, grad_gate_p, preferred_element_type=jnp.float32
        )
        micro_up = jnp.einsum(
            "ecd,ecf->edf", expert_in, grad_up_p, preferred_element_type=jnp.float32
        )
        expert_local = add_all(expert_local, (micro_gate, micro_up, micro_down))
        grad_back = expert_trade(grad_in.astype(jnp.bfloat16)).reshape(slot_count, model_width)
        grad_normed = jnp.sum(
            grad_back[slot_index].reshape(quarter, TOP, model_width).astype(jnp.float32), axis=1
        ) + jnp.dot(grad_logits, router_wide.T, precision=highest)
        router_acc = router_acc + jnp.dot(
            normed_two.astype(jnp.float32).T, grad_logits, precision=highest
        )
        mix_acc = mix_acc + jnp.sum(grad_normed * unit_two, axis=0)
        grad_scaled = grad_normed * mix_gain
        grad_mixed_rows = grad_rows + scale_two * (
            grad_scaled - unit_two * jnp.mean(grad_scaled * unit_two, axis=1, keepdims=True)
        )
        grad_mixed = lax.all_to_all(
            grad_mixed_rows.reshape(1, quarter, model_width),
            "col",
            split_axis=2,
            concat_axis=0,
            tiled=True,
        ).reshape(tok_dev, width_part)
        grad_branch = (resid_scale * grad_mixed).astype(jnp.bfloat16)
        grad_branch_all = gather_rows(grad_branch)
        micro_out = jnp.dot(attended_all.T, grad_branch_all, preferred_element_type=jnp.float32)
        grad_attended = sum_cols(
            jnp.dot(grad_branch_all, w_out.T, preferred_element_type=jnp.float32)
        )
        grad_att_low = grad_attended.astype(jnp.bfloat16).reshape(
            tok_dev, kv_here, group_size, HEAD_DIM
        )
        probs_again = jnp.exp(scores - log_total)
        grad_probs = jnp.einsum(
            "qhgd,khd->hgqk", grad_att_low, values_all, preferred_element_type=jnp.float32
        )
        grad_scores = probs_again * (
            grad_probs - jnp.sum(probs_again * grad_probs, axis=-1, keepdims=True)
        )
        grad_raw = (grad_scores * attn_scale).astype(jnp.bfloat16)
        probs_again_low = probs_again.astype(jnp.bfloat16)
        grad_query = jnp.einsum(
            "hgqk,khd->qhgd", grad_raw, keys_all, preferred_element_type=jnp.float32
        )
        grad_key_part = jnp.einsum(
            "hgqk,qhgd->khd", grad_raw, query_grp, preferred_element_type=jnp.float32
        )
        grad_value_part = jnp.einsum(
            "hgqk,qhgd->khd", probs_again_low, grad_att_low, preferred_element_type=jnp.float32
        )
        grad_key, grad_value = sum_cols(
            (
                grad_key_part.reshape(group_tokens, kv_here * HEAD_DIM),
                grad_value_part.reshape(group_tokens, kv_here * HEAD_DIM),
            )
        )
        grad_query_p = (
            rotate(grad_query.reshape(tok_dev, heads_here, HEAD_DIM), -sin_table, cos_table)
            .astype(jnp.bfloat16)
            .reshape(tok_dev, heads_here * HEAD_DIM)
        )
        grad_key_p = (
            rotate(grad_key.reshape(tok_dev, kv_here, HEAD_DIM), -sin_table, cos_table)
            .astype(jnp.bfloat16)
            .reshape(tok_dev, kv_here * HEAD_DIM)
        )
        grad_value_p = grad_value.astype(jnp.bfloat16)
        query_all, key_all, value_all = gather_cols((grad_query_p, grad_key_p, grad_value_p))
        micro_query = jnp.dot(normed_all.T, query_all, preferred_element_type=jnp.float32)
        micro_key = jnp.dot(normed_all.T, key_all, preferred_element_type=jnp.float32)
        micro_value = jnp.dot(normed_all.T, value_all, preferred_element_type=jnp.float32)
        grad_normed_one = sum_rows(
            jnp.dot(query_all, w_query.T, preferred_element_type=jnp.float32)
            + jnp.dot(key_all, w_key.T, preferred_element_type=jnp.float32)
            + jnp.dot(value_all, w_value.T, preferred_element_type=jnp.float32)
        )
        grad_scaled_one = grad_normed_one * gain_part
        inner_sum = width_total(jnp.sum(grad_scaled_one * unit_one, axis=1))
        norm_acc = norm_acc + jnp.sum(grad_normed_one * unit_one, axis=0)
        input_grads.append(
            grad_mixed
            + scale_one * (grad_scaled_one - unit_one * (inner_sum / model_width)[:, None])
        )
        attn_local = add_all(attn_local, (micro_query, micro_key, micro_value, micro_out))
    attn_summed = attn_total(attn_local)
    expert_summed = expert_total(expert_local)
    gain_full = lax.dynamic_update_slice_in_dim(
        jnp.zeros((model_width,), jnp.float32), norm_acc, col_at * width_part, 0
    )
    router_grad, gain_grad, mix_grad = lax.psum(
        (router_acc, gain_full, mix_acc), ("dp", "row", "col")
    )
    return (
        jnp.stack(layer_rows),
        jnp.stack(input_grads),
        gain_grad,
        attn_summed[0],
        attn_summed[1],
        attn_summed[2],
        attn_summed[3],
        mix_grad,
        router_grad,
        expert_summed[0],
        expert_summed[1],
        expert_summed[2],
    )


MESH = pl.DeviceIdType.MESH
ANYWHERE = pl.BlockSpec(memory_space=pl.ANY)


def group_size_of(axes):
    total = 1
    for axis in axes:
        total = total * lax.axis_size(axis)
    return total


def place_in(axes):
    at = 0
    for axis in axes:
        at = at * lax.axis_size(axis) + lax.axis_index(axis)
    return at


def device_at(axes, index):
    place = {}
    for axis in reversed(axes):
        place[axis] = index % lax.axis_size(axis)
        index = index // lax.axis_size(axis)
    return place


def meet(peers):
    barrier = pltpu.get_barrier_semaphore()
    for peer in peers:
        pl.semaphore_signal(barrier, inc=1, device_id=peer, device_id_type=MESH)
    pl.semaphore_wait(barrier, len(peers))


def send(src, dst, send_sem, recv_sem, peer):
    copy = pltpu.make_async_remote_copy(
        src_ref=src,
        dst_ref=dst,
        send_sem=send_sem,
        recv_sem=recv_sem,
        device_id=peer,
        device_id_type=MESH,
    )
    copy.start()
    return copy


def row_peers():
    row = lax.axis_index("row")
    rows = lax.axis_size("row")
    across = (row + rows // 2) % rows
    beside = row + 1 - 2 * (row % 2)
    return row, across, beside


def col_peers():
    col, cols = lax.axis_index("col"), lax.axis_size("col")
    two_on = (col + 2) % cols
    near = col + 1 - 2 * (col % 2)
    return two_on, near, (col, two_on, near, (near + 2) % cols)


def gather_line(source, target, sems, copies):
    local_sem, send_sem, col_sem, dp_sem, across_sem, beside_sem = sems
    row, across, beside = row_peers()
    rows, cols = lax.axis_size("row"), lax.axis_size("col")
    dp = lax.axis_index("dp")
    other = 1 - dp
    two_on, near, order = col_peers()
    far = (beside + rows // 2) % rows
    sent = []

    def block_of(dp_from, row_from, step):
        return (dp_from * rows + row_from) * cols + order[step]

    def arrival(block, sem):
        pltpu.make_async_copy(target.at[block], target.at[block], sem).wait()

    def pass_on(part, block, sem, peer):
        copy = send(part, target.at[block], send_sem.at[len(sent)], sem, peer)
        sent.append(copy)
        copies.append(copy)

    me = block_of(dp, row, 0)
    own = pltpu.make_async_copy(source.at[0], target.at[me], local_sem)

    def begin():
        own.start()
        pass_on(source.at[0], me, col_sem.at[1], {"col": two_on})
        pass_on(source.at[0], me, col_sem.at[2], {"col": near})

    def line(step):
        block = block_of(dp, row, step)
        part = source.at[0] if step == 0 else target.at[block]
        if step > 0:
            arrival(block, col_sem.at[step])
        if step == 1:
            pass_on(part, block, col_sem.at[3], {"col": near})
        pass_on(part, block, dp_sem.at[step], {"dp": other})
        pass_on(part, block, across_sem.at[step], {"row": across})
        pass_on(part, block, beside_sem.at[step], {"row": beside})

    def side(step):
        block = block_of(other, row, step)
        arrival(block, dp_sem.at[step])
        pass_on(target.at[block], block, beside_sem.at[cols + step], {"row": beside})
        block = block_of(dp, across, step)
        arrival(block, across_sem.at[step])
        pass_on(target.at[block], block, dp_sem.at[cols + step], {"dp": other})
        pass_on(target.at[block], block, beside_sem.at[2 * cols + step], {"row": beside})

    def corner(step):
        block = block_of(other, across, step)
        arrival(block, dp_sem.at[cols + step])
        pass_on(target.at[block], block, beside_sem.at[3 * cols + step], {"row": beside})

    def finish():
        for turn, (dp_from, row_from) in enumerate(
            ((dp, beside), (other, beside), (dp, far), (other, far))
        ):
            for step in range(cols):
                arrival(block_of(dp_from, row_from, step), beside_sem.at[turn * cols + step])
        own.wait()

    return begin, line, side, corner, finish


def gather_sems():
    cols = lax.axis_size("col")
    return [
        pltpu.SemaphoreType.DMA,
        pltpu.SemaphoreType.DMA((40,)),
        pltpu.SemaphoreType.DMA((cols,)),
        pltpu.SemaphoreType.DMA((2 * cols,)),
        pltpu.SemaphoreType.DMA((2 * cols,)),
        pltpu.SemaphoreType.DMA((4 * cols,)),
    ]


def nt(left, right):
    return lax.dot_general(
        left, right, (((1,), (1,)), ((), ())), preferred_element_type=jnp.float32
    )


def tn(left, right):
    return lax.dot_general(
        left, right, (((0,), (0,)), ((), ())), preferred_element_type=jnp.float32
    )


def norm_rows(x, gain):
    scale = lax.rsqrt(jnp.mean(x * x, axis=1, keepdims=True) + eps_norm)
    return scale, (x * scale * gain).astype(jnp.bfloat16)


def turn(values, cos_table, sin_table):
    lane = lax.broadcasted_iota(jnp.int32, values.shape, 1)
    ahead = pltpu.roll(values, values.shape[1] - HEAD_DIM // 2, 1)
    behind = pltpu.roll(values, HEAD_DIM // 2, 1)
    return values * cos_table + jnp.where(lane % HEAD_DIM < HEAD_DIM // 2, ahead, behind) * sin_table


def key_extent(block, rows, total):
    return min(total, -(-(block + 1) * rows // 128) * 128)


def visible(doc_col, doc_row, block, rows, extent):
    query = block * rows + lax.broadcasted_iota(jnp.int32, (rows, extent), 0)
    keys = lax.broadcasted_iota(jnp.int32, (rows, extent), 1)
    same = doc_col[block * rows : (block + 1) * rows, 0:1] == doc_row[0:1, 0:extent]
    return same & (keys <= query)


def attend(query, key, allowed):
    scores = jnp.where(allowed, nt(query, key) * attn_scale, -1e30)
    raised = jnp.exp(scores - jnp.max(scores, axis=1, keepdims=True))
    return raised / jnp.sum(raised, axis=1, keepdims=True)


def front_kernel(
    x,
    w_qkv,
    w_out,
    picks,
    cot,
    w_gate,
    w_up,
    w_down,
    gain_one,
    gain_two,
    cos_table,
    sin_table,
    doc_col,
    doc_row,
    router_t,
    table,
    x_all,
    w_mine,
    w_out_mine,
    cot_all,
    normed_all,
    qkv,
    attended,
    mixed,
    gates_own,
    rows_part,
    mix_part,
    scores,
    grads_gu,
    grads_down,
    w_out_all,
    picks_all,
    x_own,
    att_own,
    normed_two,
    gate_up,
    down,
    down_grad,
    pool_rows,
    pool_cots,
    kept_in,
    kept_dy,
    kept_dye,
    kept_act,
    kept_gate,
    kept_up,
    gate_proj,
    up_proj,
    kept_weight,
    ranks,
    upper,
    load_sem,
    store_sem,
    grad_local,
    grad_send,
    grad_recv,
    local_sem,
    send_sem,
    x_sem,
    q_sem,
    o_sem,
    own_sem,
    att_send,
    att_recv,
    ship_local,
    ship_send,
    ship_recv,
    *line_sems,
):
    row, across, beside = row_peers()
    rows, cols = lax.axis_size("row"), lax.axis_size("col")
    col, dp = lax.axis_index("col"), lax.axis_index("dp")
    other = 1 - dp
    far = (beside + rows // 2) % rows
    plane = ("row", "col")
    size, me = group_size_of(plane), place_in(plane)
    low = jnp.bfloat16
    meet(
        [device_at(plane, (me + step) % size) for step in range(1, size)] + [{"dp": other}]
    )
    copies, locals_, sent, moved = [], [], [], []
    picks_line = gather_line(picks, picks_all, line_sems[0:6], copies)
    cot_line = gather_line(cot, cot_all, line_sems[6:12], copies)
    norm_line = gather_line(normed_two, normed_all, line_sems[12:18], copies)

    def pass_on(src, dst, sem, peer):
        sent.append(send(src, dst, send_sem.at[len(sent)], sem, peer))

    def arrival(ref, sem):
        pltpu.make_async_copy(ref, ref, sem).wait()

    def local(src, dst):
        copy = pltpu.make_async_copy(src, dst, local_sem.at[len(locals_)])
        copy.start()
        locals_.append(copy)

    slice_rows, ff_width = w_gate.shape[1:]
    down_rows = w_down.shape[1]
    chunks = w_down.shape[2] // ff_width

    def weight_parts(to, at):
        parts = [
            (w_gate.at[to], gate_up.at[at, 0:slice_rows]),
            (w_up.at[to], gate_up.at[at, slice_rows : 2 * slice_rows]),
        ]
        for chunk in range(chunks):
            parts.append(
                (
                    w_down.at[to, :, chunk * ff_width : (chunk + 1) * ff_width],
                    down.at[at, chunk * down_rows : (chunk + 1) * down_rows],
                )
            )
        return parts

    def ship(first, last, which=range(2)):
        for step in range(first, last):
            to = (me + step) % size
            for part in which:
                source, target = weight_parts(to, me)[part]
                moved.append(
                    send(
                        source,
                        target,
                        ship_send.at[part, step],
                        ship_recv.at[part, step],
                        device_at(plane, to),
                    )
                )

    def shipped(which):
        for step in range(1, size):
            for part in which:
                arrival(
                    weight_parts(me, (me + size - step) % size)[part][1], ship_recv.at[part, step]
                )

    def origin(step):
        return (col + cols - step) % cols

    two_on, near, order = col_peers()

    micro, depth, width = x.shape
    quarter = depth // cols
    half_depth = w_out.shape[1]

    def lanes_of(at):
        return pl.ds(pl.multiple_of(at * width, width), width)

    def lanes(step):
        return lanes_of(order[step])

    def x_at(row_from, step):
        return x_all.at[pl.ds(pl.multiple_of(row_from * depth, depth), depth), lanes(step)]

    def out_at(row_from, step, half):
        first = pl.multiple_of((row_from * 2 + half) * half_depth, half_depth)
        return w_out_all.at[pl.ds(first, half_depth), lanes(step)]

    def own_at(m, step):
        return x_own.at[pl.ds(m * quarter, quarter), lanes_of(origin(step))]

    my_x = x_at(row, 0)
    for step in range(1, cols):
        to = (col + step) % cols
        if step < 3:
            peer = (two_on, near)[step - 1]
            pass_on(x.at[peer // 2], my_x, x_sem.at[step], {"col": peer})
        pass_on(w_qkv.at[to % 2, dp], w_mine.at[col, dp], q_sem.at[step], {"col": to})
    local(x.at[col // 2], my_x)
    local(w_qkv.at[col % 2], w_mine.at[col])
    for half in range(2):
        local(w_out.at[half], out_at(row, 0, half))
    pass_on(x.at[col // 2], my_x, x_sem.at[cols], {"row": across})
    pass_on(x.at[col // 2], my_x, x_sem.at[2 * cols], {"row": beside})
    for step in range(1, cols):
        to = (col + step) % cols
        if step < 3:
            peer = (two_on, near)[step - 1]
            pass_on(w_out.at[dp], out_at(row, 0, dp), o_sem.at[step], {"col": peer})
        first = pl.multiple_of(to * quarter, quarter)
        for m in range(micro):
            pass_on(
                x.at[m, pl.ds(first, quarter)],
                own_at(m, 0),
                own_sem.at[m * cols + step],
                {"col": to},
            )
    for m in range(micro):
        local(x.at[m, pl.ds(pl.multiple_of(col * quarter, quarter), quarter)], own_at(m, 0))
    for half in range(2):
        pass_on(w_out.at[half], out_at(row, 0, half), o_sem.at[(2 + half) * cols], {"row": across})
        pass_on(w_out.at[half], out_at(row, 0, half), o_sem.at[(4 + half) * cols], {"row": beside})
    for step in range(1, cols):
        part = x_at(row, step)
        arrival(part, x_sem.at[step])
        if step == 1:
            pass_on(part, part, x_sem.at[3], {"col": near})
        pass_on(part, part, x_sem.at[cols + step], {"row": across})
        pass_on(part, part, x_sem.at[2 * cols + step], {"row": beside})
        part = w_mine.at[origin(step), dp]
        arrival(part, q_sem.at[step])
        pass_on(part, part, q_sem.at[cols + step], {"dp": other})
    for step in range(cols):
        part = x_at(across, step)
        arrival(part, x_sem.at[cols + step])
        pass_on(part, part, x_sem.at[3 * cols + step], {"row": beside})
    for step in range(1, cols):
        part = out_at(row, step, dp)
        arrival(part, o_sem.at[step])
        if step == 1:
            pass_on(part, part, o_sem.at[3], {"col": near})
        pass_on(part, part, o_sem.at[cols + step], {"dp": other})
        pass_on(part, part, o_sem.at[2 * cols + step], {"row": across})
        pass_on(part, part, o_sem.at[4 * cols + step], {"row": beside})
    picks_line[0]()
    cot_line[0]()
    for source, target in weight_parts(me, me):
        local(source, target)
    for step in range(1, cols):
        arrival(w_mine.at[origin(step), other], q_sem.at[cols + step])
    for at, row_from in enumerate((beside, far)):
        for step in range(cols):
            arrival(x_at(row_from, step), x_sem.at[(2 + at) * cols + step])
    for copy in locals_[:6]:
        copy.wait()

    tokens, model_width = x_all.shape
    projection = w_mine[...].reshape(model_width, w_mine.shape[3])
    for block in range(rows):
        part = slice(block * depth, (block + 1) * depth)
        _, normed = norm_rows(x_all[part, :].astype(jnp.float32), gain_one[...])
        values = project(normed, projection)
        cosine, sine = cos_table[part, :], sin_table[part, :]
        for at in range(2):
            piece = slice(at * 128, (at + 1) * 128)
            qkv[part, piece] = turn(values[:, piece], cosine, sine).astype(low)
        qkv[part, 256:] = values[:, 256:].astype(low)
    heads = attended.shape[2] // HEAD_DIM
    kv_at = heads * HEAD_DIM
    for block in range(rows):
        extent = key_extent(block, depth, tokens)
        allowed = visible(doc_col, doc_row, block, depth, extent)
        key = qkv[0:extent, kv_at : kv_at + HEAD_DIM]
        value = qkv[0:extent, kv_at + HEAD_DIM : kv_at + 2 * HEAD_DIM]
        outs = []
        for head in range(heads):
            query = qkv[
                block * depth : (block + 1) * depth, head * HEAD_DIM : (head + 1) * HEAD_DIM
            ]
            outs.append(project(attend(query, key, allowed).astype(low), value))
        out = jnp.concatenate(outs, axis=1).astype(low)
        attended[block * cols : (block + 1) * cols] = out.reshape(cols, quarter, out.shape[1])
    for step in range(1, size):
        to = (me + step) % size
        moved.append(
            send(
                attended.at[to],
                att_own.at[me],
                att_send.at[step],
                att_recv.at[step],
                device_at(plane, to),
            )
        )
    stay = pltpu.make_async_copy(attended.at[me], att_own.at[me], att_send.at[0])
    stay.start()
    ship(1, 5)
    for step in range(1, cols):
        part = out_at(row, step, other)
        arrival(part, o_sem.at[cols + step])
        pass_on(part, part, o_sem.at[3 * cols + step], {"row": across})
        pass_on(part, part, o_sem.at[5 * cols + step], {"row": beside})
    for step in range(cols):
        picks_line[1](step)
        cot_line[1](step)
    for at in range(2):
        for step in range(cols):
            half = at if step == 0 else (dp if at == 0 else other)
            part = out_at(across, step, half)
            arrival(part, o_sem.at[(2 + at) * cols + step])
            pass_on(part, part, o_sem.at[(6 + at) * cols + step], {"row": beside})
    for at, row_from in enumerate((beside, far)):
        for step in range(cols):
            for part in range(2):
                half = part if step == 0 else (dp if part == 0 else other)
                arrival(out_at(row_from, step, half), o_sem.at[(4 + 2 * at + part) * cols + step])
    for step in range(1, cols):
        for m in range(micro):
            arrival(own_at(m, step), own_sem.at[m * cols + step])
    stay.wait()
    for step in range(1, size):
        arrival(att_own.at[(me + size - step) % size], att_recv.at[step])
    pairs = cols // micro
    for m in range(micro):
        total = jnp.zeros((quarter, model_width), jnp.float32)
        for row_from in range(rows):
            for pair in range(pairs):
                first = (row_from * pairs + pair) * kv_at
                total = total + project(
                    att_own[row_from * cols + m * pairs + pair],
                    w_out_all[first : first + kv_at, :],
                )
        part = slice(m * quarter, (m + 1) * quarter)
        value = x_own[part, :].astype(jnp.float32) + resid_scale * total
        mixed[part, :] = value
        normed_two[0, part, :] = norm_rows(value, gain_two[...])[1]

    begin, line, side, corner, finish = norm_line
    begin()
    for step in range(cols):
        picks_line[2](step)
        cot_line[2](step)
        ship(5 + 2 * step, 7 + 2 * step)
    for step in range(cols):
        line(step)
    ship(5 + 2 * cols, size)
    ship(1, size, range(2, 2 + chunks))
    logits = jnp.where(table[...] > 0, nt(normed_two[0], router_t[...]), -jnp.inf)
    raised = jnp.exp(logits - jnp.max(logits, axis=1, keepdims=True))
    gates_own[...] = raised / jnp.sum(raised, axis=1, keepdims=True)
    w_out_mine[...] = w_out_all[
        pl.ds(pl.multiple_of((row * 2 + col % 2) * kv_at, kv_at), kv_at), :
    ]
    for step in range(cols):
        picks_line[3](step)
        cot_line[3](step)
        side(step)
    for step in range(cols):
        corner(step)
    picks_line[4]()
    cot_line[4]()
    finish()

    everyone = ("dp", "row", "col")
    expert = place_in(everyone)
    tiles, slots = kept_in.shape[0], kept_in.shape[1]
    padded = pool_rows.shape[2]
    block_rows = micro * quarter
    span = cols * padded
    pool_rows[...] = jnp.zeros_like(pool_rows)
    pool_cots[...] = jnp.zeros_like(pool_cots)
    upper[...] = (
        lax.broadcasted_iota(jnp.int32, upper.shape, 0)
        < lax.broadcasted_iota(jnp.int32, upper.shape, 1)
    ).astype(low)

    def pool(tile, slot):
        for at, (source, target) in enumerate(((normed_all, pool_rows), (cot_all, pool_cots))):
            yield pltpu.make_async_copy(
                source.at[pl.ds(tile * cols, cols)],
                target.at[slot, :, 0:block_rows],
                load_sem.at[at, slot],
            )

    for copy in pool(0, 0):
        copy.start()
    slot_of = lax.broadcasted_iota(jnp.int32, (slots, span), 0)

    def picked(tile):
        return slot_of == ranks[tile][0:1, :]

    @pl.loop(0, tiles)
    def _(tile):
        slot = tile % 2
        for copy in pool(tile, slot):
            copy.wait()

        @pl.when(tile + 1 < tiles)
        def _():
            for copy in pool(tile + 1, 1 - slot):
                copy.start()

        rows_here = pool_rows[slot].reshape(span, model_width)
        logits = nt(router_t[...], rows_here)[0 : picks_all.shape[0], :]
        ids = lax.broadcasted_iota(jnp.int32, logits.shape, 0)
        names = jnp.concatenate([picks_all[tile * cols + at] for at in range(cols)], axis=1)
        chosen = ids == names[0:1, :]
        for choice in range(1, names.shape[0]):
            chosen = chosen | (ids == names[choice : choice + 1, :])
        logits = jnp.where(chosen, logits, -1e30)
        raised = jnp.where(chosen, jnp.exp(logits - jnp.max(logits, axis=0, keepdims=True)), 0.0)
        total = jnp.sum(raised, axis=0, keepdims=True)
        mine = ids == expert
        gate = jnp.sum(jnp.where(mine, raised, 0.0), axis=0, keepdims=True) / jnp.where(
            total > 0, total, 1.0
        )
        here = jnp.max(jnp.where(mine & chosen, 1.0, 0.0), axis=0, keepdims=True)
        before = project(jnp.broadcast_to(here, (16, span)).astype(low), upper[...])[0:1, :]
        rank = jnp.where(here > 0, before.astype(jnp.int32), -1)
        ranks[tile] = jnp.broadcast_to(rank, ranks.shape[1:])
        select = slot_of == rank
        kept_weight[tile] = jnp.broadcast_to(
            jnp.sum(jnp.where(select, gate, 0.0), axis=1, keepdims=True), kept_weight.shape[1:]
        )
        select = select.astype(low)
        kept_in[tile] = project(select, rows_here).astype(low)
        kept_dy[tile] = project(select, pool_cots[slot].reshape(span, model_width)).astype(low)

    shipped(range(2))
    for copy in locals_[6:]:
        copy.wait()
    gate_w = gate_up[:, 0:slice_rows, :].reshape(model_width, ff_width)
    up_w = gate_up[:, slice_rows : 2 * slice_rows, :].reshape(model_width, ff_width)

    def down_w(chunk):
        at = chunk * down_rows
        return down[:, at : at + down_rows, :].reshape(ff_width, ff_width)

    def two(ref, pair):
        part = ref[pl.ds(2 * pair, 2)]
        return part.reshape(2 * slots, part.shape[2])

    def put(ref, pair, value):
        ref[pl.ds(2 * pair, 2)] = value.reshape(2, slots, value.shape[1])

    @pl.loop(0, tiles // 2)
    def _(pair):
        rows_in = two(kept_in, pair)
        gate_value = project(rows_in, gate_w)
        up_value = project(rows_in, up_w)
        put(gate_proj, pair, gate_value)
        put(up_proj, pair, up_value)
        put(kept_act, pair, (gate_value / (1.0 + jnp.exp(-gate_value)) * up_value).astype(low))
        weight = two(kept_weight, pair)[:, 0:1]
        grad_mix = resid_scale * two(kept_dy, pair).astype(jnp.float32)
        put(kept_dye, pair, (weight * grad_mix).astype(low))

    def all_of(ref):
        value = ref[...]
        return value.reshape(tiles * slots, value.shape[2])

    act_all = all_of(kept_act)
    for chunk in range(chunks):
        grad = tn(act_all, all_of(kept_dye.at[:, :, chunk * ff_width : (chunk + 1) * ff_width]))
        at = chunk * down_rows
        down_grad[:, at : at + down_rows, :] = grad.astype(low).reshape(size, down_rows, ff_width)
    home = pltpu.make_async_copy(down_grad.at[me], grads_down.at[me], grad_local)
    home.start()
    given = []
    for step in range(1, size):
        to = (me + step) % size
        given.append(
            send(
                down_grad.at[to],
                grads_down.at[me],
                grad_send.at[step],
                grad_recv.at[step],
                device_at(plane, to),
            )
        )
    shipped(range(2, 2 + chunks))

    def spill(tile, slot):
        for at, (source, target) in enumerate(((pool_rows, rows_part), (pool_cots, mix_part))):
            yield pltpu.make_async_copy(
                source.at[slot, :, 0:block_rows],
                target.at[pl.ds(tile * cols, cols)],
                store_sem.at[at, slot],
            )

    @pl.loop(0, tiles // 2)
    def _(pair):
        act = two(kept_act, pair)
        grad_out = two(kept_dye, pair)
        gate_value, up_value = two(gate_proj, pair), two(up_proj, pair)
        weight = two(kept_weight, pair)[:, 0:1]
        score = jnp.zeros((2 * slots, 1), jnp.float32)
        grad_act = jnp.zeros((2 * slots, ff_width), jnp.float32)

        @pl.when(pair > 0)
        def _():
            for at in range(2):
                for copy in spill(2 * pair - 2 + at, at):
                    copy.wait()

        selects = [picked(2 * pair + at).astype(low) for at in range(2)]
        for chunk in range(chunks):
            lanes = slice(chunk * ff_width, (chunk + 1) * ff_width)
            part = down_w(chunk)
            out = project(act, part).astype(low).astype(jnp.float32)
            grad_mix = resid_scale * kept_dy[pl.ds(2 * pair, 2), :, lanes].reshape(
                2 * slots, ff_width
            ).astype(jnp.float32)
            score = score + jnp.sum(grad_mix * out, axis=1, keepdims=True)
            mixed_rows = (weight * out).astype(low)
            for at in range(2):
                pool_cots[at, :, :, lanes] = (
                    tn(selects[at], mixed_rows[at * slots : (at + 1) * slots])
                    .astype(low)
                    .reshape(cols, padded, ff_width)
                )
            grad_act = grad_act + nt(grad_out[:, lanes], part)
        sigmoid = 1.0 / (1.0 + jnp.exp(-gate_value))
        grad_gate = (
            grad_act * up_value * (sigmoid + gate_value * sigmoid * (1.0 - sigmoid))
        ).astype(low)
        grad_up = (grad_act * (gate_value * sigmoid)).astype(low)
        put(kept_gate, pair, grad_gate)
        put(kept_up, pair, grad_up)
        grad_in = (nt(grad_gate, gate_w) + nt(grad_up, up_w)).astype(low)
        for at in range(2):
            tile = 2 * pair + at
            part = slice(at * slots, (at + 1) * slots)
            pool_rows[at] = (
                tn(selects[at], grad_in[part]).astype(low).reshape(cols, padded, model_width)
            )
            line_of = jnp.sum(jnp.where(picked(tile), score[part], 0.0), axis=0, keepdims=True)
            for block in range(cols):
                scores[tile * cols + block] = jnp.broadcast_to(
                    line_of[:, block * padded : (block + 1) * padded], scores.shape[1:]
                )
            for copy in spill(tile, at):
                copy.start()

    rows_all = all_of(kept_in)
    for at, kept in ((0, kept_gate), (slice_rows, kept_up)):
        grad = tn(rows_all, all_of(kept)).astype(low)
        grads_gu[:, at : at + slice_rows, :] = grad.reshape(size, slice_rows, ff_width)
    for at in range(2):
        for copy in spill(tiles - 2 + at, at):
            copy.wait()
    home.wait()
    for copy in given:
        copy.wait()
    for copy in moved + copies + sent:
        copy.wait_send()


def front(number, x, w_qkv, w_out, picks, cot, experts, gains, tables, docs, routing, heads_width):
    cols, rows = lax.axis_size("col"), lax.axis_size("row")
    total, plane = group_size_of(("dp", "row", "col")), group_size_of(("row", "col"))
    micro, depth, part_width = x.shape
    width, tokens, low = part_width * cols, depth * rows, jnp.bfloat16
    wide = jnp.float32
    quarter = depth // cols
    _, slice_rows, ff_width = experts[0].shape
    down_depth = slice_rows * plane // ff_width * experts[2].shape[1]
    tiles = total // cols
    slots = cols * micro * (quarter * 3 // 8)
    vmem = pl.BlockSpec(memory_space=pltpu.VMEM)
    shape, dma = jax.ShapeDtypeStruct, pltpu.SemaphoreType.DMA
    pool = pltpu.VMEM((2, cols, 128, width), low)
    return pl.pallas_call(
        front_kernel,
        out_shape=[
            shape((tokens, width), low),
            shape((cols,) + w_qkv.shape[1:], low),
            shape((heads_width, width), low),
            shape((total,) + cot.shape, low),
            shape((total,) + cot.shape, low),
            shape((tokens, w_qkv.shape[3]), low),
            shape((plane, quarter, heads_width), low),
            shape((micro * quarter, width), wide),
            shape((micro * quarter, 128), wide),
            shape((total,) + cot.shape, low),
            shape((total,) + cot.shape, low),
            shape((total, 8, 128), wide),
            shape((plane, 2 * slice_rows, ff_width), low),
            shape((plane, down_depth, ff_width), low),
        ],
        in_specs=[ANYWHERE] * 8 + [vmem] * 8,
        out_specs=[vmem] * 3
        + [ANYWHERE] * 2
        + [vmem] * 4
        + [ANYWHERE] * 2
        + [vmem] * 2
        + [ANYWHERE],
        scratch_shapes=[
            pltpu.VMEM((rows * 2 * w_out.shape[1], width), low),
            pltpu.VMEM((total,) + picks.shape, picks.dtype),
            pltpu.VMEM((micro * quarter, width), low),
            pltpu.VMEM((plane, quarter, heads_width), low),
            pltpu.VMEM((1, micro * quarter, width), low),
            pltpu.VMEM((plane, 2 * slice_rows, ff_width), low),
            pltpu.VMEM((plane, down_depth, ff_width), low),
            pltpu.VMEM((plane, down_depth, ff_width), low),
            pool,
            pool,
            pltpu.VMEM((tiles, slots, width), low),
            pltpu.VMEM((tiles, slots, width), low),
            pltpu.VMEM((tiles, slots, width), low),
            pltpu.VMEM((tiles, slots, ff_width), low),
            pltpu.VMEM((tiles, slots, ff_width), low),
            pltpu.VMEM((tiles, slots, ff_width), low),
            pltpu.VMEM((tiles, slots, ff_width), wide),
            pltpu.VMEM((tiles, slots, ff_width), wide),
            pltpu.VMEM((tiles, slots, 128), wide),
            pltpu.VMEM((tiles, 8, cols * 128), jnp.int32),
            pltpu.VMEM((cols * 128, cols * 128), low),
            dma((2, 2)),
            dma((2, 2)),
            dma,
            dma((plane,)),
            dma((plane,)),
            dma((12,)),
            dma((72,)),
            dma((4 * cols,)),
            dma((2 * cols,)),
            dma((8 * cols,)),
            dma((micro * cols,)),
            dma((plane,)),
            dma((plane,)),
            dma,
            dma((8, plane)),
            dma((8, plane)),
        ]
        + gather_sems() * 3,
        compiler_params=pltpu.CompilerParams(
            collective_id=number, has_side_effects=True, vmem_limit_bytes=63 * 2**20
        ),
        name="front" + str(number),
    )(x, w_qkv, w_out, picks[None], cot[None], *experts, *gains, *tables, *docs, *routing)


def sum_scratch(block):
    cols = lax.axis_size("col")
    low = jnp.bfloat16
    return [
        pltpu.VMEM((4 * cols,) + block, low),
        pltpu.VMEM((4 * cols,) + block, low),
        pltpu.VMEM((4 * cols,) + block, low),
        pltpu.VMEM((3 * cols,) + block, low),
        pltpu.VMEM((cols,) + block, low),
        pltpu.SemaphoreType.DMA((4 * cols,)),
        pltpu.SemaphoreType.DMA((48,)),
        pltpu.SemaphoreType.DMA((4 * cols,)),
        pltpu.SemaphoreType.DMA((cols,)),
        pltpu.SemaphoreType.DMA((2 * cols,)),
        pltpu.SemaphoreType.DMA((cols,)),
    ]


def sum_steps(partial, sems, copies):
    (
        near,
        mine,
        passed,
        stage,
        last,
        local_sem,
        send_sem,
        beside_sem,
        first_sem,
        second_sem,
        col_sem,
    ) = sems
    row, across, beside = row_peers()
    rows, cols = lax.axis_size("row"), lax.axis_size("col")
    col, dp = lax.axis_index("col"), lax.axis_index("dp")
    other = 1 - dp
    low = jnp.bfloat16
    two_on, beside_col, _ = col_peers()
    order = (beside_col, (beside_col + 2) % cols, two_on, col)
    sent = []

    def pass_on(src, dst, sem, peer):
        copy = send(src, dst, send_sem.at[len(sent)], sem, peer)
        sent.append(copy)
        copies.append(copy)

    def arrival(ref, sem):
        pltpu.make_async_copy(ref, ref, sem).wait()

    def block_of(dp_to, row_to, col_to):
        return (dp_to * rows + row_to) * cols + col_to

    far = (beside + rows // 2) % rows
    theirs = ((other, far), (other, beside), (dp, far), (dp, beside))
    ours = ((other, across), (other, row), (dp, across), (dp, row))

    def start():
        for turn in range(4):
            for at in range(cols):
                slot = turn * cols + at
                pass_on(
                    partial.at[block_of(*theirs[turn], order[at])],
                    near.at[slot],
                    beside_sem.at[slot],
                    {"row": beside},
                )
                pltpu.make_async_copy(
                    partial.at[block_of(*ours[turn], order[at])], mine.at[slot], local_sem.at[slot]
                ).start()

    def combine(target, *parts):
        rows_each = 16

        @pl.loop(0, target.shape[0] // rows_each)
        def _(at):
            lines = pl.ds(pl.multiple_of(at * rows_each, rows_each), rows_each)
            value = parts[0][lines, :].astype(jnp.float32)
            for part in parts[1:]:
                value = value + part[lines, :].astype(jnp.float32)
            target[lines, :] = value.astype(target.dtype)

    def chip(slot):
        arrival(mine.at[slot], local_sem.at[slot])
        arrival(near.at[slot], beside_sem.at[slot])
        return mine.at[slot], near.at[slot]

    def diagonal():
        for at in range(cols):
            combine(passed.at[at], *chip(at))
            peer = {"dp": other} if at < 2 else {"row": across}
            pass_on(passed.at[at], stage.at[at], first_sem.at[at], peer)

    def middle():
        for at in range(cols):
            for turn, here, peer in ((1, at >= 2, {"dp": other}), (2, at < 2, {"row": across})):
                slot = turn * cols + at
                parts = chip(slot)
                if here:
                    arrival(stage.at[at], first_sem.at[at])
                    parts = parts + (stage.at[at],)
                combine(passed.at[slot], *parts)
                pass_on(passed.at[slot], stage.at[slot], second_sem.at[slot - cols], peer)

    def chip_total(at):
        parts = chip(3 * cols + at)
        for turn in (1, 2):
            slot = turn * cols + at
            arrival(stage.at[slot], second_sem.at[slot - cols])
            parts = parts + (stage.at[slot],)
        return parts

    def spread():
        for at in range(2):
            combine(passed.at[3 * cols + at], *chip_total(at))
            pass_on(passed.at[3 * cols + at], last.at[at], col_sem.at[at], {"col": beside_col})
        parts = chip_total(2)
        arrival(last.at[1], col_sem.at[1])
        combine(passed.at[3 * cols + 2], *parts, last.at[1])
        pass_on(passed.at[3 * cols + 2], last.at[2], col_sem.at[2], {"col": two_on})

    def total(target):
        parts = chip_total(3)
        for at in (0, 2):
            arrival(last.at[at], col_sem.at[at])
            parts = parts + (last.at[at],)
        combine(target, *parts)

    return start, diagonal, middle, spread, total


def back_kernel(
    partial,
    mix_part,
    grads,
    scores,
    normed_all,
    mixed,
    cot,
    gates,
    router_t,
    gain_one,
    gain_two,
    x_all,
    w_mine,
    w_out_mine,
    qkv,
    attended,
    cos_table,
    sin_table,
    doc_col,
    doc_row,
    mix_out,
    grads_own,
    dw_pair,
    do_pair,
    router_pair,
    x_grads,
    lines_all,
    scores_in,
    branch,
    branch_all,
    logits,
    logits_all,
    plane_rows,
    rotated,
    values_grad,
    grad_att,
    grad_qkv,
    normed,
    heads,
    heads_near,
    heads_across,
    heads_pair,
    heads_passed,
    dw_send,
    dw_in,
    do_send,
    do_in,
    x_send,
    lines,
    rows_total,
    score_local,
    score_send,
    score_recv,
    ship_local,
    ship_send,
    ship_recv,
    plane_sem,
    gather_send,
    branch_col,
    branch_across,
    branch_beside,
    logits_col,
    logits_across,
    logits_beside,
    heads_send,
    near_sem,
    across_sem,
    pair_sem,
    part_local,
    part_send,
    dw_sem,
    do_sem,
    x_sem,
    swap_sem,
    *groups,
):
    row, across, beside = row_peers()
    rows, cols = lax.axis_size("row"), lax.axis_size("col")
    col, dp = lax.axis_index("col"), lax.axis_index("dp")
    other = 1 - dp
    far = (beside + rows // 2) % rows
    half = col % 2
    pair = col + 1 - 2 * half
    everyone, plane = ("dp", "row", "col"), ("row", "col")
    size, me = group_size_of(everyone), place_in(everyone)
    plane_size, plane_me = group_size_of(plane), place_in(plane)
    low, wide = jnp.bfloat16, jnp.float32
    copies, moved, parts, small, locals_ = [], [], [], [], []
    meet([device_at(everyone, (me + step) % size) for step in range(1, size)])

    def arrival(ref, sem):
        pltpu.make_async_copy(ref, ref, sem).wait()

    def ship(first, last):
        for step in range(first, last):
            to = (plane_me + step) % plane_size
            moved.append(
                send(
                    grads.at[to],
                    grads_own.at[plane_me],
                    ship_send.at[step],
                    ship_recv.at[step],
                    device_at(plane, to),
                )
            )

    def keep(src, dst):
        copy = pltpu.make_async_copy(src, dst, part_local.at[len(locals_)])
        copy.start()
        locals_.append(copy)

    rows_sum = sum_steps(partial, groups[0:11], copies)
    mix_sum = sum_steps(
        mix_part, groups[0:3] + groups[11:12] + groups[4:5] + groups[12:18], copies
    )
    line_local, line_send, line_recv = groups[18:]

    score_own = pltpu.make_async_copy(scores.at[me], scores_in.at[me], score_local)
    score_own.start()
    for step in range(1, size):
        to = (me + step) % size
        small.append(
            send(
                scores.at[to],
                scores_in.at[me],
                score_send.at[step],
                score_recv.at[step],
                device_at(everyone, to),
            )
        )
    rows_sum[0]()
    keep(grads.at[plane_me], grads_own.at[plane_me])
    ship(1, 5)
    tokens, model_width = x_all.shape
    depth = tokens // rows
    for block in range(rows):
        part = slice(block * depth, (block + 1) * depth)
        normed[part, :] = norm_rows(x_all[part, :].astype(wide), gain_one[...])[1]
    rows_sum[1]()
    rows_sum[2]()
    rows_sum[3]()
    score_own.wait()
    for copy in small:
        copy.wait()
    gate = gates[...]
    scored = jnp.concatenate(
        [scores_in[:, 0, :], jnp.zeros((128 - size, 128), wide)], axis=0
    ).T[: gate.shape[0], :]
    grad_logits = gate * (scored - jnp.sum(gate * scored, axis=1, keepdims=True))
    routed = jnp.dot(
        grad_logits, router_t[...].astype(wide), precision=highest, preferred_element_type=wide
    )
    logits[0] = jnp.concatenate(
        [grad_logits, jnp.zeros((128 - gate.shape[0], 128), wide)], axis=0
    ).T[: logits.shape[1], :]
    value = mixed[...]
    scale_two = lax.rsqrt(jnp.mean(value * value, axis=1, keepdims=True) + eps_norm)
    unit_two = value * scale_two
    rows_sum[4](rows_total)
    grad_normed = rows_total[...] + routed
    mix_row = jnp.sum(grad_normed * unit_two, axis=0, keepdims=True)
    grad_scaled = grad_normed * gain_two[...]
    grad_mixed = cot[...].astype(wide) + scale_two * (
        grad_scaled - unit_two * jnp.mean(grad_scaled * unit_two, axis=1, keepdims=True)
    )
    quarter = branch.shape[1]
    for m in range(2):
        branch[m] = (resid_scale * grad_mixed[m * quarter : (m + 1) * quarter, :]).astype(low)

    sent = []

    def pass_on(src, dst, sem, peer):
        sent.append(send(src, dst, gather_send.at[len(sent)], sem, peer))

    def origin(step):
        return (col + cols - step) % cols

    two_on, near, order = col_peers()
    for step, to in ((1, two_on), (2, near)):
        pass_on(branch.at[to // 2], branch_all.at[plane_me], branch_col.at[step], {"col": to})
        pass_on(logits.at[0], logits_all.at[plane_me], logits_col.at[step], {"col": to})
    keep(branch.at[col // 2], branch_all.at[plane_me])
    keep(logits.at[0], logits_all.at[plane_me])
    plans = (
        (branch.at[col // 2], branch_all, branch_col, branch_across, branch_beside),
        (logits.at[0], logits_all, logits_col, logits_across, logits_beside),
    )
    for step in range(cols):
        for mine, target, col_sem, side_sem, core_sem in plans:
            part = target.at[row * cols + order[step]]
            if step > 0:
                arrival(part, col_sem.at[step])
            if step == 1:
                pass_on(part, part, col_sem.at[3], {"col": near})
            source = mine if step == 0 else part
            pass_on(source, part, side_sem.at[step], {"row": across})
            pass_on(source, part, core_sem.at[step], {"row": beside})
    ship(5, 11)
    for step in range(cols):
        for mine, target, col_sem, side_sem, core_sem in plans:
            part = target.at[across * cols + order[step]]
            arrival(part, side_sem.at[step])
            pass_on(part, part, core_sem.at[cols + step], {"row": beside})
    for at, row_from in enumerate((beside, far)):
        for step in range(cols):
            for mine, target, col_sem, side_sem, core_sem in plans:
                arrival(target.at[row_from * cols + order[step]], core_sem.at[at * cols + step])
    for copy in locals_:
        copy.wait()
    for copy in copies:
        copy.wait_send()
    done = len(copies)
    mix_sum[0]()

    branch_rows = branch_all[...].reshape(tokens, model_width)
    kv_at = attended.shape[2]
    count = kv_at // HEAD_DIM
    grad_att[...] = nt(branch_rows, w_out_mine[...]).astype(low)
    rotated[:, kv_at : kv_at + HEAD_DIM] = jnp.zeros((tokens, HEAD_DIM), wide)
    values_grad[...] = jnp.zeros_like(values_grad)
    for block in range(rows):
        part = slice(block * depth, (block + 1) * depth)
        extent = key_extent(block, depth, tokens)
        allowed = visible(doc_col, doc_row, block, depth, extent)
        key = qkv[0:extent, kv_at : kv_at + HEAD_DIM]
        value_rows = qkv[0:extent, kv_at + HEAD_DIM : kv_at + 2 * HEAD_DIM]
        key_sum = jnp.zeros((extent, HEAD_DIM), wide)
        value_sum = jnp.zeros((extent, HEAD_DIM), wide)
        for head in range(count):
            lanes = slice(head * HEAD_DIM, (head + 1) * HEAD_DIM)
            query = qkv[part, lanes]
            probs = attend(query, key, allowed)
            grad_out = grad_att[part, lanes]
            grad_probs = nt(grad_out, value_rows)
            grad_scores = probs * (
                grad_probs - jnp.sum(probs * grad_probs, axis=1, keepdims=True)
            )
            grad_raw = (grad_scores * attn_scale).astype(low)
            rotated[part, lanes] = project(grad_raw, key)
            key_sum = key_sum + tn(grad_raw, query)
            value_sum = value_sum + tn(probs.astype(low), grad_out)
        rotated[0:extent, kv_at : kv_at + HEAD_DIM] += key_sum
        values_grad[0:extent, :] += value_sum
        if block == 1:
            mix_sum[1]()
    for at in range(2):
        piece = slice(at * 128, (at + 1) * 128)
        grad_qkv[:, piece] = turn(rotated[:, piece], cos_table[...], -sin_table[...]).astype(low)
    grad_qkv[:, 256:] = values_grad[...].astype(low)

    rows_each = heads.shape[1]
    projection = w_mine[...].reshape(model_width, w_mine.shape[3])
    heads_sent = []

    def heads_on(src, dst, sem, peer):
        heads_sent.append(send(src, dst, heads_send.at[len(heads_sent)], sem, peer))

    halves = (1 - half, half)
    for at, row_to in enumerate((far, beside, across, row)):
        for which, part in enumerate(halves):
            slot = 2 * at + which
            first = pl.multiple_of((row_to * 2 + part) * rows_each, rows_each)
            heads[slot] = nt(grad_qkv[pl.ds(first, rows_each), :], projection).astype(low)
            if at < 2:
                heads_on(heads.at[slot], heads_near.at[slot], near_sem.at[slot], {"row": beside})
    width = model_width // cols
    heads_out = attended[...].reshape(tokens, kv_at)
    for step in range(cols - 1, -1, -1):
        to = (col + step) % cols
        lanes = pl.ds(pl.multiple_of(to * width, width), width)
        dw_send[to] = tn(grad_qkv[...], normed[:, lanes]).astype(low)
        chunk = branch_all[:, :, lanes].reshape(tokens, width)
        do_send[to] = tn(heads_out, chunk).astype(low)
        if step > 0:
            parts.append(
                send(dw_send.at[to], dw_in.at[col], part_send.at[step], dw_sem.at[step], {"col": to})
            )
            parts.append(
                send(
                    do_send.at[to],
                    do_in.at[col],
                    part_send.at[cols + step],
                    do_sem.at[step],
                    {"col": to},
                )
            )
    keep(dw_send.at[col], dw_in.at[col])
    keep(do_send.at[col], do_in.at[col])

    def heads_sum(slot):
        arrival(heads_near.at[slot - 4], near_sem.at[slot - 4])
        return heads[slot].astype(wide) + heads_near[slot - 4].astype(wide)

    for which in range(2):
        heads_passed[which] = heads_sum(4 + which).astype(low)
        heads_on(
            heads_passed.at[which], heads_across.at[which], across_sem.at[which], {"row": across}
        )
    mix_sum[2]()
    ship(11, plane_size)
    router_sum = jnp.zeros((logits.shape[1], model_width), wide)
    group = plane_rows.shape[0]
    for first in range(0, plane_size, group):
        load = pltpu.make_async_copy(
            normed_all.at[pl.ds(dp * plane_size + first, group)], plane_rows, score_local
        )
        load.start()
        load.wait()
        for at in range(group):
            left = logits_all[first + at, :, 0 : 2 * quarter]
            for _ in range(3):
                piece = left.astype(low)
                left = left - piece.astype(wide)
                router_sum = router_sum + project(piece, plane_rows[at])
    router_pair[dp] = router_sum
    swaps = [
        send(router_pair.at[dp], router_pair.at[dp], swap_sem.at[0], swap_sem.at[1], {"dp": other})
    ]
    for which in range(2):
        grad_one = heads_sum(6 + which)
        arrival(heads_across.at[which], across_sem.at[which])
        grad_one = grad_one + heads_across[which].astype(wide)
        if which == 0:
            heads_passed[2] = grad_one.astype(low)
            heads_on(heads_passed.at[2], heads_pair, pair_sem, {"col": pair})
    arrival(heads_pair, pair_sem)
    grad_one = grad_one + heads_pair[...].astype(wide)
    first = (row * 2 + half) * rows_each
    x_rows = x_all[pl.ds(pl.multiple_of(first, rows_each), rows_each), :].astype(wide)
    scale_one = lax.rsqrt(jnp.mean(x_rows * x_rows, axis=1, keepdims=True) + eps_norm)
    unit_one = x_rows * scale_one
    norm_row = jnp.sum(grad_one * unit_one, axis=0, keepdims=True)
    each = rows_each // quarter
    grad_h = branch_all[pl.ds((row * 2 + half) * each, each)].reshape(rows_each, model_width)
    grad_scaled = grad_one * gain_one[...]
    grad_x = grad_h.astype(wide) * (1.0 / resid_scale) + scale_one * (
        grad_scaled - unit_one * jnp.mean(grad_scaled * unit_one, axis=1, keepdims=True)
    )
    for to in range(cols):
        x_send[to] = grad_x[:, to * width : (to + 1) * width].astype(low)
    for step in range(1, cols):
        to = (col + step) % cols
        swaps.append(
            send(
                x_send.at[to], x_grads.at[col], x_sem.at[step], x_sem.at[cols + step], {"col": to}
            )
        )
    keep(x_send.at[col], x_grads.at[col])
    steps = model_width // 128
    for at in range(steps):
        piece = slice(at * 128, (at + 1) * 128)
        lines[0, at : at + 1, :] = norm_row[:, piece]
        lines[0, steps + at : steps + at + 1, :] = mix_row[:, piece]
    home = pltpu.make_async_copy(lines.at[0], lines_all.at[me], line_local)
    home.start()
    for step in range(1, size):
        swaps.append(
            send(
                lines.at[0],
                lines_all.at[me],
                line_send.at[step],
                line_recv.at[step],
                device_at(everyone, (me + step) % size),
            )
        )
    for copy in locals_[3:]:
        copy.wait()
    for step in range(1, cols):
        arrival(dw_in.at[origin(step)], dw_sem.at[step])
        arrival(do_in.at[origin(step)], do_sem.at[step])
    for h in range(2):
        dw_pair[dp, h] = (dw_in[h].astype(wide) + dw_in[2 + h].astype(wide)).astype(low)
        do_pair[dp, h] = (do_in[h].astype(wide) + do_in[2 + h].astype(wide)).astype(low)
    swaps.append(
        send(dw_pair.at[dp], dw_pair.at[dp], swap_sem.at[2], swap_sem.at[3], {"dp": other})
    )
    swaps.append(
        send(do_pair.at[dp], do_pair.at[dp], swap_sem.at[4], swap_sem.at[5], {"dp": other})
    )
    mix_sum[3]()
    mix_sum[4](mix_out)
    home.wait()
    for copy in swaps:
        copy.wait()
    for copy in moved:
        copy.wait()
    for copy in copies[done:] + parts + sent + heads_sent:
        copy.wait_send()


def back(number, partial, mix_part, grads, scores, normed_all, *rest):
    mixed, _, _, _, _, _, x_all, w_mine, _, qkv, attended = rest[:11]
    cols, rows = lax.axis_size("col"), lax.axis_size("row")
    total, plane = group_size_of(("dp", "row", "col")), group_size_of(("row", "col"))
    low, wide = jnp.bfloat16, jnp.float32
    vmem = pl.BlockSpec(memory_space=pltpu.VMEM)
    shape, dma = jax.ShapeDtypeStruct, pltpu.SemaphoreType.DMA
    tokens, width = x_all.shape
    quarter, heads_width = attended.shape[1:]
    block = partial.shape[1:]
    part = width // cols
    qkv_width = w_mine.shape[3]
    lines = -(-2 * (width // 128) // 8) * 8
    return pl.pallas_call(
        back_kernel,
        out_shape=[
            shape(block, wide),
            shape(grads.shape, low),
            shape((2, 2, qkv_width, part), low),
            shape((2, 2, heads_width, part), low),
            shape((2, total, width), wide),
            shape((cols, tokens // (2 * rows), part), low),
            shape((total, lines, 128), wide),
        ],
        in_specs=[ANYWHERE] * 5 + [vmem] * len(rest),
        out_specs=[vmem, ANYWHERE, vmem, vmem, vmem, vmem, ANYWHERE],
        scratch_shapes=[
            pltpu.VMEM(scores.shape, wide),
            pltpu.VMEM((2, quarter, width), low),
            pltpu.VMEM((plane, quarter, width), low),
            pltpu.VMEM((1, total, 128), wide),
            pltpu.VMEM((plane, total, 128), wide),
            pltpu.VMEM((4,) + block, low),
            pltpu.VMEM((tokens, 256), wide),
            pltpu.VMEM((tokens, HEAD_DIM), wide),
            pltpu.VMEM((tokens, heads_width), low),
            pltpu.VMEM((tokens, qkv_width), low),
            pltpu.VMEM((tokens, width), low),
            pltpu.VMEM((8, tokens // (2 * rows), width), low),
            pltpu.VMEM((4, tokens // (2 * rows), width), low),
            pltpu.VMEM((2, tokens // (2 * rows), width), low),
            pltpu.VMEM((tokens // (2 * rows), width), low),
            pltpu.VMEM((3, tokens // (2 * rows), width), low),
            pltpu.VMEM((cols, qkv_width, part), low),
            pltpu.VMEM((cols, qkv_width, part), low),
            pltpu.VMEM((cols, heads_width, part), low),
            pltpu.VMEM((cols, heads_width, part), low),
            pltpu.VMEM((cols, tokens // (2 * rows), part), low),
            pltpu.VMEM((1, lines, 128), wide),
            pltpu.VMEM(block, wide),
            dma,
            dma((total,)),
            dma((total,)),
            dma,
            dma((plane,)),
            dma((plane,)),
            dma,
            dma((40,)),
            dma((cols,)),
            dma((cols,)),
            dma((2 * cols,)),
            dma((cols,)),
            dma((cols,)),
            dma((2 * cols,)),
            dma((8,)),
            dma((4,)),
            dma((2,)),
            dma,
            dma((8,)),
            dma((2 * cols,)),
            dma((cols,)),
            dma((cols,)),
            dma((2 * cols,)),
            dma((6,)),
        ]
        + sum_scratch(block)
        + [pltpu.VMEM((3 * cols,) + block, low)]
        + sum_scratch(block)[5:]
        + [dma, dma((total,)), dma((total,))],
        compiler_params=pltpu.CompilerParams(
            collective_id=number, has_side_effects=True, vmem_limit_bytes=62 * 2**20
        ),
        name="back" + str(number),
    )(partial, mix_part, grads, scores, normed_all, *rest)


def owned(
    hidden_in,
    norm_gain,
    w_query,
    w_key,
    w_value,
    w_out,
    mix_gain,
    w_router,
    w_gate,
    w_up,
    w_down,
    lengths,
    routes,
    mask,
    cotangent,
):
    everyone = ("dp", "row", "col")
    plane = ("row", "col")
    micro_count, tok_row, width_part = hidden_in.shape
    row_count = lax.axis_size("row")
    col_count = lax.axis_size("col")
    dp_count = lax.axis_size("dp")
    row_at = lax.axis_index("row")
    col_at = lax.axis_index("col")
    dp_at = lax.axis_index("dp")
    plane_count = row_count * col_count
    device_count = plane_count * dp_count
    plane_at = row_at * col_count + col_at
    model_width = width_part * col_count
    kv_here = w_key.shape[1] // HEAD_DIM
    group_size = w_query.shape[1] // w_key.shape[1]
    q_width = group_size * HEAD_DIM
    group_tokens = tok_row * row_count
    quarter = tok_row // col_count
    own_rows = micro_count * quarter
    experts_here, slice_width, ff_width = w_gate.shape
    down_slice = w_down.shape[1]
    experts_all = experts_here * dp_count
    expert_at = dp_at * plane_count + plane_at
    micro_at = col_at // kv_here
    half_at = col_at % kv_here

    masked_cot = cotangent * mask[:, :, None].astype(cotangent.dtype)

    w_qkv = jnp.concatenate(
        [
            w_query.reshape(width_part, kv_here, q_width),
            w_key.reshape(width_part, kv_here, HEAD_DIM),
            w_value.reshape(width_part, kv_here, HEAD_DIM),
        ],
        axis=2,
    ).transpose(1, 0, 2)
    qkv_width = q_width + 2 * HEAD_DIM
    picks = jnp.pad(routes.reshape(own_rows, TOP).T, ((0, 0), (0, 128 - own_rows)), constant_values=-1)
    doc_id, position = documents(lengths[:, 0][micro_at], group_tokens)
    sin_table, cos_table = (
        table[:, 0] for table in angles(position.astype(jnp.float32), HEAD_DIM)
    )
    doc_col = jnp.broadcast_to(doc_id[:, None], (group_tokens, 128))
    doc_row = jnp.broadcast_to(doc_id[None, :], (8, group_tokens))
    cos_lanes = jnp.tile(cos_table, (1, 4))
    sin_lanes = jnp.tile(jnp.concatenate([-sin_table, sin_table], axis=1), (1, 2))
    pad_experts = 128 - experts_all
    table = jnp.any(
        routes.reshape(own_rows, TOP)[:, :, None]
        == jnp.arange(experts_all, dtype=jnp.int32)[None, None, :],
        axis=1,
    )
    router_t = jnp.pad(w_router.T, ((0, pad_experts), (0, 0)))
    cot_own = masked_cot.reshape(own_rows, model_width)
    (
        x_micro,
        w_mine,
        w_out_mine,
        cot_all,
        normed_all,
        qkv,
        attended,
        mixed,
        gates_own,
        rows_part,
        mix_part,
        scores,
        grads,
        grads_down,
    ) = front(
        0,
        hidden_in,
        w_qkv.reshape(kv_here, dp_count, width_part // dp_count, qkv_width),
        w_out.reshape(dp_count, w_out.shape[0] // dp_count, w_out.shape[1]),
        picks,
        cot_own,
        (w_gate, w_up, w_down),
        (norm_gain[None], mix_gain[None]),
        (cos_lanes, sin_lanes),
        (doc_col, doc_row),
        (router_t, jnp.pad(table.astype(jnp.float32), ((0, 0), (0, pad_experts)))),
        q_width,
    )
    expert_mix, grads, qkv_sum, out_sum, router_grad, grad_input, lines = back(
        1,
        rows_part,
        mix_part,
        grads,
        scores,
        normed_all,
        mixed,
        cot_own,
        gates_own,
        router_t,
        norm_gain[None],
        mix_gain[None],
        x_micro,
        w_mine,
        w_out_mine,
        qkv,
        attended,
        cos_lanes,
        sin_lanes,
        doc_col,
        doc_row,
    )
    layer_out = (mixed + resid_scale * expert_mix).astype(jnp.bfloat16)
    out_gate = grads[:, :slice_width].astype(jnp.float32)
    out_up = grads[:, slice_width : 2 * slice_width].astype(jnp.float32)
    out_down = jnp.concatenate(
        [
            grads_down[:, at : at + down_slice]
            for at in range(0, grads_down.shape[1], down_slice)
        ],
        axis=2,
    ).astype(jnp.float32)
    grad_input = grad_input.reshape(micro_count, tok_row, width_part).astype(jnp.float32)
    qkv_sum = jnp.sum(qkv_sum.astype(jnp.float32), axis=0)
    out_sum = jnp.sum(out_sum.astype(jnp.float32), axis=0)
    router_grad = jnp.sum(router_grad, axis=0).T
    lines = jnp.sum(lines, axis=0)
    norm_grad = lines[: model_width // 128].reshape(-1)
    mix_grad = lines[model_width // 128 : 2 * (model_width // 128)].reshape(-1)
    grad_wq = qkv_sum[:, :q_width].reshape(-1, width_part).T
    grad_wk = qkv_sum[:, q_width : q_width + HEAD_DIM].reshape(-1, width_part).T
    grad_wv = qkv_sum[:, q_width + HEAD_DIM :].reshape(-1, width_part).T
    grad_wo = out_sum.reshape(w_out.shape)
    return (
        layer_out.reshape(micro_count, quarter, model_width),
        grad_input,
        norm_grad,
        grad_wq,
        grad_wk,
        grad_wv,
        grad_wo,
        mix_grad,
        router_grad,
        out_gate,
        out_up,
        out_down,
    )


def solution(mesh):
    dp_count, row_count, col_count = (mesh.shape[name] for name in ("dp", "row", "col"))

    def body(*args):
        hidden_in, w_key, w_gate = args[0], args[3], args[8]
        kv_here = w_key.shape[1] // HEAD_DIM
        one_each = w_gate.shape[0] == row_count * col_count
        pairs = hidden_in.shape[0] * kv_here == col_count
        sizes = (dp_count, row_count, col_count, kv_here) == (2, 4, 4, 2)
        return (owned if sizes and one_each and pairs else shards)(*args)

    placed = (
        P(None, ("dp", "row"), "col"),
        P(),
        P("col", "row"),
        P("col", "row"),
        P("col", "row"),
        P("row", "col"),
        P(),
        P(),
        P("dp", ("row", "col"), None),
        P("dp", ("row", "col"), None),
        P("dp", ("row", "col"), None),
        P(None, "dp", None),
        P(None, ("dp", "row", "col"), None),
        P(None, ("dp", "row", "col")),
        P(None, ("dp", "row", "col"), None),
    )
    return jax.shard_map(
        body,
        mesh=mesh,
        in_specs=placed,
        out_specs=(
            P(None, ("dp", "row", "col"), None),
            P(None, ("dp", "row"), "col"),
            P(),
            P("col", "row"),
            P("col", "row"),
            P("col", "row"),
            P("row", "col"),
            P(),
            P(),
            P("dp", ("row", "col"), None),
            P("dp", ("row", "col"), None),
            P("dp", ("row", "col"), None),
        ),
        check_vma=False,
    )
```

```python
import functools

import jax
import jax.numpy as jnp
from jax import lax
from jax.experimental import pallas as pl
from jax.experimental.pallas import tpu as pltpu
from jax.sharding import PartitionSpec as P

D = 1536
HEAD_DIM = 64
TOP = 8


eps_norm = 1e-06
resid_scale = 0.22
attn_scale = 0.015625
rope_base = 10000.0
highest = lax.Precision.HIGHEST


def shortened(shard):
    return jax.tree.map(lambda a: a.astype(jnp.bfloat16) if a.dtype == jnp.float32 else a, shard)


def documents(doc_lengths, length_all):
    doc_ends = jnp.cumsum(doc_lengths, dtype=jnp.int32)
    doc_starts = doc_ends - doc_lengths
    positions = jnp.arange(length_all, dtype=jnp.int32)
    doc_id = jnp.sum(
        (positions[:, None] >= doc_ends[None, :]).astype(jnp.int32), axis=1, dtype=jnp.int32
    )
    member = doc_id[:, None] == jnp.arange(doc_lengths.shape[0], dtype=jnp.int32)[None, :]
    doc_start = jnp.sum(jnp.where(member, doc_starts[None, :], 0), axis=1, dtype=jnp.int32)
    return (doc_id, positions - doc_start)


def angles(position, head_width):
    half_width = head_width // 2
    frequency = rope_base ** (-2.0 * jnp.arange(half_width, dtype=jnp.float32) / head_width)
    turned = position[:, None] * frequency[None, :]
    return (jnp.sin(turned)[:, None, :], jnp.cos(turned)[:, None, :])


def rotate(values, sin_table, cos_table):
    half_width = values.shape[-1] // 2
    front_half = values[..., :half_width]
    back_half = values[..., half_width:]
    return jnp.concatenate(
        [
            front_half * cos_table - back_half * sin_table,
            back_half * cos_table + front_half * sin_table,
        ],
        axis=-1,
    )


def gather_rows(value):
    return lax.all_gather(value, "row", axis=0, tiled=True)


def gather_cols(value):
    return jax.tree.map(
        lambda part, own: part.astype(own.dtype),
        lax.all_gather(shortened(value), "col", axis=0, tiled=True),
        value,
    )


def sum_cols(pieces):
    return lax.psum_scatter(pieces, "col", scatter_dimension=0, tiled=True)


def sum_rows(pieces):
    return lax.psum_scatter(pieces, "row", scatter_dimension=0, tiled=True)


def width_total(value):
    return lax.psum(value, "col")


def expert_trade(value):
    return lax.all_to_all(value, "dp", split_axis=1, concat_axis=1, tiled=True)


def attn_total(value):
    return jax.tree.map(lambda part: part.astype(jnp.float32), lax.psum(shortened(value), "dp"))


def expert_total(value):
    return jax.tree.map(
        lambda part: part.astype(jnp.float32),
        lax.psum_scatter(shortened(value), ("row", "col"), scatter_dimension=1, tiled=True),
    )


def add_all(first_set, second_set):
    return tuple((left_one + right_one for left_one, right_one in zip(first_set, second_set)))


def project(left_side, right_side):
    return jnp.dot(left_side, right_side, preferred_element_type=jnp.float32)


def shards(
    hidden_in,
    norm_gain,
    w_query,
    w_key,
    w_value,
    w_out,
    mix_gain,
    w_router,
    w_gate,
    w_up,
    w_down,
    lengths,
    routes,
    mask,
    cotangent,
):
    micro_count = hidden_in.shape[0]
    tok_dev = hidden_in.shape[1]
    width_part = hidden_in.shape[2]
    col_count = lax.axis_size("col")
    row_count = lax.axis_size("row")
    dp_count = lax.axis_size("dp")
    col_at = lax.axis_index("col")
    model_width = D
    heads_here = w_query.shape[1] // HEAD_DIM
    kv_here = w_key.shape[1] // HEAD_DIM
    group_size = heads_here // kv_here
    group_tokens = tok_dev * row_count
    quarter = tok_dev // col_count
    experts_here = w_gate.shape[0]
    experts_all = experts_here * dp_count
    capacity = quarter * 3 // 8
    slot_count = experts_all * capacity
    gain_part = lax.dynamic_slice_in_dim(norm_gain, col_at * width_part, width_part)
    router_wide = w_router.astype(jnp.float32)
    full_gate, full_up, full_down = (
        lax.all_gather(w_gate, ("row", "col"), axis=1, tiled=True),
        lax.all_gather(w_up, ("row", "col"), axis=1, tiled=True),
        lax.all_gather(w_down, ("row", "col"), axis=1, tiled=True),
    )
    expert_ids = jnp.arange(experts_all, dtype=jnp.int32)
    group_index = jnp.arange(group_tokens, dtype=jnp.int32)
    query_start = col_at * tok_dev
    query_index = query_start + jnp.arange(tok_dev, dtype=jnp.int32)
    attn_local = (
        jnp.zeros(w_query.shape, jnp.float32),
        jnp.zeros(w_key.shape, jnp.float32),
        jnp.zeros(w_value.shape, jnp.float32),
        jnp.zeros(w_out.shape, jnp.float32),
    )
    expert_local = (
        jnp.zeros(full_gate.shape, jnp.float32),
        jnp.zeros(full_up.shape, jnp.float32),
        jnp.zeros(full_down.shape, jnp.float32),
    )
    router_acc = jnp.zeros(w_router.shape, jnp.float32)
    norm_acc = jnp.zeros((width_part,), jnp.float32)
    mix_acc = jnp.zeros((model_width,), jnp.float32)
    layer_rows = []
    input_grads = []
    for step in range(micro_count):
        x_full = hidden_in[step].astype(jnp.float32)
        squares = width_total(jnp.sum(x_full * x_full, axis=1))
        scale_one = lax.rsqrt(squares / model_width + eps_norm)[:, None]
        unit_one = x_full * scale_one
        normed = (unit_one * gain_part).astype(jnp.bfloat16)
        normed_all = gather_rows(normed)
        query_p, key_p, value_p = sum_cols(
            (project(normed_all, w_query), project(normed_all, w_key), project(normed_all, w_value))
        )
        doc_all, pos_all = documents(lengths[step, 0], group_tokens)
        doc_query = lax.dynamic_slice_in_dim(doc_all, query_start, tok_dev)
        pos_query = lax.dynamic_slice_in_dim(pos_all, query_start, tok_dev).astype(jnp.float32)
        sin_table, cos_table = angles(pos_query, HEAD_DIM)
        query_rot = rotate(
            query_p.reshape(tok_dev, heads_here, HEAD_DIM), sin_table, cos_table
        ).astype(jnp.bfloat16)
        key_rot = rotate(key_p.reshape(tok_dev, kv_here, HEAD_DIM), sin_table, cos_table).astype(
            jnp.bfloat16
        )
        value_low = value_p.astype(jnp.bfloat16).reshape(tok_dev, kv_here, HEAD_DIM)
        keys_all, values_all = (
            lax.all_gather(key_rot, "col", axis=0, tiled=True),
            lax.all_gather(value_low, "col", axis=0, tiled=True),
        )
        allowed = (doc_query[:, None] == doc_all[None, :]) & (
            group_index[None, :] <= query_index[:, None]
        )
        query_grp = query_rot.reshape(tok_dev, kv_here, group_size, HEAD_DIM)
        raw_scores = jnp.einsum(
            "qhgd,khd->hgqk", query_grp, keys_all, preferred_element_type=jnp.float32
        )
        scores = jnp.where(allowed[None, None], raw_scores * attn_scale, -1e30)
        top_score = jnp.max(scores, axis=-1, keepdims=True)
        expd = jnp.exp(scores - top_score)
        row_total = jnp.sum(expd, axis=-1, keepdims=True)
        attn_probs = expd / row_total
        log_total = top_score + jnp.log(row_total)
        probs_low = attn_probs.astype(jnp.bfloat16)
        attended = jnp.einsum(
            "hgqk,khd->qhgd", probs_low, values_all, preferred_element_type=jnp.float32
        )
        attended_low = attended.reshape(tok_dev, heads_here * HEAD_DIM).astype(jnp.bfloat16)
        attended_all = gather_cols(attended_low)
        attn_branch = sum_rows(project(attended_all, w_out))
        mixed = x_full + resid_scale * attn_branch
        mixed_rows = lax.all_to_all(
            mixed.reshape(col_count, quarter, width_part),
            "col",
            split_axis=0,
            concat_axis=2,
            tiled=True,
        ).reshape(quarter, model_width)
        scale_two = lax.rsqrt(jnp.mean(mixed_rows * mixed_rows, axis=1, keepdims=True) + eps_norm)
        unit_two = mixed_rows * scale_two
        normed_two = (unit_two * mix_gain).astype(jnp.bfloat16)
        logits = project(normed_two, w_router)
        picks = routes[step]
        choose = (picks[:, :, None] == expert_ids[None, None, :]).astype(jnp.float32)
        chosen = jnp.sum(choose * logits[:, None, :], axis=-1)
        gate_weights = jax.nn.softmax(chosen, axis=-1)
        flat_picks = picks.reshape(-1)
        hit_table = (flat_picks[:, None] == expert_ids[None, :]).astype(jnp.int32)
        slot_rank = jnp.sum(
            hit_table * (jnp.cumsum(hit_table, axis=0, dtype=jnp.int32) - 1),
            axis=1,
            dtype=jnp.int32,
        )
        owner_dp = flat_picks // experts_here
        local_expert = flat_picks % experts_here
        slot_index = local_expert * (dp_count * capacity) + owner_dp * capacity + slot_rank
        token_of = (
            jnp.full((slot_count,), quarter, jnp.int32)
            .at[slot_index]
            .set(jnp.arange(quarter * TOP, dtype=jnp.int32) // TOP)
        )
        padded = jnp.concatenate([normed_two, jnp.zeros((1, model_width), jnp.bfloat16)], axis=0)
        send_rows = padded[token_of].reshape(experts_here, dp_count * capacity, model_width)
        expert_in = expert_trade(send_rows)
        gate_proj = jnp.einsum(
            "ecd,edf->ecf", expert_in, full_gate, preferred_element_type=jnp.float32
        )
        up_proj = jnp.einsum("ecd,edf->ecf", expert_in, full_up, preferred_element_type=jnp.float32)
        activated = (jax.nn.silu(gate_proj) * up_proj).astype(jnp.bfloat16)
        expert_out = jnp.einsum(
            "ecf,efd->ecd", activated, full_down, preferred_element_type=jnp.float32
        ).astype(jnp.bfloat16)
        returned = expert_trade(expert_out).reshape(slot_count, model_width)
        combined = returned[slot_index].reshape(quarter, TOP, model_width).astype(jnp.float32)
        expert_mix = jnp.sum(gate_weights[:, :, None] * combined, axis=1)
        layer_rows.append((mixed_rows + resid_scale * expert_mix).astype(jnp.bfloat16))
        grad_rows = cotangent[step].astype(jnp.float32) * mask[step][:, None].astype(jnp.float32)
        grad_mix = resid_scale * grad_rows
        grad_gates = jnp.sum(grad_mix[:, None, :] * combined, axis=-1)
        grad_chosen = gate_weights * (
            grad_gates - jnp.sum(gate_weights * grad_gates, axis=-1, keepdims=True)
        )
        grad_logits = jnp.sum(choose * grad_chosen[:, :, None], axis=1)
        gate_slots = (
            jnp.zeros((slot_count,), jnp.float32).at[slot_index].set(gate_weights.reshape(-1))
        )
        grad_pad = jnp.concatenate([grad_mix, jnp.zeros((1, model_width), jnp.float32)], axis=0)
        grad_send = (gate_slots[:, None] * grad_pad[token_of]).astype(jnp.bfloat16)
        grad_expert = expert_trade(
            grad_send.reshape(experts_here, dp_count * capacity, model_width)
        )
        grad_act = jnp.einsum(
            "ecd,efd->ecf", grad_expert, full_down, preferred_element_type=jnp.float32
        )
        micro_down = jnp.einsum(
            "ecf,ecd->efd", activated, grad_expert, preferred_element_type=jnp.float32
        )
        sigmoid_gate = jax.nn.sigmoid(gate_proj)
        silu_gate = gate_proj * sigmoid_gate
        grad_gate_p = (
            grad_act * up_proj * (sigmoid_gate + gate_proj * sigmoid_gate * (1.0 - sigmoid_gate))
        ).astype(jnp.bfloat16)
        grad_up_p = (grad_act * silu_gate).astype(jnp.bfloat16)
        grad_in = jnp.einsum(
            "ecf,edf->ecd", grad_gate_p, full_gate, preferred_element_type=jnp.float32
        ) + jnp.einsum("ecf,edf->ecd", grad_up_p, full_up, preferred_element_type=jnp.float32)
        micro_gate = jnp.einsum(
            "ecd,ecf->edf", expert_in, grad_gate_p, preferred_element_type=jnp.float32
        )
        micro_up = jnp.einsum(
            "ecd,ecf->edf", expert_in, grad_up_p, preferred_element_type=jnp.float32
        )
        expert_local = add_all(expert_local, (micro_gate, micro_up, micro_down))
        grad_back = expert_trade(grad_in.astype(jnp.bfloat16)).reshape(slot_count, model_width)
        grad_normed = jnp.sum(
            grad_back[slot_index].reshape(quarter, TOP, model_width).astype(jnp.float32), axis=1
        ) + jnp.dot(grad_logits, router_wide.T, precision=highest)
        router_acc = router_acc + jnp.dot(
            normed_two.astype(jnp.float32).T, grad_logits, precision=highest
        )
        mix_acc = mix_acc + jnp.sum(grad_normed * unit_two, axis=0)
        grad_scaled = grad_normed * mix_gain
        grad_mixed_rows = grad_rows + scale_two * (
            grad_scaled - unit_two * jnp.mean(grad_scaled * unit_two, axis=1, keepdims=True)
        )
        grad_mixed = lax.all_to_all(
            grad_mixed_rows.reshape(1, quarter, model_width),
            "col",
            split_axis=2,
            concat_axis=0,
            tiled=True,
        ).reshape(tok_dev, width_part)
        grad_branch = (resid_scale * grad_mixed).astype(jnp.bfloat16)
        grad_branch_all = gather_rows(grad_branch)
        micro_out = jnp.dot(attended_all.T, grad_branch_all, preferred_element_type=jnp.float32)
        grad_attended = sum_cols(
            jnp.dot(grad_branch_all, w_out.T, preferred_element_type=jnp.float32)
        )
        grad_att_low = grad_attended.astype(jnp.bfloat16).reshape(
            tok_dev, kv_here, group_size, HEAD_DIM
        )
        probs_again = jnp.exp(scores - log_total)
        grad_probs = jnp.einsum(
            "qhgd,khd->hgqk", grad_att_low, values_all, preferred_element_type=jnp.float32
        )
        grad_scores = probs_again * (
            grad_probs - jnp.sum(probs_again * grad_probs, axis=-1, keepdims=True)
        )
        grad_raw = (grad_scores * attn_scale).astype(jnp.bfloat16)
        probs_again_low = probs_again.astype(jnp.bfloat16)
        grad_query = jnp.einsum(
            "hgqk,khd->qhgd", grad_raw, keys_all, preferred_element_type=jnp.float32
        )
        grad_key_part = jnp.einsum(
            "hgqk,qhgd->khd", grad_raw, query_grp, preferred_element_type=jnp.float32
        )
        grad_value_part = jnp.einsum(
            "hgqk,qhgd->khd", probs_again_low, grad_att_low, preferred_element_type=jnp.float32
        )
        grad_key, grad_value = sum_cols(
            (
                grad_key_part.reshape(group_tokens, kv_here * HEAD_DIM),
                grad_value_part.reshape(group_tokens, kv_here * HEAD_DIM),
            )
        )
        grad_query_p = (
            rotate(grad_query.reshape(tok_dev, heads_here, HEAD_DIM), -sin_table, cos_table)
            .astype(jnp.bfloat16)
            .reshape(tok_dev, heads_here * HEAD_DIM)
        )
        grad_key_p = (
            rotate(grad_key.reshape(tok_dev, kv_here, HEAD_DIM), -sin_table, cos_table)
            .astype(jnp.bfloat16)
            .reshape(tok_dev, kv_here * HEAD_DIM)
        )
        grad_value_p = grad_value.astype(jnp.bfloat16)
        query_all, key_all, value_all = gather_cols((grad_query_p, grad_key_p, grad_value_p))
        micro_query = jnp.dot(normed_all.T, query_all, preferred_element_type=jnp.float32)
        micro_key = jnp.dot(normed_all.T, key_all, preferred_element_type=jnp.float32)
        micro_value = jnp.dot(normed_all.T, value_all, preferred_element_type=jnp.float32)
        grad_normed_one = sum_rows(
            jnp.dot(query_all, w_query.T, preferred_element_type=jnp.float32)
            + jnp.dot(key_all, w_key.T, preferred_element_type=jnp.float32)
            + jnp.dot(value_all, w_value.T, preferred_element_type=jnp.float32)
        )
        grad_scaled_one = grad_normed_one * gain_part
        inner_sum = width_total(jnp.sum(grad_scaled_one * unit_one, axis=1))
        norm_acc = norm_acc + jnp.sum(grad_normed_one * unit_one, axis=0)
        input_grads.append(
            grad_mixed
            + scale_one * (grad_scaled_one - unit_one * (inner_sum / model_width)[:, None])
        )
        attn_local = add_all(attn_local, (micro_query, micro_key, micro_value, micro_out))
    attn_summed = attn_total(attn_local)
    expert_summed = expert_total(expert_local)
    gain_full = lax.dynamic_update_slice_in_dim(
        jnp.zeros((model_width,), jnp.float32), norm_acc, col_at * width_part, 0
    )
    router_grad, gain_grad, mix_grad = lax.psum(
        (router_acc, gain_full, mix_acc), ("dp", "row", "col")
    )
    return (
        jnp.stack(layer_rows),
        jnp.stack(input_grads),
        gain_grad,
        attn_summed[0],
        attn_summed[1],
        attn_summed[2],
        attn_summed[3],
        mix_grad,
        router_grad,
        expert_summed[0],
        expert_summed[1],
        expert_summed[2],
    )


MESH = pl.DeviceIdType.MESH
ANYWHERE = pl.BlockSpec(memory_space=pl.ANY)


def group_size_of(axes):
    total = 1
    for axis in axes:
        total = total * lax.axis_size(axis)
    return total


def place_in(axes):
    at = 0
    for axis in axes:
        at = at * lax.axis_size(axis) + lax.axis_index(axis)
    return at


def device_at(axes, index):
    place = {}
    for axis in reversed(axes):
        place[axis] = index % lax.axis_size(axis)
        index = index // lax.axis_size(axis)
    return place


def meet(peers):
    barrier = pltpu.get_barrier_semaphore()
    for peer in peers:
        pl.semaphore_signal(barrier, inc=1, device_id=peer, device_id_type=MESH)
    pl.semaphore_wait(barrier, len(peers))


def send(src, dst, send_sem, recv_sem, peer):
    copy = pltpu.make_async_remote_copy(
        src_ref=src,
        dst_ref=dst,
        send_sem=send_sem,
        recv_sem=recv_sem,
        device_id=peer,
        device_id_type=MESH,
    )
    copy.start()
    return copy


def row_peers():
    row = lax.axis_index("row")
    rows = lax.axis_size("row")
    across = (row + rows // 2) % rows
    beside = row + 1 - 2 * (row % 2)
    return row, across, beside


def col_peers():
    col, cols = lax.axis_index("col"), lax.axis_size("col")
    two_on = (col + 2) % cols
    near = col + 1 - 2 * (col % 2)
    return two_on, near, (col, two_on, near, (near + 2) % cols)


def gather_line(source, target, sems, copies):
    local_sem, send_sem, col_sem, dp_sem, across_sem, beside_sem = sems
    row, across, beside = row_peers()
    rows, cols = lax.axis_size("row"), lax.axis_size("col")
    dp = lax.axis_index("dp")
    other = 1 - dp
    two_on, near, order = col_peers()
    far = (beside + rows // 2) % rows
    sent = []

    def block_of(dp_from, row_from, step):
        return (dp_from * rows + row_from) * cols + order[step]

    def arrival(block, sem):
        pltpu.make_async_copy(target.at[block], target.at[block], sem).wait()

    def pass_on(part, block, sem, peer):
        copy = send(part, target.at[block], send_sem.at[len(sent)], sem, peer)
        sent.append(copy)
        copies.append(copy)

    me = block_of(dp, row, 0)
    own = pltpu.make_async_copy(source.at[0], target.at[me], local_sem)

    def begin():
        own.start()
        pass_on(source.at[0], me, col_sem.at[1], {"col": two_on})
        pass_on(source.at[0], me, col_sem.at[2], {"col": near})

    def line(step):
        block = block_of(dp, row, step)
        part = source.at[0] if step == 0 else target.at[block]
        if step > 0:
            arrival(block, col_sem.at[step])
        if step == 1:
            pass_on(part, block, col_sem.at[3], {"col": near})
        pass_on(part, block, dp_sem.at[step], {"dp": other})
        pass_on(part, block, across_sem.at[step], {"row": across})
        pass_on(part, block, beside_sem.at[step], {"row": beside})

    def side(step):
        block = block_of(other, row, step)
        arrival(block, dp_sem.at[step])
        pass_on(target.at[block], block, beside_sem.at[cols + step], {"row": beside})
        block = block_of(dp, across, step)
        arrival(block, across_sem.at[step])
        pass_on(target.at[block], block, dp_sem.at[cols + step], {"dp": other})
        pass_on(target.at[block], block, beside_sem.at[2 * cols + step], {"row": beside})

    def corner(step):
        block = block_of(other, across, step)
        arrival(block, dp_sem.at[cols + step])
        pass_on(target.at[block], block, beside_sem.at[3 * cols + step], {"row": beside})

    def finish():
        for turn, (dp_from, row_from) in enumerate(
            ((dp, beside), (other, beside), (dp, far), (other, far))
        ):
            for step in range(cols):
                arrival(block_of(dp_from, row_from, step), beside_sem.at[turn * cols + step])
        own.wait()

    return begin, line, side, corner, finish


def gather_sems():
    cols = lax.axis_size("col")
    return [
        pltpu.SemaphoreType.DMA,
        pltpu.SemaphoreType.DMA((40,)),
        pltpu.SemaphoreType.DMA((cols,)),
        pltpu.SemaphoreType.DMA((2 * cols,)),
        pltpu.SemaphoreType.DMA((2 * cols,)),
        pltpu.SemaphoreType.DMA((4 * cols,)),
    ]


def nt(left, right):
    return lax.dot_general(
        left, right, (((1,), (1,)), ((), ())), preferred_element_type=jnp.float32
    )


def tn(left, right):
    return lax.dot_general(
        left, right, (((0,), (0,)), ((), ())), preferred_element_type=jnp.float32
    )


def norm_rows(x, gain):
    scale = lax.rsqrt(jnp.mean(x * x, axis=1, keepdims=True) + eps_norm)
    return scale, (x * scale * gain).astype(jnp.bfloat16)


def turn(values, cos_table, sin_table):
    lane = lax.broadcasted_iota(jnp.int32, values.shape, 1)
    ahead = pltpu.roll(values, values.shape[1] - HEAD_DIM // 2, 1)
    behind = pltpu.roll(values, HEAD_DIM // 2, 1)
    return values * cos_table + jnp.where(lane % HEAD_DIM < HEAD_DIM // 2, ahead, behind) * sin_table


def key_extent(block, rows, total):
    return min(total, -(-(block + 1) * rows // 128) * 128)


def visible(doc_col, doc_row, block, rows, extent):
    query = block * rows + lax.broadcasted_iota(jnp.int32, (rows, extent), 0)
    keys = lax.broadcasted_iota(jnp.int32, (rows, extent), 1)
    same = doc_col[block * rows : (block + 1) * rows, 0:1] == doc_row[0:1, 0:extent]
    return same & (keys <= query)


def attend(query, key, allowed):
    scores = jnp.where(allowed, nt(query, key) * attn_scale, -1e30)
    raised = jnp.exp(scores - jnp.max(scores, axis=1, keepdims=True))
    return raised / jnp.sum(raised, axis=1, keepdims=True)


def front_kernel(
    x,
    w_qkv,
    w_out,
    picks,
    cot,
    w_gate,
    w_up,
    w_down,
    gain_one,
    gain_two,
    cos_table,
    sin_table,
    doc_col,
    doc_row,
    router_t,
    table,
    x_all,
    w_mine,
    w_out_mine,
    cot_all,
    normed_all,
    qkv,
    attended,
    mixed,
    gates_own,
    rows_part,
    mix_part,
    scores,
    grads_gu,
    grads_down,
    w_out_all,
    picks_all,
    x_own,
    att_own,
    normed_two,
    gate_up,
    down,
    down_grad,
    pool_rows,
    pool_cots,
    kept_in,
    kept_dy,
    kept_dye,
    kept_act,
    kept_gate,
    kept_up,
    gate_proj,
    up_proj,
    kept_weight,
    ranks,
    upper,
    load_sem,
    store_sem,
    grad_local,
    grad_send,
    grad_recv,
    local_sem,
    send_sem,
    x_sem,
    q_sem,
    o_sem,
    own_sem,
    att_send,
    att_recv,
    ship_local,
    ship_send,
    ship_recv,
    *line_sems,
):
    row, across, beside = row_peers()
    rows, cols = lax.axis_size("row"), lax.axis_size("col")
    col, dp = lax.axis_index("col"), lax.axis_index("dp")
    other = 1 - dp
    far = (beside + rows // 2) % rows
    plane = ("row", "col")
    size, me = group_size_of(plane), place_in(plane)
    low = jnp.bfloat16
    meet(
        [device_at(plane, (me + step) % size) for step in range(1, size)] + [{"dp": other}]
    )
    copies, locals_, sent, moved = [], [], [], []
    picks_line = gather_line(picks, picks_all, line_sems[0:6], copies)
    cot_line = gather_line(cot, cot_all, line_sems[6:12], copies)
    norm_line = gather_line(normed_two, normed_all, line_sems[12:18], copies)

    def pass_on(src, dst, sem, peer):
        sent.append(send(src, dst, send_sem.at[len(sent)], sem, peer))

    def arrival(ref, sem):
        pltpu.make_async_copy(ref, ref, sem).wait()

    def local(src, dst):
        copy = pltpu.make_async_copy(src, dst, local_sem.at[len(locals_)])
        copy.start()
        locals_.append(copy)

    slice_rows, ff_width = w_gate.shape[1:]
    down_rows = w_down.shape[1]
    chunks = w_down.shape[2] // ff_width

    def weight_parts(to, at):
        parts = [
            (w_gate.at[to], gate_up.at[at, 0:slice_rows]),
            (w_up.at[to], gate_up.at[at, slice_rows : 2 * slice_rows]),
        ]
        for chunk in range(chunks):
            parts.append(
                (
                    w_down.at[to, :, chunk * ff_width : (chunk + 1) * ff_width],
                    down.at[at, chunk * down_rows : (chunk + 1) * down_rows],
                )
            )
        return parts

    def ship(first, last, which=range(2)):
        for step in range(first, last):
            to = (me + step) % size
            for part in which:
                source, target = weight_parts(to, me)[part]
                moved.append(
                    send(
                        source,
                        target,
                        ship_send.at[part, step],
                        ship_recv.at[part, step],
                        device_at(plane, to),
                    )
                )

    def shipped(which):
        for step in range(1, size):
            for part in which:
                arrival(
                    weight_parts(me, (me + size - step) % size)[part][1], ship_recv.at[part, step]
                )

    def origin(step):
        return (col + cols - step) % cols

    two_on, near, order = col_peers()

    micro, depth, width = x.shape
    quarter = depth // cols
    half_depth = w_out.shape[1]

    def lanes_of(at):
        return pl.ds(pl.multiple_of(at * width, width), width)

    def lanes(step):
        return lanes_of(order[step])

    def x_at(row_from, step):
        return x_all.at[pl.ds(pl.multiple_of(row_from * depth, depth), depth), lanes(step)]

    def out_at(row_from, step, half):
        first = pl.multiple_of((row_from * 2 + half) * half_depth, half_depth)
        return w_out_all.at[pl.ds(first, half_depth), lanes(step)]

    def own_at(m, step):
        return x_own.at[pl.ds(m * quarter, quarter), lanes_of(origin(step))]

    my_x = x_at(row, 0)
    for step in range(1, cols):
        to = (col + step) % cols
        if step < 3:
            peer = (two_on, near)[step - 1]
            pass_on(x.at[peer // 2], my_x, x_sem.at[step], {"col": peer})
        pass_on(w_qkv.at[to % 2, dp], w_mine.at[col, dp], q_sem.at[step], {"col": to})
    local(x.at[col // 2], my_x)
    local(w_qkv.at[col % 2], w_mine.at[col])
    for half in range(2):
        local(w_out.at[half], out_at(row, 0, half))
    pass_on(x.at[col // 2], my_x, x_sem.at[cols], {"row": across})
    pass_on(x.at[col // 2], my_x, x_sem.at[2 * cols], {"row": beside})
    for step in range(1, cols):
        to = (col + step) % cols
        if step < 3:
            peer = (two_on, near)[step - 1]
            pass_on(w_out.at[dp], out_at(row, 0, dp), o_sem.at[step], {"col": peer})
        first = pl.multiple_of(to * quarter, quarter)
        for m in range(micro):
            pass_on(
                x.at[m, pl.ds(first, quarter)],
                own_at(m, 0),
                own_sem.at[m * cols + step],
                {"col": to},
            )
    for m in range(micro):
        local(x.at[m, pl.ds(pl.multiple_of(col * quarter, quarter), quarter)], own_at(m, 0))
    for half in range(2):
        pass_on(w_out.at[half], out_at(row, 0, half), o_sem.at[(2 + half) * cols], {"row": across})
        pass_on(w_out.at[half], out_at(row, 0, half), o_sem.at[(4 + half) * cols], {"row": beside})
    for step in range(1, cols):
        part = x_at(row, step)
        arrival(part, x_sem.at[step])
        if step == 1:
            pass_on(part, part, x_sem.at[3], {"col": near})
        pass_on(part, part, x_sem.at[cols + step], {"row": across})
        pass_on(part, part, x_sem.at[2 * cols + step], {"row": beside})
        part = w_mine.at[origin(step), dp]
        arrival(part, q_sem.at[step])
        pass_on(part, part, q_sem.at[cols + step], {"dp": other})
    for step in range(cols):
        part = x_at(across, step)
        arrival(part, x_sem.at[cols + step])
        pass_on(part, part, x_sem.at[3 * cols + step], {"row": beside})
    for step in range(1, cols):
        part = out_at(row, step, dp)
        arrival(part, o_sem.at[step])
        if step == 1:
            pass_on(part, part, o_sem.at[3], {"col": near})
        pass_on(part, part, o_sem.at[cols + step], {"dp": other})
        pass_on(part, part, o_sem.at[2 * cols + step], {"row": across})
        pass_on(part, part, o_sem.at[4 * cols + step], {"row": beside})
    picks_line[0]()
    cot_line[0]()
    for source, target in weight_parts(me, me):
        local(source, target)
    for step in range(1, cols):
        arrival(w_mine.at[origin(step), other], q_sem.at[cols + step])
    for at, row_from in enumerate((beside, far)):
        for step in range(cols):
            arrival(x_at(row_from, step), x_sem.at[(2 + at) * cols + step])
    for copy in locals_[:6]:
        copy.wait()

    tokens, model_width = x_all.shape
    projection = w_mine[...].reshape(model_width, w_mine.shape[3])
    for block in range(rows):
        part = slice(block * depth, (block + 1) * depth)
        _, normed = norm_rows(x_all[part, :].astype(jnp.float32), gain_one[...])
        values = project(normed, projection)
        cosine, sine = cos_table[part, :], sin_table[part, :]
        for at in range(2):
            piece = slice(at * 128, (at + 1) * 128)
            qkv[part, piece] = turn(values[:, piece], cosine, sine).astype(low)
        qkv[part, 256:] = values[:, 256:].astype(low)
    heads = attended.shape[2] // HEAD_DIM
    kv_at = heads * HEAD_DIM
    for block in range(rows):
        extent = key_extent(block, depth, tokens)
        allowed = visible(doc_col, doc_row, block, depth, extent)
        key = qkv[0:extent, kv_at : kv_at + HEAD_DIM]
        value = qkv[0:extent, kv_at + HEAD_DIM : kv_at + 2 * HEAD_DIM]
        outs = []
        for head in range(heads):
            query = qkv[
                block * depth : (block + 1) * depth, head * HEAD_DIM : (head + 1) * HEAD_DIM
            ]
            outs.append(project(attend(query, key, allowed).astype(low), value))
        out = jnp.concatenate(outs, axis=1).astype(low)
        attended[block * cols : (block + 1) * cols] = out.reshape(cols, quarter, out.shape[1])
    for step in range(1, size):
        to = (me + step) % size
        moved.append(
            send(
                attended.at[to],
                att_own.at[me],
                att_send.at[step],
                att_recv.at[step],
                device_at(plane, to),
            )
        )
    stay = pltpu.make_async_copy(attended.at[me], att_own.at[me], att_send.at[0])
    stay.start()
    ship(1, 5)
    for step in range(1, cols):
        part = out_at(row, step, other)
        arrival(part, o_sem.at[cols + step])
        pass_on(part, part, o_sem.at[3 * cols + step], {"row": across})
        pass_on(part, part, o_sem.at[5 * cols + step], {"row": beside})
    for step in range(cols):
        picks_line[1](step)
        cot_line[1](step)
    for at in range(2):
        for step in range(cols):
            half = at if step == 0 else (dp if at == 0 else other)
            part = out_at(across, step, half)
            arrival(part, o_sem.at[(2 + at) * cols + step])
            pass_on(part, part, o_sem.at[(6 + at) * cols + step], {"row": beside})
    for at, row_from in enumerate((beside, far)):
        for step in range(cols):
            for part in range(2):
                half = part if step == 0 else (dp if part == 0 else other)
                arrival(out_at(row_from, step, half), o_sem.at[(4 + 2 * at + part) * cols + step])
    for step in range(1, cols):
        for m in range(micro):
            arrival(own_at(m, step), own_sem.at[m * cols + step])
    stay.wait()
    for step in range(1, size):
        arrival(att_own.at[(me + size - step) % size], att_recv.at[step])
    pairs = cols // micro
    for m in range(micro):
        total = jnp.zeros((quarter, model_width), jnp.float32)
        for row_from in range(rows):
            for pair in range(pairs):
                first = (row_from * pairs + pair) * kv_at
                total = total + project(
                    att_own[row_from * cols + m * pairs + pair],
                    w_out_all[first : first + kv_at, :],
                )
        part = slice(m * quarter, (m + 1) * quarter)
        value = x_own[part, :].astype(jnp.float32) + resid_scale * total
        mixed[part, :] = value
        normed_two[0, part, :] = norm_rows(value, gain_two[...])[1]

    begin, line, side, corner, finish = norm_line
    begin()
    for step in range(cols):
        picks_line[2](step)
        cot_line[2](step)
        ship(5 + 2 * step, 7 + 2 * step)
    for step in range(cols):
        line(step)
    ship(5 + 2 * cols, size)
    ship(1, size, range(2, 2 + chunks))
    logits = jnp.where(table[...] > 0, nt(normed_two[0], router_t[...]), -jnp.inf)
    raised = jnp.exp(logits - jnp.max(logits, axis=1, keepdims=True))
    gates_own[...] = raised / jnp.sum(raised, axis=1, keepdims=True)
    w_out_mine[...] = w_out_all[
        pl.ds(pl.multiple_of((row * 2 + col % 2) * kv_at, kv_at), kv_at), :
    ]
    for step in range(cols):
        picks_line[3](step)
        cot_line[3](step)
        side(step)
    for step in range(cols):
        corner(step)
    picks_line[4]()
    cot_line[4]()
    finish()

    everyone = ("dp", "row", "col")
    expert = place_in(everyone)
    tiles, slots = kept_in.shape[0], kept_in.shape[1]
    padded = pool_rows.shape[2]
    block_rows = micro * quarter
    span = cols * padded
    pool_rows[...] = jnp.zeros_like(pool_rows)
    pool_cots[...] = jnp.zeros_like(pool_cots)
    upper[...] = (
        lax.broadcasted_iota(jnp.int32, upper.shape, 0)
        < lax.broadcasted_iota(jnp.int32, upper.shape, 1)
    ).astype(low)

    def pool(tile, slot):
        for at, (source, target) in enumerate(((normed_all, pool_rows), (cot_all, pool_cots))):
            yield pltpu.make_async_copy(
                source.at[pl.ds(tile * cols, cols)],
                target.at[slot, :, 0:block_rows],
                load_sem.at[at, slot],
            )

    for copy in pool(0, 0):
        copy.start()
    slot_of = lax.broadcasted_iota(jnp.int32, (slots, span), 0)

    def picked(tile):
        return slot_of == ranks[tile][0:1, :]

    @pl.loop(0, tiles)
    def _(tile):
        slot = tile % 2
        for copy in pool(tile, slot):
            copy.wait()

        @pl.when(tile + 1 < tiles)
        def _():
            for copy in pool(tile + 1, 1 - slot):
                copy.start()

        rows_here = pool_rows[slot].reshape(span, model_width)
        logits = nt(router_t[...], rows_here)[0 : picks_all.shape[0], :]
        ids = lax.broadcasted_iota(jnp.int32, logits.shape, 0)
        names = jnp.concatenate([picks_all[tile * cols + at] for at in range(cols)], axis=1)
        chosen = ids == names[0:1, :]
        for choice in range(1, names.shape[0]):
            chosen = chosen | (ids == names[choice : choice + 1, :])
        logits = jnp.where(chosen, logits, -1e30)
        raised = jnp.where(chosen, jnp.exp(logits - jnp.max(logits, axis=0, keepdims=True)), 0.0)
        total = jnp.sum(raised, axis=0, keepdims=True)
        mine = ids == expert
        gate = jnp.sum(jnp.where(mine, raised, 0.0), axis=0, keepdims=True) / jnp.where(
            total > 0, total, 1.0
        )
        here = jnp.max(jnp.where(mine & chosen, 1.0, 0.0), axis=0, keepdims=True)
        before = project(jnp.broadcast_to(here, (16, span)).astype(low), upper[...])[0:1, :]
        rank = jnp.where(here > 0, before.astype(jnp.int32), -1)
        ranks[tile] = jnp.broadcast_to(rank, ranks.shape[1:])
        select = slot_of == rank
        kept_weight[tile] = jnp.broadcast_to(
            jnp.sum(jnp.where(select, gate, 0.0), axis=1, keepdims=True), kept_weight.shape[1:]
        )
        select = select.astype(low)
        kept_in[tile] = project(select, rows_here).astype(low)
        kept_dy[tile] = project(select, pool_cots[slot].reshape(span, model_width)).astype(low)

    shipped(range(2))
    for copy in locals_[6:]:
        copy.wait()
    gate_w = gate_up[:, 0:slice_rows, :].reshape(model_width, ff_width)
    up_w = gate_up[:, slice_rows : 2 * slice_rows, :].reshape(model_width, ff_width)

    def down_w(chunk):
        at = chunk * down_rows
        return down[:, at : at + down_rows, :].reshape(ff_width, ff_width)

    def two(ref, pair):
        part = ref[pl.ds(2 * pair, 2)]
        return part.reshape(2 * slots, part.shape[2])

    def put(ref, pair, value):
        ref[pl.ds(2 * pair, 2)] = value.reshape(2, slots, value.shape[1])

    @pl.loop(0, tiles // 2)
    def _(pair):
        rows_in = two(kept_in, pair)
        gate_value = project(rows_in, gate_w)
        up_value = project(rows_in, up_w)
        put(gate_proj, pair, gate_value)
        put(up_proj, pair, up_value)
        put(kept_act, pair, (gate_value / (1.0 + jnp.exp(-gate_value)) * up_value).astype(low))
        weight = two(kept_weight, pair)[:, 0:1]
        grad_mix = resid_scale * two(kept_dy, pair).astype(jnp.float32)
        put(kept_dye, pair, (weight * grad_mix).astype(low))

    def all_of(ref):
        value = ref[...]
        return value.reshape(tiles * slots, value.shape[2])

    act_all = all_of(kept_act)
    for chunk in range(chunks):
        grad = tn(act_all, all_of(kept_dye.at[:, :, chunk * ff_width : (chunk + 1) * ff_width]))
        at = chunk * down_rows
        down_grad[:, at : at + down_rows, :] = grad.astype(low).reshape(size, down_rows, ff_width)
    home = pltpu.make_async_copy(down_grad.at[me], grads_down.at[me], grad_local)
    home.start()
    given = []
    for step in range(1, size):
        to = (me + step) % size
        given.append(
            send(
                down_grad.at[to],
                grads_down.at[me],
                grad_send.at[step],
                grad_recv.at[step],
                device_at(plane, to),
            )
        )
    shipped(range(2, 2 + chunks))

    def spill(tile, slot):
        for at, (source, target) in enumerate(((pool_rows, rows_part), (pool_cots, mix_part))):
            yield pltpu.make_async_copy(
                source.at[slot, :, 0:block_rows],
                target.at[pl.ds(tile * cols, cols)],
                store_sem.at[at, slot],
            )

    @pl.loop(0, tiles // 2)
    def _(pair):
        act = two(kept_act, pair)
        grad_out = two(kept_dye, pair)
        gate_value, up_value = two(gate_proj, pair), two(up_proj, pair)
        weight = two(kept_weight, pair)[:, 0:1]
        score = jnp.zeros((2 * slots, 1), jnp.float32)
        grad_act = jnp.zeros((2 * slots, ff_width), jnp.float32)

        @pl.when(pair > 0)
        def _():
            for at in range(2):
                for copy in spill(2 * pair - 2 + at, at):
                    copy.wait()

        selects = [picked(2 * pair + at).astype(low) for at in range(2)]
        for chunk in range(chunks):
            lanes = slice(chunk * ff_width, (chunk + 1) * ff_width)
            part = down_w(chunk)
            out = project(act, part).astype(low).astype(jnp.float32)
            grad_mix = resid_scale * kept_dy[pl.ds(2 * pair, 2), :, lanes].reshape(
                2 * slots, ff_width
            ).astype(jnp.float32)
            score = score + jnp.sum(grad_mix * out, axis=1, keepdims=True)
            mixed_rows = (weight * out).astype(low)
            for at in range(2):
                pool_cots[at, :, :, lanes] = (
                    tn(selects[at], mixed_rows[at * slots : (at + 1) * slots])
                    .astype(low)
                    .reshape(cols, padded, ff_width)
                )
            grad_act = grad_act + nt(grad_out[:, lanes], part)
        sigmoid = 1.0 / (1.0 + jnp.exp(-gate_value))
        grad_gate = (
            grad_act * up_value * (sigmoid + gate_value * sigmoid * (1.0 - sigmoid))
        ).astype(low)
        grad_up = (grad_act * (gate_value * sigmoid)).astype(low)
        put(kept_gate, pair, grad_gate)
        put(kept_up, pair, grad_up)
        grad_in = (nt(grad_gate, gate_w) + nt(grad_up, up_w)).astype(low)
        for at in range(2):
            tile = 2 * pair + at
            part = slice(at * slots, (at + 1) * slots)
            pool_rows[at] = (
                tn(selects[at], grad_in[part]).astype(low).reshape(cols, padded, model_width)
            )
            line_of = jnp.sum(jnp.where(picked(tile), score[part], 0.0), axis=0, keepdims=True)
            for block in range(cols):
                scores[tile * cols + block] = jnp.broadcast_to(
                    line_of[:, block * padded : (block + 1) * padded], scores.shape[1:]
                )
            for copy in spill(tile, at):
                copy.start()

    rows_all = all_of(kept_in)
    for at, kept in ((0, kept_gate), (slice_rows, kept_up)):
        grad = tn(rows_all, all_of(kept)).astype(low)
        grads_gu[:, at : at + slice_rows, :] = grad.reshape(size, slice_rows, ff_width)
    for at in range(2):
        for copy in spill(tiles - 2 + at, at):
            copy.wait()
    home.wait()
    for copy in given:
        copy.wait()
    for copy in moved + copies + sent:
        copy.wait_send()


def front(number, x, w_qkv, w_out, picks, cot, experts, gains, tables, docs, routing, heads_width):
    cols, rows = lax.axis_size("col"), lax.axis_size("row")
    total, plane = group_size_of(("dp", "row", "col")), group_size_of(("row", "col"))
    micro, depth, part_width = x.shape
    width, tokens, low = part_width * cols, depth * rows, jnp.bfloat16
    wide = jnp.float32
    quarter = depth // cols
    _, slice_rows, ff_width = experts[0].shape
    down_depth = slice_rows * plane // ff_width * experts[2].shape[1]
    tiles = total // cols
    slots = cols * micro * (quarter * 3 // 8)
    vmem = pl.BlockSpec(memory_space=pltpu.VMEM)
    shape, dma = jax.ShapeDtypeStruct, pltpu.SemaphoreType.DMA
    pool = pltpu.VMEM((2, cols, 128, width), low)
    return pl.pallas_call(
        front_kernel,
        out_shape=[
            shape((tokens, width), low),
            shape((cols,) + w_qkv.shape[1:], low),
            shape((heads_width, width), low),
            shape((total,) + cot.shape, low),
            shape((total,) + cot.shape, low),
            shape((tokens, w_qkv.shape[3]), low),
            shape((plane, quarter, heads_width), low),
            shape((micro * quarter, width), wide),
            shape((micro * quarter, 128), wide),
            shape((total,) + cot.shape, low),
            shape((total,) + cot.shape, low),
            shape((total, 8, 128), wide),
            shape((plane, 2 * slice_rows, ff_width), low),
            shape((plane, down_depth, ff_width), low),
        ],
        in_specs=[ANYWHERE] * 8 + [vmem] * 8,
        out_specs=[vmem] * 3
        + [ANYWHERE] * 2
        + [vmem] * 4
        + [ANYWHERE] * 2
        + [vmem] * 2
        + [ANYWHERE],
        scratch_shapes=[
            pltpu.VMEM((rows * 2 * w_out.shape[1], width), low),
            pltpu.VMEM((total,) + picks.shape, picks.dtype),
            pltpu.VMEM((micro * quarter, width), low),
            pltpu.VMEM((plane, quarter, heads_width), low),
            pltpu.VMEM((1, micro * quarter, width), low),
            pltpu.VMEM((plane, 2 * slice_rows, ff_width), low),
            pltpu.VMEM((plane, down_depth, ff_width), low),
            pltpu.VMEM((plane, down_depth, ff_width), low),
            pool,
            pool,
            pltpu.VMEM((tiles, slots, width), low),
            pltpu.VMEM((tiles, slots, width), low),
            pltpu.VMEM((tiles, slots, width), low),
            pltpu.VMEM((tiles, slots, ff_width), low),
            pltpu.VMEM((tiles, slots, ff_width), low),
            pltpu.VMEM((tiles, slots, ff_width), low),
            pltpu.VMEM((tiles, slots, ff_width), wide),
            pltpu.VMEM((tiles, slots, ff_width), wide),
            pltpu.VMEM((tiles, slots, 128), wide),
            pltpu.VMEM((tiles, 8, cols * 128), jnp.int32),
            pltpu.VMEM((cols * 128, cols * 128), low),
            dma((2, 2)),
            dma((2, 2)),
            dma,
            dma((plane,)),
            dma((plane,)),
            dma((12,)),
            dma((72,)),
            dma((4 * cols,)),
            dma((2 * cols,)),
            dma((8 * cols,)),
            dma((micro * cols,)),
            dma((plane,)),
            dma((plane,)),
            dma,
            dma((8, plane)),
            dma((8, plane)),
        ]
        + gather_sems() * 3,
        compiler_params=pltpu.CompilerParams(
            collective_id=number, has_side_effects=True, vmem_limit_bytes=63 * 2**20
        ),
        name="front" + str(number),
    )(x, w_qkv, w_out, picks[None], cot[None], *experts, *gains, *tables, *docs, *routing)


def sum_scratch(block):
    cols = lax.axis_size("col")
    low = jnp.bfloat16
    return [
        pltpu.VMEM((4 * cols,) + block, low),
        pltpu.VMEM((4 * cols,) + block, low),
        pltpu.VMEM((4 * cols,) + block, low),
        pltpu.VMEM((3 * cols,) + block, low),
        pltpu.VMEM((cols,) + block, low),
        pltpu.SemaphoreType.DMA((4 * cols,)),
        pltpu.SemaphoreType.DMA((48,)),
        pltpu.SemaphoreType.DMA((4 * cols,)),
        pltpu.SemaphoreType.DMA((cols,)),
        pltpu.SemaphoreType.DMA((2 * cols,)),
        pltpu.SemaphoreType.DMA((cols,)),
    ]


def sum_steps(partial, sems, copies):
    (
        near,
        mine,
        passed,
        stage,
        last,
        local_sem,
        send_sem,
        beside_sem,
        first_sem,
        second_sem,
        col_sem,
    ) = sems
    row, across, beside = row_peers()
    rows, cols = lax.axis_size("row"), lax.axis_size("col")
    col, dp = lax.axis_index("col"), lax.axis_index("dp")
    other = 1 - dp
    low = jnp.bfloat16
    two_on, beside_col, _ = col_peers()
    order = (beside_col, (beside_col + 2) % cols, two_on, col)
    sent = []

    def pass_on(src, dst, sem, peer):
        copy = send(src, dst, send_sem.at[len(sent)], sem, peer)
        sent.append(copy)
        copies.append(copy)

    def arrival(ref, sem):
        pltpu.make_async_copy(ref, ref, sem).wait()

    def block_of(dp_to, row_to, col_to):
        return (dp_to * rows + row_to) * cols + col_to

    far = (beside + rows // 2) % rows
    theirs = ((other, far), (other, beside), (dp, far), (dp, beside))
    ours = ((other, across), (other, row), (dp, across), (dp, row))

    def start():
        for turn in range(4):
            for at in range(cols):
                slot = turn * cols + at
                pass_on(
                    partial.at[block_of(*theirs[turn], order[at])],
                    near.at[slot],
                    beside_sem.at[slot],
                    {"row": beside},
                )
                pltpu.make_async_copy(
                    partial.at[block_of(*ours[turn], order[at])], mine.at[slot], local_sem.at[slot]
                ).start()

    def combine(target, *parts):
        rows_each = 16

        @pl.loop(0, target.shape[0] // rows_each)
        def _(at):
            lines = pl.ds(pl.multiple_of(at * rows_each, rows_each), rows_each)
            value = parts[0][lines, :].astype(jnp.float32)
            for part in parts[1:]:
                value = value + part[lines, :].astype(jnp.float32)
            target[lines, :] = value.astype(target.dtype)

    def chip(slot):
        arrival(mine.at[slot], local_sem.at[slot])
        arrival(near.at[slot], beside_sem.at[slot])
        return mine.at[slot], near.at[slot]

    def diagonal():
        for at in range(cols):
            combine(passed.at[at], *chip(at))
            peer = {"dp": other} if at < 2 else {"row": across}
            pass_on(passed.at[at], stage.at[at], first_sem.at[at], peer)

    def middle():
        for at in range(cols):
            for turn, here, peer in ((1, at >= 2, {"dp": other}), (2, at < 2, {"row": across})):
                slot = turn * cols + at
                parts = chip(slot)
                if here:
                    arrival(stage.at[at], first_sem.at[at])
                    parts = parts + (stage.at[at],)
                combine(passed.at[slot], *parts)
                pass_on(passed.at[slot], stage.at[slot], second_sem.at[slot - cols], peer)

    def chip_total(at):
        parts = chip(3 * cols + at)
        for turn in (1, 2):
            slot = turn * cols + at
            arrival(stage.at[slot], second_sem.at[slot - cols])
            parts = parts + (stage.at[slot],)
        return parts

    def spread():
        for at in range(2):
            combine(passed.at[3 * cols + at], *chip_total(at))
            pass_on(passed.at[3 * cols + at], last.at[at], col_sem.at[at], {"col": beside_col})
        parts = chip_total(2)
        arrival(last.at[1], col_sem.at[1])
        combine(passed.at[3 * cols + 2], *parts, last.at[1])
        pass_on(passed.at[3 * cols + 2], last.at[2], col_sem.at[2], {"col": two_on})

    def total(target):
        parts = chip_total(3)
        for at in (0, 2):
            arrival(last.at[at], col_sem.at[at])
            parts = parts + (last.at[at],)
        combine(target, *parts)

    return start, diagonal, middle, spread, total


def back_kernel(
    partial,
    mix_part,
    grads,
    scores,
    normed_all,
    mixed,
    cot,
    gates,
    router_t,
    gain_one,
    gain_two,
    x_all,
    w_mine,
    w_out_mine,
    qkv,
    attended,
    cos_table,
    sin_table,
    doc_col,
    doc_row,
    mix_out,
    grads_own,
    dw_pair,
    do_pair,
    router_pair,
    x_grads,
    lines_all,
    scores_in,
    branch,
    branch_all,
    logits,
    logits_all,
    plane_rows,
    rotated,
    values_grad,
    grad_att,
    grad_qkv,
    normed,
    heads,
    heads_near,
    heads_across,
    heads_pair,
    heads_passed,
    dw_send,
    dw_in,
    do_send,
    do_in,
    x_send,
    lines,
    rows_total,
    score_local,
    score_send,
    score_recv,
    ship_local,
    ship_send,
    ship_recv,
    plane_sem,
    gather_send,
    branch_col,
    branch_across,
    branch_beside,
    logits_col,
    logits_across,
    logits_beside,
    heads_send,
    near_sem,
    across_sem,
    pair_sem,
    part_local,
    part_send,
    dw_sem,
    do_sem,
    x_sem,
    swap_sem,
    *groups,
):
    row, across, beside = row_peers()
    rows, cols = lax.axis_size("row"), lax.axis_size("col")
    col, dp = lax.axis_index("col"), lax.axis_index("dp")
    other = 1 - dp
    far = (beside + rows // 2) % rows
    half = col % 2
    pair = col + 1 - 2 * half
    everyone, plane = ("dp", "row", "col"), ("row", "col")
    size, me = group_size_of(everyone), place_in(everyone)
    plane_size, plane_me = group_size_of(plane), place_in(plane)
    low, wide = jnp.bfloat16, jnp.float32
    copies, moved, parts, small, locals_ = [], [], [], [], []
    meet([device_at(everyone, (me + step) % size) for step in range(1, size)])

    def arrival(ref, sem):
        pltpu.make_async_copy(ref, ref, sem).wait()

    def ship(first, last):
        for step in range(first, last):
            to = (plane_me + step) % plane_size
            moved.append(
                send(
                    grads.at[to],
                    grads_own.at[plane_me],
                    ship_send.at[step],
                    ship_recv.at[step],
                    device_at(plane, to),
                )
            )

    def keep(src, dst):
        copy = pltpu.make_async_copy(src, dst, part_local.at[len(locals_)])
        copy.start()
        locals_.append(copy)

    rows_sum = sum_steps(partial, groups[0:11], copies)
    mix_sum = sum_steps(
        mix_part, groups[0:3] + groups[11:12] + groups[4:5] + groups[12:18], copies
    )
    line_local, line_send, line_recv = groups[18:]

    score_own = pltpu.make_async_copy(scores.at[me], scores_in.at[me], score_local)
    score_own.start()
    for step in range(1, size):
        to = (me + step) % size
        small.append(
            send(
                scores.at[to],
                scores_in.at[me],
                score_send.at[step],
                score_recv.at[step],
                device_at(everyone, to),
            )
        )
    rows_sum[0]()
    keep(grads.at[plane_me], grads_own.at[plane_me])
    ship(1, 5)
    tokens, model_width = x_all.shape
    depth = tokens // rows
    for block in range(rows):
        part = slice(block * depth, (block + 1) * depth)
        normed[part, :] = norm_rows(x_all[part, :].astype(wide), gain_one[...])[1]
    rows_sum[1]()
    rows_sum[2]()
    rows_sum[3]()
    score_own.wait()
    for copy in small:
        copy.wait()
    gate = gates[...]
    scored = jnp.concatenate(
        [scores_in[:, 0, :], jnp.zeros((128 - size, 128), wide)], axis=0
    ).T[: gate.shape[0], :]
    grad_logits = gate * (scored - jnp.sum(gate * scored, axis=1, keepdims=True))
    routed = jnp.dot(
        grad_logits, router_t[...].astype(wide), precision=highest, preferred_element_type=wide
    )
    logits[0] = jnp.concatenate(
        [grad_logits, jnp.zeros((128 - gate.shape[0], 128), wide)], axis=0
    ).T[: logits.shape[1], :]
    value = mixed[...]
    scale_two = lax.rsqrt(jnp.mean(value * value, axis=1, keepdims=True) + eps_norm)
    unit_two = value * scale_two
    rows_sum[4](rows_total)
    grad_normed = rows_total[...] + routed
    mix_row = jnp.sum(grad_normed * unit_two, axis=0, keepdims=True)
    grad_scaled = grad_normed * gain_two[...]
    grad_mixed = cot[...].astype(wide) + scale_two * (
        grad_scaled - unit_two * jnp.mean(grad_scaled * unit_two, axis=1, keepdims=True)
    )
    quarter = branch.shape[1]
    for m in range(2):
        branch[m] = (resid_scale * grad_mixed[m * quarter : (m + 1) * quarter, :]).astype(low)

    sent = []

    def pass_on(src, dst, sem, peer):
        sent.append(send(src, dst, gather_send.at[len(sent)], sem, peer))

    def origin(step):
        return (col + cols - step) % cols

    two_on, near, order = col_peers()
    for step, to in ((1, two_on), (2, near)):
        pass_on(branch.at[to // 2], branch_all.at[plane_me], branch_col.at[step], {"col": to})
        pass_on(logits.at[0], logits_all.at[plane_me], logits_col.at[step], {"col": to})
    keep(branch.at[col // 2], branch_all.at[plane_me])
    keep(logits.at[0], logits_all.at[plane_me])
    plans = (
        (branch.at[col // 2], branch_all, branch_col, branch_across, branch_beside),
        (logits.at[0], logits_all, logits_col, logits_across, logits_beside),
    )
    for step in range(cols):
        for mine, target, col_sem, side_sem, core_sem in plans:
            part = target.at[row * cols + order[step]]
            if step > 0:
                arrival(part, col_sem.at[step])
            if step == 1:
                pass_on(part, part, col_sem.at[3], {"col": near})
            source = mine if step == 0 else part
            pass_on(source, part, side_sem.at[step], {"row": across})
            pass_on(source, part, core_sem.at[step], {"row": beside})
    ship(5, 11)
    for step in range(cols):
        for mine, target, col_sem, side_sem, core_sem in plans:
            part = target.at[across * cols + order[step]]
            arrival(part, side_sem.at[step])
            pass_on(part, part, core_sem.at[cols + step], {"row": beside})
    for at, row_from in enumerate((beside, far)):
        for step in range(cols):
            for mine, target, col_sem, side_sem, core_sem in plans:
                arrival(target.at[row_from * cols + order[step]], core_sem.at[at * cols + step])
    for copy in locals_:
        copy.wait()
    for copy in copies:
        copy.wait_send()
    done = len(copies)
    mix_sum[0]()

    branch_rows = branch_all[...].reshape(tokens, model_width)
    kv_at = attended.shape[2]
    count = kv_at // HEAD_DIM
    grad_att[...] = nt(branch_rows, w_out_mine[...]).astype(low)
    rotated[:, kv_at : kv_at + HEAD_DIM] = jnp.zeros((tokens, HEAD_DIM), wide)
    values_grad[...] = jnp.zeros_like(values_grad)
    for block in range(rows):
        part = slice(block * depth, (block + 1) * depth)
        extent = key_extent(block, depth, tokens)
        allowed = visible(doc_col, doc_row, block, depth, extent)
        key = qkv[0:extent, kv_at : kv_at + HEAD_DIM]
        value_rows = qkv[0:extent, kv_at + HEAD_DIM : kv_at + 2 * HEAD_DIM]
        key_sum = jnp.zeros((extent, HEAD_DIM), wide)
        value_sum = jnp.zeros((extent, HEAD_DIM), wide)
        for head in range(count):
            lanes = slice(head * HEAD_DIM, (head + 1) * HEAD_DIM)
            query = qkv[part, lanes]
            probs = attend(query, key, allowed)
            grad_out = grad_att[part, lanes]
            grad_probs = nt(grad_out, value_rows)
            grad_scores = probs * (
                grad_probs - jnp.sum(probs * grad_probs, axis=1, keepdims=True)
            )
            grad_raw = (grad_scores * attn_scale).astype(low)
            rotated[part, lanes] = project(grad_raw, key)
            key_sum = key_sum + tn(grad_raw, query)
            value_sum = value_sum + tn(probs.astype(low), grad_out)
        rotated[0:extent, kv_at : kv_at + HEAD_DIM] += key_sum
        values_grad[0:extent, :] += value_sum
        if block == 1:
            mix_sum[1]()
    for at in range(2):
        piece = slice(at * 128, (at + 1) * 128)
        grad_qkv[:, piece] = turn(rotated[:, piece], cos_table[...], -sin_table[...]).astype(low)
    grad_qkv[:, 256:] = values_grad[...].astype(low)

    width = model_width // cols
    heads_out = attended[...].reshape(tokens, kv_at)
    for step in range(cols - 1, -1, -1):
        to = (col + step) % cols
        lanes = pl.ds(pl.multiple_of(to * width, width), width)
        dw_send[to] = tn(grad_qkv[...], normed[:, lanes]).astype(low)
        chunk = branch_all[:, :, lanes].reshape(tokens, width)
        do_send[to] = tn(heads_out, chunk).astype(low)
        if step > 0:
            parts.append(
                send(dw_send.at[to], dw_in.at[col], part_send.at[step], dw_sem.at[step], {"col": to})
            )
            parts.append(
                send(
                    do_send.at[to],
                    do_in.at[col],
                    part_send.at[cols + step],
                    do_sem.at[step],
                    {"col": to},
                )
            )
    keep(dw_send.at[col], dw_in.at[col])
    keep(do_send.at[col], do_in.at[col])

    rows_each = heads.shape[1]
    projection = w_mine[...].reshape(model_width, w_mine.shape[3])
    heads_sent = []

    def heads_on(src, dst, sem, peer):
        heads_sent.append(send(src, dst, heads_send.at[len(heads_sent)], sem, peer))

    halves = (1 - half, half)
    for at, row_to in enumerate((far, beside, across, row)):
        for which, part in enumerate(halves):
            slot = 2 * at + which
            first = pl.multiple_of((row_to * 2 + part) * rows_each, rows_each)
            heads[slot] = nt(grad_qkv[pl.ds(first, rows_each), :], projection).astype(low)
            if at < 2:
                heads_on(heads.at[slot], heads_near.at[slot], near_sem.at[slot], {"row": beside})
    def heads_sum(slot):
        arrival(heads_near.at[slot - 4], near_sem.at[slot - 4])
        return heads[slot].astype(wide) + heads_near[slot - 4].astype(wide)

    for which in range(2):
        heads_passed[which] = heads_sum(4 + which).astype(low)
        heads_on(
            heads_passed.at[which], heads_across.at[which], across_sem.at[which], {"row": across}
        )
    mix_sum[2]()
    ship(11, plane_size)
    router_sum = jnp.zeros((logits.shape[1], model_width), wide)
    group = plane_rows.shape[0]
    for first in range(0, plane_size, group):
        load = pltpu.make_async_copy(
            normed_all.at[pl.ds(dp * plane_size + first, group)], plane_rows, score_local
        )
        load.start()
        load.wait()
        for at in range(group):
            left = logits_all[first + at, :, 0 : 2 * quarter]
            for _ in range(3):
                piece = left.astype(low)
                left = left - piece.astype(wide)
                router_sum = router_sum + project(piece, plane_rows[at])
    router_pair[dp] = router_sum
    swaps = [
        send(router_pair.at[dp], router_pair.at[dp], swap_sem.at[0], swap_sem.at[1], {"dp": other})
    ]
    for which in range(2):
        grad_one = heads_sum(6 + which)
        arrival(heads_across.at[which], across_sem.at[which])
        grad_one = grad_one + heads_across[which].astype(wide)
        if which == 0:
            heads_passed[2] = grad_one.astype(low)
            heads_on(heads_passed.at[2], heads_pair, pair_sem, {"col": pair})
    arrival(heads_pair, pair_sem)
    grad_one = grad_one + heads_pair[...].astype(wide)
    first = (row * 2 + half) * rows_each
    x_rows = x_all[pl.ds(pl.multiple_of(first, rows_each), rows_each), :].astype(wide)
    scale_one = lax.rsqrt(jnp.mean(x_rows * x_rows, axis=1, keepdims=True) + eps_norm)
    unit_one = x_rows * scale_one
    norm_row = jnp.sum(grad_one * unit_one, axis=0, keepdims=True)
    each = rows_each // quarter
    grad_h = branch_all[pl.ds((row * 2 + half) * each, each)].reshape(rows_each, model_width)
    grad_scaled = grad_one * gain_one[...]
    grad_x = grad_h.astype(wide) * (1.0 / resid_scale) + scale_one * (
        grad_scaled - unit_one * jnp.mean(grad_scaled * unit_one, axis=1, keepdims=True)
    )
    for to in range(cols):
        x_send[to] = grad_x[:, to * width : (to + 1) * width].astype(low)
    for step in range(1, cols):
        to = (col + step) % cols
        swaps.append(
            send(
                x_send.at[to], x_grads.at[col], x_sem.at[step], x_sem.at[cols + step], {"col": to}
            )
        )
    keep(x_send.at[col], x_grads.at[col])
    steps = model_width // 128
    for at in range(steps):
        piece = slice(at * 128, (at + 1) * 128)
        lines[0, at : at + 1, :] = norm_row[:, piece]
        lines[0, steps + at : steps + at + 1, :] = mix_row[:, piece]
    home = pltpu.make_async_copy(lines.at[0], lines_all.at[me], line_local)
    home.start()
    for step in range(1, size):
        swaps.append(
            send(
                lines.at[0],
                lines_all.at[me],
                line_send.at[step],
                line_recv.at[step],
                device_at(everyone, (me + step) % size),
            )
        )
    for copy in locals_[3:]:
        copy.wait()
    for step in range(1, cols):
        arrival(dw_in.at[origin(step)], dw_sem.at[step])
        arrival(do_in.at[origin(step)], do_sem.at[step])
    for h in range(2):
        dw_pair[dp, h] = (dw_in[h].astype(wide) + dw_in[2 + h].astype(wide)).astype(low)
        do_pair[dp, h] = (do_in[h].astype(wide) + do_in[2 + h].astype(wide)).astype(low)
    swaps.append(
        send(dw_pair.at[dp], dw_pair.at[dp], swap_sem.at[2], swap_sem.at[3], {"dp": other})
    )
    swaps.append(
        send(do_pair.at[dp], do_pair.at[dp], swap_sem.at[4], swap_sem.at[5], {"dp": other})
    )
    mix_sum[3]()
    mix_sum[4](mix_out)
    home.wait()
    for copy in swaps:
        copy.wait()
    for copy in moved:
        copy.wait()
    for copy in copies[done:] + parts + sent + heads_sent:
        copy.wait_send()


def back(number, partial, mix_part, grads, scores, normed_all, *rest):
    mixed, _, _, _, _, _, x_all, w_mine, _, qkv, attended = rest[:11]
    cols, rows = lax.axis_size("col"), lax.axis_size("row")
    total, plane = group_size_of(("dp", "row", "col")), group_size_of(("row", "col"))
    low, wide = jnp.bfloat16, jnp.float32
    vmem = pl.BlockSpec(memory_space=pltpu.VMEM)
    shape, dma = jax.ShapeDtypeStruct, pltpu.SemaphoreType.DMA
    tokens, width = x_all.shape
    quarter, heads_width = attended.shape[1:]
    block = partial.shape[1:]
    part = width // cols
    qkv_width = w_mine.shape[3]
    lines = -(-2 * (width // 128) // 8) * 8
    return pl.pallas_call(
        back_kernel,
        out_shape=[
            shape(block, wide),
            shape(grads.shape, low),
            shape((2, 2, qkv_width, part), low),
            shape((2, 2, heads_width, part), low),
            shape((2, total, width), wide),
            shape((cols, tokens // (2 * rows), part), low),
            shape((total, lines, 128), wide),
        ],
        in_specs=[ANYWHERE] * 5 + [vmem] * len(rest),
        out_specs=[vmem, ANYWHERE, vmem, vmem, vmem, vmem, ANYWHERE],
        scratch_shapes=[
            pltpu.VMEM(scores.shape, wide),
            pltpu.VMEM((2, quarter, width), low),
            pltpu.VMEM((plane, quarter, width), low),
            pltpu.VMEM((1, total, 128), wide),
            pltpu.VMEM((plane, total, 128), wide),
            pltpu.VMEM((4,) + block, low),
            pltpu.VMEM((tokens, 256), wide),
            pltpu.VMEM((tokens, HEAD_DIM), wide),
            pltpu.VMEM((tokens, heads_width), low),
            pltpu.VMEM((tokens, qkv_width), low),
            pltpu.VMEM((tokens, width), low),
            pltpu.VMEM((8, tokens // (2 * rows), width), low),
            pltpu.VMEM((4, tokens // (2 * rows), width), low),
            pltpu.VMEM((2, tokens // (2 * rows), width), low),
            pltpu.VMEM((tokens // (2 * rows), width), low),
            pltpu.VMEM((3, tokens // (2 * rows), width), low),
            pltpu.VMEM((cols, qkv_width, part), low),
            pltpu.VMEM((cols, qkv_width, part), low),
            pltpu.VMEM((cols, heads_width, part), low),
            pltpu.VMEM((cols, heads_width, part), low),
            pltpu.VMEM((cols, tokens // (2 * rows), part), low),
            pltpu.VMEM((1, lines, 128), wide),
            pltpu.VMEM(block, wide),
            dma,
            dma((total,)),
            dma((total,)),
            dma,
            dma((plane,)),
            dma((plane,)),
            dma,
            dma((40,)),
            dma((cols,)),
            dma((cols,)),
            dma((2 * cols,)),
            dma((cols,)),
            dma((cols,)),
            dma((2 * cols,)),
            dma((8,)),
            dma((4,)),
            dma((2,)),
            dma,
            dma((8,)),
            dma((2 * cols,)),
            dma((cols,)),
            dma((cols,)),
            dma((2 * cols,)),
            dma((6,)),
        ]
        + sum_scratch(block)
        + [pltpu.VMEM((3 * cols,) + block, low)]
        + sum_scratch(block)[5:]
        + [dma, dma((total,)), dma((total,))],
        compiler_params=pltpu.CompilerParams(
            collective_id=number, has_side_effects=True, vmem_limit_bytes=62 * 2**20
        ),
        name="back" + str(number),
    )(partial, mix_part, grads, scores, normed_all, *rest)


def owned(
    hidden_in,
    norm_gain,
    w_query,
    w_key,
    w_value,
    w_out,
    mix_gain,
    w_router,
    w_gate,
    w_up,
    w_down,
    lengths,
    routes,
    mask,
    cotangent,
):
    everyone = ("dp", "row", "col")
    plane = ("row", "col")
    micro_count, tok_row, width_part = hidden_in.shape
    row_count = lax.axis_size("row")
    col_count = lax.axis_size("col")
    dp_count = lax.axis_size("dp")
    row_at = lax.axis_index("row")
    col_at = lax.axis_index("col")
    dp_at = lax.axis_index("dp")
    plane_count = row_count * col_count
    device_count = plane_count * dp_count
    plane_at = row_at * col_count + col_at
    model_width = width_part * col_count
    kv_here = w_key.shape[1] // HEAD_DIM
    group_size = w_query.shape[1] // w_key.shape[1]
    q_width = group_size * HEAD_DIM
    group_tokens = tok_row * row_count
    quarter = tok_row // col_count
    own_rows = micro_count * quarter
    experts_here, slice_width, ff_width = w_gate.shape
    down_slice = w_down.shape[1]
    experts_all = experts_here * dp_count
    expert_at = dp_at * plane_count + plane_at
    micro_at = col_at // kv_here
    half_at = col_at % kv_here

    masked_cot = cotangent * mask[:, :, None].astype(cotangent.dtype)

    w_qkv = jnp.concatenate(
        [
            w_query.reshape(width_part, kv_here, q_width),
            w_key.reshape(width_part, kv_here, HEAD_DIM),
            w_value.reshape(width_part, kv_here, HEAD_DIM),
        ],
        axis=2,
    ).transpose(1, 0, 2)
    qkv_width = q_width + 2 * HEAD_DIM
    picks = jnp.pad(routes.reshape(own_rows, TOP).T, ((0, 0), (0, 128 - own_rows)), constant_values=-1)
    doc_id, position = documents(lengths[:, 0][micro_at], group_tokens)
    sin_table, cos_table = (
        table[:, 0] for table in angles(position.astype(jnp.float32), HEAD_DIM)
    )
    doc_col = jnp.broadcast_to(doc_id[:, None], (group_tokens, 128))
    doc_row = jnp.broadcast_to(doc_id[None, :], (8, group_tokens))
    cos_lanes = jnp.tile(cos_table, (1, 4))
    sin_lanes = jnp.tile(jnp.concatenate([-sin_table, sin_table], axis=1), (1, 2))
    pad_experts = 128 - experts_all
    table = jnp.any(
        routes.reshape(own_rows, TOP)[:, :, None]
        == jnp.arange(experts_all, dtype=jnp.int32)[None, None, :],
        axis=1,
    )
    router_t = jnp.pad(w_router.T, ((0, pad_experts), (0, 0)))
    cot_own = masked_cot.reshape(own_rows, model_width)
    (
        x_micro,
        w_mine,
        w_out_mine,
        cot_all,
        normed_all,
        qkv,
        attended,
        mixed,
        gates_own,
        rows_part,
        mix_part,
        scores,
        grads,
        grads_down,
    ) = front(
        0,
        hidden_in,
        w_qkv.reshape(kv_here, dp_count, width_part // dp_count, qkv_width),
        w_out.reshape(dp_count, w_out.shape[0] // dp_count, w_out.shape[1]),
        picks,
        cot_own,
        (w_gate, w_up, w_down),
        (norm_gain[None], mix_gain[None]),
        (cos_lanes, sin_lanes),
        (doc_col, doc_row),
        (router_t, jnp.pad(table.astype(jnp.float32), ((0, 0), (0, pad_experts)))),
        q_width,
    )
    expert_mix, grads, qkv_sum, out_sum, router_grad, grad_input, lines = back(
        1,
        rows_part,
        mix_part,
        grads,
        scores,
        normed_all,
        mixed,
        cot_own,
        gates_own,
        router_t,
        norm_gain[None],
        mix_gain[None],
        x_micro,
        w_mine,
        w_out_mine,
        qkv,
        attended,
        cos_lanes,
        sin_lanes,
        doc_col,
        doc_row,
    )
    layer_out = (mixed + resid_scale * expert_mix).astype(jnp.bfloat16)
    out_gate = grads[:, :slice_width].astype(jnp.float32)
    out_up = grads[:, slice_width : 2 * slice_width].astype(jnp.float32)
    out_down = jnp.concatenate(
        [
            grads_down[:, at : at + down_slice]
            for at in range(0, grads_down.shape[1], down_slice)
        ],
        axis=2,
    ).astype(jnp.float32)
    grad_input = grad_input.reshape(micro_count, tok_row, width_part).astype(jnp.float32)
    qkv_sum = jnp.sum(qkv_sum.astype(jnp.float32), axis=0)
    out_sum = jnp.sum(out_sum.astype(jnp.float32), axis=0)
    router_grad = jnp.sum(router_grad, axis=0).T
    lines = jnp.sum(lines, axis=0)
    norm_grad = lines[: model_width // 128].reshape(-1)
    mix_grad = lines[model_width // 128 : 2 * (model_width // 128)].reshape(-1)
    grad_wq = qkv_sum[:, :q_width].reshape(-1, width_part).T
    grad_wk = qkv_sum[:, q_width : q_width + HEAD_DIM].reshape(-1, width_part).T
    grad_wv = qkv_sum[:, q_width + HEAD_DIM :].reshape(-1, width_part).T
    grad_wo = out_sum.reshape(w_out.shape)
    return (
        layer_out.reshape(micro_count, quarter, model_width),
        grad_input,
        norm_grad,
        grad_wq,
        grad_wk,
        grad_wv,
        grad_wo,
        mix_grad,
        router_grad,
        out_gate,
        out_up,
        out_down,
    )


def solution(mesh):
    dp_count, row_count, col_count = (mesh.shape[name] for name in ("dp", "row", "col"))

    def body(*args):
        hidden_in, w_key, w_gate = args[0], args[3], args[8]
        kv_here = w_key.shape[1] // HEAD_DIM
        one_each = w_gate.shape[0] == row_count * col_count
        pairs = hidden_in.shape[0] * kv_here == col_count
        sizes = (dp_count, row_count, col_count, kv_here) == (2, 4, 4, 2)
        return (owned if sizes and one_each and pairs else shards)(*args)

    placed = (
        P(None, ("dp", "row"), "col"),
        P(),
        P("col", "row"),
        P("col", "row"),
        P("col", "row"),
        P("row", "col"),
        P(),
        P(),
        P("dp", ("row", "col"), None),
        P("dp", ("row", "col"), None),
        P("dp", ("row", "col"), None),
        P(None, "dp", None),
        P(None, ("dp", "row", "col"), None),
        P(None, ("dp", "row", "col")),
        P(None, ("dp", "row", "col"), None),
    )
    return jax.shard_map(
        body,
        mesh=mesh,
        in_specs=placed,
        out_specs=(
            P(None, ("dp", "row", "col"), None),
            P(None, ("dp", "row"), "col"),
            P(),
            P("col", "row"),
            P("col", "row"),
            P("col", "row"),
            P("row", "col"),
            P(),
            P(),
            P("dp", ("row", "col"), None),
            P("dp", ("row", "col"), None),
            P("dp", ("row", "col"), None),
        ),
        check_vma=False,
    )
```

```python
import functools

import jax
import jax.numpy as jnp
from jax import lax
from jax.experimental import pallas as pl
from jax.experimental.pallas import tpu as pltpu
from jax.sharding import PartitionSpec as P

D = 1536
HEAD_DIM = 64
TOP = 8


eps_norm = 1e-06
resid_scale = 0.22
attn_scale = 0.015625
rope_base = 10000.0
highest = lax.Precision.HIGHEST


def shortened(shard):
    return jax.tree.map(lambda a: a.astype(jnp.bfloat16) if a.dtype == jnp.float32 else a, shard)


def documents(doc_lengths, length_all):
    doc_ends = jnp.cumsum(doc_lengths, dtype=jnp.int32)
    doc_starts = doc_ends - doc_lengths
    positions = jnp.arange(length_all, dtype=jnp.int32)
    doc_id = jnp.sum(
        (positions[:, None] >= doc_ends[None, :]).astype(jnp.int32), axis=1, dtype=jnp.int32
    )
    member = doc_id[:, None] == jnp.arange(doc_lengths.shape[0], dtype=jnp.int32)[None, :]
    doc_start = jnp.sum(jnp.where(member, doc_starts[None, :], 0), axis=1, dtype=jnp.int32)
    return (doc_id, positions - doc_start)


def angles(position, head_width):
    half_width = head_width // 2
    frequency = rope_base ** (-2.0 * jnp.arange(half_width, dtype=jnp.float32) / head_width)
    turned = position[:, None] * frequency[None, :]
    return (jnp.sin(turned)[:, None, :], jnp.cos(turned)[:, None, :])


def rotate(values, sin_table, cos_table):
    half_width = values.shape[-1] // 2
    front_half = values[..., :half_width]
    back_half = values[..., half_width:]
    return jnp.concatenate(
        [
            front_half * cos_table - back_half * sin_table,
            back_half * cos_table + front_half * sin_table,
        ],
        axis=-1,
    )


def gather_rows(value):
    return lax.all_gather(value, "row", axis=0, tiled=True)


def gather_cols(value):
    return jax.tree.map(
        lambda part, own: part.astype(own.dtype),
        lax.all_gather(shortened(value), "col", axis=0, tiled=True),
        value,
    )


def sum_cols(pieces):
    return lax.psum_scatter(pieces, "col", scatter_dimension=0, tiled=True)


def sum_rows(pieces):
    return lax.psum_scatter(pieces, "row", scatter_dimension=0, tiled=True)


def width_total(value):
    return lax.psum(value, "col")


def expert_trade(value):
    return lax.all_to_all(value, "dp", split_axis=1, concat_axis=1, tiled=True)


def attn_total(value):
    return jax.tree.map(lambda part: part.astype(jnp.float32), lax.psum(shortened(value), "dp"))


def expert_total(value):
    return jax.tree.map(
        lambda part: part.astype(jnp.float32),
        lax.psum_scatter(shortened(value), ("row", "col"), scatter_dimension=1, tiled=True),
    )


def add_all(first_set, second_set):
    return tuple((left_one + right_one for left_one, right_one in zip(first_set, second_set)))


def project(left_side, right_side):
    return jnp.dot(left_side, right_side, preferred_element_type=jnp.float32)


def shards(
    hidden_in,
    norm_gain,
    w_query,
    w_key,
    w_value,
    w_out,
    mix_gain,
    w_router,
    w_gate,
    w_up,
    w_down,
    lengths,
    routes,
    mask,
    cotangent,
):
    micro_count = hidden_in.shape[0]
    tok_dev = hidden_in.shape[1]
    width_part = hidden_in.shape[2]
    col_count = lax.axis_size("col")
    row_count = lax.axis_size("row")
    dp_count = lax.axis_size("dp")
    col_at = lax.axis_index("col")
    model_width = D
    heads_here = w_query.shape[1] // HEAD_DIM
    kv_here = w_key.shape[1] // HEAD_DIM
    group_size = heads_here // kv_here
    group_tokens = tok_dev * row_count
    quarter = tok_dev // col_count
    experts_here = w_gate.shape[0]
    experts_all = experts_here * dp_count
    capacity = quarter * 3 // 8
    slot_count = experts_all * capacity
    gain_part = lax.dynamic_slice_in_dim(norm_gain, col_at * width_part, width_part)
    router_wide = w_router.astype(jnp.float32)
    full_gate, full_up, full_down = (
        lax.all_gather(w_gate, ("row", "col"), axis=1, tiled=True),
        lax.all_gather(w_up, ("row", "col"), axis=1, tiled=True),
        lax.all_gather(w_down, ("row", "col"), axis=1, tiled=True),
    )
    expert_ids = jnp.arange(experts_all, dtype=jnp.int32)
    group_index = jnp.arange(group_tokens, dtype=jnp.int32)
    query_start = col_at * tok_dev
    query_index = query_start + jnp.arange(tok_dev, dtype=jnp.int32)
    attn_local = (
        jnp.zeros(w_query.shape, jnp.float32),
        jnp.zeros(w_key.shape, jnp.float32),
        jnp.zeros(w_value.shape, jnp.float32),
        jnp.zeros(w_out.shape, jnp.float32),
    )
    expert_local = (
        jnp.zeros(full_gate.shape, jnp.float32),
        jnp.zeros(full_up.shape, jnp.float32),
        jnp.zeros(full_down.shape, jnp.float32),
    )
    router_acc = jnp.zeros(w_router.shape, jnp.float32)
    norm_acc = jnp.zeros((width_part,), jnp.float32)
    mix_acc = jnp.zeros((model_width,), jnp.float32)
    layer_rows = []
    input_grads = []
    for step in range(micro_count):
        x_full = hidden_in[step].astype(jnp.float32)
        squares = width_total(jnp.sum(x_full * x_full, axis=1))
        scale_one = lax.rsqrt(squares / model_width + eps_norm)[:, None]
        unit_one = x_full * scale_one
        normed = (unit_one * gain_part).astype(jnp.bfloat16)
        normed_all = gather_rows(normed)
        query_p, key_p, value_p = sum_cols(
            (project(normed_all, w_query), project(normed_all, w_key), project(normed_all, w_value))
        )
        doc_all, pos_all = documents(lengths[step, 0], group_tokens)
        doc_query = lax.dynamic_slice_in_dim(doc_all, query_start, tok_dev)
        pos_query = lax.dynamic_slice_in_dim(pos_all, query_start, tok_dev).astype(jnp.float32)
        sin_table, cos_table = angles(pos_query, HEAD_DIM)
        query_rot = rotate(
            query_p.reshape(tok_dev, heads_here, HEAD_DIM), sin_table, cos_table
        ).astype(jnp.bfloat16)
        key_rot = rotate(key_p.reshape(tok_dev, kv_here, HEAD_DIM), sin_table, cos_table).astype(
            jnp.bfloat16
        )
        value_low = value_p.astype(jnp.bfloat16).reshape(tok_dev, kv_here, HEAD_DIM)
        keys_all, values_all = (
            lax.all_gather(key_rot, "col", axis=0, tiled=True),
            lax.all_gather(value_low, "col", axis=0, tiled=True),
        )
        allowed = (doc_query[:, None] == doc_all[None, :]) & (
            group_index[None, :] <= query_index[:, None]
        )
        query_grp = query_rot.reshape(tok_dev, kv_here, group_size, HEAD_DIM)
        raw_scores = jnp.einsum(
            "qhgd,khd->hgqk", query_grp, keys_all, preferred_element_type=jnp.float32
        )
        scores = jnp.where(allowed[None, None], raw_scores * attn_scale, -1e30)
        top_score = jnp.max(scores, axis=-1, keepdims=True)
        expd = jnp.exp(scores - top_score)
        row_total = jnp.sum(expd, axis=-1, keepdims=True)
        attn_probs = expd / row_total
        log_total = top_score + jnp.log(row_total)
        probs_low = attn_probs.astype(jnp.bfloat16)
        attended = jnp.einsum(
            "hgqk,khd->qhgd", probs_low, values_all, preferred_element_type=jnp.float32
        )
        attended_low = attended.reshape(tok_dev, heads_here * HEAD_DIM).astype(jnp.bfloat16)
        attended_all = gather_cols(attended_low)
        attn_branch = sum_rows(project(attended_all, w_out))
        mixed = x_full + resid_scale * attn_branch
        mixed_rows = lax.all_to_all(
            mixed.reshape(col_count, quarter, width_part),
            "col",
            split_axis=0,
            concat_axis=2,
            tiled=True,
        ).reshape(quarter, model_width)
        scale_two = lax.rsqrt(jnp.mean(mixed_rows * mixed_rows, axis=1, keepdims=True) + eps_norm)
        unit_two = mixed_rows * scale_two
        normed_two = (unit_two * mix_gain).astype(jnp.bfloat16)
        logits = project(normed_two, w_router)
        picks = routes[step]
        choose = (picks[:, :, None] == expert_ids[None, None, :]).astype(jnp.float32)
        chosen = jnp.sum(choose * logits[:, None, :], axis=-1)
        gate_weights = jax.nn.softmax(chosen, axis=-1)
        flat_picks = picks.reshape(-1)
        hit_table = (flat_picks[:, None] == expert_ids[None, :]).astype(jnp.int32)
        slot_rank = jnp.sum(
            hit_table * (jnp.cumsum(hit_table, axis=0, dtype=jnp.int32) - 1),
            axis=1,
            dtype=jnp.int32,
        )
        owner_dp = flat_picks // experts_here
        local_expert = flat_picks % experts_here
        slot_index = local_expert * (dp_count * capacity) + owner_dp * capacity + slot_rank
        token_of = (
            jnp.full((slot_count,), quarter, jnp.int32)
            .at[slot_index]
            .set(jnp.arange(quarter * TOP, dtype=jnp.int32) // TOP)
        )
        padded = jnp.concatenate([normed_two, jnp.zeros((1, model_width), jnp.bfloat16)], axis=0)
        send_rows = padded[token_of].reshape(experts_here, dp_count * capacity, model_width)
        expert_in = expert_trade(send_rows)
        gate_proj = jnp.einsum(
            "ecd,edf->ecf", expert_in, full_gate, preferred_element_type=jnp.float32
        )
        up_proj = jnp.einsum("ecd,edf->ecf", expert_in, full_up, preferred_element_type=jnp.float32)
        activated = (jax.nn.silu(gate_proj) * up_proj).astype(jnp.bfloat16)
        expert_out = jnp.einsum(
            "ecf,efd->ecd", activated, full_down, preferred_element_type=jnp.float32
        ).astype(jnp.bfloat16)
        returned = expert_trade(expert_out).reshape(slot_count, model_width)
        combined = returned[slot_index].reshape(quarter, TOP, model_width).astype(jnp.float32)
        expert_mix = jnp.sum(gate_weights[:, :, None] * combined, axis=1)
        layer_rows.append((mixed_rows + resid_scale * expert_mix).astype(jnp.bfloat16))
        grad_rows = cotangent[step].astype(jnp.float32) * mask[step][:, None].astype(jnp.float32)
        grad_mix = resid_scale * grad_rows
        grad_gates = jnp.sum(grad_mix[:, None, :] * combined, axis=-1)
        grad_chosen = gate_weights * (
            grad_gates - jnp.sum(gate_weights * grad_gates, axis=-1, keepdims=True)
        )
        grad_logits = jnp.sum(choose * grad_chosen[:, :, None], axis=1)
        gate_slots = (
            jnp.zeros((slot_count,), jnp.float32).at[slot_index].set(gate_weights.reshape(-1))
        )
        grad_pad = jnp.concatenate([grad_mix, jnp.zeros((1, model_width), jnp.float32)], axis=0)
        grad_send = (gate_slots[:, None] * grad_pad[token_of]).astype(jnp.bfloat16)
        grad_expert = expert_trade(
            grad_send.reshape(experts_here, dp_count * capacity, model_width)
        )
        grad_act = jnp.einsum(
            "ecd,efd->ecf", grad_expert, full_down, preferred_element_type=jnp.float32
        )
        micro_down = jnp.einsum(
            "ecf,ecd->efd", activated, grad_expert, preferred_element_type=jnp.float32
        )
        sigmoid_gate = jax.nn.sigmoid(gate_proj)
        silu_gate = gate_proj * sigmoid_gate
        grad_gate_p = (
            grad_act * up_proj * (sigmoid_gate + gate_proj * sigmoid_gate * (1.0 - sigmoid_gate))
        ).astype(jnp.bfloat16)
        grad_up_p = (grad_act * silu_gate).astype(jnp.bfloat16)
        grad_in = jnp.einsum(
            "ecf,edf->ecd", grad_gate_p, full_gate, preferred_element_type=jnp.float32
        ) + jnp.einsum("ecf,edf->ecd", grad_up_p, full_up, preferred_element_type=jnp.float32)
        micro_gate = jnp.einsum(
            "ecd,ecf->edf", expert_in, grad_gate_p, preferred_element_type=jnp.float32
        )
        micro_up = jnp.einsum(
            "ecd,ecf->edf", expert_in, grad_up_p, preferred_element_type=jnp.float32
        )
        expert_local = add_all(expert_local, (micro_gate, micro_up, micro_down))
        grad_back = expert_trade(grad_in.astype(jnp.bfloat16)).reshape(slot_count, model_width)
        grad_normed = jnp.sum(
            grad_back[slot_index].reshape(quarter, TOP, model_width).astype(jnp.float32), axis=1
        ) + jnp.dot(grad_logits, router_wide.T, precision=highest)
        router_acc = router_acc + jnp.dot(
            normed_two.astype(jnp.float32).T, grad_logits, precision=highest
        )
        mix_acc = mix_acc + jnp.sum(grad_normed * unit_two, axis=0)
        grad_scaled = grad_normed * mix_gain
        grad_mixed_rows = grad_rows + scale_two * (
            grad_scaled - unit_two * jnp.mean(grad_scaled * unit_two, axis=1, keepdims=True)
        )
        grad_mixed = lax.all_to_all(
            grad_mixed_rows.reshape(1, quarter, model_width),
            "col",
            split_axis=2,
            concat_axis=0,
            tiled=True,
        ).reshape(tok_dev, width_part)
        grad_branch = (resid_scale * grad_mixed).astype(jnp.bfloat16)
        grad_branch_all = gather_rows(grad_branch)
        micro_out = jnp.dot(attended_all.T, grad_branch_all, preferred_element_type=jnp.float32)
        grad_attended = sum_cols(
            jnp.dot(grad_branch_all, w_out.T, preferred_element_type=jnp.float32)
        )
        grad_att_low = grad_attended.astype(jnp.bfloat16).reshape(
            tok_dev, kv_here, group_size, HEAD_DIM
        )
        probs_again = jnp.exp(scores - log_total)
        grad_probs = jnp.einsum(
            "qhgd,khd->hgqk", grad_att_low, values_all, preferred_element_type=jnp.float32
        )
        grad_scores = probs_again * (
            grad_probs - jnp.sum(probs_again * grad_probs, axis=-1, keepdims=True)
        )
        grad_raw = (grad_scores * attn_scale).astype(jnp.bfloat16)
        probs_again_low = probs_again.astype(jnp.bfloat16)
        grad_query = jnp.einsum(
            "hgqk,khd->qhgd", grad_raw, keys_all, preferred_element_type=jnp.float32
        )
        grad_key_part = jnp.einsum(
            "hgqk,qhgd->khd", grad_raw, query_grp, preferred_element_type=jnp.float32
        )
        grad_value_part = jnp.einsum(
            "hgqk,qhgd->khd", probs_again_low, grad_att_low, preferred_element_type=jnp.float32
        )
        grad_key, grad_value = sum_cols(
            (
                grad_key_part.reshape(group_tokens, kv_here * HEAD_DIM),
                grad_value_part.reshape(group_tokens, kv_here * HEAD_DIM),
            )
        )
        grad_query_p = (
            rotate(grad_query.reshape(tok_dev, heads_here, HEAD_DIM), -sin_table, cos_table)
            .astype(jnp.bfloat16)
            .reshape(tok_dev, heads_here * HEAD_DIM)
        )
        grad_key_p = (
            rotate(grad_key.reshape(tok_dev, kv_here, HEAD_DIM), -sin_table, cos_table)
            .astype(jnp.bfloat16)
            .reshape(tok_dev, kv_here * HEAD_DIM)
        )
        grad_value_p = grad_value.astype(jnp.bfloat16)
        query_all, key_all, value_all = gather_cols((grad_query_p, grad_key_p, grad_value_p))
        micro_query = jnp.dot(normed_all.T, query_all, preferred_element_type=jnp.float32)
        micro_key = jnp.dot(normed_all.T, key_all, preferred_element_type=jnp.float32)
        micro_value = jnp.dot(normed_all.T, value_all, preferred_element_type=jnp.float32)
        grad_normed_one = sum_rows(
            jnp.dot(query_all, w_query.T, preferred_element_type=jnp.float32)
            + jnp.dot(key_all, w_key.T, preferred_element_type=jnp.float32)
            + jnp.dot(value_all, w_value.T, preferred_element_type=jnp.float32)
        )
        grad_scaled_one = grad_normed_one * gain_part
        inner_sum = width_total(jnp.sum(grad_scaled_one * unit_one, axis=1))
        norm_acc = norm_acc + jnp.sum(grad_normed_one * unit_one, axis=0)
        input_grads.append(
            grad_mixed
            + scale_one * (grad_scaled_one - unit_one * (inner_sum / model_width)[:, None])
        )
        attn_local = add_all(attn_local, (micro_query, micro_key, micro_value, micro_out))
    attn_summed = attn_total(attn_local)
    expert_summed = expert_total(expert_local)
    gain_full = lax.dynamic_update_slice_in_dim(
        jnp.zeros((model_width,), jnp.float32), norm_acc, col_at * width_part, 0
    )
    router_grad, gain_grad, mix_grad = lax.psum(
        (router_acc, gain_full, mix_acc), ("dp", "row", "col")
    )
    return (
        jnp.stack(layer_rows),
        jnp.stack(input_grads),
        gain_grad,
        attn_summed[0],
        attn_summed[1],
        attn_summed[2],
        attn_summed[3],
        mix_grad,
        router_grad,
        expert_summed[0],
        expert_summed[1],
        expert_summed[2],
    )


MESH = pl.DeviceIdType.MESH
ANYWHERE = pl.BlockSpec(memory_space=pl.ANY)


def group_size_of(axes):
    total = 1
    for axis in axes:
        total = total * lax.axis_size(axis)
    return total


def place_in(axes):
    at = 0
    for axis in axes:
        at = at * lax.axis_size(axis) + lax.axis_index(axis)
    return at


def device_at(axes, index):
    place = {}
    for axis in reversed(axes):
        place[axis] = index % lax.axis_size(axis)
        index = index // lax.axis_size(axis)
    return place


def meet(peers):
    barrier = pltpu.get_barrier_semaphore()
    for peer in peers:
        pl.semaphore_signal(barrier, inc=1, device_id=peer, device_id_type=MESH)
    pl.semaphore_wait(barrier, len(peers))


def send(src, dst, send_sem, recv_sem, peer):
    copy = pltpu.make_async_remote_copy(
        src_ref=src,
        dst_ref=dst,
        send_sem=send_sem,
        recv_sem=recv_sem,
        device_id=peer,
        device_id_type=MESH,
    )
    copy.start()
    return copy


def row_peers():
    row = lax.axis_index("row")
    rows = lax.axis_size("row")
    across = (row + rows // 2) % rows
    beside = row + 1 - 2 * (row % 2)
    return row, across, beside


def col_peers():
    col, cols = lax.axis_index("col"), lax.axis_size("col")
    two_on = (col + 2) % cols
    near = col + 1 - 2 * (col % 2)
    return two_on, near, (col, two_on, near, (near + 2) % cols)


def gather_line(source, target, sems, copies):
    local_sem, send_sem, col_sem, dp_sem, across_sem, beside_sem = sems
    row, across, beside = row_peers()
    rows, cols = lax.axis_size("row"), lax.axis_size("col")
    dp = lax.axis_index("dp")
    other = 1 - dp
    two_on, near, order = col_peers()
    far = (beside + rows // 2) % rows
    sent = []

    def block_of(dp_from, row_from, step):
        return (dp_from * rows + row_from) * cols + order[step]

    def arrival(block, sem):
        pltpu.make_async_copy(target.at[block], target.at[block], sem).wait()

    def pass_on(part, block, sem, peer):
        copy = send(part, target.at[block], send_sem.at[len(sent)], sem, peer)
        sent.append(copy)
        copies.append(copy)

    me = block_of(dp, row, 0)
    own = pltpu.make_async_copy(source.at[0], target.at[me], local_sem)

    def begin():
        own.start()
        pass_on(source.at[0], me, col_sem.at[1], {"col": two_on})
        pass_on(source.at[0], me, col_sem.at[2], {"col": near})

    def line(step):
        block = block_of(dp, row, step)
        part = source.at[0] if step == 0 else target.at[block]
        if step > 0:
            arrival(block, col_sem.at[step])
        if step == 1:
            pass_on(part, block, col_sem.at[3], {"col": near})
        pass_on(part, block, dp_sem.at[step], {"dp": other})
        pass_on(part, block, across_sem.at[step], {"row": across})
        pass_on(part, block, beside_sem.at[step], {"row": beside})

    def side(step):
        block = block_of(other, row, step)
        arrival(block, dp_sem.at[step])
        pass_on(target.at[block], block, beside_sem.at[cols + step], {"row": beside})
        block = block_of(dp, across, step)
        arrival(block, across_sem.at[step])
        pass_on(target.at[block], block, dp_sem.at[cols + step], {"dp": other})
        pass_on(target.at[block], block, beside_sem.at[2 * cols + step], {"row": beside})

    def corner(step):
        block = block_of(other, across, step)
        arrival(block, dp_sem.at[cols + step])
        pass_on(target.at[block], block, beside_sem.at[3 * cols + step], {"row": beside})

    def finish():
        for turn, (dp_from, row_from) in enumerate(
            ((dp, beside), (other, beside), (dp, far), (other, far))
        ):
            for step in range(cols):
                arrival(block_of(dp_from, row_from, step), beside_sem.at[turn * cols + step])
        own.wait()

    return begin, line, side, corner, finish


def gather_sems():
    cols = lax.axis_size("col")
    return [
        pltpu.SemaphoreType.DMA,
        pltpu.SemaphoreType.DMA((40,)),
        pltpu.SemaphoreType.DMA((cols,)),
        pltpu.SemaphoreType.DMA((2 * cols,)),
        pltpu.SemaphoreType.DMA((2 * cols,)),
        pltpu.SemaphoreType.DMA((4 * cols,)),
    ]


def nt(left, right):
    return lax.dot_general(
        left, right, (((1,), (1,)), ((), ())), preferred_element_type=jnp.float32
    )


def tn(left, right):
    return lax.dot_general(
        left, right, (((0,), (0,)), ((), ())), preferred_element_type=jnp.float32
    )


def norm_rows(x, gain):
    scale = lax.rsqrt(jnp.mean(x * x, axis=1, keepdims=True) + eps_norm)
    return scale, (x * scale * gain).astype(jnp.bfloat16)


def turn(values, cos_table, sin_table):
    lane = lax.broadcasted_iota(jnp.int32, values.shape, 1)
    ahead = pltpu.roll(values, values.shape[1] - HEAD_DIM // 2, 1)
    behind = pltpu.roll(values, HEAD_DIM // 2, 1)
    return values * cos_table + jnp.where(lane % HEAD_DIM < HEAD_DIM // 2, ahead, behind) * sin_table


def key_extent(block, rows, total):
    return min(total, -(-(block + 1) * rows // 128) * 128)


def visible(doc_col, doc_row, block, rows, extent):
    query = block * rows + lax.broadcasted_iota(jnp.int32, (rows, extent), 0)
    keys = lax.broadcasted_iota(jnp.int32, (rows, extent), 1)
    same = doc_col[block * rows : (block + 1) * rows, 0:1] == doc_row[0:1, 0:extent]
    return same & (keys <= query)


def attend(query, key, allowed):
    scores = jnp.where(allowed, nt(query, key) * attn_scale, -1e30)
    raised = jnp.exp(scores - jnp.max(scores, axis=1, keepdims=True))
    return raised / jnp.sum(raised, axis=1, keepdims=True)


def front_kernel(
    x,
    w_qkv,
    w_out,
    picks,
    cot,
    w_gate,
    w_up,
    w_down,
    gain_one,
    gain_two,
    cos_table,
    sin_table,
    doc_col,
    doc_row,
    router_t,
    table,
    x_all,
    w_mine,
    w_out_mine,
    cot_all,
    normed_all,
    qkv,
    attended,
    mixed,
    gates_own,
    rows_part,
    mix_part,
    scores,
    grads_gu,
    grads_down,
    w_out_all,
    picks_all,
    x_own,
    att_own,
    normed_two,
    gate_up,
    down,
    down_grad,
    pool_rows,
    pool_cots,
    kept_in,
    kept_dy,
    kept_dye,
    kept_act,
    kept_gate,
    kept_up,
    gate_proj,
    up_proj,
    kept_weight,
    ranks,
    upper,
    load_sem,
    store_sem,
    grad_local,
    grad_send,
    grad_recv,
    local_sem,
    send_sem,
    x_sem,
    q_sem,
    o_sem,
    own_sem,
    att_send,
    att_recv,
    ship_local,
    ship_send,
    ship_recv,
    *line_sems,
):
    row, across, beside = row_peers()
    rows, cols = lax.axis_size("row"), lax.axis_size("col")
    col, dp = lax.axis_index("col"), lax.axis_index("dp")
    other = 1 - dp
    far = (beside + rows // 2) % rows
    plane = ("row", "col")
    size, me = group_size_of(plane), place_in(plane)
    low = jnp.bfloat16
    meet(
        [device_at(plane, (me + step) % size) for step in range(1, size)] + [{"dp": other}]
    )
    copies, locals_, sent, moved = [], [], [], []
    picks_line = gather_line(picks, picks_all, line_sems[0:6], copies)
    cot_line = gather_line(cot, cot_all, line_sems[6:12], copies)
    norm_line = gather_line(normed_two, normed_all, line_sems[12:18], copies)

    def pass_on(src, dst, sem, peer):
        sent.append(send(src, dst, send_sem.at[len(sent)], sem, peer))

    def arrival(ref, sem):
        pltpu.make_async_copy(ref, ref, sem).wait()

    def local(src, dst):
        copy = pltpu.make_async_copy(src, dst, local_sem.at[len(locals_)])
        copy.start()
        locals_.append(copy)

    slice_rows, ff_width = w_gate.shape[1:]
    down_rows = w_down.shape[1]
    chunks = w_down.shape[2] // ff_width

    def weight_parts(to, at):
        parts = [
            (w_gate.at[to], gate_up.at[at, 0:slice_rows]),
            (w_up.at[to], gate_up.at[at, slice_rows : 2 * slice_rows]),
        ]
        for chunk in range(chunks):
            parts.append(
                (
                    w_down.at[to, :, chunk * ff_width : (chunk + 1) * ff_width],
                    down.at[at, chunk * down_rows : (chunk + 1) * down_rows],
                )
            )
        return parts

    def ship(first, last, which=range(2)):
        for step in range(first, last):
            to = (me + step) % size
            for part in which:
                source, target = weight_parts(to, me)[part]
                moved.append(
                    send(
                        source,
                        target,
                        ship_send.at[part, step],
                        ship_recv.at[part, step],
                        device_at(plane, to),
                    )
                )

    def shipped(which):
        for step in range(1, size):
            for part in which:
                arrival(
                    weight_parts(me, (me + size - step) % size)[part][1], ship_recv.at[part, step]
                )

    def origin(step):
        return (col + cols - step) % cols

    two_on, near, order = col_peers()

    micro, depth, width = x.shape
    quarter = depth // cols
    half_depth = w_out.shape[1]

    def lanes_of(at):
        return pl.ds(pl.multiple_of(at * width, width), width)

    def lanes(step):
        return lanes_of(order[step])

    def x_at(row_from, step):
        return x_all.at[pl.ds(pl.multiple_of(row_from * depth, depth), depth), lanes(step)]

    def out_at(row_from, step, half):
        first = pl.multiple_of((row_from * 2 + half) * half_depth, half_depth)
        return w_out_all.at[pl.ds(first, half_depth), lanes(step)]

    def own_at(m, step):
        return x_own.at[pl.ds(m * quarter, quarter), lanes_of(origin(step))]

    my_x = x_at(row, 0)
    for step in range(1, cols):
        to = (col + step) % cols
        if step < 3:
            peer = (two_on, near)[step - 1]
            pass_on(x.at[peer // 2], my_x, x_sem.at[step], {"col": peer})
        pass_on(w_qkv.at[to % 2, dp], w_mine.at[col, dp], q_sem.at[step], {"col": to})
    local(x.at[col // 2], my_x)
    local(w_qkv.at[col % 2], w_mine.at[col])
    for half in range(2):
        local(w_out.at[half], out_at(row, 0, half))
    pass_on(x.at[col // 2], my_x, x_sem.at[cols], {"row": across})
    pass_on(x.at[col // 2], my_x, x_sem.at[2 * cols], {"row": beside})
    for step in range(1, cols):
        to = (col + step) % cols
        if step < 3:
            peer = (two_on, near)[step - 1]
            pass_on(w_out.at[dp], out_at(row, 0, dp), o_sem.at[step], {"col": peer})
        first = pl.multiple_of(to * quarter, quarter)
        for m in range(micro):
            pass_on(
                x.at[m, pl.ds(first, quarter)],
                own_at(m, 0),
                own_sem.at[m * cols + step],
                {"col": to},
            )
    for m in range(micro):
        local(x.at[m, pl.ds(pl.multiple_of(col * quarter, quarter), quarter)], own_at(m, 0))
    for half in range(2):
        pass_on(w_out.at[half], out_at(row, 0, half), o_sem.at[(2 + half) * cols], {"row": across})
        pass_on(w_out.at[half], out_at(row, 0, half), o_sem.at[(4 + half) * cols], {"row": beside})
    for step in range(1, cols):
        part = x_at(row, step)
        arrival(part, x_sem.at[step])
        if step == 1:
            pass_on(part, part, x_sem.at[3], {"col": near})
        pass_on(part, part, x_sem.at[cols + step], {"row": across})
        pass_on(part, part, x_sem.at[2 * cols + step], {"row": beside})
        part = w_mine.at[origin(step), dp]
        arrival(part, q_sem.at[step])
        pass_on(part, part, q_sem.at[cols + step], {"dp": other})
    for step in range(cols):
        part = x_at(across, step)
        arrival(part, x_sem.at[cols + step])
        pass_on(part, part, x_sem.at[3 * cols + step], {"row": beside})
    for step in range(1, cols):
        part = out_at(row, step, dp)
        arrival(part, o_sem.at[step])
        if step == 1:
            pass_on(part, part, o_sem.at[3], {"col": near})
        pass_on(part, part, o_sem.at[cols + step], {"dp": other})
        pass_on(part, part, o_sem.at[2 * cols + step], {"row": across})
        pass_on(part, part, o_sem.at[4 * cols + step], {"row": beside})
    picks_line[0]()
    cot_line[0]()
    for source, target in weight_parts(me, me):
        local(source, target)
    for step in range(1, cols):
        arrival(w_mine.at[origin(step), other], q_sem.at[cols + step])
    for at, row_from in enumerate((beside, far)):
        for step in range(cols):
            arrival(x_at(row_from, step), x_sem.at[(2 + at) * cols + step])
    for copy in locals_[:6]:
        copy.wait()

    tokens, model_width = x_all.shape
    projection = w_mine[...].reshape(model_width, w_mine.shape[3])
    for block in range(rows):
        part = slice(block * depth, (block + 1) * depth)
        _, normed = norm_rows(x_all[part, :].astype(jnp.float32), gain_one[...])
        values = project(normed, projection)
        cosine, sine = cos_table[part, :], sin_table[part, :]
        for at in range(2):
            piece = slice(at * 128, (at + 1) * 128)
            qkv[part, piece] = turn(values[:, piece], cosine, sine).astype(low)
        qkv[part, 256:] = values[:, 256:].astype(low)
    heads = attended.shape[2] // HEAD_DIM
    kv_at = heads * HEAD_DIM
    for block in range(rows):
        extent = key_extent(block, depth, tokens)
        allowed = visible(doc_col, doc_row, block, depth, extent)
        key = qkv[0:extent, kv_at : kv_at + HEAD_DIM]
        value = qkv[0:extent, kv_at + HEAD_DIM : kv_at + 2 * HEAD_DIM]
        outs = []
        for head in range(heads):
            query = qkv[
                block * depth : (block + 1) * depth, head * HEAD_DIM : (head + 1) * HEAD_DIM
            ]
            outs.append(project(attend(query, key, allowed).astype(low), value))
        out = jnp.concatenate(outs, axis=1).astype(low)
        attended[block * cols : (block + 1) * cols] = out.reshape(cols, quarter, out.shape[1])
    for step in range(1, size):
        to = (me + step) % size
        moved.append(
            send(
                attended.at[to],
                att_own.at[me],
                att_send.at[step],
                att_recv.at[step],
                device_at(plane, to),
            )
        )
    stay = pltpu.make_async_copy(attended.at[me], att_own.at[me], att_send.at[0])
    stay.start()
    for step in range(1, cols):
        part = out_at(row, step, other)
        arrival(part, o_sem.at[cols + step])
        pass_on(part, part, o_sem.at[3 * cols + step], {"row": across})
        pass_on(part, part, o_sem.at[5 * cols + step], {"row": beside})
    for step in range(cols):
        picks_line[1](step)
        cot_line[1](step)
    ship(1, 5)
    for at in range(2):
        for step in range(cols):
            half = at if step == 0 else (dp if at == 0 else other)
            part = out_at(across, step, half)
            arrival(part, o_sem.at[(2 + at) * cols + step])
            pass_on(part, part, o_sem.at[(6 + at) * cols + step], {"row": beside})
    for at, row_from in enumerate((beside, far)):
        for step in range(cols):
            for part in range(2):
                half = part if step == 0 else (dp if part == 0 else other)
                arrival(out_at(row_from, step, half), o_sem.at[(4 + 2 * at + part) * cols + step])
    for step in range(1, cols):
        for m in range(micro):
            arrival(own_at(m, step), own_sem.at[m * cols + step])
    stay.wait()
    for step in range(1, size):
        arrival(att_own.at[(me + size - step) % size], att_recv.at[step])
    pairs = cols // micro
    for m in range(micro):
        total = jnp.zeros((quarter, model_width), jnp.float32)
        for row_from in range(rows):
            for pair in range(pairs):
                first = (row_from * pairs + pair) * kv_at
                total = total + project(
                    att_own[row_from * cols + m * pairs + pair],
                    w_out_all[first : first + kv_at, :],
                )
        part = slice(m * quarter, (m + 1) * quarter)
        value = x_own[part, :].astype(jnp.float32) + resid_scale * total
        mixed[part, :] = value
        normed_two[0, part, :] = norm_rows(value, gain_two[...])[1]

    begin, line, side, corner, finish = norm_line
    begin()
    for step in range(cols):
        picks_line[2](step)
        cot_line[2](step)
        ship(5 + 2 * step, 7 + 2 * step)
    for step in range(cols):
        line(step)
    ship(5 + 2 * cols, size)
    ship(1, size, range(2, 2 + chunks))
    logits = jnp.where(table[...] > 0, nt(normed_two[0], router_t[...]), -jnp.inf)
    raised = jnp.exp(logits - jnp.max(logits, axis=1, keepdims=True))
    gates_own[...] = raised / jnp.sum(raised, axis=1, keepdims=True)
    w_out_mine[...] = w_out_all[
        pl.ds(pl.multiple_of((row * 2 + col % 2) * kv_at, kv_at), kv_at), :
    ]
    for step in range(cols):
        picks_line[3](step)
        cot_line[3](step)
        side(step)
    for step in range(cols):
        corner(step)
    picks_line[4]()
    cot_line[4]()
    finish()

    everyone = ("dp", "row", "col")
    expert = place_in(everyone)
    tiles, slots = kept_in.shape[0], kept_in.shape[1]
    padded = pool_rows.shape[2]
    block_rows = micro * quarter
    span = cols * padded
    pool_rows[...] = jnp.zeros_like(pool_rows)
    pool_cots[...] = jnp.zeros_like(pool_cots)
    upper[...] = (
        lax.broadcasted_iota(jnp.int32, upper.shape, 0)
        < lax.broadcasted_iota(jnp.int32, upper.shape, 1)
    ).astype(low)

    def pool(tile, slot):
        for at, (source, target) in enumerate(((normed_all, pool_rows), (cot_all, pool_cots))):
            yield pltpu.make_async_copy(
                source.at[pl.ds(tile * cols, cols)],
                target.at[slot, :, 0:block_rows],
                load_sem.at[at, slot],
            )

    for copy in pool(0, 0):
        copy.start()
    slot_of = lax.broadcasted_iota(jnp.int32, (slots, span), 0)

    def picked(tile):
        return slot_of == ranks[tile][0:1, :]

    @pl.loop(0, tiles)
    def _(tile):
        slot = tile % 2
        for copy in pool(tile, slot):
            copy.wait()

        @pl.when(tile + 1 < tiles)
        def _():
            for copy in pool(tile + 1, 1 - slot):
                copy.start()

        rows_here = pool_rows[slot].reshape(span, model_width)
        logits = nt(router_t[...], rows_here)[0 : picks_all.shape[0], :]
        ids = lax.broadcasted_iota(jnp.int32, logits.shape, 0)
        names = jnp.concatenate([picks_all[tile * cols + at] for at in range(cols)], axis=1)
        chosen = ids == names[0:1, :]
        for choice in range(1, names.shape[0]):
            chosen = chosen | (ids == names[choice : choice + 1, :])
        logits = jnp.where(chosen, logits, -1e30)
        raised = jnp.where(chosen, jnp.exp(logits - jnp.max(logits, axis=0, keepdims=True)), 0.0)
        total = jnp.sum(raised, axis=0, keepdims=True)
        mine = ids == expert
        gate = jnp.sum(jnp.where(mine, raised, 0.0), axis=0, keepdims=True) / jnp.where(
            total > 0, total, 1.0
        )
        here = jnp.max(jnp.where(mine & chosen, 1.0, 0.0), axis=0, keepdims=True)
        before = project(jnp.broadcast_to(here, (16, span)).astype(low), upper[...])[0:1, :]
        rank = jnp.where(here > 0, before.astype(jnp.int32), -1)
        ranks[tile] = jnp.broadcast_to(rank, ranks.shape[1:])
        select = slot_of == rank
        kept_weight[tile] = jnp.broadcast_to(
            jnp.sum(jnp.where(select, gate, 0.0), axis=1, keepdims=True), kept_weight.shape[1:]
        )
        select = select.astype(low)
        kept_in[tile] = project(select, rows_here).astype(low)
        kept_dy[tile] = project(select, pool_cots[slot].reshape(span, model_width)).astype(low)

    shipped(range(2))
    for copy in locals_[6:]:
        copy.wait()
    gate_w = gate_up[:, 0:slice_rows, :].reshape(model_width, ff_width)
    up_w = gate_up[:, slice_rows : 2 * slice_rows, :].reshape(model_width, ff_width)

    def down_w(chunk):
        at = chunk * down_rows
        return down[:, at : at + down_rows, :].reshape(ff_width, ff_width)

    def two(ref, pair):
        part = ref[pl.ds(2 * pair, 2)]
        return part.reshape(2 * slots, part.shape[2])

    def put(ref, pair, value):
        ref[pl.ds(2 * pair, 2)] = value.reshape(2, slots, value.shape[1])

    @pl.loop(0, tiles // 2)
    def _(pair):
        rows_in = two(kept_in, pair)
        gate_value = project(rows_in, gate_w)
        up_value = project(rows_in, up_w)
        put(gate_proj, pair, gate_value)
        put(up_proj, pair, up_value)
        put(kept_act, pair, (gate_value / (1.0 + jnp.exp(-gate_value)) * up_value).astype(low))
        weight = two(kept_weight, pair)[:, 0:1]
        grad_mix = resid_scale * two(kept_dy, pair).astype(jnp.float32)
        put(kept_dye, pair, (weight * grad_mix).astype(low))

    def all_of(ref):
        value = ref[...]
        return value.reshape(tiles * slots, value.shape[2])

    act_all = all_of(kept_act)
    for chunk in range(chunks):
        grad = tn(act_all, all_of(kept_dye.at[:, :, chunk * ff_width : (chunk + 1) * ff_width]))
        at = chunk * down_rows
        down_grad[:, at : at + down_rows, :] = grad.astype(low).reshape(size, down_rows, ff_width)
    home = pltpu.make_async_copy(down_grad.at[me], grads_down.at[me], grad_local)
    home.start()
    given = []
    for step in range(1, size):
        to = (me + step) % size
        given.append(
            send(
                down_grad.at[to],
                grads_down.at[me],
                grad_send.at[step],
                grad_recv.at[step],
                device_at(plane, to),
            )
        )
    shipped(range(2, 2 + chunks))

    def spill(tile, slot):
        for at, (source, target) in enumerate(((pool_rows, rows_part), (pool_cots, mix_part))):
            yield pltpu.make_async_copy(
                source.at[slot, :, 0:block_rows],
                target.at[pl.ds(tile * cols, cols)],
                store_sem.at[at, slot],
            )

    @pl.loop(0, tiles // 2)
    def _(pair):
        act = two(kept_act, pair)
        grad_out = two(kept_dye, pair)
        gate_value, up_value = two(gate_proj, pair), two(up_proj, pair)
        weight = two(kept_weight, pair)[:, 0:1]
        score = jnp.zeros((2 * slots, 1), jnp.float32)
        grad_act = jnp.zeros((2 * slots, ff_width), jnp.float32)

        @pl.when(pair > 0)
        def _():
            for at in range(2):
                for copy in spill(2 * pair - 2 + at, at):
                    copy.wait()

        selects = [picked(2 * pair + at).astype(low) for at in range(2)]
        for chunk in range(chunks):
            lanes = slice(chunk * ff_width, (chunk + 1) * ff_width)
            part = down_w(chunk)
            out = project(act, part).astype(low).astype(jnp.float32)
            grad_mix = resid_scale * kept_dy[pl.ds(2 * pair, 2), :, lanes].reshape(
                2 * slots, ff_width
            ).astype(jnp.float32)
            score = score + jnp.sum(grad_mix * out, axis=1, keepdims=True)
            mixed_rows = (weight * out).astype(low)
            for at in range(2):
                pool_cots[at, :, :, lanes] = (
                    tn(selects[at], mixed_rows[at * slots : (at + 1) * slots])
                    .astype(low)
                    .reshape(cols, padded, ff_width)
                )
            grad_act = grad_act + nt(grad_out[:, lanes], part)
        sigmoid = 1.0 / (1.0 + jnp.exp(-gate_value))
        grad_gate = (
            grad_act * up_value * (sigmoid + gate_value * sigmoid * (1.0 - sigmoid))
        ).astype(low)
        grad_up = (grad_act * (gate_value * sigmoid)).astype(low)
        put(kept_gate, pair, grad_gate)
        put(kept_up, pair, grad_up)
        grad_in = (nt(grad_gate, gate_w) + nt(grad_up, up_w)).astype(low)
        for at in range(2):
            tile = 2 * pair + at
            part = slice(at * slots, (at + 1) * slots)
            pool_rows[at] = (
                tn(selects[at], grad_in[part]).astype(low).reshape(cols, padded, model_width)
            )
            line_of = jnp.sum(jnp.where(picked(tile), score[part], 0.0), axis=0, keepdims=True)
            for block in range(cols):
                scores[tile * cols + block] = jnp.broadcast_to(
                    line_of[:, block * padded : (block + 1) * padded], scores.shape[1:]
                )
            for copy in spill(tile, at):
                copy.start()

    rows_all = all_of(kept_in)
    for at, kept in ((0, kept_gate), (slice_rows, kept_up)):
        grad = tn(rows_all, all_of(kept)).astype(low)
        grads_gu[:, at : at + slice_rows, :] = grad.reshape(size, slice_rows, ff_width)
    for at in range(2):
        for copy in spill(tiles - 2 + at, at):
            copy.wait()
    home.wait()
    for copy in given:
        copy.wait()
    for copy in moved + copies + sent:
        copy.wait_send()


def front(number, x, w_qkv, w_out, picks, cot, experts, gains, tables, docs, routing, heads_width):
    cols, rows = lax.axis_size("col"), lax.axis_size("row")
    total, plane = group_size_of(("dp", "row", "col")), group_size_of(("row", "col"))
    micro, depth, part_width = x.shape
    width, tokens, low = part_width * cols, depth * rows, jnp.bfloat16
    wide = jnp.float32
    quarter = depth // cols
    _, slice_rows, ff_width = experts[0].shape
    down_depth = slice_rows * plane // ff_width * experts[2].shape[1]
    tiles = total // cols
    slots = cols * micro * (quarter * 3 // 8)
    vmem = pl.BlockSpec(memory_space=pltpu.VMEM)
    shape, dma = jax.ShapeDtypeStruct, pltpu.SemaphoreType.DMA
    pool = pltpu.VMEM((2, cols, 128, width), low)
    return pl.pallas_call(
        front_kernel,
        out_shape=[
            shape((tokens, width), low),
            shape((cols,) + w_qkv.shape[1:], low),
            shape((heads_width, width), low),
            shape((total,) + cot.shape, low),
            shape((total,) + cot.shape, low),
            shape((tokens, w_qkv.shape[3]), low),
            shape((plane, quarter, heads_width), low),
            shape((micro * quarter, width), wide),
            shape((micro * quarter, 128), wide),
            shape((total,) + cot.shape, low),
            shape((total,) + cot.shape, low),
            shape((total, 8, 128), wide),
            shape((plane, 2 * slice_rows, ff_width), low),
            shape((plane, down_depth, ff_width), low),
        ],
        in_specs=[ANYWHERE] * 8 + [vmem] * 8,
        out_specs=[vmem] * 3
        + [ANYWHERE] * 2
        + [vmem] * 4
        + [ANYWHERE] * 2
        + [vmem] * 2
        + [ANYWHERE],
        scratch_shapes=[
            pltpu.VMEM((rows * 2 * w_out.shape[1], width), low),
            pltpu.VMEM((total,) + picks.shape, picks.dtype),
            pltpu.VMEM((micro * quarter, width), low),
            pltpu.VMEM((plane, quarter, heads_width), low),
            pltpu.VMEM((1, micro * quarter, width), low),
            pltpu.VMEM((plane, 2 * slice_rows, ff_width), low),
            pltpu.VMEM((plane, down_depth, ff_width), low),
            pltpu.VMEM((plane, down_depth, ff_width), low),
            pool,
            pool,
            pltpu.VMEM((tiles, slots, width), low),
            pltpu.VMEM((tiles, slots, width), low),
            pltpu.VMEM((tiles, slots, width), low),
            pltpu.VMEM((tiles, slots, ff_width), low),
            pltpu.VMEM((tiles, slots, ff_width), low),
            pltpu.VMEM((tiles, slots, ff_width), low),
            pltpu.VMEM((tiles, slots, ff_width), wide),
            pltpu.VMEM((tiles, slots, ff_width), wide),
            pltpu.VMEM((tiles, slots, 128), wide),
            pltpu.VMEM((tiles, 8, cols * 128), jnp.int32),
            pltpu.VMEM((cols * 128, cols * 128), low),
            dma((2, 2)),
            dma((2, 2)),
            dma,
            dma((plane,)),
            dma((plane,)),
            dma((12,)),
            dma((72,)),
            dma((4 * cols,)),
            dma((2 * cols,)),
            dma((8 * cols,)),
            dma((micro * cols,)),
            dma((plane,)),
            dma((plane,)),
            dma,
            dma((8, plane)),
            dma((8, plane)),
        ]
        + gather_sems() * 3,
        compiler_params=pltpu.CompilerParams(
            collective_id=number, has_side_effects=True, vmem_limit_bytes=63 * 2**20
        ),
        name="front" + str(number),
    )(x, w_qkv, w_out, picks[None], cot[None], *experts, *gains, *tables, *docs, *routing)


def sum_scratch(block):
    cols = lax.axis_size("col")
    low = jnp.bfloat16
    return [
        pltpu.VMEM((4 * cols,) + block, low),
        pltpu.VMEM((4 * cols,) + block, low),
        pltpu.VMEM((4 * cols,) + block, low),
        pltpu.VMEM((3 * cols,) + block, low),
        pltpu.VMEM((cols,) + block, low),
        pltpu.SemaphoreType.DMA((4 * cols,)),
        pltpu.SemaphoreType.DMA((48,)),
        pltpu.SemaphoreType.DMA((4 * cols,)),
        pltpu.SemaphoreType.DMA((cols,)),
        pltpu.SemaphoreType.DMA((2 * cols,)),
        pltpu.SemaphoreType.DMA((cols,)),
    ]


def sum_steps(partial, sems, copies):
    (
        near,
        mine,
        passed,
        stage,
        last,
        local_sem,
        send_sem,
        beside_sem,
        first_sem,
        second_sem,
        col_sem,
    ) = sems
    row, across, beside = row_peers()
    rows, cols = lax.axis_size("row"), lax.axis_size("col")
    col, dp = lax.axis_index("col"), lax.axis_index("dp")
    other = 1 - dp
    low = jnp.bfloat16
    two_on, beside_col, _ = col_peers()
    order = (beside_col, (beside_col + 2) % cols, two_on, col)
    sent = []

    def pass_on(src, dst, sem, peer):
        copy = send(src, dst, send_sem.at[len(sent)], sem, peer)
        sent.append(copy)
        copies.append(copy)

    def arrival(ref, sem):
        pltpu.make_async_copy(ref, ref, sem).wait()

    def block_of(dp_to, row_to, col_to):
        return (dp_to * rows + row_to) * cols + col_to

    far = (beside + rows // 2) % rows
    theirs = ((other, far), (other, beside), (dp, far), (dp, beside))
    ours = ((other, across), (other, row), (dp, across), (dp, row))

    def start():
        for turn in range(4):
            for at in range(cols):
                slot = turn * cols + at
                pass_on(
                    partial.at[block_of(*theirs[turn], order[at])],
                    near.at[slot],
                    beside_sem.at[slot],
                    {"row": beside},
                )
                pltpu.make_async_copy(
                    partial.at[block_of(*ours[turn], order[at])], mine.at[slot], local_sem.at[slot]
                ).start()

    def combine(target, *parts):
        rows_each = 16

        @pl.loop(0, target.shape[0] // rows_each)
        def _(at):
            lines = pl.ds(pl.multiple_of(at * rows_each, rows_each), rows_each)
            value = parts[0][lines, :].astype(jnp.float32)
            for part in parts[1:]:
                value = value + part[lines, :].astype(jnp.float32)
            target[lines, :] = value.astype(target.dtype)

    def chip(slot):
        arrival(mine.at[slot], local_sem.at[slot])
        arrival(near.at[slot], beside_sem.at[slot])
        return mine.at[slot], near.at[slot]

    def diagonal():
        for at in range(cols):
            combine(passed.at[at], *chip(at))
            peer = {"dp": other} if at < 2 else {"row": across}
            pass_on(passed.at[at], stage.at[at], first_sem.at[at], peer)

    def middle():
        for at in range(cols):
            for turn, here, peer in ((1, at >= 2, {"dp": other}), (2, at < 2, {"row": across})):
                slot = turn * cols + at
                parts = chip(slot)
                if here:
                    arrival(stage.at[at], first_sem.at[at])
                    parts = parts + (stage.at[at],)
                combine(passed.at[slot], *parts)
                pass_on(passed.at[slot], stage.at[slot], second_sem.at[slot - cols], peer)

    def chip_total(at):
        parts = chip(3 * cols + at)
        for turn in (1, 2):
            slot = turn * cols + at
            arrival(stage.at[slot], second_sem.at[slot - cols])
            parts = parts + (stage.at[slot],)
        return parts

    def spread():
        for at in range(2):
            combine(passed.at[3 * cols + at], *chip_total(at))
            pass_on(passed.at[3 * cols + at], last.at[at], col_sem.at[at], {"col": beside_col})
        parts = chip_total(2)
        arrival(last.at[1], col_sem.at[1])
        combine(passed.at[3 * cols + 2], *parts, last.at[1])
        pass_on(passed.at[3 * cols + 2], last.at[2], col_sem.at[2], {"col": two_on})

    def total(target):
        parts = chip_total(3)
        for at in (0, 2):
            arrival(last.at[at], col_sem.at[at])
            parts = parts + (last.at[at],)
        combine(target, *parts)

    return start, diagonal, middle, spread, total


def back_kernel(
    partial,
    mix_part,
    grads,
    scores,
    normed_all,
    mixed,
    cot,
    gates,
    router_t,
    gain_one,
    gain_two,
    x_all,
    w_mine,
    w_out_mine,
    qkv,
    attended,
    cos_table,
    sin_table,
    doc_col,
    doc_row,
    mix_out,
    grads_own,
    dw_pair,
    do_pair,
    router_pair,
    x_grads,
    lines_all,
    scores_in,
    branch,
    branch_all,
    logits,
    logits_all,
    plane_rows,
    rotated,
    values_grad,
    grad_att,
    grad_qkv,
    normed,
    heads,
    heads_near,
    heads_across,
    heads_pair,
    heads_passed,
    dw_send,
    dw_in,
    do_send,
    do_in,
    x_send,
    lines,
    rows_total,
    score_local,
    score_send,
    score_recv,
    ship_local,
    ship_send,
    ship_recv,
    plane_sem,
    gather_send,
    branch_col,
    branch_across,
    branch_beside,
    logits_col,
    logits_across,
    logits_beside,
    heads_send,
    near_sem,
    across_sem,
    pair_sem,
    part_local,
    part_send,
    dw_sem,
    do_sem,
    x_sem,
    swap_sem,
    *groups,
):
    row, across, beside = row_peers()
    rows, cols = lax.axis_size("row"), lax.axis_size("col")
    col, dp = lax.axis_index("col"), lax.axis_index("dp")
    other = 1 - dp
    far = (beside + rows // 2) % rows
    half = col % 2
    pair = col + 1 - 2 * half
    everyone, plane = ("dp", "row", "col"), ("row", "col")
    size, me = group_size_of(everyone), place_in(everyone)
    plane_size, plane_me = group_size_of(plane), place_in(plane)
    low, wide = jnp.bfloat16, jnp.float32
    copies, moved, parts, small, locals_ = [], [], [], [], []
    meet([device_at(everyone, (me + step) % size) for step in range(1, size)])

    def arrival(ref, sem):
        pltpu.make_async_copy(ref, ref, sem).wait()

    def ship(first, last):
        for step in range(first, last):
            to = (plane_me + step) % plane_size
            moved.append(
                send(
                    grads.at[to],
                    grads_own.at[plane_me],
                    ship_send.at[step],
                    ship_recv.at[step],
                    device_at(plane, to),
                )
            )

    def keep(src, dst):
        copy = pltpu.make_async_copy(src, dst, part_local.at[len(locals_)])
        copy.start()
        locals_.append(copy)

    rows_sum = sum_steps(partial, groups[0:11], copies)
    mix_sum = sum_steps(
        mix_part, groups[0:3] + groups[11:12] + groups[4:5] + groups[12:18], copies
    )
    line_local, line_send, line_recv = groups[18:]

    score_own = pltpu.make_async_copy(scores.at[me], scores_in.at[me], score_local)
    score_own.start()
    for step in range(1, size):
        to = (me + step) % size
        small.append(
            send(
                scores.at[to],
                scores_in.at[me],
                score_send.at[step],
                score_recv.at[step],
                device_at(everyone, to),
            )
        )
    rows_sum[0]()
    keep(grads.at[plane_me], grads_own.at[plane_me])
    ship(1, 5)
    tokens, model_width = x_all.shape
    depth = tokens // rows
    for block in range(rows):
        part = slice(block * depth, (block + 1) * depth)
        normed[part, :] = norm_rows(x_all[part, :].astype(wide), gain_one[...])[1]
    rows_sum[1]()
    rows_sum[2]()
    rows_sum[3]()
    score_own.wait()
    for copy in small:
        copy.wait()
    gate = gates[...]
    scored = jnp.concatenate(
        [scores_in[:, 0, :], jnp.zeros((128 - size, 128), wide)], axis=0
    ).T[: gate.shape[0], :]
    grad_logits = gate * (scored - jnp.sum(gate * scored, axis=1, keepdims=True))
    routed = jnp.dot(
        grad_logits, router_t[...].astype(wide), precision=highest, preferred_element_type=wide
    )
    logits[0] = jnp.concatenate(
        [grad_logits, jnp.zeros((128 - gate.shape[0], 128), wide)], axis=0
    ).T[: logits.shape[1], :]
    value = mixed[...]
    scale_two = lax.rsqrt(jnp.mean(value * value, axis=1, keepdims=True) + eps_norm)
    unit_two = value * scale_two
    rows_sum[4](rows_total)
    grad_normed = rows_total[...] + routed
    mix_row = jnp.sum(grad_normed * unit_two, axis=0, keepdims=True)
    grad_scaled = grad_normed * gain_two[...]
    grad_mixed = cot[...].astype(wide) + scale_two * (
        grad_scaled - unit_two * jnp.mean(grad_scaled * unit_two, axis=1, keepdims=True)
    )
    quarter = branch.shape[1]
    for m in range(2):
        branch[m] = (resid_scale * grad_mixed[m * quarter : (m + 1) * quarter, :]).astype(low)

    sent = []

    def pass_on(src, dst, sem, peer):
        sent.append(send(src, dst, gather_send.at[len(sent)], sem, peer))

    def origin(step):
        return (col + cols - step) % cols

    two_on, near, order = col_peers()
    for step, to in ((1, two_on), (2, near)):
        pass_on(branch.at[to // 2], branch_all.at[plane_me], branch_col.at[step], {"col": to})
        pass_on(logits.at[0], logits_all.at[plane_me], logits_col.at[step], {"col": to})
    keep(branch.at[col // 2], branch_all.at[plane_me])
    keep(logits.at[0], logits_all.at[plane_me])
    plans = (
        (branch.at[col // 2], branch_all, branch_col, branch_across, branch_beside),
        (logits.at[0], logits_all, logits_col, logits_across, logits_beside),
    )
    for step in range(cols):
        for mine, target, col_sem, side_sem, core_sem in plans:
            part = target.at[row * cols + order[step]]
            if step > 0:
                arrival(part, col_sem.at[step])
            if step == 1:
                pass_on(part, part, col_sem.at[3], {"col": near})
            source = mine if step == 0 else part
            pass_on(source, part, side_sem.at[step], {"row": across})
            pass_on(source, part, core_sem.at[step], {"row": beside})
    ship(5, 11)
    for step in range(cols):
        for mine, target, col_sem, side_sem, core_sem in plans:
            part = target.at[across * cols + order[step]]
            arrival(part, side_sem.at[step])
            pass_on(part, part, core_sem.at[cols + step], {"row": beside})
    for at, row_from in enumerate((beside, far)):
        for step in range(cols):
            for mine, target, col_sem, side_sem, core_sem in plans:
                arrival(target.at[row_from * cols + order[step]], core_sem.at[at * cols + step])
    for copy in locals_:
        copy.wait()
    for copy in copies:
        copy.wait_send()
    done = len(copies)
    mix_sum[0]()

    branch_rows = branch_all[...].reshape(tokens, model_width)
    kv_at = attended.shape[2]
    count = kv_at // HEAD_DIM
    grad_att[...] = nt(branch_rows, w_out_mine[...]).astype(low)
    rotated[:, kv_at : kv_at + HEAD_DIM] = jnp.zeros((tokens, HEAD_DIM), wide)
    values_grad[...] = jnp.zeros_like(values_grad)
    for block in range(rows):
        part = slice(block * depth, (block + 1) * depth)
        extent = key_extent(block, depth, tokens)
        allowed = visible(doc_col, doc_row, block, depth, extent)
        key = qkv[0:extent, kv_at : kv_at + HEAD_DIM]
        value_rows = qkv[0:extent, kv_at + HEAD_DIM : kv_at + 2 * HEAD_DIM]
        key_sum = jnp.zeros((extent, HEAD_DIM), wide)
        value_sum = jnp.zeros((extent, HEAD_DIM), wide)
        for head in range(count):
            lanes = slice(head * HEAD_DIM, (head + 1) * HEAD_DIM)
            query = qkv[part, lanes]
            probs = attend(query, key, allowed)
            grad_out = grad_att[part, lanes]
            grad_probs = nt(grad_out, value_rows)
            grad_scores = probs * (
                grad_probs - jnp.sum(probs * grad_probs, axis=1, keepdims=True)
            )
            grad_raw = (grad_scores * attn_scale).astype(low)
            rotated[part, lanes] = project(grad_raw, key)
            key_sum = key_sum + tn(grad_raw, query)
            value_sum = value_sum + tn(probs.astype(low), grad_out)
        rotated[0:extent, kv_at : kv_at + HEAD_DIM] += key_sum
        values_grad[0:extent, :] += value_sum
        if block == 1:
            mix_sum[1]()
    for at in range(2):
        piece = slice(at * 128, (at + 1) * 128)
        grad_qkv[:, piece] = turn(rotated[:, piece], cos_table[...], -sin_table[...]).astype(low)
    grad_qkv[:, 256:] = values_grad[...].astype(low)

    width = model_width // cols
    heads_out = attended[...].reshape(tokens, kv_at)
    for step in range(cols - 1, -1, -1):
        to = (col + step) % cols
        lanes = pl.ds(pl.multiple_of(to * width, width), width)
        dw_send[to] = tn(grad_qkv[...], normed[:, lanes]).astype(low)
        chunk = branch_all[:, :, lanes].reshape(tokens, width)
        do_send[to] = tn(heads_out, chunk).astype(low)
        if step > 0:
            parts.append(
                send(dw_send.at[to], dw_in.at[col], part_send.at[step], dw_sem.at[step], {"col": to})
            )
            parts.append(
                send(
                    do_send.at[to],
                    do_in.at[col],
                    part_send.at[cols + step],
                    do_sem.at[step],
                    {"col": to},
                )
            )
    keep(dw_send.at[col], dw_in.at[col])
    keep(do_send.at[col], do_in.at[col])

    rows_each = heads.shape[1]
    projection = w_mine[...].reshape(model_width, w_mine.shape[3])
    heads_sent = []

    def heads_on(src, dst, sem, peer):
        heads_sent.append(send(src, dst, heads_send.at[len(heads_sent)], sem, peer))

    halves = (1 - half, half)
    for at, row_to in enumerate((far, beside, across, row)):
        for which, part in enumerate(halves):
            slot = 2 * at + which
            first = pl.multiple_of((row_to * 2 + part) * rows_each, rows_each)
            heads[slot] = nt(grad_qkv[pl.ds(first, rows_each), :], projection).astype(low)
            if at < 2:
                heads_on(heads.at[slot], heads_near.at[slot], near_sem.at[slot], {"row": beside})
    def heads_sum(slot):
        arrival(heads_near.at[slot - 4], near_sem.at[slot - 4])
        return heads[slot].astype(wide) + heads_near[slot - 4].astype(wide)

    for which in range(2):
        heads_passed[which] = heads_sum(4 + which).astype(low)
        heads_on(
            heads_passed.at[which], heads_across.at[which], across_sem.at[which], {"row": across}
        )
    mix_sum[2]()
    ship(11, plane_size)
    router_sum = jnp.zeros((logits.shape[1], model_width), wide)
    group = plane_rows.shape[0]
    for first in range(0, plane_size, group):
        load = pltpu.make_async_copy(
            normed_all.at[pl.ds(dp * plane_size + first, group)], plane_rows, score_local
        )
        load.start()
        load.wait()
        for at in range(group):
            left = logits_all[first + at, :, 0 : 2 * quarter]
            for _ in range(3):
                piece = left.astype(low)
                left = left - piece.astype(wide)
                router_sum = router_sum + project(piece, plane_rows[at])
    router_pair[dp] = router_sum
    swaps = [
        send(router_pair.at[dp], router_pair.at[dp], swap_sem.at[0], swap_sem.at[1], {"dp": other})
    ]
    for which in range(2):
        grad_one = heads_sum(6 + which)
        arrival(heads_across.at[which], across_sem.at[which])
        grad_one = grad_one + heads_across[which].astype(wide)
        if which == 0:
            heads_passed[2] = grad_one.astype(low)
            heads_on(heads_passed.at[2], heads_pair, pair_sem, {"col": pair})
    arrival(heads_pair, pair_sem)
    grad_one = grad_one + heads_pair[...].astype(wide)
    first = (row * 2 + half) * rows_each
    x_rows = x_all[pl.ds(pl.multiple_of(first, rows_each), rows_each), :].astype(wide)
    scale_one = lax.rsqrt(jnp.mean(x_rows * x_rows, axis=1, keepdims=True) + eps_norm)
    unit_one = x_rows * scale_one
    norm_row = jnp.sum(grad_one * unit_one, axis=0, keepdims=True)
    each = rows_each // quarter
    grad_h = branch_all[pl.ds((row * 2 + half) * each, each)].reshape(rows_each, model_width)
    grad_scaled = grad_one * gain_one[...]
    grad_x = grad_h.astype(wide) * (1.0 / resid_scale) + scale_one * (
        grad_scaled - unit_one * jnp.mean(grad_scaled * unit_one, axis=1, keepdims=True)
    )
    for to in range(cols):
        x_send[to] = grad_x[:, to * width : (to + 1) * width].astype(low)
    for step in range(1, cols):
        to = (col + step) % cols
        swaps.append(
            send(
                x_send.at[to], x_grads.at[col], x_sem.at[step], x_sem.at[cols + step], {"col": to}
            )
        )
    keep(x_send.at[col], x_grads.at[col])
    steps = model_width // 128
    for at in range(steps):
        piece = slice(at * 128, (at + 1) * 128)
        lines[0, at : at + 1, :] = norm_row[:, piece]
        lines[0, steps + at : steps + at + 1, :] = mix_row[:, piece]
    home = pltpu.make_async_copy(lines.at[0], lines_all.at[me], line_local)
    home.start()
    for step in range(1, size):
        swaps.append(
            send(
                lines.at[0],
                lines_all.at[me],
                line_send.at[step],
                line_recv.at[step],
                device_at(everyone, (me + step) % size),
            )
        )
    for copy in locals_[3:]:
        copy.wait()
    for step in range(1, cols):
        arrival(dw_in.at[origin(step)], dw_sem.at[step])
        arrival(do_in.at[origin(step)], do_sem.at[step])
    for h in range(2):
        dw_pair[dp, h] = (dw_in[h].astype(wide) + dw_in[2 + h].astype(wide)).astype(low)
        do_pair[dp, h] = (do_in[h].astype(wide) + do_in[2 + h].astype(wide)).astype(low)
    swaps.append(
        send(dw_pair.at[dp], dw_pair.at[dp], swap_sem.at[2], swap_sem.at[3], {"dp": other})
    )
    swaps.append(
        send(do_pair.at[dp], do_pair.at[dp], swap_sem.at[4], swap_sem.at[5], {"dp": other})
    )
    mix_sum[3]()
    mix_sum[4](mix_out)
    home.wait()
    for copy in swaps:
        copy.wait()
    for copy in moved:
        copy.wait()
    for copy in copies[done:] + parts + sent + heads_sent:
        copy.wait_send()


def back(number, partial, mix_part, grads, scores, normed_all, *rest):
    mixed, _, _, _, _, _, x_all, w_mine, _, qkv, attended = rest[:11]
    cols, rows = lax.axis_size("col"), lax.axis_size("row")
    total, plane = group_size_of(("dp", "row", "col")), group_size_of(("row", "col"))
    low, wide = jnp.bfloat16, jnp.float32
    vmem = pl.BlockSpec(memory_space=pltpu.VMEM)
    shape, dma = jax.ShapeDtypeStruct, pltpu.SemaphoreType.DMA
    tokens, width = x_all.shape
    quarter, heads_width = attended.shape[1:]
    block = partial.shape[1:]
    part = width // cols
    qkv_width = w_mine.shape[3]
    lines = -(-2 * (width // 128) // 8) * 8
    return pl.pallas_call(
        back_kernel,
        out_shape=[
            shape(block, wide),
            shape(grads.shape, low),
            shape((2, 2, qkv_width, part), low),
            shape((2, 2, heads_width, part), low),
            shape((2, total, width), wide),
            shape((cols, tokens // (2 * rows), part), low),
            shape((total, lines, 128), wide),
        ],
        in_specs=[ANYWHERE] * 5 + [vmem] * len(rest),
        out_specs=[vmem, ANYWHERE, vmem, vmem, vmem, vmem, ANYWHERE],
        scratch_shapes=[
            pltpu.VMEM(scores.shape, wide),
            pltpu.VMEM((2, quarter, width), low),
            pltpu.VMEM((plane, quarter, width), low),
            pltpu.VMEM((1, total, 128), wide),
            pltpu.VMEM((plane, total, 128), wide),
            pltpu.VMEM((4,) + block, low),
            pltpu.VMEM((tokens, 256), wide),
            pltpu.VMEM((tokens, HEAD_DIM), wide),
            pltpu.VMEM((tokens, heads_width), low),
            pltpu.VMEM((tokens, qkv_width), low),
            pltpu.VMEM((tokens, width), low),
            pltpu.VMEM((8, tokens // (2 * rows), width), low),
            pltpu.VMEM((4, tokens // (2 * rows), width), low),
            pltpu.VMEM((2, tokens // (2 * rows), width), low),
            pltpu.VMEM((tokens // (2 * rows), width), low),
            pltpu.VMEM((3, tokens // (2 * rows), width), low),
            pltpu.VMEM((cols, qkv_width, part), low),
            pltpu.VMEM((cols, qkv_width, part), low),
            pltpu.VMEM((cols, heads_width, part), low),
            pltpu.VMEM((cols, heads_width, part), low),
            pltpu.VMEM((cols, tokens // (2 * rows), part), low),
            pltpu.VMEM((1, lines, 128), wide),
            pltpu.VMEM(block, wide),
            dma,
            dma((total,)),
            dma((total,)),
            dma,
            dma((plane,)),
            dma((plane,)),
            dma,
            dma((40,)),
            dma((cols,)),
            dma((cols,)),
            dma((2 * cols,)),
            dma((cols,)),
            dma((cols,)),
            dma((2 * cols,)),
            dma((8,)),
            dma((4,)),
            dma((2,)),
            dma,
            dma((8,)),
            dma((2 * cols,)),
            dma((cols,)),
            dma((cols,)),
            dma((2 * cols,)),
            dma((6,)),
        ]
        + sum_scratch(block)
        + [pltpu.VMEM((3 * cols,) + block, low)]
        + sum_scratch(block)[5:]
        + [dma, dma((total,)), dma((total,))],
        compiler_params=pltpu.CompilerParams(
            collective_id=number, has_side_effects=True, vmem_limit_bytes=62 * 2**20
        ),
        name="back" + str(number),
    )(partial, mix_part, grads, scores, normed_all, *rest)


def owned(
    hidden_in,
    norm_gain,
    w_query,
    w_key,
    w_value,
    w_out,
    mix_gain,
    w_router,
    w_gate,
    w_up,
    w_down,
    lengths,
    routes,
    mask,
    cotangent,
):
    everyone = ("dp", "row", "col")
    plane = ("row", "col")
    micro_count, tok_row, width_part = hidden_in.shape
    row_count = lax.axis_size("row")
    col_count = lax.axis_size("col")
    dp_count = lax.axis_size("dp")
    row_at = lax.axis_index("row")
    col_at = lax.axis_index("col")
    dp_at = lax.axis_index("dp")
    plane_count = row_count * col_count
    device_count = plane_count * dp_count
    plane_at = row_at * col_count + col_at
    model_width = width_part * col_count
    kv_here = w_key.shape[1] // HEAD_DIM
    group_size = w_query.shape[1] // w_key.shape[1]
    q_width = group_size * HEAD_DIM
    group_tokens = tok_row * row_count
    quarter = tok_row // col_count
    own_rows = micro_count * quarter
    experts_here, slice_width, ff_width = w_gate.shape
    down_slice = w_down.shape[1]
    experts_all = experts_here * dp_count
    expert_at = dp_at * plane_count + plane_at
    micro_at = col_at // kv_here
    half_at = col_at % kv_here

    masked_cot = cotangent * mask[:, :, None].astype(cotangent.dtype)

    w_qkv = jnp.concatenate(
        [
            w_query.reshape(width_part, kv_here, q_width),
            w_key.reshape(width_part, kv_here, HEAD_DIM),
            w_value.reshape(width_part, kv_here, HEAD_DIM),
        ],
        axis=2,
    ).transpose(1, 0, 2)
    qkv_width = q_width + 2 * HEAD_DIM
    picks = jnp.pad(routes.reshape(own_rows, TOP).T, ((0, 0), (0, 128 - own_rows)), constant_values=-1)
    doc_id, position = documents(lengths[:, 0][micro_at], group_tokens)
    sin_table, cos_table = (
        table[:, 0] for table in angles(position.astype(jnp.float32), HEAD_DIM)
    )
    doc_col = jnp.broadcast_to(doc_id[:, None], (group_tokens, 128))
    doc_row = jnp.broadcast_to(doc_id[None, :], (8, group_tokens))
    cos_lanes = jnp.tile(cos_table, (1, 4))
    sin_lanes = jnp.tile(jnp.concatenate([-sin_table, sin_table], axis=1), (1, 2))
    pad_experts = 128 - experts_all
    table = jnp.any(
        routes.reshape(own_rows, TOP)[:, :, None]
        == jnp.arange(experts_all, dtype=jnp.int32)[None, None, :],
        axis=1,
    )
    router_t = jnp.pad(w_router.T, ((0, pad_experts), (0, 0)))
    cot_own = masked_cot.reshape(own_rows, model_width)
    (
        x_micro,
        w_mine,
        w_out_mine,
        cot_all,
        normed_all,
        qkv,
        attended,
        mixed,
        gates_own,
        rows_part,
        mix_part,
        scores,
        grads,
        grads_down,
    ) = front(
        0,
        hidden_in,
        w_qkv.reshape(kv_here, dp_count, width_part // dp_count, qkv_width),
        w_out.reshape(dp_count, w_out.shape[0] // dp_count, w_out.shape[1]),
        picks,
        cot_own,
        (w_gate, w_up, w_down),
        (norm_gain[None], mix_gain[None]),
        (cos_lanes, sin_lanes),
        (doc_col, doc_row),
        (router_t, jnp.pad(table.astype(jnp.float32), ((0, 0), (0, pad_experts)))),
        q_width,
    )
    expert_mix, grads, qkv_sum, out_sum, router_grad, grad_input, lines = back(
        1,
        rows_part,
        mix_part,
        grads,
        scores,
        normed_all,
        mixed,
        cot_own,
        gates_own,
        router_t,
        norm_gain[None],
        mix_gain[None],
        x_micro,
        w_mine,
        w_out_mine,
        qkv,
        attended,
        cos_lanes,
        sin_lanes,
        doc_col,
        doc_row,
    )
    layer_out = (mixed + resid_scale * expert_mix).astype(jnp.bfloat16)
    out_gate = grads[:, :slice_width].astype(jnp.float32)
    out_up = grads[:, slice_width : 2 * slice_width].astype(jnp.float32)
    out_down = jnp.concatenate(
        [
            grads_down[:, at : at + down_slice]
            for at in range(0, grads_down.shape[1], down_slice)
        ],
        axis=2,
    ).astype(jnp.float32)
    grad_input = grad_input.reshape(micro_count, tok_row, width_part).astype(jnp.float32)
    qkv_sum = jnp.sum(qkv_sum.astype(jnp.float32), axis=0)
    out_sum = jnp.sum(out_sum.astype(jnp.float32), axis=0)
    router_grad = jnp.sum(router_grad, axis=0).T
    lines = jnp.sum(lines, axis=0)
    norm_grad = lines[: model_width // 128].reshape(-1)
    mix_grad = lines[model_width // 128 : 2 * (model_width // 128)].reshape(-1)
    grad_wq = qkv_sum[:, :q_width].reshape(-1, width_part).T
    grad_wk = qkv_sum[:, q_width : q_width + HEAD_DIM].reshape(-1, width_part).T
    grad_wv = qkv_sum[:, q_width + HEAD_DIM :].reshape(-1, width_part).T
    grad_wo = out_sum.reshape(w_out.shape)
    return (
        layer_out.reshape(micro_count, quarter, model_width),
        grad_input,
        norm_grad,
        grad_wq,
        grad_wk,
        grad_wv,
        grad_wo,
        mix_grad,
        router_grad,
        out_gate,
        out_up,
        out_down,
    )


def solution(mesh):
    dp_count, row_count, col_count = (mesh.shape[name] for name in ("dp", "row", "col"))

    def body(*args):
        hidden_in, w_key, w_gate = args[0], args[3], args[8]
        kv_here = w_key.shape[1] // HEAD_DIM
        one_each = w_gate.shape[0] == row_count * col_count
        pairs = hidden_in.shape[0] * kv_here == col_count
        sizes = (dp_count, row_count, col_count, kv_here) == (2, 4, 4, 2)
        return (owned if sizes and one_each and pairs else shards)(*args)

    placed = (
        P(None, ("dp", "row"), "col"),
        P(),
        P("col", "row"),
        P("col", "row"),
        P("col", "row"),
        P("row", "col"),
        P(),
        P(),
        P("dp", ("row", "col"), None),
        P("dp", ("row", "col"), None),
        P("dp", ("row", "col"), None),
        P(None, "dp", None),
        P(None, ("dp", "row", "col"), None),
        P(None, ("dp", "row", "col")),
        P(None, ("dp", "row", "col"), None),
    )
    return jax.shard_map(
        body,
        mesh=mesh,
        in_specs=placed,
        out_specs=(
            P(None, ("dp", "row", "col"), None),
            P(None, ("dp", "row"), "col"),
            P(),
            P("col", "row"),
            P("col", "row"),
            P("col", "row"),
            P("row", "col"),
            P(),
            P(),
            P("dp", ("row", "col"), None),
            P("dp", ("row", "col"), None),
            P("dp", ("row", "col"), None),
        ),
        check_vma=False,
    )
```
